32 devices in a mesh: wide: 8 (over z, y), narrow: 4 (over x, core).
Axes of the slice: x: 2, y: 2, z: 4, core: 2. Of those that a mesh axis runs over, the one named last changes fastest.
Arguments:
- layer_input: bfloat16 [8192, 1024], P('wide', 'narrow'), may hold values from -6 to 6
- out_grad: bfloat16 [8192, 1024], P('wide', 'narrow'), may hold values from -6 to 6
- lengths: int32 [8], P('wide'), may hold values from 256 to 1024, as said below
- plan: int32 [8, 2], P('wide'), may hold values from 0 to 3
- norm1_gain: float32 [1024], replicated, may hold values from 0.5 to 1.5
- w_query: bfloat16 [1024, 1024], P(None, 'narrow'), may hold values from -0.1875 to 0.1875
- w_key: bfloat16 [1024, 1024], P(None, 'narrow'), may hold values from -0.1875 to 0.1875
- w_value: bfloat16 [1024, 1024], P(None, 'narrow'), may hold values from -0.1875 to 0.1875
- w_gate: bfloat16 [1024, 1024], P(None, 'narrow'), may hold values from -0.1875 to 0.1875
- conv_query: float32 [4, 1024], P(None, 'narrow'), may hold values from -2.5 to 2.5
- conv_key: float32 [4, 1024], P(None, 'narrow'), may hold values from -2.5 to 2.5
- conv_value: float32 [4, 1024], P(None, 'narrow'), may hold values from -2.5 to 2.5
- persist_key: bfloat16 [16, 1024], P(None, 'narrow'), may hold values from -6 to 6
- persist_value: bfloat16 [16, 1024], P(None, 'narrow'), may hold values from -3 to 3
- mem_w1: bfloat16 [1024, 4096], P(None, 'narrow'), may hold values from -1.5 to 1.5
- mem_w2: bfloat16 [4096, 1024], P('narrow'), may hold values from -0.09375 to 0.09375
- w_out: bfloat16 [1024, 1024], P('narrow'), may hold values from -1.5 to 1.5
- norm2_gain: float32 [1024], replicated, may hold values from 0.5 to 1.5
- ffn_gate: bfloat16 [1024, 4096], P(None, 'narrow'), may hold values from -0.1875 to 0.1875
- ffn_up: bfloat16 [1024, 4096], P(None, 'narrow'), may hold values from -0.1875 to 0.1875
- ffn_down: bfloat16 [4096, 1024], P('narrow'), may hold values from -0.09375 to 0.09375
Outputs:
- layer_output: bfloat16 [8192, 1024], P('wide', 'narrow')
- input_grad: float32 [8192, 1024], P('wide', 'narrow')
- grad_norm1_gain: float32 [1024], P('narrow')
- grad_w_query: float32 [1024, 1024], P(None, 'narrow')
- grad_w_key: float32 [1024, 1024], P(None, 'narrow')
- grad_w_value: float32 [1024, 1024], P(None, 'narrow')
- grad_w_gate: float32 [1024, 1024], P(None, 'narrow')
- grad_conv_query: float32 [4, 1024], P(None, 'narrow')
- grad_conv_key: float32 [4, 1024], P(None, 'narrow')
- grad_conv_value: float32 [4, 1024], P(None, 'narrow')
- grad_persist_key: float32 [16, 1024], P(None, 'narrow')
- grad_persist_value: float32 [16, 1024], P(None, 'narrow')
- grad_mem_w1: float32 [1024, 4096], P(None, 'narrow')
- grad_mem_w2: float32 [4096, 1024], P('narrow')
- grad_w_out: float32 [1024, 1024], P('narrow')
- grad_norm2_gain: float32 [1024], P('narrow')
- grad_ffn_gate: float32 [1024, 4096], P(None, 'narrow')
- grad_ffn_up: float32 [1024, 4096], P(None, 'narrow')
- grad_ffn_down: float32 [4096, 1024], P('narrow')
The draws below stay inside these ranges and needn't reach their ends.
Inputs may be any that keep to these rules, and one draw needn't show every extreme that they name: lengths[s] counts the valid slots of sequence s, which are its first ones; some sequence fills all 1024 slots.
All inputs are finite; a program needn't handle non-finite values.
Results may differ from the reference program's by a relative error of at most 0.019.
Values may be sent and summed in bfloat16 or wider, within the bound.
A program may use at most 256 MiB of HBM per device.

```python
from functools import partial
import jax
import jax.numpy as jnp
from jax import lax

D = 1024
HEADS = 16
HD = 64
MH = 4096
FF = 4096
NP = 16
KW = 4
STRETCH = 512
NCH = 2
SEQS = 8
TOKENS = 8192


def draw_lengths(key, part):
    key_one, key_two = jax.random.split(key)
    drawn = jax.random.randint(key_one, (SEQS,), STRETCH // 2, NCH * STRETCH + 1)
    chosen = jax.random.randint(key_two, (), 0, SEQS)
    return jnp.where(jnp.arange(SEQS) == chosen, NCH * STRETCH, drawn).astype(jnp.int32)


def plant(values, own_key, low, largest):
    longest = values.shape.index(max(values.shape))
    spots = []
    for shift in (0, 1):
        where = [jax.random.randint(jax.random.fold_in(own_key, axis), (), 0, length) for axis, length in enumerate(values.shape)]
        where[longest] = (where[longest] + shift) % values.shape[longest]
        spots.append(tuple(where))
    return values.at[spots[0]].set(low).at[spots[1]].set(largest)


def block_levels(stream_key, shape, pieces, least, top_value):
    factor_of, own = 1.0, jax.random.fold_in(stream_key, 6)
    for axis_at, parts in pieces:
        heights = jnp.exp(jax.random.uniform(jax.random.fold_in(own, axis_at), (parts,), jnp.float32, least / len(pieces), top_value / len(pieces)))
        factor_of = factor_of * jnp.repeat(heights, shape[axis_at] // parts).reshape([-1 if axis == axis_at else 1 for axis in range(len(shape))])
    return factor_of


def bell_draw(rng, dims, width, limit, cuts=(), held_as=jnp.bfloat16):
    values = width * jax.random.normal(rng, dims, jnp.float32)
    if cuts:
        values = values * block_levels(rng, dims, cuts, -0.22, 0.18)
    return jnp.clip(values, -limit, limit).astype(held_as)


def setup_inputs(seed: int = 0) -> dict:
    arg_keys = jax.random.split(jax.random.key(seed), 22)
    return {
        "layer_input": bell_draw(arg_keys[0], (TOKENS, D), 1.0, 6.0, ((0, 8), (1, 4))),
        "out_grad": bell_draw(arg_keys[1], (TOKENS, D), 1.0, 6.0, ((0, 8), (1, 4))),
        "lengths": draw_lengths(jax.random.fold_in(arg_keys[21], 71), 0),
        "plan": plant(jax.random.randint(arg_keys[3], (SEQS, NCH), 0, 4), jax.random.fold_in(arg_keys[3], 1), 0, 3).astype(jnp.int32),
        "norm1_gain": jnp.clip(1.0 + 0.1 * jax.random.normal(arg_keys[4], (D,), jnp.float32), 0.5, 1.5),
        "w_query": bell_draw(arg_keys[5], (D, D), D ** -0.5, 0.1875, ((1, 4),)),
        "w_key": bell_draw(arg_keys[6], (D, D), D ** -0.5, 0.1875, ((1, 4),)),
        "w_value": bell_draw(arg_keys[7], (D, D), D ** -0.5, 0.1875, ((1, 4),)),
        "w_gate": bell_draw(arg_keys[8], (D, D), D ** -0.5, 0.1875, ((1, 4),)),
        "conv_query": bell_draw(arg_keys[9], (KW, D), 0.5, 2.5, ((1, 4),), jnp.float32),
        "conv_key": bell_draw(arg_keys[10], (KW, D), 0.5, 2.5, ((1, 4),), jnp.float32),
        "conv_value": bell_draw(arg_keys[11], (KW, D), 0.5, 2.5, ((1, 4),), jnp.float32),
        "persist_key": bell_draw(arg_keys[12], (NP, D), 1.0, 6.0, ((1, 4),)),
        "persist_value": bell_draw(arg_keys[13], (NP, D), 0.5, 3.0, ((1, 4),)),
        "mem_w1": bell_draw(arg_keys[14], (D, MH), 16 ** -0.5, 1.5, ((1, 4),)),
        "mem_w2": bell_draw(arg_keys[15], (MH, D), MH ** -0.5, 0.09375, ((0, 4),)),
        "w_out": bell_draw(arg_keys[16], (D, D), 16 ** -0.5, 1.5, ((0, 4),)),
        "norm2_gain": jnp.clip(1.0 + 0.1 * jax.random.normal(arg_keys[17], (D,), jnp.float32), 0.5, 1.5),
        "ffn_gate": bell_draw(arg_keys[18], (D, FF), D ** -0.5, 0.1875, ((1, 4),)),
        "ffn_up": bell_draw(arg_keys[19], (D, FF), D ** -0.5, 0.1875, ((1, 4),)),
        "ffn_down": bell_draw(arg_keys[20], (FF, D), FF ** -0.5, 0.09375, ((0, 4),)),
    }


epsilon = 1e-06
head_floor = 1.0
score_scale = 12.0

@jax.custom_vjp
def low(v):
    return lax.optimization_barrier(v.astype(jnp.bfloat16)).astype(jnp.float32)

@jax.custom_vjp
def low_back(v):
    return v

def low_keep(v):
    return (low(v), None)

def low_pass(kept, grad):
    return (grad,)

def back_keep(v):
    return (v, None)

def back_low(kept, grad):
    return (low(grad),)
low.defvjp(low_keep, low_pass)
low_back.defvjp(back_keep, back_low)

def matmul(left_side, right_side):
    return jnp.dot(left_side, right_side, precision=lax.Precision.HIGHEST, preferred_element_type=jnp.float32)

def silu_grad(values):
    logistic = jax.nn.sigmoid(values)
    return logistic * (1.0 + values * (1.0 - logistic))

def plan_rates(level_now):
    return (0.1 * jnp.exp2(level_now), 0.9 - 0.2 * level_now, 0.02 + 0.05 * level_now)

def rms_scale(values, gain_vec):
    return values * lax.rsqrt(lax.optimization_barrier(jnp.mean(values * values, axis=1, keepdims=True)) + epsilon) * gain_vec

def head_norm(values):
    row_count = values.shape[0]
    grouped = values.reshape(row_count, -1, HD)
    grouped = grouped * lax.rsqrt(lax.optimization_barrier(jnp.sum(grouped * grouped, axis=2, keepdims=True)) + head_floor)
    return grouped.reshape(row_count, -1)

def shift_down(values, offset):
    return jnp.concatenate([jnp.zeros((offset, values.shape[1]), values.dtype), values[:-offset]], axis=0)

def causal_conv(values, conv_taps):
    result = values * conv_taps[0]
    for offset in range(1, KW):
        result = result + shift_down(values, offset) * conv_taps[offset]
    return result

def visible(mask_rows):
    row_width = mask_rows.shape[0]
    places = jnp.arange(row_width)
    valid_keys = mask_rows[None, :] > 0.5
    causal = (places[None, :] <= places[:, None]) & valid_keys
    memory_seen = jnp.broadcast_to(valid_keys, (row_width, row_width))
    persistent = jnp.ones((row_width, NP), dtype=bool)
    return jnp.concatenate([persistent, memory_seen, causal], axis=1)

def memory_step(carried, block_in):
    weight_one, weight_two, moment_one, moment_two = carried
    key_rows, query_rows, value_rows, mask_rows, level_now = block_in
    step_size, momentum, forget = plan_rates(level_now)
    first_low = low(weight_one)
    second_low = low(weight_two)
    hidden_pre = low_back(matmul(key_rows, first_low))
    hidden_act = low(jax.nn.silu(hidden_pre))
    query_pre = low_back(matmul(query_rows, first_low))
    query_act = low(jax.nn.silu(query_pre))
    predicted = matmul(hidden_act, second_low)
    retrieved = matmul(query_act, second_low)
    mismatch = low_back(low((predicted - value_rows) * mask_rows[:, None] / STRETCH))
    through = low_back(matmul(mismatch, second_low.T))
    blended = low(through * silu_grad(hidden_pre))
    grad_one = low_back(matmul(key_rows.T, blended))
    grad_two = low_back(matmul(hidden_act.T, mismatch))
    moment_one = momentum * moment_one - step_size * grad_one
    moment_two = momentum * moment_two - step_size * grad_two
    weight_one = (1.0 - forget) * weight_one + moment_one
    weight_two = (1.0 - forget) * weight_two + moment_two
    return ((weight_one, weight_two, moment_one, moment_two), low_back(low(retrieved)))

def attend_block(pers_keys, pers_values, key_weight, value_weight, block_in):
    query_rows, key_rows, value_rows, memory_rows, mask_rows = block_in
    memory_keys = low(head_norm(low_back(matmul(memory_rows, key_weight))))
    memory_values = low(low_back(matmul(memory_rows, value_weight)))
    all_keys = jnp.concatenate([pers_keys, memory_keys, key_rows], axis=0)
    all_values = jnp.concatenate([pers_values, memory_values, value_rows], axis=0)
    row_width = query_rows.shape[0]
    query_heads = query_rows.reshape(row_width, HEADS, HD)
    key_heads = all_keys.reshape(-1, HEADS, HD)
    value_heads = all_values.reshape(-1, HEADS, HD)
    scores = low_back(score_scale * jnp.einsum('qhd,khd->hqk', query_heads, key_heads, precision=lax.Precision.HIGHEST))
    scores = jnp.where(visible(mask_rows)[None], scores, -1e+30)
    row_peak = lax.optimization_barrier(jnp.max(scores, axis=2, keepdims=True))
    exponent = jnp.exp(scores - row_peak)
    prob_rows = low(exponent / lax.optimization_barrier(jnp.sum(exponent, axis=2, keepdims=True)))
    mixed_rows = low_back(jnp.einsum('hqk,khd->qhd', prob_rows, value_heads, precision=lax.Precision.HIGHEST))
    return mixed_rows.reshape(row_width, -1)

def layer(params, sequence, row_mask, levels):
    gain_one, query_weight, key_weight, value_weight, gate_weight, query_taps, key_taps, value_taps, pers_key, pers_value, memory_one, memory_two, out_weight, gain_two, ffn_gate_w, ffn_up_w, ffn_down_w = params
    normed = low(rms_scale(sequence, gain_one))
    query_pre = low_back(matmul(normed, query_weight))
    key_pre = low_back(matmul(normed, key_weight))
    value_pre = low_back(matmul(normed, value_weight))
    gate_pre = low_back(matmul(normed, gate_weight))
    query_rows = low(head_norm(jax.nn.silu(causal_conv(query_pre, query_taps))))
    key_rows = low(head_norm(jax.nn.silu(causal_conv(key_pre, key_taps))))
    value_rows = low(jax.nn.silu(causal_conv(value_pre, value_taps)))
    blocks = row_mask.shape[0] // STRETCH

    def to_blocks(values):
        return values.reshape(blocks, STRETCH, values.shape[1])
    block_mask = row_mask.reshape(blocks, STRETCH)
    start = (memory_one, memory_two, jnp.zeros_like(memory_one), jnp.zeros_like(memory_two))
    final_state, recalled = lax.scan(jax.checkpoint(memory_step), start, (to_blocks(key_rows), to_blocks(query_rows), to_blocks(value_rows), block_mask, levels))
    pers_keys = low(head_norm(pers_key))
    attend = jax.checkpoint(partial(attend_block, pers_keys, pers_value, key_weight, value_weight))
    mixed = lax.map(attend, (to_blocks(query_rows), to_blocks(key_rows), to_blocks(value_rows), recalled, block_mask))
    mixed = mixed.reshape(-1, D)
    gated = low(mixed * jax.nn.sigmoid(gate_pre))
    branch = low_back(matmul(gated, out_weight))
    middle = sequence + branch
    normed_two = low(rms_scale(middle, gain_two))
    ffn_pre = low_back(matmul(normed_two, ffn_gate_w))
    up_pre = low_back(matmul(normed_two, ffn_up_w))
    hidden = low(jax.nn.silu(ffn_pre) * up_pre)
    return middle + matmul(hidden, ffn_down_w)

def add_pair(left_side, right_side):
    return left_side + right_side

def reference(layer_input, out_grad, lengths, plan, norm1_gain, w_query, w_key, w_value, w_gate, conv_query, conv_key, conv_value, persist_key, persist_value, mem_w1, mem_w2, w_out, norm2_gain, ffn_gate, ffn_up, ffn_down):
    params = tuple((tensor.astype(jnp.float32) for tensor in (norm1_gain, w_query, w_key, w_value, w_gate, conv_query, conv_key, conv_value, persist_key, persist_value, mem_w1, mem_w2, w_out, norm2_gain, ffn_gate, ffn_up, ffn_down)))
    span = NCH * STRETCH
    inputs = layer_input.astype(jnp.float32).reshape(SEQS, span, D)
    cotangents = out_grad.astype(jnp.float32).reshape(SEQS, span, D)
    places = jnp.arange(span, dtype=jnp.int32)

    def one_sequence(totals, block_in):
        sequence, cotangent, length_now, level_row = block_in
        row_mask = (places < length_now.astype(jnp.int32)).astype(jnp.float32)
        levels = level_row.astype(jnp.float32)

        def forward(weights, rows_in):
            return layer(weights, rows_in, row_mask, levels)
        result, pullback = jax.vjp(forward, params, sequence)
        weight_grads, input_grads = pullback(cotangent)
        totals = jax.tree.map(add_pair, totals, weight_grads)
        return (totals, (result, input_grads))
    zeros_start = jax.tree.map(jnp.zeros_like, params)
    totals, (outputs, input_grads) = lax.scan(one_sequence, zeros_start, (inputs, cotangents, lengths, plan))
    return (outputs.reshape(-1, D).astype(jnp.bfloat16), input_grads.reshape(-1, D), totals[0], totals[1], totals[2], totals[3], totals[4], totals[5], totals[6], totals[7], totals[8], totals[9], totals[10], totals[11], totals[12], totals[13], totals[14], totals[15], totals[16])
```

```python
import jax
import jax.numpy as jnp
from jax import lax
from jax.sharding import PartitionSpec as P

HD = 64
NP = 16
KW = 4
STRETCH = 512

epsilon = 1e-06
head_floor = 1.0
score_scale = 12.0
bf16 = jnp.bfloat16
f32 = jnp.float32


def product(left_side, right_side):
    return jnp.dot(left_side, right_side, preferred_element_type=f32)


def inner_left(left_side, right_side):
    return lax.dot_general(
        left_side, right_side, (((0,), (0,)), ((), ())), preferred_element_type=f32
    )


def inner_right(left_side, right_side):
    return lax.dot_general(
        left_side, right_side, (((1,), (1,)), ((), ())), preferred_element_type=f32
    )


def silu_grad(values):
    logistic = jax.nn.sigmoid(values)
    return logistic * (1.0 + values * (1.0 - logistic))


def silu_curve(values):
    logistic = jax.nn.sigmoid(values)
    logistic_slope = logistic * (1.0 - logistic)
    return logistic_slope * (1.0 + values * (1.0 - logistic)) + logistic * (
        1.0 - logistic - values * logistic_slope
    )


def plan_rates(level_now):
    return (0.1 * jnp.exp2(level_now), 0.9 - 0.2 * level_now, 0.02 + 0.05 * level_now)


def head_sums(values):
    width = values.shape[1]
    places = jnp.arange(width) // HD
    same_head = (places[:, None] == places[None, :]).astype(f32)
    return jnp.dot(
        values, same_head, precision=lax.Precision.HIGHEST, preferred_element_type=f32
    )


def head_norm(values):
    inv_norm = lax.rsqrt(head_sums(values * values) + head_floor)
    return (values * inv_norm, inv_norm)


def head_back(grad_rows, unit_rows, inv_norm):
    return (grad_rows - unit_rows * head_sums(grad_rows * unit_rows)) * inv_norm


def norm_back(grad_rows, unit_rows, inv_rows, gain_vec):
    scaled = grad_rows * gain_vec
    return inv_rows * (scaled - unit_rows * jnp.mean(scaled * unit_rows, axis=1, keepdims=True))


def shift_down(values, offset):
    return jnp.concatenate(
        [jnp.zeros((offset, values.shape[1]), values.dtype), values[:-offset]], axis=0
    )


def shift_up(values, offset):
    return jnp.concatenate(
        [values[offset:], jnp.zeros((offset, values.shape[1]), values.dtype)], axis=0
    )


def causal_conv(values, conv_taps):
    result = values * conv_taps[0]
    for offset in range(1, KW):
        result = result + shift_down(values, offset) * conv_taps[offset]
    return result


def conv_back(grad_rows, values, conv_taps):
    back_values = grad_rows * conv_taps[0]
    tap_grads = [jnp.sum(grad_rows * values, axis=0)]
    for offset in range(1, KW):
        back_values = back_values + shift_up(grad_rows, offset) * conv_taps[offset]
        tap_grads.append(jnp.sum(grad_rows * shift_down(values, offset), axis=0))
    return (back_values, jnp.stack(tap_grads, axis=0))


def visible(mask_rows):
    row_width = mask_rows.shape[0]
    places = jnp.arange(row_width)
    valid_keys = mask_rows[None, :] > 0.5
    causal = (places[None, :] <= places[:, None]) & valid_keys
    memory_seen = jnp.broadcast_to(valid_keys, (row_width, row_width))
    persistent = jnp.ones((row_width, NP), dtype=bool)
    return jnp.concatenate([persistent, memory_seen, causal], axis=1)


def gather_columns(values):
    return lax.all_gather(values, "narrow", axis=1, tiled=True)


def scatter_columns(values):
    return lax.psum_scatter(
        values.astype(bf16), "narrow", scatter_dimension=1, tiled=True
    ).astype(f32)


def sum_wide(values):
    return [lax.psum(v.astype(bf16), "wide").astype(f32) for v in values]


def body(
    layer_input,
    out_grad,
    lengths,
    plan,
    norm1_gain,
    w_query,
    w_key,
    w_value,
    w_gate,
    conv_query,
    conv_key,
    conv_value,
    persist_key,
    persist_value,
    mem_w1,
    mem_w2,
    w_out,
    norm2_gain,
    ffn_gate,
    ffn_up,
    ffn_down,
):
    tokens_here = layer_input.shape[0]
    local_width = w_query.shape[1]
    heads_here = local_width // HD
    blocks = tokens_here // STRETCH
    places = jnp.arange(tokens_here)
    row_mask = (places < lengths[0]).astype(f32)
    block_mask = row_mask.reshape(blocks, STRETCH)
    levels = plan[0].astype(f32)
    column_start = lax.axis_index("narrow") * local_width

    def rows_of(values, b):
        return values[b * STRETCH : (b + 1) * STRETCH]

    whole_x = gather_columns(layer_input).astype(f32)
    whole_dy = gather_columns(out_grad)
    inv_one = lax.rsqrt(jnp.mean(whole_x * whole_x, axis=1, keepdims=True) + epsilon)
    unit_one = whole_x * inv_one
    normed_one = (unit_one * norm1_gain).astype(bf16)
    key_pre = product(normed_one, w_key)
    query_pre = product(normed_one, w_query)
    value_pre = product(normed_one, w_value)
    gate_pre = product(normed_one, w_gate)
    key_conv = causal_conv(key_pre, conv_key)
    query_conv = causal_conv(query_pre, conv_query)
    value_conv = causal_conv(value_pre, conv_value)
    key_unit, key_inv = head_norm(jax.nn.silu(key_conv))
    query_unit, query_inv = head_norm(jax.nn.silu(query_conv))
    query_low = query_unit.astype(bf16)
    key_low = key_unit.astype(bf16)
    value_low = jax.nn.silu(value_conv).astype(bf16)

    weight_one, weight_two = mem_w1.astype(f32), mem_w2.astype(f32)
    moment_one = moment_two = None
    saved = []
    for b in range(blocks):
        step_size, momentum, forget = plan_rates(levels[b])
        kept = {"first": weight_one.astype(bf16), "second": weight_two.astype(bf16)}
        mask_rows = block_mask[b][:, None]
        if b < blocks - 1:
            key_rows = gather_columns(rows_of(key_low, b))
            hidden_pre = product(key_rows, kept["first"])
            hidden_act = jax.nn.silu(hidden_pre).astype(bf16)
            predicted = scatter_columns(product(hidden_act, kept["second"]))
            mismatch_here = (
                (predicted - rows_of(value_low, b).astype(f32)) * (mask_rows / STRETCH)
            ).astype(bf16)
            mismatch = gather_columns(mismatch_here)
        query_rows = gather_columns(rows_of(query_low, b))
        query_mem = product(query_rows, kept["first"])
        query_act = jax.nn.silu(query_mem).astype(bf16)
        retrieved = scatter_columns(product(query_act, kept["second"]))
        kept["recalled"] = gather_columns(retrieved.astype(bf16))
        kept.update(query_rows=query_rows, query_mem=query_mem, query_act=query_act)
        if b < blocks - 1:
            through = inner_right(mismatch, kept["second"])
            blended = (through * silu_grad(hidden_pre)).astype(bf16)
            grad_one = inner_left(key_rows, blended)
            grad_two = inner_left(hidden_act, mismatch)
            if moment_one is None:
                moment_one, moment_two = -step_size * grad_one, -step_size * grad_two
            else:
                moment_one = momentum * moment_one - step_size * grad_one
                moment_two = momentum * moment_two - step_size * grad_two
            weight_one = (1.0 - forget) * weight_one + moment_one
            weight_two = (1.0 - forget) * weight_two + moment_two
            kept.update(
                key_rows=key_rows,
                hidden_pre=hidden_pre,
                hidden_act=hidden_act,
                mismatch=mismatch,
                through=through,
                blended=blended,
            )
        saved.append(kept)

    pers_unit, pers_inv = head_norm(persist_key.astype(f32))
    pers_low = pers_unit.astype(bf16)

    def block_scores(b):
        recalled = saved[b]["recalled"]
        mem_unit, mem_inv = head_norm(product(recalled, w_key))
        mem_value = product(recalled, w_value).astype(bf16)
        all_keys = jnp.concatenate(
            [pers_low, mem_unit.astype(bf16), rows_of(key_low, b)], axis=0
        ).reshape(-1, heads_here, HD)
        all_values = jnp.concatenate(
            [persist_value, mem_value, rows_of(value_low, b)], axis=0
        ).reshape(-1, heads_here, HD)
        query_heads = rows_of(query_low, b).reshape(STRETCH, heads_here, HD)
        scores = score_scale * jnp.einsum(
            "qhd,khd->hqk", query_heads, all_keys, preferred_element_type=f32
        )
        scores = jnp.where(visible(block_mask[b])[None], scores, -1e30)
        return (mem_unit, mem_inv, all_keys, all_values, query_heads, scores)

    mixed_list = []
    for b in range(blocks):
        mem_unit, mem_inv, all_keys, all_values, query_heads, scores = block_scores(b)
        row_peak = jnp.max(scores, axis=2, keepdims=True)
        exponent = jnp.exp(scores - row_peak)
        row_total = jnp.sum(exponent, axis=2, keepdims=True)
        prob_low = (exponent / row_total).astype(bf16)
        mixed_list.append(
            jnp.einsum(
                "hqk,khd->qhd", prob_low, all_values, preferred_element_type=f32
            ).reshape(STRETCH, local_width)
        )
        saved[b].update(
            log_total=row_peak + jnp.log(row_total),
            mem_unit=mem_unit,
            mem_inv=mem_inv,
            all_keys=all_keys,
            all_values=all_values,
            query_heads=query_heads,
        )
    mixed_all = jnp.concatenate(mixed_list, axis=0)
    gate_sig = jax.nn.sigmoid(gate_pre)
    gated = (mixed_all * gate_sig).astype(bf16)
    branch_here = scatter_columns(product(gated, w_out))
    branch_full = gather_columns(branch_here.astype(bf16)).astype(f32)
    middle = whole_x + branch_full
    middle_here = layer_input.astype(f32) + branch_here
    inv_two = lax.rsqrt(jnp.mean(middle * middle, axis=1, keepdims=True) + epsilon)
    unit_two = middle * inv_two
    normed_two = (unit_two * norm2_gain).astype(bf16)
    ffn_pre = product(normed_two, ffn_gate)
    up_pre = product(normed_two, ffn_up)
    ffn_sig = jax.nn.sigmoid(ffn_pre)
    hidden_low = (ffn_pre * ffn_sig * up_pre).astype(bf16)
    back_hidden = inner_right(whole_dy, ffn_down)
    back_up_low = (back_hidden * ffn_pre * ffn_sig).astype(bf16)
    back_ffn_low = (back_hidden * up_pre * silu_grad(ffn_pre)).astype(bf16)
    back_normed_two = inner_right(back_ffn_low, ffn_gate) + inner_right(back_up_low, ffn_up)
    gain_two_part = jnp.sum(back_normed_two * unit_two, axis=0)
    middle_part = norm_back(back_normed_two, unit_two, inv_two, norm2_gain)
    back_middle_here = scatter_columns(middle_part)
    grad_ffn_down = inner_left(hidden_low, whole_dy)
    grad_ffn_gate = inner_left(normed_two, back_ffn_low)
    grad_ffn_up = inner_left(normed_two, back_up_low)
    ffn_here = scatter_columns(product(hidden_low, ffn_down))
    layer_output = (middle_here + ffn_here).astype(bf16)
    back_middle_here = back_middle_here + out_grad.astype(f32)
    back_branch = gather_columns(back_middle_here.astype(bf16))
    grad_ffn_gate, grad_ffn_up, grad_ffn_down = sum_wide(
        [grad_ffn_gate, grad_ffn_up, grad_ffn_down]
    )
    grad_w_out = inner_left(gated, back_branch)
    back_gated = inner_right(back_branch, w_out)
    back_mixed_low = (back_gated * gate_sig).astype(bf16)
    back_gate_low = (back_gated * mixed_all * gate_sig * (1.0 - gate_sig)).astype(bf16)

    back_recalled_parts = []
    mem_key_grad = mem_value_grad = 0.0
    pers_key_acc = grad_persist_value = 0.0
    back_query_att, back_key_att, back_value_att = [], [], []
    for b in range(blocks):
        kept = saved[b]
        scores = score_scale * jnp.einsum(
            "qhd,khd->hqk", kept["query_heads"], kept["all_keys"], preferred_element_type=f32
        )
        scores = jnp.where(visible(block_mask[b])[None], scores, -1e30)
        prob_rows = jnp.exp(scores - kept["log_total"])
        prob_low = prob_rows.astype(bf16)
        back_heads = rows_of(back_mixed_low, b).reshape(STRETCH, heads_here, HD)
        back_all_values = jnp.einsum(
            "hqk,qhd->khd", prob_low, back_heads, preferred_element_type=f32
        )
        back_probs = jnp.einsum(
            "qhd,khd->hqk", back_heads, kept["all_values"], preferred_element_type=f32
        )
        back_scores = (
            prob_rows * (back_probs - jnp.sum(prob_rows * back_probs, axis=2, keepdims=True))
        ).astype(bf16)
        back_query = score_scale * jnp.einsum(
            "hqk,khd->qhd", back_scores, kept["all_keys"], preferred_element_type=f32
        )
        back_all_keys = score_scale * jnp.einsum(
            "hqk,qhd->khd", back_scores, kept["query_heads"], preferred_element_type=f32
        )
        back_all_keys = back_all_keys.reshape(-1, local_width)
        back_all_values = back_all_values.reshape(-1, local_width)
        back_mem_key = head_back(
            back_all_keys[NP : NP + STRETCH], kept["mem_unit"], kept["mem_inv"]
        ).astype(bf16)
        back_mem_value = back_all_values[NP : NP + STRETCH].astype(bf16)
        back_recalled_parts.append(
            inner_right(back_mem_key, w_key) + inner_right(back_mem_value, w_value)
        )
        mem_key_grad = mem_key_grad + inner_left(kept["recalled"], back_mem_key)
        mem_value_grad = mem_value_grad + inner_left(kept["recalled"], back_mem_value)
        pers_key_acc = pers_key_acc + back_all_keys[:NP]
        grad_persist_value = grad_persist_value + back_all_values[:NP]
        back_query_att.append(back_query.reshape(STRETCH, local_width))
        back_key_att.append(back_all_keys[NP + STRETCH :])
        back_value_att.append(back_all_values[NP + STRETCH :])
    grad_persist_key = head_back(pers_key_acc, pers_unit, pers_inv)

    cot_one = cot_two = mom_one = mom_two = None
    key_total, query_total, value_total = [None] * blocks, [None] * blocks, [None] * blocks
    for b in reversed(range(blocks)):
        kept = saved[b]
        step_size, momentum, forget = plan_rates(levels[b])
        first_low, second_low = kept["first"], kept["second"]
        back_recalled = gather_columns(scatter_columns(back_recalled_parts[b]).astype(bf16))
        new_one = new_two = None
        if cot_one is None:
            key_total[b], value_total[b] = back_key_att[b], back_value_att[b]
        else:
            key_rows, hidden_pre = kept["key_rows"], kept["hidden_pre"]
            hidden_slope = silu_grad(hidden_pre)
            total_one = cot_one if mom_one is None else mom_one + cot_one
            total_two = cot_two if mom_two is None else mom_two + cot_two
            back_g1 = (-step_size * total_one).astype(bf16)
            back_g2 = (-step_size * total_two).astype(bf16)
            back_blended = product(key_rows, back_g1)
            back_through = (back_blended * hidden_slope).astype(bf16)
            mismatch_part = product(kept["hidden_act"], back_g2) + product(
                back_through, second_low
            )
            mismatch_low = scatter_columns(mismatch_part).astype(bf16)
            back_mismatch = gather_columns(mismatch_low)
            key_part = inner_right(kept["blended"], back_g1)
            back_hidden_act = inner_right(kept["mismatch"], back_g2)
            extra_pre = back_blended * kept["through"] * silu_curve(hidden_pre)
            new_one = (1.0 - forget) * cot_one
            new_two = (1.0 - forget) * cot_two + inner_left(back_through, kept["mismatch"])
        back_query_act = inner_right(back_recalled, second_low)
        back_query_pre = (back_query_act * silu_grad(kept["query_mem"])).astype(bf16)
        query_part = inner_right(back_query_pre, first_low)
        one_term = inner_left(kept["query_rows"], back_query_pre)
        two_term = inner_left(kept["query_act"], back_recalled)
        new_one = one_term if new_one is None else new_one + one_term
        new_two = two_term if new_two is None else new_two + two_term
        if cot_one is not None:
            scale_rows = (block_mask[b] / STRETCH).astype(bf16)[:, None]
            back_pred = back_mismatch * scale_rows
            value_part = -(mismatch_low.astype(f32) * scale_rows.astype(f32))
            back_hidden_act = back_hidden_act + inner_right(back_pred, second_low)
            new_two = new_two + inner_left(kept["hidden_act"], back_pred)
            back_hidden_pre = (back_hidden_act * hidden_slope + extra_pre).astype(bf16)
            key_part = key_part + inner_right(back_hidden_pre, first_low)
            new_one = new_one + inner_left(key_rows, back_hidden_pre)
            key_total[b] = back_key_att[b] + scatter_columns(key_part)
            value_total[b] = back_value_att[b] + value_part
            mom_one, mom_two = momentum * total_one, momentum * total_two
        query_total[b] = back_query_att[b] + scatter_columns(query_part)
        cot_one, cot_two = new_one, new_two
    grad_mem_w1, grad_mem_w2 = cot_one, cot_two

    back_query_total = jnp.concatenate(query_total, axis=0)
    back_key_total = jnp.concatenate(key_total, axis=0)
    back_value_total = jnp.concatenate(value_total, axis=0)
    query_conv_back = head_back(back_query_total, query_unit, query_inv) * silu_grad(query_conv)
    key_conv_back = head_back(back_key_total, key_unit, key_inv) * silu_grad(key_conv)
    value_conv_back = back_value_total * silu_grad(value_conv)
    query_pre_back, grad_conv_query = conv_back(query_conv_back, query_pre, conv_query)
    key_pre_back, grad_conv_key = conv_back(key_conv_back, key_pre, conv_key)
    value_pre_back, grad_conv_value = conv_back(value_conv_back, value_pre, conv_value)
    query_pre_low = query_pre_back.astype(bf16)
    key_pre_low = key_pre_back.astype(bf16)
    value_pre_low = value_pre_back.astype(bf16)
    back_normed_one = (
        inner_right(back_gate_low, w_gate)
        + inner_right(query_pre_low, w_query)
        + inner_right(key_pre_low, w_key)
        + inner_right(value_pre_low, w_value)
    )
    gain_one_part = jnp.sum(back_normed_one * unit_one, axis=0)
    input_part = norm_back(back_normed_one, unit_one, inv_one, norm1_gain)
    back_input_here = scatter_columns(input_part)
    grad_w_gate = inner_left(normed_one, back_gate_low)
    grad_w_query = inner_left(normed_one, query_pre_low)
    grad_w_key = inner_left(normed_one, key_pre_low) + mem_key_grad
    grad_w_value = inner_left(normed_one, value_pre_low) + mem_value_grad
    input_grad = back_middle_here + back_input_here

    gains = lax.psum(
        jnp.concatenate([gain_one_part, gain_two_part]).astype(bf16), ("narrow", "wide")
    ).astype(f32)
    full_width = whole_x.shape[1]
    grad_norm1_gain = lax.dynamic_slice_in_dim(gains, column_start, local_width, 0)
    grad_norm2_gain = lax.dynamic_slice_in_dim(gains, full_width + column_start, local_width, 0)
    late = (
        grad_w_query, grad_w_key, grad_w_value, grad_w_gate, grad_conv_query, grad_conv_key,
        grad_conv_value, grad_persist_key, grad_persist_value, grad_mem_w1, grad_mem_w2, grad_w_out,
    )
    late, (grad_ffn_gate, grad_ffn_up, grad_ffn_down) = lax.optimization_barrier(
        (tuple(v.astype(bf16) for v in late), (grad_ffn_gate, grad_ffn_up, grad_ffn_down))
    )
    (
        grad_w_query, grad_w_key, grad_w_value, grad_w_gate, grad_conv_query, grad_conv_key,
        grad_conv_value, grad_persist_key, grad_persist_value, grad_mem_w1, grad_mem_w2, grad_w_out,
    ) = sum_wide(late)
    return (
        layer_output,
        input_grad,
        grad_norm1_gain,
        grad_w_query,
        grad_w_key,
        grad_w_value,
        grad_w_gate,
        grad_conv_query,
        grad_conv_key,
        grad_conv_value,
        grad_persist_key,
        grad_persist_value,
        grad_mem_w1,
        grad_mem_w2,
        grad_w_out,
        grad_norm2_gain,
        grad_ffn_gate,
        grad_ffn_up,
        grad_ffn_down,
    )
def solution(mesh):
    return jax.shard_map(
        body,
        mesh=mesh,
        in_specs=(
            P("wide", "narrow"),
            P("wide", "narrow"),
            P("wide"),
            P("wide", None),
            P(),
            P(None, "narrow"),
            P(None, "narrow"),
            P(None, "narrow"),
            P(None, "narrow"),
            P(None, "narrow"),
            P(None, "narrow"),
            P(None, "narrow"),
            P(None, "narrow"),
            P(None, "narrow"),
            P(None, "narrow"),
            P("narrow", None),
            P("narrow", None),
            P(),
            P(None, "narrow"),
            P(None, "narrow"),
            P("narrow", None),
        ),
        out_specs=(
            P("wide", "narrow"),
            P("wide", "narrow"),
            P("narrow"),
            P(None, "narrow"),
            P(None, "narrow"),
            P(None, "narrow"),
            P(None, "narrow"),
            P(None, "narrow"),
            P(None, "narrow"),
            P(None, "narrow"),
            P(None, "narrow"),
            P(None, "narrow"),
            P(None, "narrow"),
            P("narrow", None),
            P("narrow", None),
            P("narrow"),
            P(None, "narrow"),
            P(None, "narrow"),
            P("narrow", None),
        ),
        check_vma=False,
    )
```

```python
import jax
import jax.numpy as jnp
from jax import lax
from jax.experimental import pallas as pl
from jax.experimental.pallas import tpu as pltpu
from jax.sharding import PartitionSpec as P

HD = 64
NP = 16
KW = 4
STRETCH = 512

epsilon = 1e-06
head_floor = 1.0
score_scale = 12.0
bf16 = jnp.bfloat16
f32 = jnp.float32


def product(left_side, right_side):
    return jnp.dot(left_side, right_side, preferred_element_type=f32)


def inner_left(left_side, right_side):
    return lax.dot_general(
        left_side, right_side, (((0,), (0,)), ((), ())), preferred_element_type=f32
    )


def inner_right(left_side, right_side):
    return lax.dot_general(
        left_side, right_side, (((1,), (1,)), ((), ())), preferred_element_type=f32
    )


def silu_grad(values):
    logistic = jax.nn.sigmoid(values)
    return logistic * (1.0 + values * (1.0 - logistic))


def silu_curve(values):
    logistic = jax.nn.sigmoid(values)
    logistic_slope = logistic * (1.0 - logistic)
    return logistic_slope * (1.0 + values * (1.0 - logistic)) + logistic * (
        1.0 - logistic - values * logistic_slope
    )


def plan_rates(level_now):
    return (0.1 * jnp.exp2(level_now), 0.9 - 0.2 * level_now, 0.02 + 0.05 * level_now)


def head_sums(values):
    width = values.shape[1]
    places = jnp.arange(width) // HD
    same_head = (places[:, None] == places[None, :]).astype(f32)
    return jnp.dot(
        values, same_head, precision=lax.Precision.HIGHEST, preferred_element_type=f32
    )


def head_norm(values):
    inv_norm = lax.rsqrt(head_sums(values * values) + head_floor)
    return (values * inv_norm, inv_norm)


def head_back(grad_rows, unit_rows, inv_norm):
    return (grad_rows - unit_rows * head_sums(grad_rows * unit_rows)) * inv_norm


def norm_back(grad_rows, unit_rows, inv_rows, gain_vec):
    scaled = grad_rows * gain_vec
    return inv_rows * (scaled - unit_rows * jnp.mean(scaled * unit_rows, axis=1, keepdims=True))


def shift_down(values, offset):
    return jnp.concatenate(
        [jnp.zeros((offset, values.shape[1]), values.dtype), values[:-offset]], axis=0
    )


def shift_up(values, offset):
    return jnp.concatenate(
        [values[offset:], jnp.zeros((offset, values.shape[1]), values.dtype)], axis=0
    )


def causal_conv(values, conv_taps):
    result = values * conv_taps[0]
    for offset in range(1, KW):
        result = result + shift_down(values, offset) * conv_taps[offset]
    return result


def conv_back(grad_rows, values, conv_taps):
    back_values = grad_rows * conv_taps[0]
    tap_grads = [jnp.sum(grad_rows * values, axis=0)]
    for offset in range(1, KW):
        back_values = back_values + shift_up(grad_rows, offset) * conv_taps[offset]
        tap_grads.append(jnp.sum(grad_rows * shift_down(values, offset), axis=0))
    return (back_values, jnp.stack(tap_grads, axis=0))


def visible(mask_rows):
    row_width = mask_rows.shape[0]
    places = jnp.arange(row_width)
    valid_keys = mask_rows[None, :] > 0.5
    causal = (places[None, :] <= places[:, None]) & valid_keys
    memory_seen = jnp.broadcast_to(valid_keys, (row_width, row_width))
    persistent = jnp.ones((row_width, NP), dtype=bool)
    return jnp.concatenate([persistent, memory_seen, causal], axis=1)


def gather_columns(values):
    return lax.all_gather(values, "narrow", axis=1, tiled=True)


def scatter_columns(values):
    return lax.psum_scatter(
        values.astype(bf16), "narrow", scatter_dimension=1, tiled=True
    ).astype(f32)


def sum_wide(values):
    return [lax.psum(v.astype(bf16), "wide").astype(f32) for v in values]


MESH = pl.DeviceIdType.MESH
ANY = pl.BlockSpec(memory_space=pl.ANY)
SCALARS = pl.BlockSpec(memory_space=pltpu.SMEM)
VMEM_LIMIT = 60 << 20


def group_places():
    me = lax.axis_index("narrow")
    core = lax.rem(me, 2)
    sib = me + 1 - 2 * core
    opp = lax.rem(me + 2, 4)
    diag = lax.rem(sib + 2, 4)
    return me, sib, opp, diag


def cols(index, width=256):
    return pl.ds(pl.multiple_of(index * width, width), width)


def enter_group(sib, opp):
    barrier = pltpu.get_barrier_semaphore()
    for peer in (sib, opp):
        pl.semaphore_signal(barrier, inc=1, device_id={"narrow": peer}, device_id_type=MESH)
    pl.semaphore_wait(barrier, 2)


class Wire:
    def __init__(self, send, recv):
        self.send, self.recv, self.used = send, recv, 0

    def to(self, source, target, device, axis="narrow"):
        k = self.used
        self.used += 1
        return pltpu.make_async_remote_copy(
            src_ref=source,
            dst_ref=target,
            send_sem=self.send.at[k],
            recv_sem=self.recv.at[k],
            device_id={axis: device},
            device_id_type=MESH,
        )


class Local:
    def __init__(self, sems):
        self.sems, self.used, self.open = sems, 0, []

    def start(self, source, target, late=False):
        copy = pltpu.make_async_copy(source, target, self.sems.at[self.used])
        self.used += 1
        copy.start()
        if late:
            self.open.append(copy)
        return copy

    def finish(self):
        for copy in self.open:
            copy.wait()
        self.open = []


class Gather:
    def __init__(self, wire, full, rows, places):
        me, sib, opp, diag = places
        own = full.at[rows, cols(me)]
        passed = full.at[rows, cols(opp)]
        self.far = wire.to(own, own, opp)
        self.near = wire.to(own, own, sib)
        self.relayed = wire.to(passed, passed, sib)

    def start(self):
        self.far.start()
        self.near.start()

    def relay(self):
        self.far.wait_recv()
        self.relayed.start()

    def end(self):
        self.near.wait_recv()
        self.relayed.wait_recv()

    def drain(self):
        self.far.wait_send()
        self.near.wait_send()
        self.relayed.wait_send()


class Scatter:
    def __init__(self, wire, part, rows, first, passed, last, places):
        me, sib, opp, diag = places
        self.part, self.rows, self.places = part, rows, places
        self.first, self.passed, self.last = first, passed, last
        self.pass_on = wire.to(part.at[rows, cols(diag)], first.at[1, rows], sib)
        self.keep = wire.to(part.at[rows, cols(sib)], first.at[0, rows], sib)
        self.far = wire.to(passed.at[rows], last.at[rows], opp)

    def start(self):
        self.pass_on.start()
        self.keep.start()

    def middle(self):
        me, sib, opp, diag = self.places
        self.pass_on.wait_recv()
        self.passed[self.rows] = (
            self.part[self.rows, cols(opp)].astype(f32) + self.first[1, self.rows].astype(f32)
        ).astype(bf16)
        self.far.start()

    def end(self):
        me, sib, opp, diag = self.places
        self.keep.wait_recv()
        near = self.part[self.rows, cols(me)].astype(f32) + self.first[0, self.rows].astype(f32)
        self.far.wait_recv()
        return near + self.last[self.rows].astype(f32)

    def drain(self):
        self.pass_on.wait_send()
        self.keep.wait_send()
        self.far.wait_send()


def scatter_room(rows):
    return [
        pltpu.VMEM((2, rows, 256), bf16),
        pltpu.VMEM((rows, 256), bf16),
        pltpu.VMEM((rows, 256), bf16),
    ]


def sems(count):
    return [
        pltpu.SemaphoreType.DMA((count,)),
        pltpu.SemaphoreType.DMA((count,)),
    ]


def shaped(shape, dtype=None):
    return jax.ShapeDtypeStruct(shape, bf16 if dtype is None else dtype)


def call(kernel, collective, outs, ins, scratch, flops, moved):
    return pl.pallas_call(
        kernel,
        out_shape=outs,
        in_specs=[SCALARS if s else ANY for s in ins],
        out_specs=[ANY] * len(outs),
        scratch_shapes=scratch,
        compiler_params=pltpu.CompilerParams(
            collective_id=collective, has_side_effects=True, vmem_limit_bytes=VMEM_LIMIT
        ),
        cost_estimate=pl.CostEstimate(flops=flops, bytes_accessed=moved, transcendentals=0),
        name=kernel.__name__,
    )


def memory_forward(
    key_in, query_in, value_in, one_in, two_in, rates,
    key_out, query_out, pre_out, act_out, mis_out, thr_out, ble_out, qpre_out, qact_out,
    rec_out, one_out, two_out,
    key, query, value, one, two, pre, act, part, mis, thr, ble, qpre, qact, qpart, rec,
    next_one, next_two, first, passed, last, qfirst, qpassed, qlast,
    send, recv, local_sems,
):
    places = group_places()
    me, sib, opp, diag = places
    wire, local = Wire(send, recv), Local(local_sems)
    half, block = STRETCH // 2, STRETCH
    get_key = local.start(key_in.at[pl.ds(0, block)], key.at[:, cols(me)])
    get_query = local.start(query_in, query.at[:, cols(me)])
    get_one = local.start(one_in, one)
    get_two = local.start(two_in, two)
    get_value = local.start(value_in.at[pl.ds(0, block)], value)
    enter_group(sib, opp)
    pieces = [pl.ds(c * half, half) for c in range(2)]
    blocks = [pl.ds(b * block, block) for b in range(2)]
    get_key.wait()
    keys = [Gather(wire, key, rows, places) for rows in pieces]
    for g in keys:
        g.start()
    get_one.wait()
    get_two.wait()
    get_query.wait()
    get_value.wait()
    queries = [Gather(wire, query, rows, places) for rows in blocks]
    sums = [Scatter(wire, part, rows, first, passed, last, places) for rows in pieces]
    for c in range(2):
        rows = pieces[c]
        keys[c].relay()
        if c == 1:
            queries[0].start()
            sums[0].middle()
        keys[c].end()
        hidden = jnp.dot(key[rows, :], one[...], preferred_element_type=f32)
        pre[rows, :] = hidden.astype(bf16)
        act[rows, :] = (hidden * jax.nn.sigmoid(hidden)).astype(bf16)
        part[rows, :] = jnp.dot(act[rows, :], two[...], preferred_element_type=f32).astype(bf16)
        sums[c].start()
    local.start(key, key_out, late=True)
    local.start(pre, pre_out, late=True)
    local.start(act, act_out, late=True)
    sums[1].middle()
    misses = [Gather(wire, mis, rows, places) for rows in pieces]
    for c in range(2):
        rows = pieces[c]
        predicted = sums[c].end()
        index = lax.broadcasted_iota(jnp.int32, (half, 1), 0) + c * half
        scale = jnp.where(index.astype(f32) < rates[0], 1.0 / STRETCH, 0.0)
        mis[rows, cols(me)] = ((predicted - value[rows, :].astype(f32)) * scale).astype(bf16)
        misses[c].start()
    queries[0].relay()
    queries[1].start()
    queries[0].end()
    qsums = [Scatter(wire, qpart, rows, qfirst, qpassed, qlast, places) for rows in blocks]

    def read(b, weight_one, weight_two):
        rows = blocks[b]
        asked = jnp.dot(query[rows, :], weight_one[...], preferred_element_type=f32)
        qpre[rows, :] = asked.astype(bf16)
        qact[rows, :] = (asked * jax.nn.sigmoid(asked)).astype(bf16)
        qpart[rows, :] = jnp.dot(
            qact[rows, :], weight_two[...], preferred_element_type=f32
        ).astype(bf16)
        qsums[b].start()

    misses[0].relay()
    read(0, one, two)
    misses[1].relay()
    for c in range(2):
        rows = pieces[c]
        misses[c].end()
        through = lax.dot_general(
            mis[rows, :], two[...], (((1,), (1,)), ((), ())), preferred_element_type=f32
        )
        thr[rows, :] = through.astype(bf16)
        ble[rows, :] = (through * silu_grad(pre[rows, :].astype(f32))).astype(bf16)
    qsums[0].middle()
    local.start(mis, mis_out, late=True)
    local.start(thr, thr_out, late=True)
    local.start(ble, ble_out, late=True)
    step_size, keep = rates[1], rates[2]

    def update(c, carried):
        rows = pl.ds(pl.multiple_of(c * half, half), half)
        grad = lax.dot_general(
            key[:, rows], ble[...], (((0,), (0,)), ((), ())), preferred_element_type=f32
        )
        next_one[rows, :] = (keep * one[rows, :].astype(f32) - step_size * grad).astype(bf16)
        grad = lax.dot_general(
            act[:, rows], mis[...], (((0,), (0,)), ((), ())), preferred_element_type=f32
        )
        next_two[rows, :] = (keep * two[rows, :].astype(f32) - step_size * grad).astype(bf16)
        return carried

    lax.fori_loop(0, 4, update, 0)
    local.start(next_one, one_out, late=True)
    local.start(next_two, two_out, late=True)
    queries[1].relay()
    reads = [Gather(wire, rec, rows, places) for rows in blocks]
    rec[blocks[0], cols(me)] = qsums[0].end().astype(bf16)
    reads[0].start()
    queries[1].end()
    local.start(query, query_out, late=True)
    read(1, next_one, next_two)
    local.start(qpre, qpre_out, late=True)
    local.start(qact, qact_out, late=True)
    qsums[1].middle()
    reads[0].relay()
    rec[blocks[1], cols(me)] = qsums[1].end().astype(bf16)
    reads[1].start()
    reads[0].end()
    local.start(rec.at[blocks[0]], rec_out.at[blocks[0]], late=True)
    reads[1].relay()
    reads[1].end()
    local.start(rec.at[blocks[1]], rec_out.at[blocks[1]], late=True)
    for item in keys + queries + sums + misses + qsums + reads:
        item.drain()
    local.finish()


def run_memory_forward(key_low, query_low, value_low, mem_w1, mem_w2, rates):
    block, tokens, width, units = STRETCH, query_low.shape[0], mem_w1.shape[0], mem_w1.shape[1]
    small, big, square = (block, width), (tokens, width), (width, units)
    return call(
        memory_forward, 1,
        [shaped(small), shaped(big), shaped(small), shaped(small), shaped(small), shaped(small),
         shaped(small), shaped(big), shaped(big), shaped(big), shaped(square), shaped(square)],
        (0, 0, 0, 0, 0, 1),
        [pltpu.VMEM(small, bf16), pltpu.VMEM(big, bf16), pltpu.VMEM((block, 256), bf16),
         pltpu.VMEM(square, bf16), pltpu.VMEM(square, bf16)]
        + [pltpu.VMEM(small, bf16)] * 6
        + [pltpu.VMEM(big, bf16)] * 4
        + [pltpu.VMEM(square, bf16)] * 2
        + scatter_room(block) + scatter_room(tokens)
        + sems(40) + [pltpu.SemaphoreType.DMA((24,))],
        9 * 2 * block * width * units, 24 << 20,
    )(key_low, query_low, value_low, mem_w1, mem_w2, rates)


KEY_ROWS = 2 * STRETCH + 128


def silu(values):
    return values * jax.nn.sigmoid(values)


def head_ones():
    left = lax.broadcasted_iota(jnp.int32, (256, 256), 0) // HD
    right = lax.broadcasted_iota(jnp.int32, (256, 256), 1) // HD
    return (left == right).astype(f32).astype(bf16)


def split_sums(values, ones):
    high = values.astype(bf16)
    rest = (values - high.astype(f32)).astype(bf16)
    return jnp.dot(high, ones, preferred_element_type=f32) + jnp.dot(
        rest, ones, preferred_element_type=f32
    )


def head_only(values, head):
    lane_head = lax.broadcasted_iota(jnp.int32, values.shape, 1) // HD
    return jnp.where(lane_head == head, values.astype(f32), 0.0).astype(bf16)


def key_bias(first_row, rows, valid, flipped):
    shape = (KEY_ROWS, rows) if flipped else (rows, KEY_ROWS)
    slot = lax.broadcasted_iota(jnp.int32, shape, 0 if flipped else 1)
    row = lax.broadcasted_iota(jnp.int32, shape, 1 if flipped else 0) + first_row
    memory = (slot < STRETCH) & (slot.astype(f32) < valid)
    place = slot - STRETCH
    causal = (place >= 0) & (place <= row) & (place.astype(f32) < valid) & (slot < 2 * STRETCH)
    persistent = (slot >= 2 * STRETCH) & (slot < 2 * STRETCH + NP)
    return jnp.where(memory | causal | persistent, 0.0, -1e30)


def attend_forward(
    query_in, key_in, value_in, rec_in, wk_in, wv_in, pk_in, pv_in, gate_in, wo_in, dy_in, rates,
    branch_out, here_out, mixed_out, gated_out, dy_out,
    query, key, value, rec, wk, wv, gate, wo, dy, keys, values, bias, mixed, gated, part, branch,
    here, first, passed, last, send, recv, local_sems,
):
    places = group_places()
    me, sib, opp, diag = places
    wire, local = Wire(send, recv), Local(local_sems)
    half, block = STRETCH // 2, STRETCH
    loads = [
        local.start(dy_in, dy.at[:, cols(me)]),
        local.start(rec_in, rec), local.start(wk_in, wk), local.start(wv_in, wv),
        local.start(query_in, query), local.start(key_in, key), local.start(value_in, value),
        local.start(gate_in, gate), local.start(wo_in, wo),
        local.start(pk_in, keys.at[pl.ds(2 * block, NP)]),
        local.start(pv_in, values.at[pl.ds(2 * block, NP)]),
    ]
    keys[pl.ds(2 * block + NP, 128 - NP), :] = jnp.zeros((128 - NP, 256), bf16)
    values[pl.ds(2 * block + NP, 128 - NP), :] = jnp.zeros((128 - NP, 256), bf16)
    enter_group(sib, opp)
    for item in loads:
        item.wait()
    blocks = [pl.ds(b * block, block) for b in range(2)]
    pieces = [pl.ds(c * half, half) for c in range(4)]
    grads = [Gather(wire, dy, rows, places) for rows in blocks]
    grads[0].start()
    ones = head_ones()
    sums = [Scatter(wire, part, rows, first, passed, last, places) for rows in pieces]
    joins = [Gather(wire, branch, rows, places) for rows in pieces]

    def finish(c):
        rows = pieces[c]
        got = sums[c].end()
        here[rows, :] = got
        branch[rows, cols(me)] = got.astype(bf16)
        joins[c].start()

    for c in range(4):
        b, rows = c // 2, pieces[c]
        if c % 2 == 0:
            memory = rec[blocks[b], :]
            made = jnp.dot(memory, wk[...], preferred_element_type=f32)
            inv = lax.rsqrt(split_sums(made * made, ones) + head_floor)
            keys[pl.ds(0, block), :] = (made * inv).astype(bf16)
            values[pl.ds(0, block), :] = jnp.dot(
                memory, wv[...], preferred_element_type=f32
            ).astype(bf16)
            keys[pl.ds(block, block), :] = key[blocks[b], :]
            values[pl.ds(block, block), :] = value[blocks[b], :]
        bias[...] = key_bias((c % 2) * half, half, rates[0] - float(b * block), False)

        def one_head(head, total):
            asked = head_only(query[rows, :], head)
            scores = lax.dot_general(
                asked, keys[...], (((1,), (1,)), ((), ())), preferred_element_type=f32
            )
            weights = jnp.exp(score_scale * scores + bias[...])
            inv = 1.0 / jnp.sum(weights, axis=1, keepdims=True)
            read = jnp.dot(
                (weights * inv).astype(bf16), values[...], preferred_element_type=f32
            )
            lane_head = lax.broadcasted_iota(jnp.int32, read.shape, 1) // HD
            return jnp.where(lane_head == head, read, total)

        got = lax.fori_loop(0, 4, one_head, jnp.zeros((half, 256), f32))
        mixed[rows, :] = got.astype(bf16)
        gated[rows, :] = (got * jax.nn.sigmoid(gate[rows, :].astype(f32))).astype(bf16)
        part[rows, :] = jnp.dot(gated[rows, :], wo[...], preferred_element_type=f32).astype(bf16)
        sums[c].start()
        if c == 0:
            grads[0].relay()
            grads[1].start()
            sums[0].middle()
        if c == 1:
            sums[1].middle()
            grads[0].end()
            finish(0)
        if c == 2:
            grads[1].relay()
            sums[2].middle()
            joins[0].relay()
            finish(1)
    grads[1].end()
    local.start(dy, dy_out, late=True)
    local.start(mixed, mixed_out, late=True)
    local.start(gated, gated_out, late=True)
    sums[3].middle()
    finish(2)
    joins[1].relay()
    finish(3)
    local.start(here, here_out, late=True)
    joins[2].relay()
    joins[3].relay()
    for item in joins:
        item.end()
    local.start(branch, branch_out, late=True)
    for item in grads + sums + joins:
        item.drain()
    local.finish()


def run_attend_forward(query, key, value, rec, wk, wv, pk, pv, gate, wo, dy, rates):
    tokens, width, local_width = query.shape[0], rec.shape[1], query.shape[1]
    tall, full = (tokens, local_width), (tokens, width)
    vm = lambda shape, dtype=None: pltpu.VMEM(shape, bf16 if dtype is None else dtype)
    return call(
        attend_forward, 2,
        [shaped(full), shaped(tall, f32), shaped(tall), shaped(tall), shaped(full)],
        (0,) * 11 + (1,),
        [vm(tall), vm(tall), vm(tall), vm(full), vm((width, local_width)), vm((width, local_width)),
         vm(tall), vm((local_width, width)), vm(full), vm((KEY_ROWS, local_width)),
         vm((KEY_ROWS, local_width)), vm((STRETCH // 2, KEY_ROWS), f32), vm(tall), vm(tall),
         vm(full), vm(full), vm(tall, f32)]
        + scatter_room(tokens) + sems(40) + [pltpu.SemaphoreType.DMA((24,))],
        8 << 30, 16 << 20,
    )(query, key, value, rec, wk, wv, pk, pv, gate, wo, dy, rates)


def feed_forward(
    x_in, branch_in, here_in, dy_in, xl_in, dyl_in, gain_in, gate_in, up_in, down_in,
    out_out, bm_out, bb_out, gain_out, gg_out, gu_out, gd_out,
    x, branch, here, dy, xl, dyl, gain, gate, up, down, normed, hidden, bup, bffn, part, part_two,
    out, bm, bb, gain_sum, gg, gu, gd, first, passed, last, first_two, passed_two, last_two,
    send, recv, local_sems,
):
    places = group_places()
    me, sib, opp, diag = places
    wire, local = Wire(send, recv), Local(local_sems)
    loads = [
        local.start(s, t)
        for s, t in (
            (x_in, x), (branch_in, branch), (gain_in, gain), (gate_in, gate), (up_in, up),
            (dy_in, dy), (down_in, down), (here_in, here), (xl_in, xl), (dyl_in, dyl),
        )
    ]
    tokens, width = x.shape
    count = 4
    size = tokens // count
    pieces = [pl.ds(c * size, size) for c in range(count)]
    enter_group(sib, opp)
    for item in loads:
        item.wait()
    sums = [Scatter(wire, part, rows, first, passed, last, places) for rows in pieces]
    outs = [Scatter(wire, part_two, rows, first_two, passed_two, last_two, places) for rows in pieces]
    joins = [Gather(wire, bb, rows, places) for rows in pieces]
    gain_sum[...] = jnp.zeros_like(gain_sum)

    def finish(c):
        rows = pieces[c]
        got = sums[c].end().astype(bf16).astype(f32) + dyl[rows, :].astype(f32)
        bm[rows, :] = got
        bb[rows, cols(me)] = got.astype(bf16)
        joins[c].start()

    for c in range(count):
        rows = pieces[c]
        middle = x[rows, :].astype(f32) + branch[rows, :].astype(f32)
        inv = lax.rsqrt(jnp.mean(middle * middle, axis=1, keepdims=True) + epsilon)
        normed[rows, :] = (middle * inv * gain[...]).astype(bf16)
        pre = jnp.dot(normed[rows, :], gate[...], preferred_element_type=f32)
        lift = jnp.dot(normed[rows, :], up[...], preferred_element_type=f32)
        back = lax.dot_general(
            dy[rows, :], down[...], (((1,), (1,)), ((), ())), preferred_element_type=f32
        )
        sig = jax.nn.sigmoid(pre)
        act = pre * sig
        hidden[rows, :] = (act * lift).astype(bf16)
        bup[rows, :] = (back * act).astype(bf16)
        bffn[rows, :] = (back * lift * (sig * (1.0 + pre * (1.0 - sig)))).astype(bf16)
        back = lax.dot_general(
            bffn[rows, :], gate[...], (((1,), (1,)), ((), ())), preferred_element_type=f32
        ) + lax.dot_general(
            bup[rows, :], up[...], (((1,), (1,)), ((), ())), preferred_element_type=f32
        )
        middle = x[rows, :].astype(f32) + branch[rows, :].astype(f32)
        unit = middle * inv
        gain_sum[...] += jnp.sum(back * unit, axis=0, keepdims=True)
        back = back * gain[...]
        part[rows, :] = (
            inv * (back - unit * jnp.mean(back * unit, axis=1, keepdims=True))
        ).astype(bf16)
        sums[c].start()
        if c >= 1:
            sums[c - 1].middle()
        if c >= 2:
            finish(c - 2)
        if c >= 3:
            joins[c - 3].relay()
    local.start(gain_sum, gain_out, late=True)
    sums[3].middle()
    finish(2)
    joins[1].relay()

    def final(c):
        rows = pieces[c]
        got = outs[c].end()
        out[rows, :] = (xl[rows, :].astype(f32) + here[rows, :] + got).astype(bf16)

    def grad(left, right, target, k):
        lanes = pl.ds(k * 256, 256)
        target[lanes, :] = lax.dot_general(
            left[:, lanes], right[...], (((0,), (0,)), ((), ())), preferred_element_type=f32
        ).astype(bf16)

    for c in range(count):
        rows = pieces[c]
        part_two[rows, :] = jnp.dot(
            hidden[rows, :], down[...], preferred_element_type=f32
        ).astype(bf16)
        outs[c].start()
        if c == 0:
            finish(3)
            joins[2].relay()
    joins[3].relay()
    for c in range(count):
        grad(normed, bffn, gg, c)
        outs[c].middle()
    local.start(gg, gg_out, late=True)
    local.start(bm, bm_out, late=True)
    for item in joins:
        item.end()
    local.start(bb, bb_out, late=True)
    for c in range(count):
        grad(normed, bup, gu, c)
    local.start(gu, gu_out, late=True)
    for c in range(count):
        grad(hidden, dy, gd, c)
    local.start(gd, gd_out, late=True)
    for c in range(count):
        final(c)
    local.start(out, out_out, late=True)
    for item in sums + outs + joins:
        item.drain()
    local.finish()


def run_feed_forward(x, branch, here, dy, xl, dyl, gain, gate, up, down):
    full, tall, square = x.shape, xl.shape, gate.shape
    vm = lambda shape, dtype=None: pltpu.VMEM(shape, bf16 if dtype is None else dtype)
    row = (1, full[1])
    return call(
        feed_forward, 3,
        [shaped(tall), shaped(tall, f32), shaped(full), shaped(row, f32), shaped(square),
         shaped(square), shaped(square)],
        (0,) * 10,
        [vm(full), vm(full), vm(tall, f32), vm(full), vm(tall), vm(tall), vm(row, f32), vm(square),
         vm(square), vm(square), vm(full), vm(full), vm(full), vm(full), vm(full), vm(full),
         vm(tall), vm(tall, f32), vm(full), vm(row, f32), vm(square), vm(square), vm(square)]
        + scatter_room(full[0]) + scatter_room(full[0]) + sems(40)
        + [pltpu.SemaphoreType.DMA((24,))],
        19 << 30, 24 << 20,
    )(x, branch, here, dy, xl, dyl, gain, gate, up, down)


def wide_places():
    at = lax.axis_index("wide")
    y, z = lax.rem(at, 2), lax.div(at, 2)
    facing = at + 1 - 2 * y
    others = [lax.rem(z + d, 4) for d in (1, 2, 3)]
    return y, z, facing, others, [2 * other + y for other in others]


def enter_all(sib, opp, wide):
    y, z, facing, others, peers = wide
    barrier = pltpu.get_barrier_semaphore()
    for peer in (sib, opp):
        pl.semaphore_signal(barrier, inc=1, device_id={"narrow": peer}, device_id_type=MESH)
    for peer in (facing, *peers):
        pl.semaphore_signal(barrier, inc=1, device_id={"wide": peer}, device_id_type=MESH)
    pl.semaphore_wait(barrier, 6)


class WideSum:
    ahead = 2

    def __init__(self, wire, local, wide, chunks, got, parts, done):
        y, z, facing, others, peers = wide
        self.local, self.got, self.parts, self.done = local, got, parts, done
        self.items, at, small = [], 0, 0
        for source, start, target, goal, rows in chunks:
            half, quarter = rows // 2, rows // 8
            away = pl.ds(start + pl.multiple_of((1 - y) * half, half), half)
            mine = pl.ds(start + pl.multiple_of(y * half, half), half)
            lands = pl.ds(goal + pl.multiple_of(y * half, half), half)
            spot = pl.ds(goal + pl.multiple_of(y * half + z * quarter, quarter), quarter)
            room = pl.ds(at, half)
            own = pl.ds(at + pl.multiple_of(z * quarter, quarter), quarter)
            slot = pl.ds(small, quarter)
            item = {
                "mine": source.at[mine], "room": room, "own": own, "slot": slot,
                "spot": target.at[spot],
                "one": wire.to(source.at[away], got.at[room], facing, "wide"),
                "two": [
                    wire.to(
                        got.at[pl.ds(at + pl.multiple_of(other * quarter, quarter), quarter)],
                        parts.at[d, slot], peer, "wide",
                    )
                    for d, (other, peer) in enumerate(zip(others, peers))
                ],
                "three": [wire.to(done.at[slot], target.at[spot], peer, "wide") for peer in peers],
                "four": wire.to(target.at[lands], target.at[lands], facing, "wide"),
            }
            self.items.append(item)
            at, small = at + half, small + quarter
        count = len(self.items)
        self.steps, self.begun, self.ready, self.wanted = [], 0, count, 0
        for i in range(count + 2):
            if i < count:
                self.steps.append((self.halve, i))
            if 0 <= i - 1 < count:
                self.steps.append((self.total, i - 1))
            if 0 <= i - 2 < count:
                self.steps.append((self.back, i - 2))
        self.steps += [(self.last, i) for i in range(count)]
        self.next = 0

    def open(self, ready):
        self.ready = ready
        self.begin(self.wanted)

    def begin(self, upto):
        self.wanted = max(self.wanted, upto)
        while self.begun < min(upto, self.ready, len(self.items)):
            self.items[self.begun]["one"].start()
            self.begun += 1

    def halve(self, i):
        item = self.items[i]
        item["one"].wait_recv()
        self.begin(i + 1 + self.ahead)
        self.got[item["room"], :] = (
            self.got[item["room"], :].astype(f32) + item["mine"][...].astype(f32)
        ).astype(bf16)
        for copy in item["two"]:
            copy.start()

    def total(self, i):
        item = self.items[i]
        for copy in item["two"]:
            copy.wait_recv()
        value = self.got[item["own"], :].astype(f32)
        for d in range(3):
            value = value + self.parts[d, item["slot"], :].astype(f32)
        self.done[item["slot"], :] = value.astype(bf16)
        for copy in item["three"]:
            copy.start()
        item["local"] = self.local.start(self.done.at[item["slot"]], item["spot"])

    def back(self, i):
        item = self.items[i]
        for copy in item["three"]:
            copy.wait_recv()
        item["local"].wait()
        item["four"].start()

    def last(self, i):
        self.items[i]["four"].wait_recv()

    def go(self, count=None):
        stop = len(self.steps) if count is None else min(self.next + count, len(self.steps))
        while self.next < stop:
            step, i = self.steps[self.next]
            step(i)
            self.next += 1

    def drain(self):
        for item in self.items:
            item["one"].wait_send()
            item["four"].wait_send()
            for copy in item["two"] + item["three"]:
                copy.wait_send()


def wide_room(rows):
    return [
        pltpu.VMEM((rows // 2, 1024), bf16),
        pltpu.VMEM((3, rows // 8, 1024), bf16),
        pltpu.VMEM((rows // 8, 1024), bf16),
    ]


def nt(left, right):
    return lax.dot_general(left, right, (((1,), (1,)), ((), ())), preferred_element_type=f32)


def tn(left, right):
    return lax.dot_general(left, right, (((0,), (0,)), ((), ())), preferred_element_type=f32)


def attend_backward(
    query_in, key_in, value_in, rec_in, wk_in, wv_in, pk_in, pv_in, gate_in, wo_in, mixed_in,
    gated_in, bb_in, side_in, rates,
    side_out, gwo_out, bgate_out, gmk_out, gmv_out, bq_out, bk_out, bv_out, bpk_out, bpv_out, late_out, brec_out,
    query, key, value, rec, wk, wv, gate, wo, mixed, gated, bb, keys, values, bias, bmix, bgate, gwo,
    gmk, gmv, bq, bk, bv, kacc, vacc, pkacc, pvacc, bmk, bmv, part, brec, side, first, passed, last,
    got, parts, done, send, recv, local_sems,
):
    places = group_places()
    me, sib, opp, diag = places
    wire, local = Wire(send, recv), Local(local_sems)
    wide = wide_places()
    half, block = STRETCH // 2, STRETCH
    get_side = local.start(side_in.at[pl.ds(0, side.shape[0])], side)
    loads = [
        local.start(s, t)
        for s, t in (
            (bb_in, bb), (wo_in, wo), (gate_in, gate), (mixed_in, mixed), (gated_in, gated),
            (rec_in, rec), (wk_in, wk), (wv_in, wv), (query_in, query), (key_in, key),
            (value_in, value), (pk_in, keys.at[pl.ds(2 * block, NP)]),
            (pv_in, values.at[pl.ds(2 * block, NP)]),
        )
    ]
    keys[pl.ds(2 * block + NP, 128 - NP), :] = jnp.zeros((128 - NP, 256), bf16)
    values[pl.ds(2 * block + NP, 128 - NP), :] = jnp.zeros((128 - NP, 256), bf16)
    pkacc[...] = jnp.zeros_like(pkacc)
    pvacc[...] = jnp.zeros_like(pvacc)
    gmk[...] = jnp.zeros_like(gmk)
    gmv[...] = jnp.zeros_like(gmv)
    enter_all(sib, opp, wide)
    get_side.wait()
    adds = WideSum(
        wire, local, wide,
        [(side, i * 256, side_out, i * 256, 256) for i in range(side.shape[0] // 256)],
        got, parts, done,
    )
    adds.begin(adds.ahead)
    for item in loads:
        item.wait()

    def through_gate(c, carried):
        rows = pl.ds(pl.multiple_of(c * half, half), half)
        back = nt(bb[rows, :], wo[...])
        sig = jax.nn.sigmoid(gate[rows, :].astype(f32))
        bmix[rows, :] = (back * sig).astype(bf16)
        bgate[rows, :] = (back * mixed[rows, :].astype(f32) * sig * (1.0 - sig)).astype(bf16)
        return carried

    lax.fori_loop(0, 4, through_gate, 0)
    local.start(bgate, bgate_out, late=True)
    gwo[...] = tn(gated[...], bb[...]).astype(bf16)
    local.start(gwo, gwo_out, late=True)
    ones = head_ones()
    pieces = [pl.ds(c * half, half) for c in range(2)]
    sums = [Scatter(wire, part, rows, first, passed, last, places) for rows in pieces]
    joins = [Gather(wire, brec, rows, places) for rows in pieces]
    for b in (1, 0):
        rows = pl.ds(b * block, block)
        memory = rec[rows, :]
        made = jnp.dot(memory, wk[...], preferred_element_type=f32)
        inv = lax.rsqrt(split_sums(made * made, ones) + head_floor)
        keys[pl.ds(0, block), :] = (made * inv).astype(bf16)
        values[pl.ds(0, block), :] = jnp.dot(memory, wv[...], preferred_element_type=f32).astype(bf16)
        keys[pl.ds(block, block), :] = key[rows, :]
        values[pl.ds(block, block), :] = value[rows, :]
        bias[...] = key_bias(0, block, rates[0] - float(b * block), True)
        kacc[...] = jnp.zeros_like(kacc)
        vacc[...] = jnp.zeros_like(vacc)

        def one_head(head, total):
            asked = head_only(query[rows, :], head)
            back = head_only(bmix[rows, :], head)
            weights = jnp.exp(score_scale * nt(keys[...], asked) + bias[...])
            weights = weights * (1.0 / jnp.sum(weights, axis=0, keepdims=True))
            vacc[...] += jnp.dot(weights.astype(bf16), back, preferred_element_type=f32)
            slope = nt(values[...], back)
            slope = (
                weights * (slope - jnp.sum(weights * slope, axis=0, keepdims=True))
            ).astype(bf16)
            kacc[...] += jnp.dot(slope, asked, preferred_element_type=f32)
            read = tn(slope, keys[...])
            lane_head = lax.broadcasted_iota(jnp.int32, read.shape, 1) // HD
            return jnp.where(lane_head == head, read, total)

        asked_back = lax.fori_loop(0, 2, one_head, jnp.zeros((block, 256), f32))
        adds.go(2)
        bq[rows, :] = score_scale * lax.fori_loop(2, 4, one_head, asked_back)
        adds.go(2)
        bk[rows, :] = score_scale * kacc[pl.ds(block, block), :]
        bv[rows, :] = vacc[pl.ds(block, block), :]
        pkacc[...] += score_scale * kacc[pl.ds(2 * block, NP), :]
        pvacc[...] += vacc[pl.ds(2 * block, NP), :]
        made = jnp.dot(memory, wk[...], preferred_element_type=f32)
        unit = made * inv
        back = score_scale * kacc[pl.ds(0, block), :]
        bmk[...] = ((back - unit * split_sums(back * unit, ones)) * inv).astype(bf16)
        bmv[...] = vacc[pl.ds(0, block), :].astype(bf16)
        if b == 0:
            for c in range(2):
                brec[pieces[c], cols(me)] = sums[c].end().astype(bf16)
                joins[c].start()
            for item in sums:
                item.drain()
        for c in range(2):
            part[pieces[c], :] = (
                nt(bmk[pieces[c], :], wk[...]) + nt(bmv[pieces[c], :], wv[...])
            ).astype(bf16)
            if b == 1:
                sums[c].start()
        adds.go(1)
        gmk[...] += tn(memory, bmk[...])
        if b == 1:
            sums[0].middle()
        gmv[...] += tn(memory, bmv[...])
        if b == 1:
            sums[1].middle()
    local.start(part, late_out, late=True)
    for s, t in (
        (gmk, gmk_out), (gmv, gmv_out), (bq, bq_out), (bk, bk_out), (bv, bv_out),
        (pkacc, bpk_out), (pvacc, bpv_out),
    ):
        local.start(s, t, late=True)
    for item in joins:
        item.relay()
    for item in joins:
        item.end()
    local.start(brec, brec_out, late=True)
    adds.go()
    adds.drain()
    for item in joins:
        item.drain()
    local.finish()


def run_attend_backward(
    query, key, value, rec, wk, wv, pk, pv, gate, wo, mixed, gated, bb, side, rates, side_rows
):
    tokens, width, local_width = query.shape[0], rec.shape[1], query.shape[1]
    tall, full, half = (tokens, local_width), (tokens, width), (STRETCH, width)
    weight, small, square = (width, local_width), (NP, local_width), (STRETCH, local_width)
    padded = (KEY_ROWS, local_width)
    vm = lambda shape, dtype=None: pltpu.VMEM(shape, bf16 if dtype is None else dtype)
    return call(
        attend_backward, 4,
        [shaped((side_rows, width)), shaped((local_width, width)), shaped(tall), shaped(weight, f32),
         shaped(weight, f32),
         shaped(tall, f32), shaped(tall, f32), shaped(tall, f32), shaped(small, f32),
         shaped(small, f32), shaped(half), shaped(half)],
        (0,) * 14 + (1,),
        [vm(tall), vm(tall), vm(tall), vm(full), vm(weight), vm(weight), vm(tall),
         vm((local_width, width)), vm(tall), vm(tall), vm(full), vm(padded), vm(padded),
         vm((KEY_ROWS, STRETCH), f32), vm(tall), vm(tall), vm((local_width, width)),
         vm(weight, f32), vm(weight, f32), vm(tall, f32), vm(tall, f32), vm(tall, f32),
         vm(padded, f32), vm(padded, f32), vm(small, f32), vm(small, f32), vm(square), vm(square),
         vm(half), vm(half), vm((side_rows, width))]
        + scatter_room(STRETCH) + wide_room(side_rows) + sems(16 + side_rows // 32)
        + [pltpu.SemaphoreType.DMA((48,))],
        16 << 30, 20 << 20,
    )(query, key, value, rec, wk, wv, pk, pv, gate, wo, mixed, gated, bb, side, rates)


def memory_backward(
    brec_in, late_in, key_in, query_in, pre_in, act_in, mis_in, thr_in, ble_in, qpre_in, qact_in,
    one_in, two_in, next_one_in, next_two_in, left_in, right_in, rates,
    left_out, right_out, gone_out, gtwo_out, kpart_out, qpart_out, vpart_out,
    brec, late, key, query, pre, act, mis, thr, ble, qpre, qact, one, two, next_one, next_two,
    cone, ctwo, bble, bhid, kpart, early, bthr, bqm, mpart, bmis, bpre, klow, qlow, kout, qout, vout, left, right,
    lfirst, lpassed, llast, mfirst, mpassed, mlast, qfirst, qpassed, qlast, kfirst, kpassed, klast,
    got, parts, done, send, recv, local_sems,
):
    places = group_places()
    me, sib, opp, diag = places
    wire, local = Wire(send, recv), Local(local_sems)
    wide = wide_places()
    half, block = STRETCH // 2, STRETCH
    start = left_in.shape[0] - left.shape[0]
    get_left = local.start(left_in.at[pl.ds(start, left.shape[0])], left)
    get_right = local.start(right_in, right)
    loads = [
        local.start(s, t)
        for s, t in (
            (late_in, late), (brec_in, brec), (next_two_in, next_two), (qpre_in, qpre),
            (next_one_in, next_one), (query_in, query), (qact_in, qact), (key_in, key), (pre_in, pre),
            (act_in, act), (two_in, two), (mis_in, mis), (one_in, one), (thr_in, thr), (ble_in, ble),
        )
    ]
    enter_all(sib, opp, wide)
    pieces = [pl.ds(c * half, half) for c in range(2)]
    blocks = [pl.ds(b * block, block) for b in range(2)]
    whole = pl.ds(0, block)
    lates = Scatter(wire, late, whole, lfirst, lpassed, llast, places)
    early_join = Gather(wire, early, whole, places)
    sums = [Scatter(wire, mpart, rows, mfirst, mpassed, mlast, places) for rows in pieces]
    joins = [Gather(wire, bmis, rows, places) for rows in pieces]
    asks = [Scatter(wire, qlow, rows, qfirst, qpassed, qlast, places) for rows in blocks]
    tells = [Scatter(wire, klow, rows, kfirst, kpassed, klast, places) for rows in pieces]
    get_left.wait()
    get_right.wait()
    adds = WideSum(
        wire, local, wide,
        [(left, i * 256, left_out, i * 256, 256) for i in range(left.shape[0] // 256)]
        + [(right, i * 256, right_out, i * 256, 256) for i in range(right.shape[0] // 256)],
        got, parts, done,
    )
    adds.begin(adds.ahead)
    loads[0].wait()
    lates.start()
    for item in loads[1:]:
        item.wait()
    step_size, keep = rates[1], rates[2]

    def slope_of(values):
        sig = jax.nn.sigmoid(values)
        return sig * (1.0 + values * (1.0 - sig))

    def ask_back(c, source, row_start, weight_one, weight_two):
        rows = pl.ds(row_start + c * half, half)
        back = nt(source[pieces[c], :], weight_two[...])
        bqm[pieces[c], :] = (back * slope_of(qpre[rows, :].astype(f32))).astype(bf16)
        qlow[rows, :] = nt(bqm[pieces[c], :], weight_one[...]).astype(bf16)

    for c in range(2):
        ask_back(c, brec, block, next_one, next_two)
        if c == 0:
            lates.middle()
    asks[1].start()
    early[:, cols(me)] = lates.end().astype(bf16)
    early_join.start()

    def first_sums(c, carried):
        rows = pl.ds(pl.multiple_of(c * half, half), half)
        grad = tn(query[blocks[1], rows], bqm[...])
        cone[rows, :] = keep * grad
        next_one[rows, :] = (-step_size * grad).astype(bf16)
        grad = tn(qact[blocks[1], rows], brec[...])
        ctwo[rows, :] = keep * grad
        next_two[rows, :] = (-step_size * grad).astype(bf16)
        return carried

    adds.go(1)
    lax.fori_loop(0, 4, first_sums, 0)
    adds.go(2)
    for c in range(2):
        rows = pieces[c]
        back = jnp.dot(key[rows, :], next_one[...], preferred_element_type=f32)
        bble[rows, :] = back.astype(bf16)
        bthr[rows, :] = (back * slope_of(pre[rows, :].astype(f32))).astype(bf16)
        mpart[rows, :] = (
            jnp.dot(act[rows, :], next_two[...], preferred_element_type=f32)
            + jnp.dot(bthr[rows, :], two[...], preferred_element_type=f32)
        ).astype(bf16)
        sums[c].start()
        if c == 0:
            early_join.relay()
    sums[0].middle()
    adds.go(1)
    for c in range(2):
        bhid[pieces[c], :] = nt(mis[pieces[c], :], next_two[...]).astype(bf16)
        if c == 0:
            sums[1].middle()
    early_join.end()
    for c in range(2):
        rows = pieces[c]
        got = sums[c].end().astype(bf16)
        index = lax.broadcasted_iota(jnp.int32, (half, 1), 0) + c * half
        scale = jnp.where(index.astype(f32) < rates[0], 1.0 / STRETCH, 0.0)
        bmis[rows, cols(me)] = got
        joins[c].start()
        vout[rows, :] = -(got.astype(f32) * scale)
    local.start(vout, vpart_out, late=True)
    adds.go(2)
    for c in range(2):
        ask_back(c, early, 0, one, two)
    joins[0].relay()
    asks[0].start()
    for c in range(2):
        kpart[pieces[c], :] = nt(ble[pieces[c], :], next_one[...]).astype(bf16)
        if c == 0:
            joins[1].relay()
    asks[1].middle()
    adds.go(2)

    def second_sums(c, carried):
        rows = pl.ds(pl.multiple_of(c * half, half), half)
        cone[rows, :] += tn(query[blocks[0], rows], bqm[...])
        ctwo[rows, :] += tn(bthr[:, rows], mis[...]) + tn(qact[blocks[0], rows], early[...])
        return carried

    for c in range(2):
        rows = pieces[c]
        joins[c].end()
        joins[c].drain()
        index = lax.broadcasted_iota(jnp.int32, (half, 1), 0) + c * half
        scale = jnp.where(index.astype(f32) < rates[0], 1.0 / STRETCH, 0.0)
        bmis[rows, :] = (bmis[rows, :].astype(f32) * scale).astype(bf16)
        values = pre[rows, :].astype(f32)
        sig = jax.nn.sigmoid(values)
        drop = 1.0 - sig
        slant = sig * drop
        curve = slant * (1.0 + values * drop) + sig * (drop - values * slant)
        back = bhid[rows, :].astype(f32) + nt(bmis[rows, :], two[...])
        bpre[rows, :] = (
            back * (sig * (1.0 + values * drop))
            + bble[rows, :].astype(f32) * thr[rows, :].astype(f32) * curve
        ).astype(bf16)
        klow[rows, :] = (kpart[rows, :].astype(f32) + nt(bpre[rows, :], one[...])).astype(bf16)
        tells[c].start()
    asks[0].middle()
    adds.go(1)
    lax.fori_loop(0, 2, second_sums, 0)
    tells[0].middle()
    tells[1].middle()
    adds.go(2)
    lax.fori_loop(2, 4, second_sums, 0)
    adds.go(2)

    def last_sums(c, carried):
        rows = pl.ds(pl.multiple_of(c * half, half), half)
        next_one[rows, :] = (cone[rows, :] + tn(key[:, rows], bpre[...])).astype(bf16)
        next_two[rows, :] = (ctwo[rows, :] + tn(act[:, rows], bmis[...])).astype(bf16)
        return carried

    lax.fori_loop(0, 2, last_sums, 0)
    adds.go(1)
    lax.fori_loop(2, 4, last_sums, 0)
    adds.go(1)
    local.start(next_one, gone_out, late=True)
    local.start(next_two, gtwo_out, late=True)
    for b in (1, 0):
        qout[blocks[b], :] = asks[b].end()
    local.start(qout, qpart_out, late=True)
    for c in range(2):
        kout[pieces[c], :] = tells[c].end()
    local.start(kout, kpart_out, late=True)
    adds.go()
    adds.drain()
    for item in [lates, early_join] + sums + asks + tells:
        item.drain()
    local.finish()


def run_memory_backward(
    brec, late, key, query, pre, act, mis, thr, ble, qpre, qact, one, two, next_one, next_two, left,
    right, rates, left_rows,
):
    half, full, square = brec.shape, query.shape, one.shape
    vm = lambda shape, dtype=None: pltpu.VMEM(shape, bf16 if dtype is None else dtype)
    tall, small = (full[0], 256), (half[0], 256)
    return call(
        memory_backward, 5,
        [shaped((left_rows, square[1])), shaped(right.shape), shaped(square), shaped(square),
         shaped(small, f32), shaped(tall, f32), shaped(small, f32)],
        (0,) * 17 + (1,),
        [vm(half), vm(half), vm(half), vm(full), vm(half), vm(half), vm(half), vm(half), vm(half),
         vm(full), vm(full), vm(square), vm(square), vm(square), vm(square), vm(square, f32),
         vm(square, f32), vm(half), vm(half), vm(half), vm(half), vm(half), vm(half),
         vm(half), vm(half), vm(half), vm(half), vm(full), vm(small, f32), vm(tall, f32),
         vm(small, f32), vm((left_rows, square[1])), vm(right.shape)]
        + scatter_room(half[0]) + scatter_room(half[0]) + scatter_room(full[0]) + scatter_room(half[0])
        + wide_room(left_rows + right.shape[0]) + sems(40 + (left_rows + right.shape[0]) // 32)
        + [pltpu.SemaphoreType.DMA((48,))],
        18 * 2 * half[0] * square[0] * square[1], 32 << 20,
    )(brec, late, key, query, pre, act, mis, thr, ble, qpre, qact, one, two, next_one, next_two, left,
      right, rates)


def moved_down(values, offset):
    if offset == 0:
        return values
    row = lax.broadcasted_iota(jnp.int32, values.shape, 0)
    return jnp.where(row < offset, 0.0, pltpu.roll(values, offset, 0))


def moved_up(values, offset):
    if offset == 0:
        return values
    rows = values.shape[0]
    row = lax.broadcasted_iota(jnp.int32, values.shape, 0)
    return jnp.where(row >= rows - offset, 0.0, pltpu.roll(values, rows - offset, 0))


def finish_layer(
    x_in, gain_in, wq_in, wk_in, wv_in, wg_in, taps_in, qpre_in, kpre_in, vpre_in, bq_in, bk_in, bv_in,
    qpart_in, kpart_in, vpart_in, bgate_in, gmk_in, gmv_in, pk_in, bpk_in, bpv_in, gaintwo_in, bm_in,
    gwo_in, sum_a_in, sum_b_in, sum_c_in,
    ig_out, sum_a_out, sum_b_out, sum_c_out, packed_out, extra_out,
    x, gain, weights, taps, qpre, kpre, vpre, bq, bk, bv, qpart, kpart, vpart, cot, gmk, gmv, pk, bpk,
    bpv, gaintwo, bm, extra, sum_a, sum_b, sum_c, packed, normed, part, ig, conv_rows,
    first, passed, last, got, parts, done, send, recv, local_sems,
):
    places = group_places()
    me, sib, opp, diag = places
    wire, local = Wire(send, recv), Local(local_sems)
    wide = wide_places()
    tokens, width = x.shape
    block, small = STRETCH, gwo_in.shape[0]
    lanes = [pl.ds(i * 256, 256) for i in range(4)]
    sums_in = [
        local.start(s, t) for s, t in ((sum_a_in, sum_a), (sum_b_in, sum_b), (sum_c_in, sum_c))
    ]
    loads = [
        local.start(s, t)
        for s, t in (
            (qpre_in, qpre), (bq_in, bq), (qpart_in, qpart), (taps_in, taps), (kpre_in, kpre),
            (bk_in, bk), (kpart_in, kpart), (vpre_in, vpre), (bv_in, bv), (vpart_in, vpart),
            (x_in, x), (gain_in, gain), (wq_in, weights.at[:, lanes[0]]),
            (wk_in, weights.at[:, lanes[1]]), (wv_in, weights.at[:, lanes[2]]),
            (wg_in, weights.at[:, lanes[3]]), (bgate_in, cot.at[:, lanes[3]]), (gmk_in, gmk),
            (gmv_in, gmv), (pk_in, pk), (bpk_in, bpk), (bpv_in, bpv), (gaintwo_in, gaintwo),
            (bm_in, bm), (gwo_in, extra.at[pl.ds(0, small)]),
        )
    ]
    enter_all(sib, opp, wide)
    for item in sums_in:
        item.wait()
    chunks = []
    for source, target in (
        (sum_a, sum_a_out), (sum_b, sum_b_out), (sum_c, sum_c_out), (packed, packed_out),
    ):
        chunks += [(source, i * 256, target, i * 256, 256) for i in range(source.shape[0] // 256)]
    chunks += [(extra, 0, extra_out, 0, small), (extra, small, extra_out, small, 128)]
    adds = WideSum(wire, local, wide, chunks, got, parts, done)
    early = len(chunks) - 6
    adds.ready = early
    adds.begin(adds.ahead)
    for item in loads:
        item.wait()
    ones = head_ones()

    def through_conv(pre, taps_at, back, normal):
        values = pre[...]
        conv = values * taps[pl.ds(taps_at, 1), :]
        for j in range(1, KW):
            conv = conv + moved_down(values, j) * taps[pl.ds(taps_at + j, 1), :]
        sig = jax.nn.sigmoid(conv)
        if normal:
            act = conv * sig
            inv = lax.rsqrt(split_sums(act * act, ones) + head_floor)
            unit = act * inv
            back = (back - unit * split_sums(back * unit, ones)) * inv
        back = back * (sig * (1.0 + conv * (1.0 - sig)))
        for j in range(KW):
            conv_rows[pl.ds(taps_at + j, 1), :] = jnp.sum(
                back * moved_down(values, j), axis=0, keepdims=True
            )
        result = back * taps[pl.ds(taps_at, 1), :]
        for j in range(1, KW):
            result = result + moved_up(back, j) * taps[pl.ds(taps_at + j, 1), :]
        return result.astype(bf16)

    conv_rows[...] = jnp.zeros_like(conv_rows)
    cot[:, lanes[0]] = through_conv(qpre, 0, bq[...] + qpart[...], True)
    bk[pl.ds(0, block), :] += kpart[...]
    cot[:, lanes[1]] = through_conv(kpre, KW, bk[...], True)
    adds.go(1)
    bv[pl.ds(0, block), :] += vpart[...]
    cot[:, lanes[2]] = through_conv(vpre, 2 * KW, bv[...], False)
    pieces = [pl.ds(c * 256, 256) for c in range(tokens // 256)]
    sums = [Scatter(wire, part, rows, first, passed, last, places) for rows in pieces]
    tail_rows = pl.ds(tokens, 16)
    gains = Scatter(wire, part, tail_rows, first, passed, last, places)
    gain_sum = jnp.zeros((1, width), f32)
    for c, rows in enumerate(pieces):
        back = nt(cot[rows, :], weights[...])
        values = x[rows, :].astype(f32)
        inv = lax.rsqrt(jnp.mean(values * values, axis=1, keepdims=True) + epsilon)
        unit = values * inv
        normed[rows, :] = (unit * gain[...]).astype(bf16)
        gain_sum = gain_sum + jnp.sum(back * unit, axis=0, keepdims=True)
        back = back * gain[...]
        part[rows, :] = (
            inv * (back - unit * jnp.mean(back * unit, axis=1, keepdims=True))
        ).astype(bf16)
        sums[c].start()
        if c >= 1:
            sums[c - 1].middle()
    row = lax.broadcasted_iota(jnp.int32, (16, width), 0)
    part[tail_rows, :] = jnp.where(
        row == 0, gain_sum, jnp.where(row == 1, gaintwo[...], 0.0)
    ).astype(bf16)
    gains.start()
    adds.go(2)

    for c in range(width // 256):
        rows = pieces[c]
        packed[rows, :] = tn(normed[:, rows], cot[...]).astype(bf16)
    packed[:, lanes[1]] = (packed[:, lanes[1]].astype(f32) + gmk[...]).astype(bf16)
    packed[:, lanes[2]] = (packed[:, lanes[2]].astype(f32) + gmv[...]).astype(bf16)
    adds.open(early + 4)
    adds.go(1)
    sums[-1].middle()
    gains.middle()
    extra[pl.ds(small, 128), :] = jnp.zeros((128, width), bf16)
    start = pk[...].astype(f32)
    inv = lax.rsqrt(split_sums(start * start, ones) + head_floor)
    unit = start * inv
    back = bpk[...]
    slim = pl.ds(small, 16)
    extra[slim, lanes[0]] = ((back - unit * split_sums(back * unit, ones)) * inv).astype(bf16)
    extra[slim, lanes[1]] = bpv[...].astype(bf16)
    extra[slim, lanes[2]] = conv_rows[...].astype(bf16)
    extra[slim, lanes[3]] = gains.end().astype(bf16)
    adds.open(len(chunks))
    adds.go(4)
    for c, rows in enumerate(pieces):
        ig[rows, :] = bm[rows, :] + sums[c].end()
    local.start(ig, ig_out, late=True)
    adds.go()
    adds.drain()
    for item in sums + [gains]:
        item.drain()
    local.finish()


def run_finish_layer(
    x, gain, wq, wk, wv, wg, taps, qpre, kpre, vpre, bq, bk, bv, qpart, kpart, vpart, bgate, gmk, gmv,
    pk, bpk, bpv, gaintwo, bm, gwo, sum_a, sum_b, sum_c,
):
    vm = lambda value, dtype=None: pltpu.VMEM(
        value if isinstance(value, tuple) else value.shape,
        dtype or (bf16 if isinstance(value, tuple) else value.dtype),
    )
    tokens, width = x.shape
    extra = (gwo.shape[0] + 128, width)
    square = (width, width)
    total = sum_a.shape[0] + sum_b.shape[0] + sum_c.shape[0] + width + extra[0]
    chunk_count = total // 256 + 2
    return call(
        finish_layer, 6,
        [shaped(bm.shape, f32), shaped(sum_a.shape), shaped(sum_b.shape), shaped(sum_c.shape),
         shaped(square), shaped(extra)],
        (0,) * 28,
        [vm(x), vm(gain), vm(square), vm(taps), vm(qpre), vm(kpre), vm(vpre), vm(bq), vm(bk), vm(bv),
         vm(qpart), vm(kpart), vm(vpart), vm((tokens, width)), vm(gmk), vm(gmv), vm(pk), vm(bpk),
         vm(bpv), vm(gaintwo), vm(bm), vm(extra), vm(sum_a), vm(sum_b), vm(sum_c), vm(square),
         vm((tokens, width)), vm((tokens + 16, width)), vm(bm), vm((16, 256), f32)]
        + scatter_room(tokens + 16) + wide_room(total) + sems(8 * chunk_count + 24)
        + [pltpu.SemaphoreType.DMA((64 + chunk_count,))],
        8 << 30, 64 << 20,
    )(
        x, gain, wq, wk, wv, wg, taps, qpre, kpre, vpre, bq, bk, bv, qpart, kpart, vpart, bgate, gmk,
        gmv, pk, bpk, bpv, gaintwo, bm, gwo, sum_a, sum_b, sum_c,
    )


def plain_body(
    layer_input,
    out_grad,
    lengths,
    plan,
    norm1_gain,
    w_query,
    w_key,
    w_value,
    w_gate,
    conv_query,
    conv_key,
    conv_value,
    persist_key,
    persist_value,
    mem_w1,
    mem_w2,
    w_out,
    norm2_gain,
    ffn_gate,
    ffn_up,
    ffn_down,
):
    tokens_here = layer_input.shape[0]
    local_width = w_query.shape[1]
    heads_here = local_width // HD
    blocks = tokens_here // STRETCH
    places = jnp.arange(tokens_here)
    row_mask = (places < lengths[0]).astype(f32)
    block_mask = row_mask.reshape(blocks, STRETCH)
    levels = plan[0].astype(f32)
    column_start = lax.axis_index("narrow") * local_width

    def rows_of(values, b):
        return values[b * STRETCH : (b + 1) * STRETCH]

    whole_x = gather_columns(layer_input).astype(f32)
    whole_dy = gather_columns(out_grad)
    inv_one = lax.rsqrt(jnp.mean(whole_x * whole_x, axis=1, keepdims=True) + epsilon)
    unit_one = whole_x * inv_one
    normed_one = (unit_one * norm1_gain).astype(bf16)
    key_pre = product(normed_one, w_key)
    query_pre = product(normed_one, w_query)
    value_pre = product(normed_one, w_value)
    gate_pre = product(normed_one, w_gate)
    key_conv = causal_conv(key_pre, conv_key)
    query_conv = causal_conv(query_pre, conv_query)
    value_conv = causal_conv(value_pre, conv_value)
    key_unit, key_inv = head_norm(jax.nn.silu(key_conv))
    query_unit, query_inv = head_norm(jax.nn.silu(query_conv))
    query_low = query_unit.astype(bf16)
    key_low = key_unit.astype(bf16)
    value_low = jax.nn.silu(value_conv).astype(bf16)

    weight_one, weight_two = mem_w1.astype(f32), mem_w2.astype(f32)
    moment_one = moment_two = None
    saved = []
    for b in range(blocks):
        step_size, momentum, forget = plan_rates(levels[b])
        kept = {"first": weight_one.astype(bf16), "second": weight_two.astype(bf16)}
        mask_rows = block_mask[b][:, None]
        if b < blocks - 1:
            key_rows = gather_columns(rows_of(key_low, b))
            hidden_pre = product(key_rows, kept["first"])
            hidden_act = jax.nn.silu(hidden_pre).astype(bf16)
            predicted = scatter_columns(product(hidden_act, kept["second"]))
            mismatch_here = (
                (predicted - rows_of(value_low, b).astype(f32)) * (mask_rows / STRETCH)
            ).astype(bf16)
            mismatch = gather_columns(mismatch_here)
        query_rows = gather_columns(rows_of(query_low, b))
        query_mem = product(query_rows, kept["first"])
        query_act = jax.nn.silu(query_mem).astype(bf16)
        retrieved = scatter_columns(product(query_act, kept["second"]))
        kept["recalled"] = gather_columns(retrieved.astype(bf16))
        kept.update(query_rows=query_rows, query_mem=query_mem, query_act=query_act)
        if b < blocks - 1:
            through = inner_right(mismatch, kept["second"])
            blended = (through * silu_grad(hidden_pre)).astype(bf16)
            grad_one = inner_left(key_rows, blended)
            grad_two = inner_left(hidden_act, mismatch)
            if moment_one is None:
                moment_one, moment_two = -step_size * grad_one, -step_size * grad_two
            else:
                moment_one = momentum * moment_one - step_size * grad_one
                moment_two = momentum * moment_two - step_size * grad_two
            weight_one = (1.0 - forget) * weight_one + moment_one
            weight_two = (1.0 - forget) * weight_two + moment_two
            kept.update(
                key_rows=key_rows,
                hidden_pre=hidden_pre,
                hidden_act=hidden_act,
                mismatch=mismatch,
                through=through,
                blended=blended,
            )
        saved.append(kept)

    pers_unit, pers_inv = head_norm(persist_key.astype(f32))
    pers_low = pers_unit.astype(bf16)

    def block_scores(b):
        recalled = saved[b]["recalled"]
        mem_unit, mem_inv = head_norm(product(recalled, w_key))
        mem_value = product(recalled, w_value).astype(bf16)
        all_keys = jnp.concatenate(
            [pers_low, mem_unit.astype(bf16), rows_of(key_low, b)], axis=0
        ).reshape(-1, heads_here, HD)
        all_values = jnp.concatenate(
            [persist_value, mem_value, rows_of(value_low, b)], axis=0
        ).reshape(-1, heads_here, HD)
        query_heads = rows_of(query_low, b).reshape(STRETCH, heads_here, HD)
        scores = score_scale * jnp.einsum(
            "qhd,khd->hqk", query_heads, all_keys, preferred_element_type=f32
        )
        scores = jnp.where(visible(block_mask[b])[None], scores, -1e30)
        return (mem_unit, mem_inv, all_keys, all_values, query_heads, scores)

    mixed_list = []
    for b in range(blocks):
        mem_unit, mem_inv, all_keys, all_values, query_heads, scores = block_scores(b)
        row_peak = jnp.max(scores, axis=2, keepdims=True)
        exponent = jnp.exp(scores - row_peak)
        row_total = jnp.sum(exponent, axis=2, keepdims=True)
        prob_low = (exponent / row_total).astype(bf16)
        mixed_list.append(
            jnp.einsum(
                "hqk,khd->qhd", prob_low, all_values, preferred_element_type=f32
            ).reshape(STRETCH, local_width)
        )
        saved[b].update(
            log_total=row_peak + jnp.log(row_total),
            mem_unit=mem_unit,
            mem_inv=mem_inv,
            all_keys=all_keys,
            all_values=all_values,
            query_heads=query_heads,
        )
    mixed_all = jnp.concatenate(mixed_list, axis=0)
    gate_sig = jax.nn.sigmoid(gate_pre)
    gated = (mixed_all * gate_sig).astype(bf16)
    branch_here = scatter_columns(product(gated, w_out))
    branch_full = gather_columns(branch_here.astype(bf16)).astype(f32)
    middle = whole_x + branch_full
    middle_here = layer_input.astype(f32) + branch_here
    inv_two = lax.rsqrt(jnp.mean(middle * middle, axis=1, keepdims=True) + epsilon)
    unit_two = middle * inv_two
    normed_two = (unit_two * norm2_gain).astype(bf16)
    ffn_pre = product(normed_two, ffn_gate)
    up_pre = product(normed_two, ffn_up)
    ffn_sig = jax.nn.sigmoid(ffn_pre)
    hidden_low = (ffn_pre * ffn_sig * up_pre).astype(bf16)
    back_hidden = inner_right(whole_dy, ffn_down)
    back_up_low = (back_hidden * ffn_pre * ffn_sig).astype(bf16)
    back_ffn_low = (back_hidden * up_pre * silu_grad(ffn_pre)).astype(bf16)
    back_normed_two = inner_right(back_ffn_low, ffn_gate) + inner_right(back_up_low, ffn_up)
    gain_two_part = jnp.sum(back_normed_two * unit_two, axis=0)
    middle_part = norm_back(back_normed_two, unit_two, inv_two, norm2_gain)
    back_middle_here = scatter_columns(middle_part)
    grad_ffn_down = inner_left(hidden_low, whole_dy)
    grad_ffn_gate = inner_left(normed_two, back_ffn_low)
    grad_ffn_up = inner_left(normed_two, back_up_low)
    ffn_here = scatter_columns(product(hidden_low, ffn_down))
    layer_output = (middle_here + ffn_here).astype(bf16)
    back_middle_here = back_middle_here + out_grad.astype(f32)
    back_branch = gather_columns(back_middle_here.astype(bf16))
    grad_ffn_gate, grad_ffn_up, grad_ffn_down = sum_wide(
        [grad_ffn_gate, grad_ffn_up, grad_ffn_down]
    )
    grad_w_out = inner_left(gated, back_branch)
    back_gated = inner_right(back_branch, w_out)
    back_mixed_low = (back_gated * gate_sig).astype(bf16)
    back_gate_low = (back_gated * mixed_all * gate_sig * (1.0 - gate_sig)).astype(bf16)

    back_recalled_parts = []
    mem_key_grad = mem_value_grad = 0.0
    pers_key_acc = grad_persist_value = 0.0
    back_query_att, back_key_att, back_value_att = [], [], []
    for b in range(blocks):
        kept = saved[b]
        scores = score_scale * jnp.einsum(
            "qhd,khd->hqk", kept["query_heads"], kept["all_keys"], preferred_element_type=f32
        )
        scores = jnp.where(visible(block_mask[b])[None], scores, -1e30)
        prob_rows = jnp.exp(scores - kept["log_total"])
        prob_low = prob_rows.astype(bf16)
        back_heads = rows_of(back_mixed_low, b).reshape(STRETCH, heads_here, HD)
        back_all_values = jnp.einsum(
            "hqk,qhd->khd", prob_low, back_heads, preferred_element_type=f32
        )
        back_probs = jnp.einsum(
            "qhd,khd->hqk", back_heads, kept["all_values"], preferred_element_type=f32
        )
        back_scores = (
            prob_rows * (back_probs - jnp.sum(prob_rows * back_probs, axis=2, keepdims=True))
        ).astype(bf16)
        back_query = score_scale * jnp.einsum(
            "hqk,khd->qhd", back_scores, kept["all_keys"], preferred_element_type=f32
        )
        back_all_keys = score_scale * jnp.einsum(
            "hqk,qhd->khd", back_scores, kept["query_heads"], preferred_element_type=f32
        )
        back_all_keys = back_all_keys.reshape(-1, local_width)
        back_all_values = back_all_values.reshape(-1, local_width)
        back_mem_key = head_back(
            back_all_keys[NP : NP + STRETCH], kept["mem_unit"], kept["mem_inv"]
        ).astype(bf16)
        back_mem_value = back_all_values[NP : NP + STRETCH].astype(bf16)
        back_recalled_parts.append(
            inner_right(back_mem_key, w_key) + inner_right(back_mem_value, w_value)
        )
        mem_key_grad = mem_key_grad + inner_left(kept["recalled"], back_mem_key)
        mem_value_grad = mem_value_grad + inner_left(kept["recalled"], back_mem_value)
        pers_key_acc = pers_key_acc + back_all_keys[:NP]
        grad_persist_value = grad_persist_value + back_all_values[:NP]
        back_query_att.append(back_query.reshape(STRETCH, local_width))
        back_key_att.append(back_all_keys[NP + STRETCH :])
        back_value_att.append(back_all_values[NP + STRETCH :])
    grad_persist_key = head_back(pers_key_acc, pers_unit, pers_inv)

    cot_one = cot_two = mom_one = mom_two = None
    key_total, query_total, value_total = [None] * blocks, [None] * blocks, [None] * blocks
    for b in reversed(range(blocks)):
        kept = saved[b]
        step_size, momentum, forget = plan_rates(levels[b])
        first_low, second_low = kept["first"], kept["second"]
        back_recalled = gather_columns(scatter_columns(back_recalled_parts[b]).astype(bf16))
        new_one = new_two = None
        if cot_one is None:
            key_total[b], value_total[b] = back_key_att[b], back_value_att[b]
        else:
            key_rows, hidden_pre = kept["key_rows"], kept["hidden_pre"]
            hidden_slope = silu_grad(hidden_pre)
            total_one = cot_one if mom_one is None else mom_one + cot_one
            total_two = cot_two if mom_two is None else mom_two + cot_two
            back_g1 = (-step_size * total_one).astype(bf16)
            back_g2 = (-step_size * total_two).astype(bf16)
            back_blended = product(key_rows, back_g1)
            back_through = (back_blended * hidden_slope).astype(bf16)
            mismatch_part = product(kept["hidden_act"], back_g2) + product(
                back_through, second_low
            )
            mismatch_low = scatter_columns(mismatch_part).astype(bf16)
            back_mismatch = gather_columns(mismatch_low)
            key_part = inner_right(kept["blended"], back_g1)
            back_hidden_act = inner_right(kept["mismatch"], back_g2)
            extra_pre = back_blended * kept["through"] * silu_curve(hidden_pre)
            new_one = (1.0 - forget) * cot_one
            new_two = (1.0 - forget) * cot_two + inner_left(back_through, kept["mismatch"])
        back_query_act = inner_right(back_recalled, second_low)
        back_query_pre = (back_query_act * silu_grad(kept["query_mem"])).astype(bf16)
        query_part = inner_right(back_query_pre, first_low)
        one_term = inner_left(kept["query_rows"], back_query_pre)
        two_term = inner_left(kept["query_act"], back_recalled)
        new_one = one_term if new_one is None else new_one + one_term
        new_two = two_term if new_two is None else new_two + two_term
        if cot_one is not None:
            scale_rows = (block_mask[b] / STRETCH).astype(bf16)[:, None]
            back_pred = back_mismatch * scale_rows
            value_part = -(mismatch_low.astype(f32) * scale_rows.astype(f32))
            back_hidden_act = back_hidden_act + inner_right(back_pred, second_low)
            new_two = new_two + inner_left(kept["hidden_act"], back_pred)
            back_hidden_pre = (back_hidden_act * hidden_slope + extra_pre).astype(bf16)
            key_part = key_part + inner_right(back_hidden_pre, first_low)
            new_one = new_one + inner_left(key_rows, back_hidden_pre)
            key_total[b] = back_key_att[b] + scatter_columns(key_part)
            value_total[b] = back_value_att[b] + value_part
            mom_one, mom_two = momentum * total_one, momentum * total_two
        query_total[b] = back_query_att[b] + scatter_columns(query_part)
        cot_one, cot_two = new_one, new_two
    grad_mem_w1, grad_mem_w2 = cot_one, cot_two

    back_query_total = jnp.concatenate(query_total, axis=0)
    back_key_total = jnp.concatenate(key_total, axis=0)
    back_value_total = jnp.concatenate(value_total, axis=0)
    query_conv_back = head_back(back_query_total, query_unit, query_inv) * silu_grad(query_conv)
    key_conv_back = head_back(back_key_total, key_unit, key_inv) * silu_grad(key_conv)
    value_conv_back = back_value_total * silu_grad(value_conv)
    query_pre_back, grad_conv_query = conv_back(query_conv_back, query_pre, conv_query)
    key_pre_back, grad_conv_key = conv_back(key_conv_back, key_pre, conv_key)
    value_pre_back, grad_conv_value = conv_back(value_conv_back, value_pre, conv_value)
    query_pre_low = query_pre_back.astype(bf16)
    key_pre_low = key_pre_back.astype(bf16)
    value_pre_low = value_pre_back.astype(bf16)
    back_normed_one = (
        inner_right(back_gate_low, w_gate)
        + inner_right(query_pre_low, w_query)
        + inner_right(key_pre_low, w_key)
        + inner_right(value_pre_low, w_value)
    )
    gain_one_part = jnp.sum(back_normed_one * unit_one, axis=0)
    input_part = norm_back(back_normed_one, unit_one, inv_one, norm1_gain)
    back_input_here = scatter_columns(input_part)
    grad_w_gate = inner_left(normed_one, back_gate_low)
    grad_w_query = inner_left(normed_one, query_pre_low)
    grad_w_key = inner_left(normed_one, key_pre_low) + mem_key_grad
    grad_w_value = inner_left(normed_one, value_pre_low) + mem_value_grad
    input_grad = back_middle_here + back_input_here

    gains = lax.psum(
        jnp.concatenate([gain_one_part, gain_two_part]).astype(bf16), ("narrow", "wide")
    ).astype(f32)
    full_width = whole_x.shape[1]
    grad_norm1_gain = lax.dynamic_slice_in_dim(gains, column_start, local_width, 0)
    grad_norm2_gain = lax.dynamic_slice_in_dim(gains, full_width + column_start, local_width, 0)
    late = (
        grad_w_query, grad_w_key, grad_w_value, grad_w_gate, grad_conv_query, grad_conv_key,
        grad_conv_value, grad_persist_key, grad_persist_value, grad_mem_w1, grad_mem_w2, grad_w_out,
    )
    late, (grad_ffn_gate, grad_ffn_up, grad_ffn_down) = lax.optimization_barrier(
        (tuple(v.astype(bf16) for v in late), (grad_ffn_gate, grad_ffn_up, grad_ffn_down))
    )
    (
        grad_w_query, grad_w_key, grad_w_value, grad_w_gate, grad_conv_query, grad_conv_key,
        grad_conv_value, grad_persist_key, grad_persist_value, grad_mem_w1, grad_mem_w2, grad_w_out,
    ) = sum_wide(late)
    return (
        layer_output,
        input_grad,
        grad_norm1_gain,
        grad_w_query,
        grad_w_key,
        grad_w_value,
        grad_w_gate,
        grad_conv_query,
        grad_conv_key,
        grad_conv_value,
        grad_persist_key,
        grad_persist_value,
        grad_mem_w1,
        grad_mem_w2,
        grad_w_out,
        grad_norm2_gain,
        grad_ffn_gate,
        grad_ffn_up,
        grad_ffn_down,
    )

def linked_body(
    layer_input, out_grad, lengths, plan, norm1_gain, w_query, w_key, w_value, w_gate,
    conv_query, conv_key, conv_value, persist_key, persist_value, mem_w1, mem_w2, w_out,
    norm2_gain, ffn_gate, ffn_up, ffn_down,
):
    step_size, momentum, forget = plan_rates(plan[0, 0].astype(f32))
    rates = jnp.stack([lengths[0].astype(f32), step_size, 1.0 - forget])
    rates = jnp.concatenate([rates, jnp.zeros((5,), f32)])
    low_x = gather_columns(layer_input)
    whole_x = low_x.astype(f32)
    inv_one = lax.rsqrt(jnp.mean(whole_x * whole_x, axis=1, keepdims=True) + epsilon)
    unit_one = whole_x * inv_one
    normed_one = (unit_one * norm1_gain).astype(bf16)
    key_pre = product(normed_one, w_key)
    query_pre = product(normed_one, w_query)
    value_pre = product(normed_one, w_value)
    gate_pre = product(normed_one, w_gate).astype(bf16)
    key_conv = causal_conv(key_pre, conv_key)
    query_conv = causal_conv(query_pre, conv_query)
    value_conv = causal_conv(value_pre, conv_value)
    key_unit, key_inv = head_norm(jax.nn.silu(key_conv))
    query_unit, query_inv = head_norm(jax.nn.silu(query_conv))
    query_low = query_unit.astype(bf16)
    key_low = key_unit.astype(bf16)
    value_low = jax.nn.silu(value_conv).astype(bf16)
    pers_unit, pers_inv = head_norm(persist_key.astype(f32))
    pers_low = pers_unit.astype(bf16)

    keys, queries, pre, act, mis, thr, ble, qpre, qact, rec, next_one, next_two = run_memory_forward(
        key_low, query_low, value_low, mem_w1, mem_w2, rates
    )
    branch, branch_here, mixed, gated, whole_dy = run_attend_forward(
        query_low, key_low, value_low, rec, w_key, w_value, pers_low, persist_value, gate_pre,
        w_out, out_grad, rates,
    )
    layer_output, back_middle, back_branch, gain_two, grad_ffn_gate, grad_ffn_up, grad_ffn_down = (
        run_feed_forward(
            low_x, branch, branch_here, whole_dy, layer_input, out_grad, norm2_gain[None], ffn_gate,
            ffn_up, ffn_down,
        )
    )
    side_rows = 768
    (
        gate_first, grad_w_out, back_gate, mem_key_grad, mem_value_grad, back_query_att, back_key_att,
        back_value_att, pers_key_acc, grad_persist_value, late_rec, back_rec,
    ) = run_attend_backward(
        query_low, key_low, value_low, rec, w_key, w_value, pers_low, persist_value, gate_pre,
        w_out, mixed, gated, back_branch, grad_ffn_gate, rates, side_rows,
    )
    gate_second, grad_ffn_up, grad_mem_w1, grad_mem_w2, key_part, query_part, value_part = run_memory_backward(
        back_rec, late_rec, keys, queries, pre, act, mis, thr, ble, qpre, qact, mem_w1, mem_w2,
        next_one, next_two, grad_ffn_gate, grad_ffn_up, rates, grad_ffn_gate.shape[0] - side_rows,
    )
    taps = jnp.concatenate([conv_query, conv_key, conv_value], axis=0)
    input_grad, grad_ffn_down, grad_mem_w1, grad_mem_w2, packed, extra = run_finish_layer(
        low_x, norm1_gain[None], w_query, w_key, w_value, w_gate, taps, query_pre, key_pre, value_pre,
        back_query_att, back_key_att, back_value_att, query_part, key_part, value_part, back_gate,
        mem_key_grad, mem_value_grad, persist_key, pers_key_acc, grad_persist_value, gain_two,
        back_middle, grad_w_out, grad_ffn_down, grad_mem_w1, grad_mem_w2,
    )
    grad_ffn_gate = jnp.concatenate([gate_first, gate_second], axis=0)
    local_width, start = w_query.shape[1], w_out.shape[0]
    parts = [packed[:, i * local_width : (i + 1) * local_width].astype(f32) for i in range(4)]
    small = extra[start : start + 16].astype(f32)
    pers_key, pers_value, convs, gains = [
        small[:, i * local_width : (i + 1) * local_width] for i in range(4)
    ]
    return (
        layer_output, input_grad, gains[0], *parts, convs[0:4], convs[4:8], convs[8:12], pers_key,
        pers_value, grad_mem_w1.astype(f32), grad_mem_w2.astype(f32), extra[:start].astype(f32),
        gains[1], grad_ffn_gate.astype(f32), grad_ffn_up.astype(f32), grad_ffn_down.astype(f32),
    )


def body(*arrays):
    tokens_here, local_width = arrays[0].shape
    width, units = arrays[14].shape
    linked = (
        (lax.axis_size("wide"), lax.axis_size("narrow")) == (8, 4)
        and local_width == 256
        and tokens_here == 2 * STRETCH
        and (width, units) == (1024, 1024)
        and arrays[18].shape == (1024, 1024)
    )
    return linked_body(*arrays) if linked else plain_body(*arrays)


def solution(mesh):
    return jax.shard_map(
        body,
        mesh=mesh,
        in_specs=(
            P("wide", "narrow"),
            P("wide", "narrow"),
            P("wide"),
            P("wide", None),
            P(),
            P(None, "narrow"),
            P(None, "narrow"),
            P(None, "narrow"),
            P(None, "narrow"),
            P(None, "narrow"),
            P(None, "narrow"),
            P(None, "narrow"),
            P(None, "narrow"),
            P(None, "narrow"),
            P(None, "narrow"),
            P("narrow", None),
            P("narrow", None),
            P(),
            P(None, "narrow"),
            P(None, "narrow"),
            P("narrow", None),
        ),
        out_specs=(
            P("wide", "narrow"),
            P("wide", "narrow"),
            P("narrow"),
            P(None, "narrow"),
            P(None, "narrow"),
            P(None, "narrow"),
            P(None, "narrow"),
            P(None, "narrow"),
            P(None, "narrow"),
            P(None, "narrow"),
            P(None, "narrow"),
            P(None, "narrow"),
            P(None, "narrow"),
            P("narrow", None),
            P("narrow", None),
            P("narrow"),
            P(None, "narrow"),
            P(None, "narrow"),
            P("narrow", None),
        ),
        check_vma=False,
    )
```

```python
import jax
import jax.numpy as jnp
from jax import lax
from jax.experimental import pallas as pl
from jax.experimental.pallas import tpu as pltpu
from jax.sharding import PartitionSpec as P

HD = 64
NP = 16
KW = 4
STRETCH = 512

epsilon = 1e-06
head_floor = 1.0
score_scale = 12.0
bf16 = jnp.bfloat16
f32 = jnp.float32


def product(left_side, right_side):
    return jnp.dot(left_side, right_side, preferred_element_type=f32)


def inner_left(left_side, right_side):
    return lax.dot_general(
        left_side, right_side, (((0,), (0,)), ((), ())), preferred_element_type=f32
    )


def inner_right(left_side, right_side):
    return lax.dot_general(
        left_side, right_side, (((1,), (1,)), ((), ())), preferred_element_type=f32
    )


def silu_grad(values):
    logistic = jax.nn.sigmoid(values)
    return logistic * (1.0 + values * (1.0 - logistic))


def silu_curve(values):
    logistic = jax.nn.sigmoid(values)
    logistic_slope = logistic * (1.0 - logistic)
    return logistic_slope * (1.0 + values * (1.0 - logistic)) + logistic * (
        1.0 - logistic - values * logistic_slope
    )


def plan_rates(level_now):
    return (0.1 * jnp.exp2(level_now), 0.9 - 0.2 * level_now, 0.02 + 0.05 * level_now)


def head_sums(values):
    width = values.shape[1]
    places = jnp.arange(width) // HD
    same_head = (places[:, None] == places[None, :]).astype(f32)
    return jnp.dot(
        values, same_head, precision=lax.Precision.HIGHEST, preferred_element_type=f32
    )


def head_norm(values):
    inv_norm = lax.rsqrt(head_sums(values * values) + head_floor)
    return (values * inv_norm, inv_norm)


def head_back(grad_rows, unit_rows, inv_norm):
    return (grad_rows - unit_rows * head_sums(grad_rows * unit_rows)) * inv_norm


def norm_back(grad_rows, unit_rows, inv_rows, gain_vec):
    scaled = grad_rows * gain_vec
    return inv_rows * (scaled - unit_rows * jnp.mean(scaled * unit_rows, axis=1, keepdims=True))


def shift_down(values, offset):
    return jnp.concatenate(
        [jnp.zeros((offset, values.shape[1]), values.dtype), values[:-offset]], axis=0
    )


def shift_up(values, offset):
    return jnp.concatenate(
        [values[offset:], jnp.zeros((offset, values.shape[1]), values.dtype)], axis=0
    )


def causal_conv(values, conv_taps):
    result = values * conv_taps[0]
    for offset in range(1, KW):
        result = result + shift_down(values, offset) * conv_taps[offset]
    return result


def conv_back(grad_rows, values, conv_taps):
    back_values = grad_rows * conv_taps[0]
    tap_grads = [jnp.sum(grad_rows * values, axis=0)]
    for offset in range(1, KW):
        back_values = back_values + shift_up(grad_rows, offset) * conv_taps[offset]
        tap_grads.append(jnp.sum(grad_rows * shift_down(values, offset), axis=0))
    return (back_values, jnp.stack(tap_grads, axis=0))


def visible(mask_rows):
    row_width = mask_rows.shape[0]
    places = jnp.arange(row_width)
    valid_keys = mask_rows[None, :] > 0.5
    causal = (places[None, :] <= places[:, None]) & valid_keys
    memory_seen = jnp.broadcast_to(valid_keys, (row_width, row_width))
    persistent = jnp.ones((row_width, NP), dtype=bool)
    return jnp.concatenate([persistent, memory_seen, causal], axis=1)


def gather_columns(values):
    return lax.all_gather(values, "narrow", axis=1, tiled=True)


def scatter_columns(values):
    return lax.psum_scatter(
        values.astype(bf16), "narrow", scatter_dimension=1, tiled=True
    ).astype(f32)


def sum_wide(values):
    return [lax.psum(v.astype(bf16), "wide").astype(f32) for v in values]


MESH = pl.DeviceIdType.MESH
ANY = pl.BlockSpec(memory_space=pl.ANY)
SCALARS = pl.BlockSpec(memory_space=pltpu.SMEM)
VMEM_LIMIT = 60 << 20


def group_places():
    me = lax.axis_index("narrow")
    core = lax.rem(me, 2)
    sib = me + 1 - 2 * core
    opp = lax.rem(me + 2, 4)
    diag = lax.rem(sib + 2, 4)
    return me, sib, opp, diag


def cols(index, width=256):
    return pl.ds(pl.multiple_of(index * width, width), width)


def enter_group(sib, opp):
    barrier = pltpu.get_barrier_semaphore()
    for peer in (sib, opp):
        pl.semaphore_signal(barrier, inc=1, device_id={"narrow": peer}, device_id_type=MESH)
    pl.semaphore_wait(barrier, 2)


class Wire:
    def __init__(self, send, recv):
        self.send, self.recv, self.used = send, recv, 0

    def to(self, source, target, device, axis="narrow"):
        k = self.used
        self.used += 1
        return pltpu.make_async_remote_copy(
            src_ref=source,
            dst_ref=target,
            send_sem=self.send.at[k],
            recv_sem=self.recv.at[k],
            device_id={axis: device},
            device_id_type=MESH,
        )


class Local:
    def __init__(self, sems):
        self.sems, self.used, self.open = sems, 0, []

    def start(self, source, target, late=False):
        copy = pltpu.make_async_copy(source, target, self.sems.at[self.used])
        self.used += 1
        copy.start()
        if late:
            self.open.append(copy)
        return copy

    def finish(self):
        for copy in self.open:
            copy.wait()
        self.open = []


class Gather:
    def __init__(self, wire, full, rows, places):
        me, sib, opp, diag = places
        own = full.at[rows, cols(me)]
        passed = full.at[rows, cols(opp)]
        self.far = wire.to(own, own, opp)
        self.near = wire.to(own, own, sib)
        self.relayed = wire.to(passed, passed, sib)

    def start(self):
        self.far.start()
        self.near.start()

    def relay(self):
        self.far.wait_recv()
        self.relayed.start()

    def end(self):
        self.near.wait_recv()
        self.relayed.wait_recv()

    def drain(self):
        self.far.wait_send()
        self.near.wait_send()
        self.relayed.wait_send()


class Scatter:
    def __init__(self, wire, part, rows, first, passed, last, places):
        me, sib, opp, diag = places
        self.part, self.rows, self.places = part, rows, places
        self.first, self.passed, self.last = first, passed, last
        self.pass_on = wire.to(part.at[rows, cols(diag)], first.at[1, rows], sib)
        self.keep = wire.to(part.at[rows, cols(sib)], first.at[0, rows], sib)
        self.far = wire.to(passed.at[rows], last.at[rows], opp)

    def start(self):
        self.pass_on.start()
        self.keep.start()

    def middle(self):
        me, sib, opp, diag = self.places
        self.pass_on.wait_recv()
        self.passed[self.rows] = (
            self.part[self.rows, cols(opp)].astype(f32) + self.first[1, self.rows].astype(f32)
        ).astype(bf16)
        self.far.start()

    def end(self):
        me, sib, opp, diag = self.places
        self.keep.wait_recv()
        near = self.part[self.rows, cols(me)].astype(f32) + self.first[0, self.rows].astype(f32)
        self.far.wait_recv()
        return near + self.last[self.rows].astype(f32)

    def drain(self):
        self.pass_on.wait_send()
        self.keep.wait_send()
        self.far.wait_send()


def scatter_room(rows):
    return [
        pltpu.VMEM((2, rows, 256), bf16),
        pltpu.VMEM((rows, 256), bf16),
        pltpu.VMEM((rows, 256), bf16),
    ]


def sems(count):
    return [
        pltpu.SemaphoreType.DMA((count,)),
        pltpu.SemaphoreType.DMA((count,)),
    ]


def shaped(shape, dtype=None):
    return jax.ShapeDtypeStruct(shape, bf16 if dtype is None else dtype)


def call(kernel, collective, outs, ins, scratch, flops, moved):
    return pl.pallas_call(
        kernel,
        out_shape=outs,
        in_specs=[SCALARS if s else ANY for s in ins],
        out_specs=[ANY] * len(outs),
        scratch_shapes=scratch,
        compiler_params=pltpu.CompilerParams(
            collective_id=collective, has_side_effects=True, vmem_limit_bytes=VMEM_LIMIT
        ),
        cost_estimate=pl.CostEstimate(flops=flops, bytes_accessed=moved, transcendentals=0),
        name=kernel.__name__,
    )


def memory_forward(
    key_in, query_in, value_in, one_in, two_in, rates,
    key_out, query_out, pre_out, act_out, mis_out, thr_out, ble_out, qpre_out, qact_out,
    rec_out, one_out, two_out,
    key, query, value, one, two, pre, act, part, mis, thr, ble, qpre, qact, qpart, rec,
    next_one, next_two, first, passed, last, qfirst, qpassed, qlast,
    send, recv, local_sems,
):
    places = group_places()
    me, sib, opp, diag = places
    wire, local = Wire(send, recv), Local(local_sems)
    half, block = STRETCH // 2, STRETCH
    get_key = local.start(key_in.at[pl.ds(0, block)], key.at[:, cols(me)])
    get_query = local.start(query_in, query.at[:, cols(me)])
    get_one = local.start(one_in, one)
    get_two = local.start(two_in, two)
    get_value = local.start(value_in.at[pl.ds(0, block)], value)
    enter_group(sib, opp)
    pieces = [pl.ds(c * half, half) for c in range(2)]
    blocks = [pl.ds(b * block, block) for b in range(2)]
    get_key.wait()
    keys = [Gather(wire, key, rows, places) for rows in pieces]
    for g in keys:
        g.start()
    get_one.wait()
    get_two.wait()
    get_query.wait()
    get_value.wait()
    queries = [Gather(wire, query, rows, places) for rows in blocks]
    sums = [Scatter(wire, part, rows, first, passed, last, places) for rows in pieces]
    for c in range(2):
        rows = pieces[c]
        keys[c].relay()
        if c == 1:
            queries[0].start()
            sums[0].middle()
        keys[c].end()
        hidden = jnp.dot(key[rows, :], one[...], preferred_element_type=f32)
        pre[rows, :] = hidden.astype(bf16)
        act[rows, :] = (hidden * jax.nn.sigmoid(hidden)).astype(bf16)
        part[rows, :] = jnp.dot(act[rows, :], two[...], preferred_element_type=f32).astype(bf16)
        sums[c].start()
    local.start(key, key_out, late=True)
    local.start(pre, pre_out, late=True)
    local.start(act, act_out, late=True)
    sums[1].middle()
    misses = [Gather(wire, mis, rows, places) for rows in pieces]
    for c in range(2):
        rows = pieces[c]
        predicted = sums[c].end()
        index = lax.broadcasted_iota(jnp.int32, (half, 1), 0) + c * half
        scale = jnp.where(index.astype(f32) < rates[0], 1.0 / STRETCH, 0.0)
        mis[rows, cols(me)] = ((predicted - value[rows, :].astype(f32)) * scale).astype(bf16)
        misses[c].start()
    queries[0].relay()
    queries[1].start()
    queries[0].end()
    qsums = [Scatter(wire, qpart, rows, qfirst, qpassed, qlast, places) for rows in blocks]

    def read(b, weight_one, weight_two):
        rows = blocks[b]
        asked = jnp.dot(query[rows, :], weight_one[...], preferred_element_type=f32)
        qpre[rows, :] = asked.astype(bf16)
        qact[rows, :] = (asked * jax.nn.sigmoid(asked)).astype(bf16)
        qpart[rows, :] = jnp.dot(
            qact[rows, :], weight_two[...], preferred_element_type=f32
        ).astype(bf16)
        qsums[b].start()

    misses[0].relay()
    read(0, one, two)
    misses[1].relay()
    for c in range(2):
        rows = pieces[c]
        misses[c].end()
        through = lax.dot_general(
            mis[rows, :], two[...], (((1,), (1,)), ((), ())), preferred_element_type=f32
        )
        thr[rows, :] = through.astype(bf16)
        ble[rows, :] = (through * silu_grad(pre[rows, :].astype(f32))).astype(bf16)
    qsums[0].middle()
    local.start(mis, mis_out, late=True)
    local.start(thr, thr_out, late=True)
    local.start(ble, ble_out, late=True)
    step_size, keep = rates[1], rates[2]

    def update(c, carried):
        rows = pl.ds(pl.multiple_of(c * half, half), half)
        grad = lax.dot_general(
            key[:, rows], ble[...], (((0,), (0,)), ((), ())), preferred_element_type=f32
        )
        next_one[rows, :] = (keep * one[rows, :].astype(f32) - step_size * grad).astype(bf16)
        grad = lax.dot_general(
            act[:, rows], mis[...], (((0,), (0,)), ((), ())), preferred_element_type=f32
        )
        next_two[rows, :] = (keep * two[rows, :].astype(f32) - step_size * grad).astype(bf16)
        return carried

    lax.fori_loop(0, 4, update, 0)
    local.start(next_one, one_out, late=True)
    local.start(next_two, two_out, late=True)
    queries[1].relay()
    reads = [Gather(wire, rec, rows, places) for rows in blocks]
    rec[blocks[0], cols(me)] = qsums[0].end().astype(bf16)
    reads[0].start()
    queries[1].end()
    local.start(query, query_out, late=True)
    read(1, next_one, next_two)
    local.start(qpre, qpre_out, late=True)
    local.start(qact, qact_out, late=True)
    qsums[1].middle()
    reads[0].relay()
    rec[blocks[1], cols(me)] = qsums[1].end().astype(bf16)
    reads[1].start()
    reads[0].end()
    local.start(rec.at[blocks[0]], rec_out.at[blocks[0]], late=True)
    reads[1].relay()
    reads[1].end()
    local.start(rec.at[blocks[1]], rec_out.at[blocks[1]], late=True)
    for item in keys + queries + sums + misses + qsums + reads:
        item.drain()
    local.finish()


def run_memory_forward(key_low, query_low, value_low, mem_w1, mem_w2, rates):
    block, tokens, width, units = STRETCH, query_low.shape[0], mem_w1.shape[0], mem_w1.shape[1]
    small, big, square = (block, width), (tokens, width), (width, units)
    return call(
        memory_forward, 1,
        [shaped(small), shaped(big), shaped(small), shaped(small), shaped(small), shaped(small),
         shaped(small), shaped(big), shaped(big), shaped(big), shaped(square), shaped(square)],
        (0, 0, 0, 0, 0, 1),
        [pltpu.VMEM(small, bf16), pltpu.VMEM(big, bf16), pltpu.VMEM((block, 256), bf16),
         pltpu.VMEM(square, bf16), pltpu.VMEM(square, bf16)]
        + [pltpu.VMEM(small, bf16)] * 6
        + [pltpu.VMEM(big, bf16)] * 4
        + [pltpu.VMEM(square, bf16)] * 2
        + scatter_room(block) + scatter_room(tokens)
        + sems(40) + [pltpu.SemaphoreType.DMA((24,))],
        9 * 2 * block * width * units, 24 << 20,
    )(key_low, query_low, value_low, mem_w1, mem_w2, rates)


KEY_ROWS = 2 * STRETCH + 128


def silu(values):
    return values * jax.nn.sigmoid(values)


def head_ones():
    left = lax.broadcasted_iota(jnp.int32, (256, 256), 0) // HD
    right = lax.broadcasted_iota(jnp.int32, (256, 256), 1) // HD
    return (left == right).astype(f32).astype(bf16)


def split_sums(values, ones):
    high = values.astype(bf16)
    rest = (values - high.astype(f32)).astype(bf16)
    return jnp.dot(high, ones, preferred_element_type=f32) + jnp.dot(
        rest, ones, preferred_element_type=f32
    )


def head_only(values, head):
    lane_head = lax.broadcasted_iota(jnp.int32, values.shape, 1) // HD
    return jnp.where(lane_head == head, values.astype(f32), 0.0).astype(bf16)


def key_bias(first_row, rows, valid, flipped):
    shape = (KEY_ROWS, rows) if flipped else (rows, KEY_ROWS)
    slot = lax.broadcasted_iota(jnp.int32, shape, 0 if flipped else 1)
    row = lax.broadcasted_iota(jnp.int32, shape, 1 if flipped else 0) + first_row
    memory = (slot < STRETCH) & (slot.astype(f32) < valid)
    place = slot - STRETCH
    causal = (place >= 0) & (place <= row) & (place.astype(f32) < valid) & (slot < 2 * STRETCH)
    persistent = (slot >= 2 * STRETCH) & (slot < 2 * STRETCH + NP)
    return jnp.where(memory | causal | persistent, 0.0, -1e30)


def attend_forward(
    query_in, key_in, value_in, rec_in, wk_in, wv_in, pk_in, pv_in, gate_in, wo_in, dy_in, rates,
    branch_out, here_out, mixed_out, gated_out, dy_out,
    query, key, value, rec, wk, wv, gate, wo, dy, keys, values, bias, mixed, gated, part, branch,
    here, first, passed, last, send, recv, local_sems,
):
    places = group_places()
    me, sib, opp, diag = places
    wire, local = Wire(send, recv), Local(local_sems)
    half, block = STRETCH // 2, STRETCH
    loads = [
        local.start(dy_in, dy.at[:, cols(me)]),
        local.start(rec_in, rec), local.start(wk_in, wk), local.start(wv_in, wv),
        local.start(query_in, query), local.start(key_in, key), local.start(value_in, value),
        local.start(gate_in, gate), local.start(wo_in, wo),
        local.start(pk_in, keys.at[pl.ds(2 * block, NP)]),
        local.start(pv_in, values.at[pl.ds(2 * block, NP)]),
    ]
    keys[pl.ds(2 * block + NP, 128 - NP), :] = jnp.zeros((128 - NP, 256), bf16)
    values[pl.ds(2 * block + NP, 128 - NP), :] = jnp.zeros((128 - NP, 256), bf16)
    enter_group(sib, opp)
    for item in loads:
        item.wait()
    blocks = [pl.ds(b * block, block) for b in range(2)]
    pieces = [pl.ds(c * half, half) for c in range(4)]
    grads = [Gather(wire, dy, rows, places) for rows in blocks]
    grads[0].start()
    ones = head_ones()
    sums = [Scatter(wire, part, rows, first, passed, last, places) for rows in pieces]
    joins = [Gather(wire, branch, rows, places) for rows in pieces]

    def finish(c):
        rows = pieces[c]
        got = sums[c].end()
        here[rows, :] = got
        branch[rows, cols(me)] = got.astype(bf16)
        joins[c].start()

    for c in range(4):
        b, rows = c // 2, pieces[c]
        if c % 2 == 0:
            memory = rec[blocks[b], :]
            made = jnp.dot(memory, wk[...], preferred_element_type=f32)
            inv = lax.rsqrt(split_sums(made * made, ones) + head_floor)
            keys[pl.ds(0, block), :] = (made * inv).astype(bf16)
            values[pl.ds(0, block), :] = jnp.dot(
                memory, wv[...], preferred_element_type=f32
            ).astype(bf16)
            keys[pl.ds(block, block), :] = key[blocks[b], :]
            values[pl.ds(block, block), :] = value[blocks[b], :]
        bias[...] = key_bias((c % 2) * half, half, rates[0] - float(b * block), False)

        def one_head(head, total):
            asked = head_only(query[rows, :], head)
            scores = lax.dot_general(
                asked, keys[...], (((1,), (1,)), ((), ())), preferred_element_type=f32
            )
            weights = jnp.exp(score_scale * scores + bias[...])
            inv = 1.0 / jnp.sum(weights, axis=1, keepdims=True)
            read = jnp.dot(
                (weights * inv).astype(bf16), values[...], preferred_element_type=f32
            )
            lane_head = lax.broadcasted_iota(jnp.int32, read.shape, 1) // HD
            return jnp.where(lane_head == head, read, total)

        got = lax.fori_loop(0, 4, one_head, jnp.zeros((half, 256), f32))
        mixed[rows, :] = got.astype(bf16)
        gated[rows, :] = (got * jax.nn.sigmoid(gate[rows, :].astype(f32))).astype(bf16)
        part[rows, :] = jnp.dot(gated[rows, :], wo[...], preferred_element_type=f32).astype(bf16)
        sums[c].start()
        if c == 0:
            grads[0].relay()
            grads[1].start()
            sums[0].middle()
        if c == 1:
            sums[1].middle()
            grads[0].end()
            finish(0)
        if c == 2:
            grads[1].relay()
            sums[2].middle()
            joins[0].relay()
            finish(1)
    grads[1].end()
    local.start(dy, dy_out, late=True)
    local.start(mixed, mixed_out, late=True)
    local.start(gated, gated_out, late=True)
    sums[3].middle()
    finish(2)
    joins[1].relay()
    finish(3)
    local.start(here, here_out, late=True)
    joins[2].relay()
    joins[3].relay()
    for item in joins:
        item.end()
    local.start(branch, branch_out, late=True)
    for item in grads + sums + joins:
        item.drain()
    local.finish()


def run_attend_forward(query, key, value, rec, wk, wv, pk, pv, gate, wo, dy, rates):
    tokens, width, local_width = query.shape[0], rec.shape[1], query.shape[1]
    tall, full = (tokens, local_width), (tokens, width)
    vm = lambda shape, dtype=None: pltpu.VMEM(shape, bf16 if dtype is None else dtype)
    return call(
        attend_forward, 2,
        [shaped(full), shaped(tall, f32), shaped(tall), shaped(tall), shaped(full)],
        (0,) * 11 + (1,),
        [vm(tall), vm(tall), vm(tall), vm(full), vm((width, local_width)), vm((width, local_width)),
         vm(tall), vm((local_width, width)), vm(full), vm((KEY_ROWS, local_width)),
         vm((KEY_ROWS, local_width)), vm((STRETCH // 2, KEY_ROWS), f32), vm(tall), vm(tall),
         vm(full), vm(full), vm(tall, f32)]
        + scatter_room(tokens) + sems(40) + [pltpu.SemaphoreType.DMA((24,))],
        8 << 30, 16 << 20,
    )(query, key, value, rec, wk, wv, pk, pv, gate, wo, dy, rates)


def feed_forward(
    x_in, branch_in, here_in, dy_in, xl_in, dyl_in, gain_in, gate_in, up_in, down_in,
    out_out, bm_out, bb_out, gain_out, gg_out, gu_out, gd_out,
    x, branch, here, dy, xl, dyl, gain, gate, up, down, normed, hidden, bup, bffn, part, part_two,
    out, bm, bb, gain_sum, gg, gu, gd, first, passed, last, first_two, passed_two, last_two,
    send, recv, local_sems,
):
    places = group_places()
    me, sib, opp, diag = places
    wire, local = Wire(send, recv), Local(local_sems)
    loads = [
        local.start(s, t)
        for s, t in (
            (x_in, x), (branch_in, branch), (gain_in, gain), (gate_in, gate), (up_in, up),
            (dy_in, dy), (down_in, down), (here_in, here), (xl_in, xl), (dyl_in, dyl),
        )
    ]
    tokens, width = x.shape
    count = 4
    size = tokens // count
    pieces = [pl.ds(c * size, size) for c in range(count)]
    enter_group(sib, opp)
    for item in loads:
        item.wait()
    sums = [Scatter(wire, part, rows, first, passed, last, places) for rows in pieces]
    outs = [Scatter(wire, part_two, rows, first_two, passed_two, last_two, places) for rows in pieces]
    joins = [Gather(wire, bb, rows, places) for rows in pieces]
    gain_sum[...] = jnp.zeros_like(gain_sum)

    def finish(c):
        rows = pieces[c]
        got = sums[c].end().astype(bf16).astype(f32) + dyl[rows, :].astype(f32)
        bm[rows, :] = got
        bb[rows, cols(me)] = got.astype(bf16)
        joins[c].start()

    for c in range(count):
        rows = pieces[c]
        middle = x[rows, :].astype(f32) + branch[rows, :].astype(f32)
        inv = lax.rsqrt(jnp.mean(middle * middle, axis=1, keepdims=True) + epsilon)
        normed[rows, :] = (middle * inv * gain[...]).astype(bf16)
        pre = jnp.dot(normed[rows, :], gate[...], preferred_element_type=f32)
        lift = jnp.dot(normed[rows, :], up[...], preferred_element_type=f32)
        back = lax.dot_general(
            dy[rows, :], down[...], (((1,), (1,)), ((), ())), preferred_element_type=f32
        )
        sig = jax.nn.sigmoid(pre)
        act = pre * sig
        hidden[rows, :] = (act * lift).astype(bf16)
        bup[rows, :] = (back * act).astype(bf16)
        bffn[rows, :] = (back * lift * (sig * (1.0 + pre * (1.0 - sig)))).astype(bf16)
        back = lax.dot_general(
            bffn[rows, :], gate[...], (((1,), (1,)), ((), ())), preferred_element_type=f32
        ) + lax.dot_general(
            bup[rows, :], up[...], (((1,), (1,)), ((), ())), preferred_element_type=f32
        )
        middle = x[rows, :].astype(f32) + branch[rows, :].astype(f32)
        unit = middle * inv
        gain_sum[...] += jnp.sum(back * unit, axis=0, keepdims=True)
        back = back * gain[...]
        part[rows, :] = (
            inv * (back - unit * jnp.mean(back * unit, axis=1, keepdims=True))
        ).astype(bf16)
        sums[c].start()
        if c >= 1:
            sums[c - 1].middle()
        if c >= 2:
            finish(c - 2)
        if c >= 3:
            joins[c - 3].relay()
    local.start(gain_sum, gain_out, late=True)
    sums[3].middle()
    finish(2)
    joins[1].relay()

    def final(c):
        rows = pieces[c]
        got = outs[c].end()
        out[rows, :] = (xl[rows, :].astype(f32) + here[rows, :] + got).astype(bf16)

    def grad(left, right, target, k):
        lanes = pl.ds(k * 256, 256)
        target[lanes, :] = lax.dot_general(
            left[:, lanes], right[...], (((0,), (0,)), ((), ())), preferred_element_type=f32
        ).astype(bf16)

    for c in range(count):
        rows = pieces[c]
        part_two[rows, :] = jnp.dot(
            hidden[rows, :], down[...], preferred_element_type=f32
        ).astype(bf16)
        outs[c].start()
        if c == 0:
            finish(3)
            joins[2].relay()
    joins[3].relay()
    for c in range(count):
        grad(normed, bffn, gg, c)
        outs[c].middle()
    local.start(gg, gg_out, late=True)
    local.start(bm, bm_out, late=True)
    for item in joins:
        item.end()
    local.start(bb, bb_out, late=True)
    for c in range(count):
        grad(normed, bup, gu, c)
    local.start(gu, gu_out, late=True)
    for c in range(count):
        grad(hidden, dy, gd, c)
    local.start(gd, gd_out, late=True)
    for c in range(count):
        final(c)
    local.start(out, out_out, late=True)
    for item in sums + outs + joins:
        item.drain()
    local.finish()


def run_feed_forward(x, branch, here, dy, xl, dyl, gain, gate, up, down):
    full, tall, square = x.shape, xl.shape, gate.shape
    vm = lambda shape, dtype=None: pltpu.VMEM(shape, bf16 if dtype is None else dtype)
    row = (1, full[1])
    return call(
        feed_forward, 3,
        [shaped(tall), shaped(tall, f32), shaped(full), shaped(row, f32), shaped(square),
         shaped(square), shaped(square)],
        (0,) * 10,
        [vm(full), vm(full), vm(tall, f32), vm(full), vm(tall), vm(tall), vm(row, f32), vm(square),
         vm(square), vm(square), vm(full), vm(full), vm(full), vm(full), vm(full), vm(full),
         vm(tall), vm(tall, f32), vm(full), vm(row, f32), vm(square), vm(square), vm(square)]
        + scatter_room(full[0]) + scatter_room(full[0]) + sems(40)
        + [pltpu.SemaphoreType.DMA((24,))],
        19 << 30, 24 << 20,
    )(x, branch, here, dy, xl, dyl, gain, gate, up, down)


def wide_places():
    at = lax.axis_index("wide")
    y, z = lax.rem(at, 2), lax.div(at, 2)
    facing = at + 1 - 2 * y
    others = [lax.rem(z + d, 4) for d in (1, 2, 3)]
    return y, z, facing, others, [2 * other + y for other in others]


def enter_all(sib, opp, wide):
    y, z, facing, others, peers = wide
    barrier = pltpu.get_barrier_semaphore()
    for peer in (sib, opp):
        pl.semaphore_signal(barrier, inc=1, device_id={"narrow": peer}, device_id_type=MESH)
    for peer in (facing, *peers):
        pl.semaphore_signal(barrier, inc=1, device_id={"wide": peer}, device_id_type=MESH)
    pl.semaphore_wait(barrier, 6)


class WideSum:
    ahead = 2

    def __init__(self, wire, copy_sems, wide, chunks, mine, got, parts, done, ring):
        y, z, facing, others, peers = wide
        half, quarter = 128, 32
        self.mine, self.got, self.parts, self.done, self.ring = mine, got, parts, done, ring
        self.items = []
        for k, (source, start, target, goal) in enumerate(chunks):
            slot = k % ring
            away = pl.ds(start + pl.multiple_of((1 - y) * half, half), half)
            here = pl.ds(start + pl.multiple_of(y * half, half), half)
            lands = pl.ds(goal + pl.multiple_of(y * half, half), half)
            spot = pl.ds(goal + pl.multiple_of(y * half + z * quarter, quarter), quarter)
            self.items.append({
                "slot": slot,
                "own": pl.ds(pl.multiple_of(z * quarter, quarter), quarter),
                "load": pltpu.make_async_copy(source.at[here], mine.at[slot], copy_sems.at[2 * k]),
                "keep": pltpu.make_async_copy(
                    done.at[slot], target.at[spot], copy_sems.at[2 * k + 1]
                ),
                "one": wire.to(source.at[away], got.at[slot], facing, "wide"),
                "two": [
                    wire.to(
                        got.at[slot, pl.ds(pl.multiple_of(other * quarter, quarter), quarter)],
                        parts.at[slot, d], peer, "wide",
                    )
                    for d, (other, peer) in enumerate(zip(others, peers))
                ],
                "three": [wire.to(done.at[slot], target.at[spot], peer, "wide") for peer in peers],
                "four": wire.to(target.at[lands], target.at[lands], facing, "wide"),
            })
        count = len(self.items)
        self.steps, self.begun, self.ready, self.wanted, self.next = [], 0, count, 0, 0
        for i in range(count + 4):
            if 0 <= i - 4 < count:
                self.steps.append((self.last, i - 4))
            if i < count:
                self.steps.append((self.halve, i))
            if 0 <= i - 1 < count:
                self.steps.append((self.total, i - 1))
            if 0 <= i - 2 < count:
                self.steps.append((self.back, i - 2))

    def open(self, ready):
        self.ready = ready
        self.begin(self.wanted)

    def begin(self, upto):
        self.wanted = max(self.wanted, upto)
        while self.begun < min(upto, self.ready, len(self.items)):
            self.items[self.begun]["load"].start()
            self.items[self.begun]["one"].start()
            self.begun += 1

    def halve(self, i):
        item, slot = self.items[i], self.items[i]["slot"]
        self.begin(i + 1)
        item["one"].wait_recv()
        self.begin(i + 1 + self.ahead)
        item["load"].wait()
        self.got[slot] = (
            self.got[slot].astype(f32) + self.mine[slot].astype(f32)
        ).astype(bf16)
        for copy in item["two"]:
            copy.start()

    def total(self, i):
        item, slot = self.items[i], self.items[i]["slot"]
        for copy in item["two"]:
            copy.wait_recv()
        value = self.got[slot, item["own"], :].astype(f32)
        for d in range(3):
            value = value + self.parts[slot, d].astype(f32)
        self.done[slot] = value.astype(bf16)
        for copy in item["three"]:
            copy.start()
        item["keep"].start()

    def back(self, i):
        item = self.items[i]
        for copy in item["three"]:
            copy.wait_recv()
        item["keep"].wait()
        item["one"].wait_send()
        for copy in item["two"] + item["three"]:
            copy.wait_send()
        item["four"].start()

    def last(self, i):
        self.items[i]["four"].wait_recv()
        self.items[i]["four"].wait_send()

    def go(self, count=None):
        stop = len(self.steps) if count is None else min(self.next + count, len(self.steps))
        while self.next < stop:
            step, i = self.steps[self.next]
            if step == self.halve and i >= self.ready:
                break
            step(i)
            self.next += 1


def wide_room(ring):
    return [
        pltpu.VMEM((ring, 128, 1024), bf16),
        pltpu.VMEM((ring, 128, 1024), bf16),
        pltpu.VMEM((ring, 3, 32, 1024), bf16),
        pltpu.VMEM((ring, 32, 1024), bf16),
    ]


def nt(left, right):
    return lax.dot_general(left, right, (((1,), (1,)), ((), ())), preferred_element_type=f32)


def tn(left, right):
    return lax.dot_general(left, right, (((0,), (0,)), ((), ())), preferred_element_type=f32)


def slope_of(values):
    sig = jax.nn.sigmoid(values)
    return sig * (1.0 + values * (1.0 - sig))


def moved_down(values, offset):
    row = lax.broadcasted_iota(jnp.int32, values.shape, 0)
    return jnp.where(row < offset, 0.0, pltpu.roll(values, offset, 0))


def moved_up(values, offset):
    rows = values.shape[0]
    row = lax.broadcasted_iota(jnp.int32, values.shape, 0)
    return jnp.where(row >= rows - offset, 0.0, pltpu.roll(values, rows - offset, 0))


RING = 6


def backward_layer(
    query_in, key_in, value_in, rec_in, wq_in, wk_in, wv_in, wg_in, pk_in, pkl_in, pv_in, gate_in, wo_in,
    mixed_in, gated_in, bb_in, keys_in, queries_in, pre_in, act_in, mis_in, thr_in, ble_in, qpre_in,
    qact_in, one_in, two_in, next_one_in, next_two_in, x_in, gain_in, taps_in, cq_in, ck_in, cv_in,
    gaintwo_in, bm_in, gg_in, gu_in, gd_in, rates,
    ig_out, gg_out, gu_out, gd_out, gone_out, gtwo_out, packed_out, extra_out,
    gone_mid, gtwo_mid, packed_mid, extra_mid, bgate_mid, gmk_mid, gmv_mid, bq_mid, bk_mid, bv_mid,
    qpart_mid, kpart_mid, vpart_mid,
    brec, late, early, bmis, pkacc, pvacc,
    a_first, a_passed, a_last, l_first, l_passed, l_last, m_first, m_passed, m_last,
    q_first, q_passed, q_last, k_first, k_passed, k_last, t_first, t_passed, t_last,
    mine, got, parts, done, send, recv, local_sems, copy_sems,
):
    places = group_places()
    me, sib, opp, diag = places
    wire, local = Wire(send, recv), Local(local_sems)
    wide = wide_places()
    half, block = STRETCH // 2, STRETCH
    tokens, width = x_in.shape
    slim = wo_in.shape[0]
    chunks = []
    for source, target in (
        (gg_in, gg_out), (gu_in, gu_out), (gd_in, gd_out), (gone_mid, gone_out),
        (gtwo_mid, gtwo_out), (packed_mid, packed_out), (extra_mid, extra_out),
    ):
        chunks += [(source, i * 256, target, i * 256) for i in range(source.shape[0] // 256)]
    adds = WideSum(wire, copy_sems, wide, chunks, mine, got, parts, done, RING)
    adds.ready = 3 * width // 256
    enter_all(sib, opp, wide)
    adds.begin(adds.ahead)
    pieces = [pl.ds(c * half, half) for c in range(2)]
    blocks = [pl.ds(b * block, block) for b in range(2)]
    whole = pl.ds(0, block)
    lanes = [pl.ds(i * 256, 256) for i in range(4)]
    early_join = Gather(wire, early, whole, places)
    misses = [Gather(wire, bmis, rows, places) for rows in pieces]
    recs = [Gather(wire, brec, rows, places) for rows in pieces]

    def attend(
        query, key, value, rec, wk, wv, gate, wo, mixed, gated, bb, keys, values, bias, bmix, bgate,
        gwo, gmk, gmv, bq, bk, bv, kacc, vacc, bmk, bmv, part,
    ):
        loads = [
            local.start(s, t)
            for s, t in (
                (bb_in, bb), (wo_in, wo), (gate_in, gate), (mixed_in, mixed), (gated_in, gated),
                (rec_in, rec), (wk_in, wk), (wv_in, wv), (query_in, query), (key_in, key),
                (value_in, value), (pkl_in, keys.at[pl.ds(2 * block, NP)]),
                (pv_in, values.at[pl.ds(2 * block, NP)]),
            )
        ]
        keys[pl.ds(2 * block + NP, 128 - NP), :] = jnp.zeros((128 - NP, 256), bf16)
        values[pl.ds(2 * block + NP, 128 - NP), :] = jnp.zeros((128 - NP, 256), bf16)
        pkacc[...] = jnp.zeros_like(pkacc)
        pvacc[...] = jnp.zeros_like(pvacc)
        gmk[...] = jnp.zeros_like(gmk)
        gmv[...] = jnp.zeros_like(gmv)
        for item in loads:
            item.wait()

        def through_gate(c, carried):
            rows = pl.ds(pl.multiple_of(c * half, half), half)
            back = nt(bb[rows, :], wo[...])
            sig = jax.nn.sigmoid(gate[rows, :].astype(f32))
            bmix[rows, :] = (back * sig).astype(bf16)
            bgate[rows, :] = (back * mixed[rows, :].astype(f32) * sig * (1.0 - sig)).astype(bf16)
            return carried

        lax.fori_loop(0, 4, through_gate, 0)
        local.start(bgate, bgate_mid, late=True)
        gwo[...] = tn(gated[...], bb[...]).astype(bf16)
        local.start(gwo, extra_mid.at[pl.ds(0, slim)], late=True)
        ones = head_ones()
        sums = [Scatter(wire, part, rows, a_first, a_passed, a_last, places) for rows in pieces]
        adds.go(2)
        for b in (1, 0):
            rows = blocks[b]
            memory = rec[rows, :]
            made = jnp.dot(memory, wk[...], preferred_element_type=f32)
            inv = lax.rsqrt(split_sums(made * made, ones) + head_floor)
            keys[pl.ds(0, block), :] = (made * inv).astype(bf16)
            values[pl.ds(0, block), :] = jnp.dot(
                memory, wv[...], preferred_element_type=f32
            ).astype(bf16)
            keys[pl.ds(block, block), :] = key[rows, :]
            values[pl.ds(block, block), :] = value[rows, :]
            bias[...] = key_bias(0, block, rates[0] - float(b * block), True)
            kacc[...] = jnp.zeros_like(kacc)
            vacc[...] = jnp.zeros_like(vacc)

            def one_head(head, total):
                asked = head_only(query[rows, :], head)
                back = head_only(bmix[rows, :], head)
                weights = jnp.exp(score_scale * nt(keys[...], asked) + bias[...])
                weights = weights * (1.0 / jnp.sum(weights, axis=0, keepdims=True))
                vacc[...] += jnp.dot(weights.astype(bf16), back, preferred_element_type=f32)
                slope = nt(values[...], back)
                slope = (
                    weights * (slope - jnp.sum(weights * slope, axis=0, keepdims=True))
                ).astype(bf16)
                kacc[...] += jnp.dot(slope, asked, preferred_element_type=f32)
                read = tn(slope, keys[...])
                lane_head = lax.broadcasted_iota(jnp.int32, read.shape, 1) // HD
                return jnp.where(lane_head == head, read, total)

            asked_back = lax.fori_loop(0, 2, one_head, jnp.zeros((block, 256), f32))
            adds.go(3)
            bq[rows, :] = score_scale * lax.fori_loop(2, 4, one_head, asked_back)
            adds.go(3)
            bk[rows, :] = score_scale * kacc[pl.ds(block, block), :]
            bv[rows, :] = vacc[pl.ds(block, block), :]
            pkacc[...] += score_scale * kacc[pl.ds(2 * block, NP), :]
            pvacc[...] += vacc[pl.ds(2 * block, NP), :]
            unit = jnp.dot(memory, wk[...], preferred_element_type=f32) * inv
            back = score_scale * kacc[pl.ds(0, block), :]
            bmk[...] = ((back - unit * split_sums(back * unit, ones)) * inv).astype(bf16)
            bmv[...] = vacc[pl.ds(0, block), :].astype(bf16)
            for c in range(2):
                target = part if b == 1 else late
                target[pieces[c], :] = (
                    nt(bmk[pieces[c], :], wk[...]) + nt(bmv[pieces[c], :], wv[...])
                ).astype(bf16)
                if b == 1:
                    sums[c].start()
                else:
                    brec[pieces[c], cols(me)] = sums[c].end().astype(bf16)
                    recs[c].start()
            gmk[...] += tn(memory, bmk[...])
            if b == 1:
                sums[0].middle()
            gmv[...] += tn(memory, bmv[...])
            if b == 1:
                sums[1].middle()
            adds.go(2)
        for s, t in ((gmk, gmk_mid), (gmv, gmv_mid), (bq, bq_mid), (bk, bk_mid), (bv, bv_mid)):
            local.start(s, t, late=True)
        for item in recs:
            item.relay()
        for item in sums:
            item.drain()
        adds.go(1)
        local.finish()

    def remember(
        key, query, pre, act, mis, thr, ble, qpre, qact, one, two, next_one, next_two, cone, ctwo, bble,
        bthr, bqm, mpart, bpre, klow, qlow, kout, qout, vout,
    ):
        loads = [
            local.start(s, t)
            for s, t in (
                (next_two_in, next_two), (qpre_in, qpre), (next_one_in, next_one),
                (queries_in, query), (qact_in, qact), (keys_in, key), (pre_in, pre), (act_in, act),
                (two_in, two), (mis_in, mis), (one_in, one), (thr_in, thr), (ble_in, ble),
            )
        ]
        lates = Scatter(wire, late, whole, l_first, l_passed, l_last, places)
        sums = [Scatter(wire, mpart, rows, m_first, m_passed, m_last, places) for rows in pieces]
        asks = [Scatter(wire, qlow, rows, q_first, q_passed, q_last, places) for rows in blocks]
        tells = [Scatter(wire, klow, rows, k_first, k_passed, k_last, places) for rows in pieces]
        lates.start()
        for item in loads:
            item.wait()
        for item in recs:
            item.end()
            item.drain()
        step_size, keep = rates[1], rates[2]

        def ask_back(c, source, row_start, weight_one, weight_two):
            rows = pl.ds(row_start + c * half, half)
            back = nt(source[pieces[c], :], weight_two[...])
            bqm[pieces[c], :] = (back * slope_of(qpre[rows, :].astype(f32))).astype(bf16)
            qlow[rows, :] = nt(bqm[pieces[c], :], weight_one[...]).astype(bf16)

        for c in range(2):
            ask_back(c, brec, block, next_one, next_two)
            if c == 0:
                lates.middle()
        asks[1].start()
        early[:, cols(me)] = lates.end().astype(bf16)
        early_join.start()
        adds.go(2)

        def first_sums(c, carried):
            rows = pl.ds(pl.multiple_of(c * half, half), half)
            grad = tn(query[blocks[1], rows], bqm[...])
            cone[rows, :] = keep * grad
            next_one[rows, :] = (-step_size * grad).astype(bf16)
            grad = tn(qact[blocks[1], rows], brec[...])
            ctwo[rows, :] = keep * grad
            next_two[rows, :] = (-step_size * grad).astype(bf16)
            return carried

        lax.fori_loop(0, 4, first_sums, 0)
        adds.go(2)
        for c in range(2):
            rows = pieces[c]
            back = jnp.dot(key[rows, :], next_one[...], preferred_element_type=f32)
            bble[rows, :] = back.astype(bf16)
            bthr[rows, :] = (back * slope_of(pre[rows, :].astype(f32))).astype(bf16)
            mpart[rows, :] = (
                jnp.dot(act[rows, :], next_two[...], preferred_element_type=f32)
                + jnp.dot(bthr[rows, :], two[...], preferred_element_type=f32)
            ).astype(bf16)
            sums[c].start()
            if c == 0:
                early_join.relay()
        sums[0].middle()
        asks[1].middle()
        adds.go(2)
        sums[1].middle()
        early_join.end()
        for c in range(2):
            ask_back(c, early, 0, one, two)
        asks[0].start()
        adds.go(1)
        for c in range(2):
            rows = pieces[c]
            back = sums[c].end().astype(bf16)
            index = lax.broadcasted_iota(jnp.int32, (half, 1), 0) + c * half
            scale = jnp.where(index.astype(f32) < rates[0], 1.0 / STRETCH, 0.0)
            bmis[rows, cols(me)] = back
            misses[c].start()
            vout[rows, :] = -(back.astype(f32) * scale)
        local.start(vout, vpart_mid, late=True)

        def second_sums(c, carried):
            rows = pl.ds(pl.multiple_of(c * half, half), half)
            cone[rows, :] += tn(query[blocks[0], rows], bqm[...])
            ctwo[rows, :] += tn(bthr[:, rows], mis[...]) + tn(qact[blocks[0], rows], early[...])
            return carried

        lax.fori_loop(0, 2, second_sums, 0)
        misses[0].relay()
        asks[0].middle()
        adds.go(2)
        lax.fori_loop(2, 4, second_sums, 0)
        misses[1].relay()
        adds.go(1)
        for c in range(2):
            rows = pieces[c]
            misses[c].end()
            misses[c].drain()
            index = lax.broadcasted_iota(jnp.int32, (half, 1), 0) + c * half
            scale = jnp.where(index.astype(f32) < rates[0], 1.0 / STRETCH, 0.0)
            bmis[rows, :] = (bmis[rows, :].astype(f32) * scale).astype(bf16)
            values = pre[rows, :].astype(f32)
            sig = jax.nn.sigmoid(values)
            drop = 1.0 - sig
            slant = sig * drop
            curve = slant * (1.0 + values * drop) + sig * (drop - values * slant)
            back = nt(mis[rows, :], next_two[...]) + nt(bmis[rows, :], two[...])
            bpre[rows, :] = (
                back * (sig * (1.0 + values * drop))
                + bble[rows, :].astype(f32) * thr[rows, :].astype(f32) * curve
            ).astype(bf16)
            klow[rows, :] = (
                nt(ble[rows, :], next_one[...]) + nt(bpre[rows, :], one[...])
            ).astype(bf16)
            tells[c].start()
        adds.go(2)
        tells[0].middle()
        tells[1].middle()

        def last_sums(c, carried):
            rows = pl.ds(pl.multiple_of(c * half, half), half)
            next_one[rows, :] = (cone[rows, :] + tn(key[:, rows], bpre[...])).astype(bf16)
            next_two[rows, :] = (ctwo[rows, :] + tn(act[:, rows], bmis[...])).astype(bf16)
            return carried

        lax.fori_loop(0, 4, last_sums, 0)
        local.start(next_one, gone_mid, late=True)
        local.start(next_two, gtwo_mid, late=True)
        adds.go(2)
        for b in (1, 0):
            qout[blocks[b], :] = asks[b].end()
        local.start(qout, qpart_mid, late=True)
        for c in range(2):
            kout[pieces[c], :] = tells[c].end()
        local.start(kout, kpart_mid, late=True)
        for item in [lates, early_join] + sums + asks + tells:
            item.drain()
        local.finish()
        adds.open(adds.ready + 2 * width // 256)

    def finish(
        x, gain, weights, taps, qpre, kpre, vpre, bq, bk, bv, qpart, kpart, vpart, cot, gmk, gmv, pk,
        gaintwo, bm, extra, packed, normed, part, ig, conv_rows,
    ):
        loads = [
            local.start(s, t)
            for s, t in (
                (cq_in, qpre), (bq_mid, bq), (qpart_mid, qpart), (taps_in, taps), (ck_in, kpre),
                (bk_mid, bk), (kpart_mid, kpart), (cv_in, vpre), (bv_mid, bv), (vpart_mid, vpart),
                (x_in, x), (gain_in, gain), (wq_in, weights.at[:, lanes[0]]),
                (wk_in, weights.at[:, lanes[1]]), (wv_in, weights.at[:, lanes[2]]),
                (wg_in, weights.at[:, lanes[3]]), (bgate_mid, cot.at[:, lanes[3]]),
                (gmk_mid, gmk), (gmv_mid, gmv), (pk_in, pk), (gaintwo_in, gaintwo), (bm_in, bm),
            )
        ]
        adds.go(1)
        for item in loads:
            item.wait()
        ones = head_ones()

        def through_conv(pre, at, back, normal):
            values = pre[...]
            conv = values * taps[pl.ds(at, 1), :]
            for j in range(1, KW):
                conv = conv + moved_down(values, j) * taps[pl.ds(at + j, 1), :]
            sig = jax.nn.sigmoid(conv)
            if normal:
                act = conv * sig
                inv = lax.rsqrt(split_sums(act * act, ones) + head_floor)
                unit = act * inv
                back = (back - unit * split_sums(back * unit, ones)) * inv
            back = back * (sig * (1.0 + conv * (1.0 - sig)))
            result = back * taps[pl.ds(at, 1), :]
            conv_rows[pl.ds(at, 1), :] = jnp.sum(back * values, axis=0, keepdims=True)
            for j in range(1, KW):
                conv_rows[pl.ds(at + j, 1), :] = jnp.sum(
                    back * moved_down(values, j), axis=0, keepdims=True
                )
                result = result + moved_up(back, j) * taps[pl.ds(at + j, 1), :]
            return result.astype(bf16)

        conv_rows[...] = jnp.zeros_like(conv_rows)
        cot[:, lanes[0]] = through_conv(qpre, 0, bq[...] + qpart[...], True)
        adds.go(1)
        bk[whole, :] += kpart[...]
        cot[:, lanes[1]] = through_conv(kpre, KW, bk[...], True)
        adds.go(1)
        bv[whole, :] += vpart[...]
        cot[:, lanes[2]] = through_conv(vpre, 2 * KW, bv[...], False)
        adds.go(1)
        rows_of_x = [pl.ds(c * 256, 256) for c in range(tokens // 256)]
        sums = [Scatter(wire, part, rows, t_first, t_passed, t_last, places) for rows in rows_of_x]
        tail_rows = pl.ds(tokens, 16)
        gains = Scatter(wire, part, tail_rows, t_first, t_passed, t_last, places)
        gain_sum = jnp.zeros((1, width), f32)
        for c, rows in enumerate(rows_of_x):
            back = nt(cot[rows, :], weights[...])
            values = x[rows, :].astype(f32)
            inv = lax.rsqrt(jnp.mean(values * values, axis=1, keepdims=True) + epsilon)
            unit = values * inv
            normed[rows, :] = (unit * gain[...]).astype(bf16)
            gain_sum = gain_sum + jnp.sum(back * unit, axis=0, keepdims=True)
            back = back * gain[...]
            part[rows, :] = (
                inv * (back - unit * jnp.mean(back * unit, axis=1, keepdims=True))
            ).astype(bf16)
            sums[c].start()
            if c >= 1:
                sums[c - 1].middle()
            adds.go(1)
        row = lax.broadcasted_iota(jnp.int32, (16, width), 0)
        part[tail_rows, :] = jnp.where(
            row == 0, gain_sum, jnp.where(row == 1, gaintwo[...], 0.0)
        ).astype(bf16)
        gains.start()
        for c in range(width // 256):
            rows = rows_of_x[c]
            packed[rows, :] = tn(normed[:, rows], cot[...]).astype(bf16)
            if c % 2:
                adds.go(1)
        packed[:, lanes[1]] = (packed[:, lanes[1]].astype(f32) + gmk[...]).astype(bf16)
        packed[:, lanes[2]] = (packed[:, lanes[2]].astype(f32) + gmv[...]).astype(bf16)
        local.start(packed, packed_mid, late=True)
        sums[-1].middle()
        gains.middle()
        extra[...] = jnp.zeros_like(extra)
        start = pk[...].astype(f32)
        inv = lax.rsqrt(split_sums(start * start, ones) + head_floor)
        unit = start * inv
        back = pkacc[...]
        top = pl.ds(0, 16)
        extra[top, lanes[0]] = ((back - unit * split_sums(back * unit, ones)) * inv).astype(bf16)
        extra[top, lanes[1]] = pvacc[...].astype(bf16)
        extra[top, lanes[2]] = conv_rows[...].astype(bf16)
        adds.go(1)
        extra[top, lanes[3]] = gains.end().astype(bf16)
        local.start(extra, extra_mid.at[pl.ds(slim, 256)], late=True)
        for c, rows in enumerate(rows_of_x):
            ig[rows, :] = bm[rows, :] + sums[c].end()
        local.start(ig, ig_out, late=True)
        local.finish()
        adds.open(len(chunks))
        for item in sums + [gains]:
            item.drain()

    vm = lambda shape, dtype=None: pltpu.VMEM(shape, bf16 if dtype is None else dtype)
    lw = query_in.shape[1]
    tall, full, flat, weight = (tokens, lw), (tokens, width), (block, width), (width, lw)
    padded, small, square = (KEY_ROWS, lw), (block, lw), one_in.shape
    pl.run_scoped(
        attend,
        vm(tall), vm(tall), vm(tall), vm(full), vm(weight), vm(weight), vm(tall), vm((lw, width)),
        vm(tall), vm(tall), vm(full), vm(padded), vm(padded), vm((KEY_ROWS, block), f32), vm(tall),
        vm(tall), vm((lw, width)), vm(weight, f32), vm(weight, f32), vm(tall, f32), vm(tall, f32),
        vm(tall, f32), vm(padded, f32), vm(padded, f32), vm(small), vm(small), vm(flat),
    )
    pl.run_scoped(
        remember,
        vm(flat), vm(full), vm(flat), vm(flat), vm(flat), vm(flat), vm(flat), vm(full), vm(full),
        vm(square), vm(square), vm(square), vm(square), vm(square, f32), vm(square, f32), vm(flat),
        vm(flat), vm(flat), vm(flat), vm(flat), vm(flat), vm(full), vm(small, f32), vm(tall, f32),
        vm(small, f32),
    )
    row = (1, width)
    pl.run_scoped(
        finish,
        vm(full), vm(row, f32), vm((width, width)), vm(taps_in.shape, f32), vm(tall, f32),
        vm(tall, f32), vm(tall, f32), vm(tall, f32), vm(tall, f32), vm(tall, f32), vm(tall, f32),
        vm(small, f32), vm(small, f32), vm(full), vm(weight, f32), vm(weight, f32), vm((NP, lw)),
        vm(row, f32), vm(tall, f32), vm((256, width)), vm((width, width)), vm(full),
        vm((tokens + 16, width)), vm(tall, f32), vm((16, 256), f32),
    )
    adds.go()


def run_backward_layer(*arrays):
    query, wo, one, x = arrays[0], arrays[12], arrays[25], arrays[29]
    tokens, width = x.shape
    lw = query.shape[1]
    tall, flat, weight, square = (tokens, lw), (STRETCH, width), (width, lw), (width, width)
    small, extra = (STRETCH, lw), (wo.shape[0] + 256, width)
    count = (6 * width + extra[0]) // 256
    vm = lambda shape, dtype=None: pltpu.VMEM(shape, bf16 if dtype is None else dtype)
    sums = [shaped(square)] * 3 + [shaped(one.shape)] * 2 + [shaped(square), shaped(extra)]
    return call(
        backward_layer, 4,
        [shaped(tall, f32)] + sums
        + [shaped(one.shape), shaped(one.shape), shaped(square), shaped(extra), shaped(tall),
           shaped(weight, f32), shaped(weight, f32), shaped(tall, f32), shaped(tall, f32),
           shaped(tall, f32), shaped(tall, f32), shaped(small, f32), shaped(small, f32)],
        (0,) * 40 + (1,),
        [vm(flat), vm(flat), vm(flat), vm(flat), vm((NP, lw), f32), vm((NP, lw), f32)]
        + scatter_room(STRETCH) * 3 + scatter_room(tokens) + scatter_room(STRETCH)
        + scatter_room(tokens + 16) + wide_room(RING)
        + sems(8 * count + 80) + [pltpu.SemaphoreType.DMA((96,)), pltpu.SemaphoreType.DMA((2 * count,))],
        45 << 30, 100 << 20,
    )(*arrays)[:8]


def plain_body(
    layer_input,
    out_grad,
    lengths,
    plan,
    norm1_gain,
    w_query,
    w_key,
    w_value,
    w_gate,
    conv_query,
    conv_key,
    conv_value,
    persist_key,
    persist_value,
    mem_w1,
    mem_w2,
    w_out,
    norm2_gain,
    ffn_gate,
    ffn_up,
    ffn_down,
):
    tokens_here = layer_input.shape[0]
    local_width = w_query.shape[1]
    heads_here = local_width // HD
    blocks = tokens_here // STRETCH
    places = jnp.arange(tokens_here)
    row_mask = (places < lengths[0]).astype(f32)
    block_mask = row_mask.reshape(blocks, STRETCH)
    levels = plan[0].astype(f32)
    column_start = lax.axis_index("narrow") * local_width

    def rows_of(values, b):
        return values[b * STRETCH : (b + 1) * STRETCH]

    whole_x = gather_columns(layer_input).astype(f32)
    whole_dy = gather_columns(out_grad)
    inv_one = lax.rsqrt(jnp.mean(whole_x * whole_x, axis=1, keepdims=True) + epsilon)
    unit_one = whole_x * inv_one
    normed_one = (unit_one * norm1_gain).astype(bf16)
    key_pre = product(normed_one, w_key)
    query_pre = product(normed_one, w_query)
    value_pre = product(normed_one, w_value)
    gate_pre = product(normed_one, w_gate)
    key_conv = causal_conv(key_pre, conv_key)
    query_conv = causal_conv(query_pre, conv_query)
    value_conv = causal_conv(value_pre, conv_value)
    key_unit, key_inv = head_norm(jax.nn.silu(key_conv))
    query_unit, query_inv = head_norm(jax.nn.silu(query_conv))
    query_low = query_unit.astype(bf16)
    key_low = key_unit.astype(bf16)
    value_low = jax.nn.silu(value_conv).astype(bf16)

    weight_one, weight_two = mem_w1.astype(f32), mem_w2.astype(f32)
    moment_one = moment_two = None
    saved = []
    for b in range(blocks):
        step_size, momentum, forget = plan_rates(levels[b])
        kept = {"first": weight_one.astype(bf16), "second": weight_two.astype(bf16)}
        mask_rows = block_mask[b][:, None]
        if b < blocks - 1:
            key_rows = gather_columns(rows_of(key_low, b))
            hidden_pre = product(key_rows, kept["first"])
            hidden_act = jax.nn.silu(hidden_pre).astype(bf16)
            predicted = scatter_columns(product(hidden_act, kept["second"]))
            mismatch_here = (
                (predicted - rows_of(value_low, b).astype(f32)) * (mask_rows / STRETCH)
            ).astype(bf16)
            mismatch = gather_columns(mismatch_here)
        query_rows = gather_columns(rows_of(query_low, b))
        query_mem = product(query_rows, kept["first"])
        query_act = jax.nn.silu(query_mem).astype(bf16)
        retrieved = scatter_columns(product(query_act, kept["second"]))
        kept["recalled"] = gather_columns(retrieved.astype(bf16))
        kept.update(query_rows=query_rows, query_mem=query_mem, query_act=query_act)
        if b < blocks - 1:
            through = inner_right(mismatch, kept["second"])
            blended = (through * silu_grad(hidden_pre)).astype(bf16)
            grad_one = inner_left(key_rows, blended)
            grad_two = inner_left(hidden_act, mismatch)
            if moment_one is None:
                moment_one, moment_two = -step_size * grad_one, -step_size * grad_two
            else:
                moment_one = momentum * moment_one - step_size * grad_one
                moment_two = momentum * moment_two - step_size * grad_two
            weight_one = (1.0 - forget) * weight_one + moment_one
            weight_two = (1.0 - forget) * weight_two + moment_two
            kept.update(
                key_rows=key_rows,
                hidden_pre=hidden_pre,
                hidden_act=hidden_act,
                mismatch=mismatch,
                through=through,
                blended=blended,
            )
        saved.append(kept)

    pers_unit, pers_inv = head_norm(persist_key.astype(f32))
    pers_low = pers_unit.astype(bf16)

    def block_scores(b):
        recalled = saved[b]["recalled"]
        mem_unit, mem_inv = head_norm(product(recalled, w_key))
        mem_value = product(recalled, w_value).astype(bf16)
        all_keys = jnp.concatenate(
            [pers_low, mem_unit.astype(bf16), rows_of(key_low, b)], axis=0
        ).reshape(-1, heads_here, HD)
        all_values = jnp.concatenate(
            [persist_value, mem_value, rows_of(value_low, b)], axis=0
        ).reshape(-1, heads_here, HD)
        query_heads = rows_of(query_low, b).reshape(STRETCH, heads_here, HD)
        scores = score_scale * jnp.einsum(
            "qhd,khd->hqk", query_heads, all_keys, preferred_element_type=f32
        )
        scores = jnp.where(visible(block_mask[b])[None], scores, -1e30)
        return (mem_unit, mem_inv, all_keys, all_values, query_heads, scores)

    mixed_list = []
    for b in range(blocks):
        mem_unit, mem_inv, all_keys, all_values, query_heads, scores = block_scores(b)
        row_peak = jnp.max(scores, axis=2, keepdims=True)
        exponent = jnp.exp(scores - row_peak)
        row_total = jnp.sum(exponent, axis=2, keepdims=True)
        prob_low = (exponent / row_total).astype(bf16)
        mixed_list.append(
            jnp.einsum(
                "hqk,khd->qhd", prob_low, all_values, preferred_element_type=f32
            ).reshape(STRETCH, local_width)
        )
        saved[b].update(
            log_total=row_peak + jnp.log(row_total),
            mem_unit=mem_unit,
            mem_inv=mem_inv,
            all_keys=all_keys,
            all_values=all_values,
            query_heads=query_heads,
        )
    mixed_all = jnp.concatenate(mixed_list, axis=0)
    gate_sig = jax.nn.sigmoid(gate_pre)
    gated = (mixed_all * gate_sig).astype(bf16)
    branch_here = scatter_columns(product(gated, w_out))
    branch_full = gather_columns(branch_here.astype(bf16)).astype(f32)
    middle = whole_x + branch_full
    middle_here = layer_input.astype(f32) + branch_here
    inv_two = lax.rsqrt(jnp.mean(middle * middle, axis=1, keepdims=True) + epsilon)
    unit_two = middle * inv_two
    normed_two = (unit_two * norm2_gain).astype(bf16)
    ffn_pre = product(normed_two, ffn_gate)
    up_pre = product(normed_two, ffn_up)
    ffn_sig = jax.nn.sigmoid(ffn_pre)
    hidden_low = (ffn_pre * ffn_sig * up_pre).astype(bf16)
    back_hidden = inner_right(whole_dy, ffn_down)
    back_up_low = (back_hidden * ffn_pre * ffn_sig).astype(bf16)
    back_ffn_low = (back_hidden * up_pre * silu_grad(ffn_pre)).astype(bf16)
    back_normed_two = inner_right(back_ffn_low, ffn_gate) + inner_right(back_up_low, ffn_up)
    gain_two_part = jnp.sum(back_normed_two * unit_two, axis=0)
    middle_part = norm_back(back_normed_two, unit_two, inv_two, norm2_gain)
    back_middle_here = scatter_columns(middle_part)
    grad_ffn_down = inner_left(hidden_low, whole_dy)
    grad_ffn_gate = inner_left(normed_two, back_ffn_low)
    grad_ffn_up = inner_left(normed_two, back_up_low)
    ffn_here = scatter_columns(product(hidden_low, ffn_down))
    layer_output = (middle_here + ffn_here).astype(bf16)
    back_middle_here = back_middle_here + out_grad.astype(f32)
    back_branch = gather_columns(back_middle_here.astype(bf16))
    grad_ffn_gate, grad_ffn_up, grad_ffn_down = sum_wide(
        [grad_ffn_gate, grad_ffn_up, grad_ffn_down]
    )
    grad_w_out = inner_left(gated, back_branch)
    back_gated = inner_right(back_branch, w_out)
    back_mixed_low = (back_gated * gate_sig).astype(bf16)
    back_gate_low = (back_gated * mixed_all * gate_sig * (1.0 - gate_sig)).astype(bf16)

    back_recalled_parts = []
    mem_key_grad = mem_value_grad = 0.0
    pers_key_acc = grad_persist_value = 0.0
    back_query_att, back_key_att, back_value_att = [], [], []
    for b in range(blocks):
        kept = saved[b]
        scores = score_scale * jnp.einsum(
            "qhd,khd->hqk", kept["query_heads"], kept["all_keys"], preferred_element_type=f32
        )
        scores = jnp.where(visible(block_mask[b])[None], scores, -1e30)
        prob_rows = jnp.exp(scores - kept["log_total"])
        prob_low = prob_rows.astype(bf16)
        back_heads = rows_of(back_mixed_low, b).reshape(STRETCH, heads_here, HD)
        back_all_values = jnp.einsum(
            "hqk,qhd->khd", prob_low, back_heads, preferred_element_type=f32
        )
        back_probs = jnp.einsum(
            "qhd,khd->hqk", back_heads, kept["all_values"], preferred_element_type=f32
        )
        back_scores = (
            prob_rows * (back_probs - jnp.sum(prob_rows * back_probs, axis=2, keepdims=True))
        ).astype(bf16)
        back_query = score_scale * jnp.einsum(
            "hqk,khd->qhd", back_scores, kept["all_keys"], preferred_element_type=f32
        )
        back_all_keys = score_scale * jnp.einsum(
            "hqk,qhd->khd", back_scores, kept["query_heads"], preferred_element_type=f32
        )
        back_all_keys = back_all_keys.reshape(-1, local_width)
        back_all_values = back_all_values.reshape(-1, local_width)
        back_mem_key = head_back(
            back_all_keys[NP : NP + STRETCH], kept["mem_unit"], kept["mem_inv"]
        ).astype(bf16)
        back_mem_value = back_all_values[NP : NP + STRETCH].astype(bf16)
        back_recalled_parts.append(
            inner_right(back_mem_key, w_key) + inner_right(back_mem_value, w_value)
        )
        mem_key_grad = mem_key_grad + inner_left(kept["recalled"], back_mem_key)
        mem_value_grad = mem_value_grad + inner_left(kept["recalled"], back_mem_value)
        pers_key_acc = pers_key_acc + back_all_keys[:NP]
        grad_persist_value = grad_persist_value + back_all_values[:NP]
        back_query_att.append(back_query.reshape(STRETCH, local_width))
        back_key_att.append(back_all_keys[NP + STRETCH :])
        back_value_att.append(back_all_values[NP + STRETCH :])
    grad_persist_key = head_back(pers_key_acc, pers_unit, pers_inv)

    cot_one = cot_two = mom_one = mom_two = None
    key_total, query_total, value_total = [None] * blocks, [None] * blocks, [None] * blocks
    for b in reversed(range(blocks)):
        kept = saved[b]
        step_size, momentum, forget = plan_rates(levels[b])
        first_low, second_low = kept["first"], kept["second"]
        back_recalled = gather_columns(scatter_columns(back_recalled_parts[b]).astype(bf16))
        new_one = new_two = None
        if cot_one is None:
            key_total[b], value_total[b] = back_key_att[b], back_value_att[b]
        else:
            key_rows, hidden_pre = kept["key_rows"], kept["hidden_pre"]
            hidden_slope = silu_grad(hidden_pre)
            total_one = cot_one if mom_one is None else mom_one + cot_one
            total_two = cot_two if mom_two is None else mom_two + cot_two
            back_g1 = (-step_size * total_one).astype(bf16)
            back_g2 = (-step_size * total_two).astype(bf16)
            back_blended = product(key_rows, back_g1)
            back_through = (back_blended * hidden_slope).astype(bf16)
            mismatch_part = product(kept["hidden_act"], back_g2) + product(
                back_through, second_low
            )
            mismatch_low = scatter_columns(mismatch_part).astype(bf16)
            back_mismatch = gather_columns(mismatch_low)
            key_part = inner_right(kept["blended"], back_g1)
            back_hidden_act = inner_right(kept["mismatch"], back_g2)
            extra_pre = back_blended * kept["through"] * silu_curve(hidden_pre)
            new_one = (1.0 - forget) * cot_one
            new_two = (1.0 - forget) * cot_two + inner_left(back_through, kept["mismatch"])
        back_query_act = inner_right(back_recalled, second_low)
        back_query_pre = (back_query_act * silu_grad(kept["query_mem"])).astype(bf16)
        query_part = inner_right(back_query_pre, first_low)
        one_term = inner_left(kept["query_rows"], back_query_pre)
        two_term = inner_left(kept["query_act"], back_recalled)
        new_one = one_term if new_one is None else new_one + one_term
        new_two = two_term if new_two is None else new_two + two_term
        if cot_one is not None:
            scale_rows = (block_mask[b] / STRETCH).astype(bf16)[:, None]
            back_pred = back_mismatch * scale_rows
            value_part = -(mismatch_low.astype(f32) * scale_rows.astype(f32))
            back_hidden_act = back_hidden_act + inner_right(back_pred, second_low)
            new_two = new_two + inner_left(kept["hidden_act"], back_pred)
            back_hidden_pre = (back_hidden_act * hidden_slope + extra_pre).astype(bf16)
            key_part = key_part + inner_right(back_hidden_pre, first_low)
            new_one = new_one + inner_left(key_rows, back_hidden_pre)
            key_total[b] = back_key_att[b] + scatter_columns(key_part)
            value_total[b] = back_value_att[b] + value_part
            mom_one, mom_two = momentum * total_one, momentum * total_two
        query_total[b] = back_query_att[b] + scatter_columns(query_part)
        cot_one, cot_two = new_one, new_two
    grad_mem_w1, grad_mem_w2 = cot_one, cot_two

    back_query_total = jnp.concatenate(query_total, axis=0)
    back_key_total = jnp.concatenate(key_total, axis=0)
    back_value_total = jnp.concatenate(value_total, axis=0)
    query_conv_back = head_back(back_query_total, query_unit, query_inv) * silu_grad(query_conv)
    key_conv_back = head_back(back_key_total, key_unit, key_inv) * silu_grad(key_conv)
    value_conv_back = back_value_total * silu_grad(value_conv)
    query_pre_back, grad_conv_query = conv_back(query_conv_back, query_pre, conv_query)
    key_pre_back, grad_conv_key = conv_back(key_conv_back, key_pre, conv_key)
    value_pre_back, grad_conv_value = conv_back(value_conv_back, value_pre, conv_value)
    query_pre_low = query_pre_back.astype(bf16)
    key_pre_low = key_pre_back.astype(bf16)
    value_pre_low = value_pre_back.astype(bf16)
    back_normed_one = (
        inner_right(back_gate_low, w_gate)
        + inner_right(query_pre_low, w_query)
        + inner_right(key_pre_low, w_key)
        + inner_right(value_pre_low, w_value)
    )
    gain_one_part = jnp.sum(back_normed_one * unit_one, axis=0)
    input_part = norm_back(back_normed_one, unit_one, inv_one, norm1_gain)
    back_input_here = scatter_columns(input_part)
    grad_w_gate = inner_left(normed_one, back_gate_low)
    grad_w_query = inner_left(normed_one, query_pre_low)
    grad_w_key = inner_left(normed_one, key_pre_low) + mem_key_grad
    grad_w_value = inner_left(normed_one, value_pre_low) + mem_value_grad
    input_grad = back_middle_here + back_input_here

    gains = lax.psum(
        jnp.concatenate([gain_one_part, gain_two_part]).astype(bf16), ("narrow", "wide")
    ).astype(f32)
    full_width = whole_x.shape[1]
    grad_norm1_gain = lax.dynamic_slice_in_dim(gains, column_start, local_width, 0)
    grad_norm2_gain = lax.dynamic_slice_in_dim(gains, full_width + column_start, local_width, 0)
    late = (
        grad_w_query, grad_w_key, grad_w_value, grad_w_gate, grad_conv_query, grad_conv_key,
        grad_conv_value, grad_persist_key, grad_persist_value, grad_mem_w1, grad_mem_w2, grad_w_out,
    )
    late, (grad_ffn_gate, grad_ffn_up, grad_ffn_down) = lax.optimization_barrier(
        (tuple(v.astype(bf16) for v in late), (grad_ffn_gate, grad_ffn_up, grad_ffn_down))
    )
    (
        grad_w_query, grad_w_key, grad_w_value, grad_w_gate, grad_conv_query, grad_conv_key,
        grad_conv_value, grad_persist_key, grad_persist_value, grad_mem_w1, grad_mem_w2, grad_w_out,
    ) = sum_wide(late)
    return (
        layer_output,
        input_grad,
        grad_norm1_gain,
        grad_w_query,
        grad_w_key,
        grad_w_value,
        grad_w_gate,
        grad_conv_query,
        grad_conv_key,
        grad_conv_value,
        grad_persist_key,
        grad_persist_value,
        grad_mem_w1,
        grad_mem_w2,
        grad_w_out,
        grad_norm2_gain,
        grad_ffn_gate,
        grad_ffn_up,
        grad_ffn_down,
    )

def linked_body(
    layer_input, out_grad, lengths, plan, norm1_gain, w_query, w_key, w_value, w_gate,
    conv_query, conv_key, conv_value, persist_key, persist_value, mem_w1, mem_w2, w_out,
    norm2_gain, ffn_gate, ffn_up, ffn_down,
):
    step_size, momentum, forget = plan_rates(plan[0, 0].astype(f32))
    rates = jnp.stack([lengths[0].astype(f32), step_size, 1.0 - forget])
    rates = jnp.concatenate([rates, jnp.zeros((5,), f32)])
    low_x = gather_columns(layer_input)
    whole_x = low_x.astype(f32)
    inv_one = lax.rsqrt(jnp.mean(whole_x * whole_x, axis=1, keepdims=True) + epsilon)
    unit_one = whole_x * inv_one
    normed_one = (unit_one * norm1_gain).astype(bf16)
    key_pre = product(normed_one, w_key)
    query_pre = product(normed_one, w_query)
    value_pre = product(normed_one, w_value)
    gate_pre = product(normed_one, w_gate).astype(bf16)
    key_conv = causal_conv(key_pre, conv_key)
    query_conv = causal_conv(query_pre, conv_query)
    value_conv = causal_conv(value_pre, conv_value)
    key_unit, key_inv = head_norm(jax.nn.silu(key_conv))
    query_unit, query_inv = head_norm(jax.nn.silu(query_conv))
    query_low = query_unit.astype(bf16)
    key_low = key_unit.astype(bf16)
    value_low = jax.nn.silu(value_conv).astype(bf16)
    pers_unit, pers_inv = head_norm(persist_key.astype(f32))
    pers_low = pers_unit.astype(bf16)

    keys, queries, pre, act, mis, thr, ble, qpre, qact, rec, next_one, next_two = run_memory_forward(
        key_low, query_low, value_low, mem_w1, mem_w2, rates
    )
    branch, branch_here, mixed, gated, whole_dy = run_attend_forward(
        query_low, key_low, value_low, rec, w_key, w_value, pers_low, persist_value, gate_pre,
        w_out, out_grad, rates,
    )
    layer_output, back_middle, back_branch, gain_two, grad_ffn_gate, grad_ffn_up, grad_ffn_down = (
        run_feed_forward(
            low_x, branch, branch_here, whole_dy, layer_input, out_grad, norm2_gain[None], ffn_gate,
            ffn_up, ffn_down,
        )
    )
    taps = jnp.concatenate([conv_query, conv_key, conv_value], axis=0)
    (
        input_grad, grad_ffn_gate, grad_ffn_up, grad_ffn_down, grad_mem_w1, grad_mem_w2, packed, extra,
    ) = run_backward_layer(
        query_low, key_low, value_low, rec, w_query, w_key, w_value, w_gate, persist_key, pers_low,
        persist_value, gate_pre, w_out, mixed, gated, back_branch, keys, queries, pre, act, mis, thr,
        ble, qpre, qact, mem_w1, mem_w2, next_one, next_two, low_x, norm1_gain[None], taps, query_pre,
        key_pre, value_pre, gain_two, back_middle, grad_ffn_gate, grad_ffn_up, grad_ffn_down, rates,
    )
    local_width, start = w_query.shape[1], w_out.shape[0]
    parts = [packed[:, i * local_width : (i + 1) * local_width].astype(f32) for i in range(4)]
    small = extra[start : start + 16].astype(f32)
    pers_key, pers_value, convs, gains = [
        small[:, i * local_width : (i + 1) * local_width] for i in range(4)
    ]
    return (
        layer_output, input_grad, gains[0], *parts, convs[0:4], convs[4:8], convs[8:12], pers_key,
        pers_value, grad_mem_w1.astype(f32), grad_mem_w2.astype(f32), extra[:start].astype(f32),
        gains[1], grad_ffn_gate.astype(f32), grad_ffn_up.astype(f32), grad_ffn_down.astype(f32),
    )


def body(*arrays):
    tokens_here, local_width = arrays[0].shape
    width, units = arrays[14].shape
    linked = (
        (lax.axis_size("wide"), lax.axis_size("narrow")) == (8, 4)
        and local_width == 256
        and tokens_here == 2 * STRETCH
        and (width, units) == (1024, 1024)
        and arrays[18].shape == (1024, 1024)
    )
    return linked_body(*arrays) if linked else plain_body(*arrays)


def solution(mesh):
    return jax.shard_map(
        body,
        mesh=mesh,
        in_specs=(
            P("wide", "narrow"),
            P("wide", "narrow"),
            P("wide"),
            P("wide", None),
            P(),
            P(None, "narrow"),
            P(None, "narrow"),
            P(None, "narrow"),
            P(None, "narrow"),
            P(None, "narrow"),
            P(None, "narrow"),
            P(None, "narrow"),
            P(None, "narrow"),
            P(None, "narrow"),
            P(None, "narrow"),
            P("narrow", None),
            P("narrow", None),
            P(),
            P(None, "narrow"),
            P(None, "narrow"),
            P("narrow", None),
        ),
        out_specs=(
            P("wide", "narrow"),
            P("wide", "narrow"),
            P("narrow"),
            P(None, "narrow"),
            P(None, "narrow"),
            P(None, "narrow"),
            P(None, "narrow"),
            P(None, "narrow"),
            P(None, "narrow"),
            P(None, "narrow"),
            P(None, "narrow"),
            P(None, "narrow"),
            P(None, "narrow"),
            P("narrow", None),
            P("narrow", None),
            P("narrow"),
            P(None, "narrow"),
            P(None, "narrow"),
            P("narrow", None),
        ),
        check_vma=False,
    )
```

```python
import jax
import jax.numpy as jnp
from jax import lax
from jax.experimental import pallas as pl
from jax.experimental.pallas import tpu as pltpu
from jax.sharding import PartitionSpec as P

HD = 64
NP = 16
KW = 4
STRETCH = 512

epsilon = 1e-06
head_floor = 1.0
score_scale = 12.0
bf16 = jnp.bfloat16
f32 = jnp.float32


def product(left_side, right_side):
    return jnp.dot(left_side, right_side, preferred_element_type=f32)


def inner_left(left_side, right_side):
    return lax.dot_general(
        left_side, right_side, (((0,), (0,)), ((), ())), preferred_element_type=f32
    )


def inner_right(left_side, right_side):
    return lax.dot_general(
        left_side, right_side, (((1,), (1,)), ((), ())), preferred_element_type=f32
    )


def silu_grad(values):
    logistic = jax.nn.sigmoid(values)
    return logistic * (1.0 + values * (1.0 - logistic))


def silu_curve(values):
    logistic = jax.nn.sigmoid(values)
    logistic_slope = logistic * (1.0 - logistic)
    return logistic_slope * (1.0 + values * (1.0 - logistic)) + logistic * (
        1.0 - logistic - values * logistic_slope
    )


def plan_rates(level_now):
    return (0.1 * jnp.exp2(level_now), 0.9 - 0.2 * level_now, 0.02 + 0.05 * level_now)


def head_sums(values):
    width = values.shape[1]
    places = jnp.arange(width) // HD
    same_head = (places[:, None] == places[None, :]).astype(f32)
    return jnp.dot(
        values, same_head, precision=lax.Precision.HIGHEST, preferred_element_type=f32
    )


def head_norm(values):
    inv_norm = lax.rsqrt(head_sums(values * values) + head_floor)
    return (values * inv_norm, inv_norm)


def head_back(grad_rows, unit_rows, inv_norm):
    return (grad_rows - unit_rows * head_sums(grad_rows * unit_rows)) * inv_norm


def norm_back(grad_rows, unit_rows, inv_rows, gain_vec):
    scaled = grad_rows * gain_vec
    return inv_rows * (scaled - unit_rows * jnp.mean(scaled * unit_rows, axis=1, keepdims=True))


def shift_down(values, offset):
    return jnp.concatenate(
        [jnp.zeros((offset, values.shape[1]), values.dtype), values[:-offset]], axis=0
    )


def shift_up(values, offset):
    return jnp.concatenate(
        [values[offset:], jnp.zeros((offset, values.shape[1]), values.dtype)], axis=0
    )


def causal_conv(values, conv_taps):
    result = values * conv_taps[0]
    for offset in range(1, KW):
        result = result + shift_down(values, offset) * conv_taps[offset]
    return result


def conv_back(grad_rows, values, conv_taps):
    back_values = grad_rows * conv_taps[0]
    tap_grads = [jnp.sum(grad_rows * values, axis=0)]
    for offset in range(1, KW):
        back_values = back_values + shift_up(grad_rows, offset) * conv_taps[offset]
        tap_grads.append(jnp.sum(grad_rows * shift_down(values, offset), axis=0))
    return (back_values, jnp.stack(tap_grads, axis=0))


def visible(mask_rows):
    row_width = mask_rows.shape[0]
    places = jnp.arange(row_width)
    valid_keys = mask_rows[None, :] > 0.5
    causal = (places[None, :] <= places[:, None]) & valid_keys
    memory_seen = jnp.broadcast_to(valid_keys, (row_width, row_width))
    persistent = jnp.ones((row_width, NP), dtype=bool)
    return jnp.concatenate([persistent, memory_seen, causal], axis=1)


def gather_columns(values):
    return lax.all_gather(values, "narrow", axis=1, tiled=True)


def scatter_columns(values):
    return lax.psum_scatter(
        values.astype(bf16), "narrow", scatter_dimension=1, tiled=True
    ).astype(f32)


def sum_wide(values):
    return [lax.psum(v.astype(bf16), "wide").astype(f32) for v in values]


MESH = pl.DeviceIdType.MESH
ANY = pl.BlockSpec(memory_space=pl.ANY)
SCALARS = pl.BlockSpec(memory_space=pltpu.SMEM)
VMEM_LIMIT = 60 << 20


def group_places():
    me = lax.axis_index("narrow")
    core = lax.rem(me, 2)
    sib = me + 1 - 2 * core
    opp = lax.rem(me + 2, 4)
    diag = lax.rem(sib + 2, 4)
    return me, sib, opp, diag


def cols(index, width=256):
    return pl.ds(pl.multiple_of(index * width, width), width)


def enter_group(sib, opp):
    barrier = pltpu.get_barrier_semaphore()
    for peer in (sib, opp):
        pl.semaphore_signal(barrier, inc=1, device_id={"narrow": peer}, device_id_type=MESH)
    pl.semaphore_wait(barrier, 2)


class Wire:
    def __init__(self, send, recv):
        self.send, self.recv, self.used = send, recv, 0

    def to(self, source, target, device, axis="narrow"):
        k = self.used
        self.used += 1
        return pltpu.make_async_remote_copy(
            src_ref=source,
            dst_ref=target,
            send_sem=self.send.at[k],
            recv_sem=self.recv.at[k],
            device_id={axis: device},
            device_id_type=MESH,
        )


class Local:
    def __init__(self, sems):
        self.sems, self.used, self.open = sems, 0, []

    def start(self, source, target, late=False):
        copy = pltpu.make_async_copy(source, target, self.sems.at[self.used])
        self.used += 1
        copy.start()
        if late:
            self.open.append(copy)
        return copy

    def finish(self):
        for copy in self.open:
            copy.wait()
        self.open = []


class Gather:
    def __init__(self, wire, full, rows, places):
        me, sib, opp, diag = places
        own = full.at[rows, cols(me)]
        passed = full.at[rows, cols(opp)]
        self.far = wire.to(own, own, opp)
        self.near = wire.to(own, own, sib)
        self.relayed = wire.to(passed, passed, sib)

    def start(self):
        self.far.start()
        self.near.start()

    def relay(self):
        self.far.wait_recv()
        self.relayed.start()

    def end(self):
        self.near.wait_recv()
        self.relayed.wait_recv()

    def drain(self):
        self.far.wait_send()
        self.near.wait_send()
        self.relayed.wait_send()


class Scatter:
    def __init__(self, wire, part, rows, first, passed, last, places):
        me, sib, opp, diag = places
        self.part, self.rows, self.places = part, rows, places
        self.first, self.passed, self.last = first, passed, last
        self.pass_on = wire.to(part.at[rows, cols(diag)], first.at[1, rows], sib)
        self.keep = wire.to(part.at[rows, cols(sib)], first.at[0, rows], sib)
        self.far = wire.to(passed.at[rows], last.at[rows], opp)

    def start(self):
        self.pass_on.start()
        self.keep.start()

    def middle(self):
        me, sib, opp, diag = self.places
        self.pass_on.wait_recv()
        self.passed[self.rows] = (
            self.part[self.rows, cols(opp)].astype(f32) + self.first[1, self.rows].astype(f32)
        ).astype(bf16)
        self.far.start()

    def end(self):
        me, sib, opp, diag = self.places
        self.keep.wait_recv()
        near = self.part[self.rows, cols(me)].astype(f32) + self.first[0, self.rows].astype(f32)
        self.far.wait_recv()
        return near + self.last[self.rows].astype(f32)

    def drain(self):
        self.pass_on.wait_send()
        self.keep.wait_send()
        self.far.wait_send()


def scatter_room(rows):
    return [
        pltpu.VMEM((2, rows, 256), bf16),
        pltpu.VMEM((rows, 256), bf16),
        pltpu.VMEM((rows, 256), bf16),
    ]


def sems(count):
    return [
        pltpu.SemaphoreType.DMA((count,)),
        pltpu.SemaphoreType.DMA((count,)),
    ]


def shaped(shape, dtype=None):
    return jax.ShapeDtypeStruct(shape, bf16 if dtype is None else dtype)


def call(kernel, collective, outs, ins, scratch, flops, moved):
    return pl.pallas_call(
        kernel,
        out_shape=outs,
        in_specs=[SCALARS if s else ANY for s in ins],
        out_specs=[ANY] * len(outs),
        scratch_shapes=scratch,
        compiler_params=pltpu.CompilerParams(
            collective_id=collective, has_side_effects=True, vmem_limit_bytes=VMEM_LIMIT
        ),
        cost_estimate=pl.CostEstimate(flops=flops, bytes_accessed=moved, transcendentals=0),
        name=kernel.__name__,
    )


def memory_forward(
    key_in, query_in, value_in, one_in, two_in, rates,
    key_out, query_out, pre_out, act_out, mis_out, thr_out, ble_out, qpre_out, qact_out,
    rec_out, one_out, two_out,
    key, query, value, one, two, pre, act, part, mis, thr, ble, qpre, qact, qpart, rec,
    next_one, next_two, first, passed, last, qfirst, qpassed, qlast,
    send, recv, local_sems,
):
    places = group_places()
    me, sib, opp, diag = places
    wire, local = Wire(send, recv), Local(local_sems)
    half, block = STRETCH // 2, STRETCH
    get_key = local.start(key_in.at[pl.ds(0, block)], key.at[:, cols(me)])
    get_query = local.start(query_in, query.at[:, cols(me)])
    get_one = local.start(one_in, one)
    get_two = local.start(two_in, two)
    get_value = local.start(value_in.at[pl.ds(0, block)], value)
    enter_group(sib, opp)
    pieces = [pl.ds(c * half, half) for c in range(2)]
    blocks = [pl.ds(b * block, block) for b in range(2)]
    get_key.wait()
    keys = [Gather(wire, key, rows, places) for rows in pieces]
    for g in keys:
        g.start()
    get_one.wait()
    get_two.wait()
    get_query.wait()
    get_value.wait()
    queries = [Gather(wire, query, rows, places) for rows in blocks]
    sums = [Scatter(wire, part, rows, first, passed, last, places) for rows in pieces]
    for c in range(2):
        rows = pieces[c]
        keys[c].relay()
        if c == 1:
            queries[0].start()
            sums[0].middle()
        keys[c].end()
        hidden = jnp.dot(key[rows, :], one[...], preferred_element_type=f32)
        pre[rows, :] = hidden.astype(bf16)
        act[rows, :] = (hidden * jax.nn.sigmoid(hidden)).astype(bf16)
        part[rows, :] = jnp.dot(act[rows, :], two[...], preferred_element_type=f32).astype(bf16)
        sums[c].start()
    local.start(key, key_out, late=True)
    local.start(pre, pre_out, late=True)
    local.start(act, act_out, late=True)
    sums[1].middle()
    misses = [Gather(wire, mis, rows, places) for rows in pieces]
    for c in range(2):
        rows = pieces[c]
        predicted = sums[c].end()
        index = lax.broadcasted_iota(jnp.int32, (half, 1), 0) + c * half
        scale = jnp.where(index.astype(f32) < rates[0], 1.0 / STRETCH, 0.0)
        mis[rows, cols(me)] = ((predicted - value[rows, :].astype(f32)) * scale).astype(bf16)
        misses[c].start()
    queries[0].relay()
    queries[1].start()
    queries[0].end()
    qsums = [Scatter(wire, qpart, rows, qfirst, qpassed, qlast, places) for rows in blocks]

    def read(b, weight_one, weight_two):
        rows = blocks[b]
        asked = jnp.dot(query[rows, :], weight_one[...], preferred_element_type=f32)
        qpre[rows, :] = asked.astype(bf16)
        qact[rows, :] = (asked * jax.nn.sigmoid(asked)).astype(bf16)
        qpart[rows, :] = jnp.dot(
            qact[rows, :], weight_two[...], preferred_element_type=f32
        ).astype(bf16)
        qsums[b].start()

    misses[0].relay()
    read(0, one, two)
    misses[1].relay()
    for c in range(2):
        rows = pieces[c]
        misses[c].end()
        through = lax.dot_general(
            mis[rows, :], two[...], (((1,), (1,)), ((), ())), preferred_element_type=f32
        )
        thr[rows, :] = through.astype(bf16)
        ble[rows, :] = (through * silu_grad(pre[rows, :].astype(f32))).astype(bf16)
    qsums[0].middle()
    local.start(mis, mis_out, late=True)
    local.start(thr, thr_out, late=True)
    local.start(ble, ble_out, late=True)
    step_size, keep = rates[1], rates[2]

    def update(c, carried):
        rows = pl.ds(pl.multiple_of(c * half, half), half)
        grad = lax.dot_general(
            key[:, rows], ble[...], (((0,), (0,)), ((), ())), preferred_element_type=f32
        )
        next_one[rows, :] = (keep * one[rows, :].astype(f32) - step_size * grad).astype(bf16)
        grad = lax.dot_general(
            act[:, rows], mis[...], (((0,), (0,)), ((), ())), preferred_element_type=f32
        )
        next_two[rows, :] = (keep * two[rows, :].astype(f32) - step_size * grad).astype(bf16)
        return carried

    lax.fori_loop(0, 4, update, 0)
    local.start(next_one, one_out, late=True)
    local.start(next_two, two_out, late=True)
    queries[1].relay()
    reads = [Gather(wire, rec, rows, places) for rows in blocks]
    rec[blocks[0], cols(me)] = qsums[0].end().astype(bf16)
    reads[0].start()
    queries[1].end()
    local.start(query, query_out, late=True)
    read(1, next_one, next_two)
    local.start(qpre, qpre_out, late=True)
    local.start(qact, qact_out, late=True)
    qsums[1].middle()
    reads[0].relay()
    rec[blocks[1], cols(me)] = qsums[1].end().astype(bf16)
    reads[1].start()
    reads[0].end()
    local.start(rec.at[blocks[0]], rec_out.at[blocks[0]], late=True)
    reads[1].relay()
    reads[1].end()
    local.start(rec.at[blocks[1]], rec_out.at[blocks[1]], late=True)
    for item in keys + queries + sums + misses + qsums + reads:
        item.drain()
    local.finish()


def run_memory_forward(key_low, query_low, value_low, mem_w1, mem_w2, rates):
    block, tokens, width, units = STRETCH, query_low.shape[0], mem_w1.shape[0], mem_w1.shape[1]
    small, big, square = (block, width), (tokens, width), (width, units)
    return call(
        memory_forward, 1,
        [shaped(small), shaped(big), shaped(small), shaped(small), shaped(small), shaped(small),
         shaped(small), shaped(big), shaped(big), shaped(big), shaped(square), shaped(square)],
        (0, 0, 0, 0, 0, 1),
        [pltpu.VMEM(small, bf16), pltpu.VMEM(big, bf16), pltpu.VMEM((block, 256), bf16),
         pltpu.VMEM(square, bf16), pltpu.VMEM(square, bf16)]
        + [pltpu.VMEM(small, bf16)] * 6
        + [pltpu.VMEM(big, bf16)] * 4
        + [pltpu.VMEM(square, bf16)] * 2
        + scatter_room(block) + scatter_room(tokens)
        + sems(40) + [pltpu.SemaphoreType.DMA((24,))],
        9 * 2 * block * width * units, 24 << 20,
    )(key_low, query_low, value_low, mem_w1, mem_w2, rates)


KEY_ROWS = 2 * STRETCH + 128


def silu(values):
    return values * jax.nn.sigmoid(values)


def head_ones():
    left = lax.broadcasted_iota(jnp.int32, (256, 256), 0) // HD
    right = lax.broadcasted_iota(jnp.int32, (256, 256), 1) // HD
    return (left == right).astype(f32).astype(bf16)


def split_sums(values, ones):
    high = values.astype(bf16)
    rest = (values - high.astype(f32)).astype(bf16)
    return jnp.dot(high, ones, preferred_element_type=f32) + jnp.dot(
        rest, ones, preferred_element_type=f32
    )


def head_only(values, head):
    lane_head = lax.broadcasted_iota(jnp.int32, values.shape, 1) // HD
    return jnp.where(lane_head == head, values.astype(f32), 0.0).astype(bf16)


def key_bias(first_row, rows, valid, flipped):
    shape = (KEY_ROWS, rows) if flipped else (rows, KEY_ROWS)
    slot = lax.broadcasted_iota(jnp.int32, shape, 0 if flipped else 1)
    row = lax.broadcasted_iota(jnp.int32, shape, 1 if flipped else 0) + first_row
    memory = (slot < STRETCH) & (slot.astype(f32) < valid)
    place = slot - STRETCH
    causal = (place >= 0) & (place <= row) & (place.astype(f32) < valid) & (slot < 2 * STRETCH)
    persistent = (slot >= 2 * STRETCH) & (slot < 2 * STRETCH + NP)
    return jnp.where(memory | causal | persistent, 0.0, -1e30)


def attend_forward(
    query_in, key_in, value_in, rec_in, wk_in, wv_in, pk_in, pv_in, gate_in, wo_in, dy_in, rates,
    branch_out, here_out, mixed_out, gated_out, dy_out,
    query, key, value, rec, wk, wv, gate, wo, dy, keys, values, bias, mixed, gated, part, branch,
    here, first, passed, last, send, recv, local_sems,
):
    places = group_places()
    me, sib, opp, diag = places
    wire, local = Wire(send, recv), Local(local_sems)
    half, block = STRETCH // 2, STRETCH
    loads = [
        local.start(dy_in, dy.at[:, cols(me)]),
        local.start(rec_in, rec), local.start(wk_in, wk), local.start(wv_in, wv),
        local.start(query_in, query), local.start(key_in, key), local.start(value_in, value),
        local.start(gate_in, gate), local.start(wo_in, wo),
        local.start(pk_in, keys.at[pl.ds(2 * block, NP)]),
        local.start(pv_in, values.at[pl.ds(2 * block, NP)]),
    ]
    keys[pl.ds(2 * block + NP, 128 - NP), :] = jnp.zeros((128 - NP, 256), bf16)
    values[pl.ds(2 * block + NP, 128 - NP), :] = jnp.zeros((128 - NP, 256), bf16)
    enter_group(sib, opp)
    for item in loads:
        item.wait()
    blocks = [pl.ds(b * block, block) for b in range(2)]
    pieces = [pl.ds(c * half, half) for c in range(4)]
    grads = [Gather(wire, dy, rows, places) for rows in blocks]
    grads[0].start()
    ones = head_ones()
    sums = [Scatter(wire, part, rows, first, passed, last, places) for rows in pieces]
    joins = [Gather(wire, branch, rows, places) for rows in pieces]

    def finish(c):
        rows = pieces[c]
        got = sums[c].end()
        here[rows, :] = got
        branch[rows, cols(me)] = got.astype(bf16)
        joins[c].start()

    for c in range(4):
        b, rows = c // 2, pieces[c]
        if c % 2 == 0:
            memory = rec[blocks[b], :]
            made = jnp.dot(memory, wk[...], preferred_element_type=f32)
            inv = lax.rsqrt(split_sums(made * made, ones) + head_floor)
            keys[pl.ds(0, block), :] = (made * inv).astype(bf16)
            values[pl.ds(0, block), :] = jnp.dot(
                memory, wv[...], preferred_element_type=f32
            ).astype(bf16)
            keys[pl.ds(block, block), :] = key[blocks[b], :]
            values[pl.ds(block, block), :] = value[blocks[b], :]
        bias[...] = key_bias((c % 2) * half, half, rates[0] - float(b * block), False)

        def one_head(head, total):
            asked = head_only(query[rows, :], head)
            scores = lax.dot_general(
                asked, keys[...], (((1,), (1,)), ((), ())), preferred_element_type=f32
            )
            weights = jnp.exp(score_scale * scores + bias[...])
            inv = 1.0 / jnp.sum(weights, axis=1, keepdims=True)
            read = jnp.dot(
                (weights * inv).astype(bf16), values[...], preferred_element_type=f32
            )
            lane_head = lax.broadcasted_iota(jnp.int32, read.shape, 1) // HD
            return jnp.where(lane_head == head, read, total)

        got = lax.fori_loop(0, 4, one_head, jnp.zeros((half, 256), f32))
        mixed[rows, :] = got.astype(bf16)
        gated[rows, :] = (got * jax.nn.sigmoid(gate[rows, :].astype(f32))).astype(bf16)
        part[rows, :] = jnp.dot(gated[rows, :], wo[...], preferred_element_type=f32).astype(bf16)
        sums[c].start()
        if c == 0:
            grads[0].relay()
            grads[1].start()
            sums[0].middle()
        if c == 1:
            sums[1].middle()
            grads[0].end()
            finish(0)
        if c == 2:
            grads[1].relay()
            sums[2].middle()
            joins[0].relay()
            finish(1)
    grads[1].end()
    local.start(dy, dy_out, late=True)
    local.start(mixed, mixed_out, late=True)
    local.start(gated, gated_out, late=True)
    sums[3].middle()
    finish(2)
    joins[1].relay()
    finish(3)
    local.start(here, here_out, late=True)
    joins[2].relay()
    joins[3].relay()
    for item in joins:
        item.end()
    local.start(branch, branch_out, late=True)
    for item in grads + sums + joins:
        item.drain()
    local.finish()


def run_attend_forward(query, key, value, rec, wk, wv, pk, pv, gate, wo, dy, rates):
    tokens, width, local_width = query.shape[0], rec.shape[1], query.shape[1]
    tall, full = (tokens, local_width), (tokens, width)
    vm = lambda shape, dtype=None: pltpu.VMEM(shape, bf16 if dtype is None else dtype)
    return call(
        attend_forward, 2,
        [shaped(full), shaped(tall, f32), shaped(tall), shaped(tall), shaped(full)],
        (0,) * 11 + (1,),
        [vm(tall), vm(tall), vm(tall), vm(full), vm((width, local_width)), vm((width, local_width)),
         vm(tall), vm((local_width, width)), vm(full), vm((KEY_ROWS, local_width)),
         vm((KEY_ROWS, local_width)), vm((STRETCH // 2, KEY_ROWS), f32), vm(tall), vm(tall),
         vm(full), vm(full), vm(tall, f32)]
        + scatter_room(tokens) + sems(40) + [pltpu.SemaphoreType.DMA((24,))],
        8 << 30, 16 << 20,
    )(query, key, value, rec, wk, wv, pk, pv, gate, wo, dy, rates)


def wide_places():
    at = lax.axis_index("wide")
    bits = (lax.rem(at, 2), lax.rem(lax.div(at, 2), 2), lax.div(at, 4))
    return bits, tuple(at + step * (1 - 2 * bit) for step, bit in zip((1, 2, 4), bits))


def enter_all(sib, opp, wide):
    barrier = pltpu.get_barrier_semaphore()
    for peer in (sib, opp):
        pl.semaphore_signal(barrier, inc=1, device_id={"narrow": peer}, device_id_type=MESH)
    for peer in wide[1]:
        pl.semaphore_signal(barrier, inc=1, device_id={"wide": peer}, device_id_type=MESH)
    pl.semaphore_wait(barrier, 5)


class WideSum:
    ahead = 2
    orders = ((0, 1, 2), (0, 1, 2), (1, 0, 2), (0, 1, 2))

    def __init__(self, wire, copy_sems, wide, chunks, room, ring):
        bits, peers = wide
        self.mine, self.got, self.more, self.rest, self.done = room
        self.items = []
        for k, (source, start, target, goal) in enumerate(chunks):
            slot = k % ring
            order = self.orders[k % len(self.orders)]
            a, b, c = [bits[d] for d in order]
            pa, pb, pc = [peers[d] for d in order]
            off = lambda bit, size: pl.multiple_of(bit * size, size)
            first = goal + off(a, 128)
            second = first + off(b, 64)
            third = second + off(c, 32)
            spots = [target.at[pl.ds(at, size)] for at, size in ((third, 32), (second, 64), (first, 128))]
            self.items.append({
                "slot": slot,
                "half": pl.ds(off(b, 64), 64),
                "quarter": pl.ds(off(c, 32), 32),
                "load": pltpu.make_async_copy(
                    source.at[pl.ds(start + off(a, 128), 128)], self.mine.at[slot], copy_sems.at[2 * k]
                ),
                "keep": pltpu.make_async_copy(self.done.at[slot], spots[0], copy_sems.at[2 * k + 1]),
                "one": wire.to(
                    source.at[pl.ds(start + off(1 - a, 128), 128)], self.got.at[slot], pa, "wide"
                ),
                "two": wire.to(
                    self.got.at[slot, pl.ds(off(1 - b, 64), 64)], self.more.at[slot], pb, "wide"
                ),
                "three": wire.to(
                    self.more.at[slot, pl.ds(off(1 - c, 32), 32)], self.rest.at[slot], pc, "wide"
                ),
                "four": wire.to(self.done.at[slot], spots[0], pc, "wide"),
                "five": wire.to(spots[1], spots[1], pb, "wide"),
                "six": wire.to(spots[2], spots[2], pa, "wide"),
            })
        count = len(self.items)
        self.steps, self.begun, self.ready, self.wanted, self.next = [], 0, count, 0, 0
        stages = ((self.last, 6), (self.halve, 0), (self.again, 1), (self.total, 2), (self.back, 3),
                  (self.most, 4))
        for i in range(count + 6):
            for stage, lag in stages:
                if 0 <= i - lag < count:
                    self.steps.append((stage, i - lag))

    def open(self, ready):
        self.ready = ready
        self.begin(self.wanted)

    def begin(self, upto):
        self.wanted = max(self.wanted, upto)
        while self.begun < min(upto, self.ready, len(self.items)):
            self.items[self.begun]["load"].start()
            self.items[self.begun]["one"].start()
            self.begun += 1

    def halve(self, i):
        item, slot = self.items[i], self.items[i]["slot"]
        self.begin(i + 1)
        item["one"].wait_recv()
        self.begin(i + 1 + self.ahead)
        item["load"].wait()
        self.got[slot] = (
            self.got[slot].astype(f32) + self.mine[slot].astype(f32)
        ).astype(bf16)
        item["two"].start()

    def again(self, i):
        item, slot = self.items[i], self.items[i]["slot"]
        item["two"].wait_recv()
        self.more[slot] = (
            self.more[slot].astype(f32) + self.got[slot, item["half"], :].astype(f32)
        ).astype(bf16)
        item["three"].start()

    def total(self, i):
        item, slot = self.items[i], self.items[i]["slot"]
        item["three"].wait_recv()
        self.done[slot] = (
            self.rest[slot].astype(f32) + self.more[slot, item["quarter"], :].astype(f32)
        ).astype(bf16)
        for name in ("one", "two", "three"):
            item[name].wait_send()
        item["four"].start()
        item["keep"].start()

    def back(self, i):
        item = self.items[i]
        item["four"].wait_recv()
        item["keep"].wait()
        item["four"].wait_send()
        item["five"].start()

    def most(self, i):
        item = self.items[i]
        item["five"].wait_recv()
        item["five"].wait_send()
        item["six"].start()

    def last(self, i):
        self.items[i]["six"].wait_recv()
        self.items[i]["six"].wait_send()

    def go(self, count=None):
        stop = len(self.steps) if count is None else min(self.next + count, len(self.steps))
        while self.next < stop:
            step, i = self.steps[self.next]
            if step == self.halve and i >= self.ready:
                break
            step(i)
            self.next += 1


def wide_room(ring):
    return [
        pltpu.VMEM((ring, rows, 1024), bf16) for rows in (128, 128, 64, 32, 32)
    ]


def nt(left, right):
    return lax.dot_general(left, right, (((1,), (1,)), ((), ())), preferred_element_type=f32)


def tn(left, right):
    return lax.dot_general(left, right, (((0,), (0,)), ((), ())), preferred_element_type=f32)


def slope_of(values):
    sig = jax.nn.sigmoid(values)
    return sig * (1.0 + values * (1.0 - sig))


def moved_down(values, offset):
    row = lax.broadcasted_iota(jnp.int32, values.shape, 0)
    return jnp.where(row < offset, 0.0, pltpu.roll(values, offset, 0))


def moved_up(values, offset):
    rows = values.shape[0]
    row = lax.broadcasted_iota(jnp.int32, values.shape, 0)
    return jnp.where(row >= rows - offset, 0.0, pltpu.roll(values, rows - offset, 0))


RING = 8


def backward_layer(
    query_in, key_in, value_in, rec_in, wq_in, wk_in, wv_in, wg_in, pk_in, pkl_in, pv_in, gate_in, wo_in,
    mixed_in, gated_in, keys_in, queries_in, pre_in, act_in, mis_in, thr_in, ble_in, qpre_in,
    qact_in, one_in, two_in, next_one_in, next_two_in, x_in, gain_in, taps_in, cq_in, ck_in, cv_in,
    gaintwo_in, branch_in, here_in, dy_in, fgate_in, fup_in, fdown_in, rates,
    ig_out, lo_out, gg_out, gu_out, gd_out, gone_out, gtwo_out, packed_out, extra_out,
    gg_mid, gu_mid, gd_mid, bm_mid, gone_mid, gtwo_mid, packed_mid, extra_mid, bgate_mid, gmk_mid, gmv_mid, bq_mid, bk_mid, bv_mid,
    qpart_mid, kpart_mid, vpart_mid,
    brec, late, bb, gaintwo, pkacc, pvacc,
    a_first, a_passed, a_last, l_first, l_passed, l_last, m_first, m_passed, m_last,
    q_first, q_passed, q_last, k_first, k_passed, k_last, t_first, t_passed, t_last,
    mine, got, more, rest, done, send, recv, local_sems, copy_sems,
):
    places = group_places()
    me, sib, opp, diag = places
    wire, local = Wire(send, recv), Local(local_sems)
    wide = wide_places()
    half, block = STRETCH // 2, STRETCH
    tokens, width = x_in.shape
    slim = wo_in.shape[0]
    chunks = []
    for source, target in (
        (gg_mid, gg_out), (gu_mid, gu_out), (gd_mid, gd_out), (gone_mid, gone_out),
        (gtwo_mid, gtwo_out), (packed_mid, packed_out), (extra_mid, extra_out),
    ):
        chunks += [(source, i * 256, target, i * 256) for i in range(source.shape[0] // 256)]
    adds = WideSum(wire, copy_sems, wide, chunks, (mine, got, more, rest, done), RING)
    adds.ready = 0
    adds.begin(adds.ahead)
    pieces = [pl.ds(c * half, half) for c in range(2)]
    blocks = [pl.ds(b * block, block) for b in range(2)]
    whole = pl.ds(0, block)
    lanes = [pl.ds(i * 256, 256) for i in range(4)]
    early, bmis = bb.at[pl.ds(0, block)], bb.at[pl.ds(block, block)]
    early_join = Gather(wire, early, whole, places)
    misses = [Gather(wire, bmis, rows, places) for rows in pieces]
    recs = [Gather(wire, brec, rows, places) for rows in pieces]

    def feed(
        x, branch, here, dy, gain, gate, up, down, normed, hidden, bup, bffn, part, part_two, out, bm
    ):
        loads = [
            local.start(s, t)
            for s, t in (
                (x_in, x), (branch_in, branch), (gaintwo_in, gain), (fgate_in, gate), (fup_in, up),
                (dy_in, dy), (fdown_in, down), (here_in, here),
            )
        ]
        size = 256
        count = tokens // size
        parts_of = [pl.ds(c * size, size) for c in range(count)]
        enter_all(sib, opp, wide)
        for item in loads:
            item.wait()
        sums = [Scatter(wire, part, rows, t_first, t_passed, t_last, places) for rows in parts_of]
        outs = [Scatter(wire, part_two, rows, q_first, q_passed, q_last, places) for rows in parts_of]
        joins = [Gather(wire, bb, rows, places) for rows in parts_of]
        gaintwo[...] = jnp.zeros_like(gaintwo)

        def settle(c):
            rows = parts_of[c]
            back = sums[c].end().astype(bf16).astype(f32) + dy[rows, cols(me)].astype(f32)
            bm[rows, :] = back
            bb[rows, cols(me)] = back.astype(bf16)
            joins[c].start()

        for c in range(count):
            rows = parts_of[c]
            middle = x[rows, :].astype(f32) + branch[rows, :].astype(f32)
            inv = lax.rsqrt(jnp.mean(middle * middle, axis=1, keepdims=True) + epsilon)
            normed[rows, :] = (middle * inv * gain[...]).astype(bf16)
            pre = jnp.dot(normed[rows, :], gate[...], preferred_element_type=f32)
            lift = jnp.dot(normed[rows, :], up[...], preferred_element_type=f32)
            back = nt(dy[rows, :], down[...])
            sig = jax.nn.sigmoid(pre)
            act = pre * sig
            hidden[rows, :] = (act * lift).astype(bf16)
            bup[rows, :] = (back * act).astype(bf16)
            bffn[rows, :] = (back * lift * (sig * (1.0 + pre * (1.0 - sig)))).astype(bf16)
            back = nt(bffn[rows, :], gate[...]) + nt(bup[rows, :], up[...])
            middle = x[rows, :].astype(f32) + branch[rows, :].astype(f32)
            unit = middle * inv
            gaintwo[...] += jnp.sum(back * unit, axis=0, keepdims=True)
            back = back * gain[...]
            part[rows, :] = (
                inv * (back - unit * jnp.mean(back * unit, axis=1, keepdims=True))
            ).astype(bf16)
            sums[c].start()
            if c >= 1:
                sums[c - 1].middle()
            if c >= 2:
                settle(c - 2)
            if c >= 3:
                joins[c - 3].relay()

        def grads(left, right, keep, target, k):
            rows = parts_of[k]
            keep[rows, :] = tn(left[:, rows], right[...]).astype(bf16)
            return local.start(keep.at[rows], target.at[rows])

        copies = [grads(normed, bffn, gate, gg_mid, 0)]
        sums[3].middle()
        settle(2)
        joins[1].relay()
        for k in range(1, 4):
            copies.append(grads(normed, bffn, gate, gg_mid, k))
            copies.pop(0).wait()
            adds.open(adds.ready + 1)
            if k == 1:
                settle(3)
                joins[2].relay()
        for c, rows in enumerate(parts_of):
            part_two[rows, :] = jnp.dot(
                hidden[rows, :], down[...], preferred_element_type=f32
            ).astype(bf16)
            outs[c].start()
            if c == 1:
                joins[3].relay()
                copies.pop(0).wait()
                adds.open(adds.ready + 1)
                adds.go(2)
        for k in range(4):
            copies.append(grads(normed, bup, up, gu_mid, k))
            outs[k].middle()
        adds.go(3)
        for item in copies:
            item.wait()
        adds.open(adds.ready + 4)
        copies = [grads(hidden, dy, down, gd_mid, k) for k in range(4)]
        local.start(bm, bm_mid, late=True)
        adds.go(3)
        for c, rows in enumerate(parts_of):
            total = x[rows, cols(me)].astype(f32) + here[rows, :] + outs[c].end()
            out[rows, :] = total.astype(bf16)
        local.start(out, lo_out, late=True)
        for item in joins:
            item.end()
        for item in copies:
            item.wait()
        adds.open(adds.ready + 4)
        for item in sums + outs + joins:
            item.drain()
        local.finish()

    def attend(
        query, key, value, rec, wk, wv, gate, wo, mixed, gated, keys, values, bias, bmix, bgate,
        gwo, gmk, gmv, bq, bk, bv, kacc, vacc, bmk, bmv, part,
    ):
        loads = [
            local.start(s, t)
            for s, t in (
                (wo_in, wo), (gate_in, gate), (mixed_in, mixed), (gated_in, gated),
                (rec_in, rec), (wk_in, wk), (wv_in, wv), (query_in, query), (key_in, key),
                (value_in, value), (pkl_in, keys.at[pl.ds(2 * block, NP)]),
                (pv_in, values.at[pl.ds(2 * block, NP)]),
            )
        ]
        keys[pl.ds(2 * block + NP, 128 - NP), :] = jnp.zeros((128 - NP, 256), bf16)
        values[pl.ds(2 * block + NP, 128 - NP), :] = jnp.zeros((128 - NP, 256), bf16)
        pkacc[...] = jnp.zeros_like(pkacc)
        pvacc[...] = jnp.zeros_like(pvacc)
        gmk[...] = jnp.zeros_like(gmk)
        gmv[...] = jnp.zeros_like(gmv)
        for item in loads:
            item.wait()

        def through_gate(c, carried):
            rows = pl.ds(pl.multiple_of(c * half, half), half)
            back = nt(bb[rows, :], wo[...])
            sig = jax.nn.sigmoid(gate[rows, :].astype(f32))
            bmix[rows, :] = (back * sig).astype(bf16)
            bgate[rows, :] = (back * mixed[rows, :].astype(f32) * sig * (1.0 - sig)).astype(bf16)
            return carried

        lax.fori_loop(0, 4, through_gate, 0)
        local.start(bgate, bgate_mid, late=True)
        gwo[...] = tn(gated[...], bb[...]).astype(bf16)
        local.start(gwo, extra_mid.at[pl.ds(0, slim)], late=True)
        ones = head_ones()
        sums = [Scatter(wire, part, rows, a_first, a_passed, a_last, places) for rows in pieces]
        adds.go(3)
        for b in (1, 0):
            rows = blocks[b]
            memory = rec[rows, :]
            made = jnp.dot(memory, wk[...], preferred_element_type=f32)
            inv = lax.rsqrt(split_sums(made * made, ones) + head_floor)
            keys[pl.ds(0, block), :] = (made * inv).astype(bf16)
            values[pl.ds(0, block), :] = jnp.dot(
                memory, wv[...], preferred_element_type=f32
            ).astype(bf16)
            keys[pl.ds(block, block), :] = key[rows, :]
            values[pl.ds(block, block), :] = value[rows, :]
            bias[...] = key_bias(0, block, rates[0] - float(b * block), True)
            kacc[...] = jnp.zeros_like(kacc)
            vacc[...] = jnp.zeros_like(vacc)

            def one_head(head, total):
                asked = head_only(query[rows, :], head)
                back = head_only(bmix[rows, :], head)
                weights = jnp.exp(score_scale * nt(keys[...], asked) + bias[...])
                weights = weights * (1.0 / jnp.sum(weights, axis=0, keepdims=True))
                vacc[...] += jnp.dot(weights.astype(bf16), back, preferred_element_type=f32)
                slope = nt(values[...], back)
                slope = (
                    weights * (slope - jnp.sum(weights * slope, axis=0, keepdims=True))
                ).astype(bf16)
                kacc[...] += jnp.dot(slope, asked, preferred_element_type=f32)
                read = tn(slope, keys[...])
                lane_head = lax.broadcasted_iota(jnp.int32, read.shape, 1) // HD
                return jnp.where(lane_head == head, read, total)

            asked_back = lax.fori_loop(0, 2, one_head, jnp.zeros((block, 256), f32))
            adds.go(5)
            bq[rows, :] = score_scale * lax.fori_loop(2, 4, one_head, asked_back)
            adds.go(5)
            bk[rows, :] = score_scale * kacc[pl.ds(block, block), :]
            bv[rows, :] = vacc[pl.ds(block, block), :]
            pkacc[...] += score_scale * kacc[pl.ds(2 * block, NP), :]
            pvacc[...] += vacc[pl.ds(2 * block, NP), :]
            unit = jnp.dot(memory, wk[...], preferred_element_type=f32) * inv
            back = score_scale * kacc[pl.ds(0, block), :]
            bmk[...] = ((back - unit * split_sums(back * unit, ones)) * inv).astype(bf16)
            bmv[...] = vacc[pl.ds(0, block), :].astype(bf16)
            for c in range(2):
                target = part if b == 1 else late
                target[pieces[c], :] = (
                    nt(bmk[pieces[c], :], wk[...]) + nt(bmv[pieces[c], :], wv[...])
                ).astype(bf16)
                if b == 1:
                    sums[c].start()
                else:
                    brec[pieces[c], cols(me)] = sums[c].end().astype(bf16)
                    recs[c].start()
            gmk[...] += tn(memory, bmk[...])
            if b == 1:
                sums[0].middle()
            gmv[...] += tn(memory, bmv[...])
            if b == 1:
                sums[1].middle()
            adds.go(3)
        for s, t in ((gmk, gmk_mid), (gmv, gmv_mid), (bq, bq_mid), (bk, bk_mid), (bv, bv_mid)):
            local.start(s, t, late=True)
        for item in recs:
            item.relay()
        for item in sums:
            item.drain()
        adds.go(2)
        local.finish()

    def remember(
        key, query, pre, act, mis, thr, ble, qpre, qact, one, two, next_one, next_two, cone, ctwo, bble,
        bthr, bqm, mpart, bpre, klow, qlow, kout, qout, vout,
    ):
        loads = [
            local.start(s, t)
            for s, t in (
                (next_two_in, next_two), (qpre_in, qpre), (next_one_in, next_one),
                (queries_in, query), (qact_in, qact), (keys_in, key), (pre_in, pre), (act_in, act),
                (two_in, two), (mis_in, mis), (one_in, one), (thr_in, thr), (ble_in, ble),
            )
        ]
        lates = Scatter(wire, late, whole, l_first, l_passed, l_last, places)
        sums = [Scatter(wire, mpart, rows, m_first, m_passed, m_last, places) for rows in pieces]
        asks = [Scatter(wire, qlow, rows, q_first, q_passed, q_last, places) for rows in blocks]
        tells = [Scatter(wire, klow, rows, k_first, k_passed, k_last, places) for rows in pieces]
        lates.start()
        for item in loads:
            item.wait()
        for item in recs:
            item.end()
            item.drain()
        step_size, keep = rates[1], rates[2]

        def ask_back(c, source, row_start, weight_one, weight_two):
            rows = pl.ds(row_start + c * half, half)
            back = nt(source[pieces[c], :], weight_two[...])
            bqm[pieces[c], :] = (back * slope_of(qpre[rows, :].astype(f32))).astype(bf16)
            qlow[rows, :] = nt(bqm[pieces[c], :], weight_one[...]).astype(bf16)

        for c in range(2):
            ask_back(c, brec, block, next_one, next_two)
            if c == 0:
                lates.middle()
        asks[1].start()
        early[:, cols(me)] = lates.end().astype(bf16)
        early_join.start()
        adds.go(3)

        def first_sums(c, carried):
            rows = pl.ds(pl.multiple_of(c * half, half), half)
            grad = tn(query[blocks[1], rows], bqm[...])
            cone[rows, :] = keep * grad
            next_one[rows, :] = (-step_size * grad).astype(bf16)
            grad = tn(qact[blocks[1], rows], brec[...])
            ctwo[rows, :] = keep * grad
            next_two[rows, :] = (-step_size * grad).astype(bf16)
            return carried

        lax.fori_loop(0, 4, first_sums, 0)
        adds.go(3)
        for c in range(2):
            rows = pieces[c]
            back = jnp.dot(key[rows, :], next_one[...], preferred_element_type=f32)
            bble[rows, :] = back.astype(bf16)
            bthr[rows, :] = (back * slope_of(pre[rows, :].astype(f32))).astype(bf16)
            mpart[rows, :] = (
                jnp.dot(act[rows, :], next_two[...], preferred_element_type=f32)
                + jnp.dot(bthr[rows, :], two[...], preferred_element_type=f32)
            ).astype(bf16)
            sums[c].start()
            if c == 0:
                early_join.relay()
        sums[0].middle()
        asks[1].middle()
        adds.go(3)
        sums[1].middle()
        early_join.end()
        for c in range(2):
            ask_back(c, early, 0, one, two)
        asks[0].start()
        adds.go(2)
        for c in range(2):
            rows = pieces[c]
            back = sums[c].end().astype(bf16)
            index = lax.broadcasted_iota(jnp.int32, (half, 1), 0) + c * half
            scale = jnp.where(index.astype(f32) < rates[0], 1.0 / STRETCH, 0.0)
            bmis[rows, cols(me)] = back
            misses[c].start()
            vout[rows, :] = -(back.astype(f32) * scale)
        local.start(vout, vpart_mid, late=True)

        def second_sums(c, carried):
            rows = pl.ds(pl.multiple_of(c * half, half), half)
            cone[rows, :] += tn(query[blocks[0], rows], bqm[...])
            ctwo[rows, :] += tn(bthr[:, rows], mis[...]) + tn(qact[blocks[0], rows], early[...])
            return carried

        lax.fori_loop(0, 2, second_sums, 0)
        misses[0].relay()
        asks[0].middle()
        adds.go(3)
        lax.fori_loop(2, 4, second_sums, 0)
        misses[1].relay()
        adds.go(2)
        for c in range(2):
            rows = pieces[c]
            misses[c].end()
            misses[c].drain()
            index = lax.broadcasted_iota(jnp.int32, (half, 1), 0) + c * half
            scale = jnp.where(index.astype(f32) < rates[0], 1.0 / STRETCH, 0.0)
            bmis[rows, :] = (bmis[rows, :].astype(f32) * scale).astype(bf16)
            values = pre[rows, :].astype(f32)
            sig = jax.nn.sigmoid(values)
            drop = 1.0 - sig
            slant = sig * drop
            curve = slant * (1.0 + values * drop) + sig * (drop - values * slant)
            back = nt(mis[rows, :], next_two[...]) + nt(bmis[rows, :], two[...])
            bpre[rows, :] = (
                back * (sig * (1.0 + values * drop))
                + bble[rows, :].astype(f32) * thr[rows, :].astype(f32) * curve
            ).astype(bf16)
            klow[rows, :] = (
                nt(ble[rows, :], next_one[...]) + nt(bpre[rows, :], one[...])
            ).astype(bf16)
            tells[c].start()
        adds.go(3)
        tells[0].middle()
        tells[1].middle()

        def last_sums(c, carried):
            rows = pl.ds(pl.multiple_of(c * half, half), half)
            next_one[rows, :] = (cone[rows, :] + tn(key[:, rows], bpre[...])).astype(bf16)
            next_two[rows, :] = (ctwo[rows, :] + tn(act[:, rows], bmis[...])).astype(bf16)
            return carried

        lax.fori_loop(0, 4, last_sums, 0)
        local.start(next_one, gone_mid, late=True)
        local.start(next_two, gtwo_mid, late=True)
        adds.go(3)
        for b in (1, 0):
            qout[blocks[b], :] = asks[b].end()
        local.start(qout, qpart_mid, late=True)
        for c in range(2):
            kout[pieces[c], :] = tells[c].end()
        local.start(kout, kpart_mid, late=True)
        for item in [lates, early_join] + sums + asks + tells:
            item.drain()
        local.finish()
        adds.open(adds.ready + 2 * width // 256)

    def finish(
        x, gain, weights, taps, qpre, kpre, vpre, bq, bk, bv, qpart, kpart, vpart, cot, gmk, gmv, pk,
        bm, extra, packed, normed, part, ig, conv_rows,
    ):
        loads = [
            local.start(s, t)
            for s, t in (
                (cq_in, qpre), (bq_mid, bq), (qpart_mid, qpart), (taps_in, taps), (ck_in, kpre),
                (bk_mid, bk), (kpart_mid, kpart), (cv_in, vpre), (bv_mid, bv), (vpart_mid, vpart),
                (x_in, x), (gain_in, gain), (wq_in, weights.at[:, lanes[0]]),
                (wk_in, weights.at[:, lanes[1]]), (wv_in, weights.at[:, lanes[2]]),
                (wg_in, weights.at[:, lanes[3]]), (bgate_mid, cot.at[:, lanes[3]]),
                (gmk_mid, gmk), (gmv_mid, gmv), (pk_in, pk), (bm_mid, bm),
            )
        ]
        adds.go(2)
        for item in loads:
            item.wait()
        ones = head_ones()

        def through_conv(pre, at, back, normal):
            values = pre[...]
            conv = values * taps[pl.ds(at, 1), :]
            for j in range(1, KW):
                conv = conv + moved_down(values, j) * taps[pl.ds(at + j, 1), :]
            sig = jax.nn.sigmoid(conv)
            if normal:
                act = conv * sig
                inv = lax.rsqrt(split_sums(act * act, ones) + head_floor)
                unit = act * inv
                back = (back - unit * split_sums(back * unit, ones)) * inv
            back = back * (sig * (1.0 + conv * (1.0 - sig)))
            result = back * taps[pl.ds(at, 1), :]
            conv_rows[pl.ds(at, 1), :] = jnp.sum(back * values, axis=0, keepdims=True)
            for j in range(1, KW):
                conv_rows[pl.ds(at + j, 1), :] = jnp.sum(
                    back * moved_down(values, j), axis=0, keepdims=True
                )
                result = result + moved_up(back, j) * taps[pl.ds(at + j, 1), :]
            return result.astype(bf16)

        conv_rows[...] = jnp.zeros_like(conv_rows)
        cot[:, lanes[0]] = through_conv(qpre, 0, bq[...] + qpart[...], True)
        adds.go(2)
        bk[whole, :] += kpart[...]
        cot[:, lanes[1]] = through_conv(kpre, KW, bk[...], True)
        adds.go(2)
        bv[whole, :] += vpart[...]
        cot[:, lanes[2]] = through_conv(vpre, 2 * KW, bv[...], False)
        adds.go(2)
        rows_of_x = [pl.ds(c * 256, 256) for c in range(tokens // 256)]
        sums = [Scatter(wire, part, rows, t_first, t_passed, t_last, places) for rows in rows_of_x]
        tail_rows = pl.ds(tokens, 16)
        gains = Scatter(wire, part, tail_rows, t_first, t_passed, t_last, places)
        gain_sum = jnp.zeros((1, width), f32)
        for c, rows in enumerate(rows_of_x):
            back = nt(cot[rows, :], weights[...])
            values = x[rows, :].astype(f32)
            inv = lax.rsqrt(jnp.mean(values * values, axis=1, keepdims=True) + epsilon)
            unit = values * inv
            normed[rows, :] = (unit * gain[...]).astype(bf16)
            gain_sum = gain_sum + jnp.sum(back * unit, axis=0, keepdims=True)
            back = back * gain[...]
            part[rows, :] = (
                inv * (back - unit * jnp.mean(back * unit, axis=1, keepdims=True))
            ).astype(bf16)
            sums[c].start()
            if c >= 1:
                sums[c - 1].middle()
            adds.go(2)
        row = lax.broadcasted_iota(jnp.int32, (16, width), 0)
        part[tail_rows, :] = jnp.where(
            row == 0, gain_sum, jnp.where(row == 1, gaintwo[...], 0.0)
        ).astype(bf16)
        gains.start()
        for c in range(width // 256):
            rows = rows_of_x[c]
            packed[rows, :] = tn(normed[:, rows], cot[...]).astype(bf16)
            if c % 2:
                adds.go(2)
        packed[:, lanes[1]] = (packed[:, lanes[1]].astype(f32) + gmk[...]).astype(bf16)
        packed[:, lanes[2]] = (packed[:, lanes[2]].astype(f32) + gmv[...]).astype(bf16)
        local.start(packed, packed_mid, late=True)
        sums[-1].middle()
        gains.middle()
        extra[...] = jnp.zeros_like(extra)
        start = pk[...].astype(f32)
        inv = lax.rsqrt(split_sums(start * start, ones) + head_floor)
        unit = start * inv
        back = pkacc[...]
        top = pl.ds(0, 16)
        extra[top, lanes[0]] = ((back - unit * split_sums(back * unit, ones)) * inv).astype(bf16)
        extra[top, lanes[1]] = pvacc[...].astype(bf16)
        extra[top, lanes[2]] = conv_rows[...].astype(bf16)
        adds.go(2)
        extra[top, lanes[3]] = gains.end().astype(bf16)
        local.start(extra, extra_mid.at[pl.ds(slim, 256)], late=True)
        for c, rows in enumerate(rows_of_x):
            ig[rows, :] = bm[rows, :] + sums[c].end()
        local.start(ig, ig_out, late=True)
        local.finish()
        adds.open(len(chunks))
        for item in sums + [gains]:
            item.drain()

    vm = lambda shape, dtype=None: pltpu.VMEM(shape, bf16 if dtype is None else dtype)
    lw = query_in.shape[1]
    tall, full, flat, weight = (tokens, lw), (tokens, width), (block, width), (width, lw)
    padded, small, square = (KEY_ROWS, lw), (block, lw), one_in.shape
    row = (1, width)
    pl.run_scoped(
        feed,
        vm(full), vm(full), vm(tall, f32), vm(full), vm(row, f32), vm(square), vm(square), vm(square),
        vm(full), vm(full), vm(full), vm(full), vm(full), vm(full), vm(tall), vm(tall, f32),
    )
    pl.run_scoped(
        attend,
        vm(tall), vm(tall), vm(tall), vm(full), vm(weight), vm(weight), vm(tall), vm((lw, width)),
        vm(tall), vm(tall), vm(padded), vm(padded), vm((KEY_ROWS, block), f32), vm(tall),
        vm(tall), vm((lw, width)), vm(weight, f32), vm(weight, f32), vm(tall, f32), vm(tall, f32),
        vm(tall, f32), vm(padded, f32), vm(padded, f32), vm(small), vm(small), vm(flat),
    )
    pl.run_scoped(
        remember,
        vm(flat), vm(full), vm(flat), vm(flat), vm(flat), vm(flat), vm(flat), vm(full), vm(full),
        vm(square), vm(square), vm(square), vm(square), vm(square, f32), vm(square, f32), vm(flat),
        vm(flat), vm(flat), vm(flat), vm(flat), vm(flat), vm(full), vm(small, f32), vm(tall, f32),
        vm(small, f32),
    )
    pl.run_scoped(
        finish,
        vm(full), vm(row, f32), vm((width, width)), vm(taps_in.shape, f32), vm(tall, f32),
        vm(tall, f32), vm(tall, f32), vm(tall, f32), vm(tall, f32), vm(tall, f32), vm(tall, f32),
        vm(small, f32), vm(small, f32), vm(full), vm(weight, f32), vm(weight, f32), vm((NP, lw)),
        vm(tall, f32), vm((256, width)), vm((width, width)), vm(full),
        vm((tokens + 16, width)), vm(tall, f32), vm((16, 256), f32),
    )
    adds.go()


def run_backward_layer(*arrays):
    query, wo, one, x = arrays[0], arrays[12], arrays[24], arrays[28]
    tokens, width = x.shape
    lw = query.shape[1]
    tall, flat, weight, square = (tokens, lw), (STRETCH, width), (width, lw), (width, width)
    small, extra = (STRETCH, lw), (wo.shape[0] + 256, width)
    count = (6 * width + extra[0]) // 256
    vm = lambda shape, dtype=None: pltpu.VMEM(shape, bf16 if dtype is None else dtype)
    sums = [shaped(square)] * 3 + [shaped(one.shape)] * 2 + [shaped(square), shaped(extra)]
    return call(
        backward_layer, 4,
        [shaped(tall, f32), shaped(tall)] + sums
        + [shaped(square)] * 3
        + [shaped(tall, f32), shaped(one.shape), shaped(one.shape), shaped(square), shaped(extra),
           shaped(tall), shaped(weight, f32), shaped(weight, f32), shaped(tall, f32),
           shaped(tall, f32), shaped(tall, f32), shaped(tall, f32), shaped(small, f32),
           shaped(small, f32)],
        (0,) * (len(arrays) - 1) + (1,),
        [vm(flat), vm(flat), vm((tokens, width)), vm((1, width), f32), vm((NP, lw), f32),
         vm((NP, lw), f32)]
        + scatter_room(STRETCH) * 3 + scatter_room(tokens) + scatter_room(STRETCH)
        + scatter_room(tokens + 16) + wide_room(RING)
        + sems(6 * count + 120)
        + [pltpu.SemaphoreType.DMA((160,)), pltpu.SemaphoreType.DMA((2 * count,))],
        65 << 30, 120 << 20,
    )(*arrays)[:9]


def plain_body(
    layer_input,
    out_grad,
    lengths,
    plan,
    norm1_gain,
    w_query,
    w_key,
    w_value,
    w_gate,
    conv_query,
    conv_key,
    conv_value,
    persist_key,
    persist_value,
    mem_w1,
    mem_w2,
    w_out,
    norm2_gain,
    ffn_gate,
    ffn_up,
    ffn_down,
):
    tokens_here = layer_input.shape[0]
    local_width = w_query.shape[1]
    heads_here = local_width // HD
    blocks = tokens_here // STRETCH
    places = jnp.arange(tokens_here)
    row_mask = (places < lengths[0]).astype(f32)
    block_mask = row_mask.reshape(blocks, STRETCH)
    levels = plan[0].astype(f32)
    column_start = lax.axis_index("narrow") * local_width

    def rows_of(values, b):
        return values[b * STRETCH : (b + 1) * STRETCH]

    whole_x = gather_columns(layer_input).astype(f32)
    whole_dy = gather_columns(out_grad)
    inv_one = lax.rsqrt(jnp.mean(whole_x * whole_x, axis=1, keepdims=True) + epsilon)
    unit_one = whole_x * inv_one
    normed_one = (unit_one * norm1_gain).astype(bf16)
    key_pre = product(normed_one, w_key)
    query_pre = product(normed_one, w_query)
    value_pre = product(normed_one, w_value)
    gate_pre = product(normed_one, w_gate)
    key_conv = causal_conv(key_pre, conv_key)
    query_conv = causal_conv(query_pre, conv_query)
    value_conv = causal_conv(value_pre, conv_value)
    key_unit, key_inv = head_norm(jax.nn.silu(key_conv))
    query_unit, query_inv = head_norm(jax.nn.silu(query_conv))
    query_low = query_unit.astype(bf16)
    key_low = key_unit.astype(bf16)
    value_low = jax.nn.silu(value_conv).astype(bf16)

    weight_one, weight_two = mem_w1.astype(f32), mem_w2.astype(f32)
    moment_one = moment_two = None
    saved = []
    for b in range(blocks):
        step_size, momentum, forget = plan_rates(levels[b])
        kept = {"first": weight_one.astype(bf16), "second": weight_two.astype(bf16)}
        mask_rows = block_mask[b][:, None]
        if b < blocks - 1:
            key_rows = gather_columns(rows_of(key_low, b))
            hidden_pre = product(key_rows, kept["first"])
            hidden_act = jax.nn.silu(hidden_pre).astype(bf16)
            predicted = scatter_columns(product(hidden_act, kept["second"]))
            mismatch_here = (
                (predicted - rows_of(value_low, b).astype(f32)) * (mask_rows / STRETCH)
            ).astype(bf16)
            mismatch = gather_columns(mismatch_here)
        query_rows = gather_columns(rows_of(query_low, b))
        query_mem = product(query_rows, kept["first"])
        query_act = jax.nn.silu(query_mem).astype(bf16)
        retrieved = scatter_columns(product(query_act, kept["second"]))
        kept["recalled"] = gather_columns(retrieved.astype(bf16))
        kept.update(query_rows=query_rows, query_mem=query_mem, query_act=query_act)
        if b < blocks - 1:
            through = inner_right(mismatch, kept["second"])
            blended = (through * silu_grad(hidden_pre)).astype(bf16)
            grad_one = inner_left(key_rows, blended)
            grad_two = inner_left(hidden_act, mismatch)
            if moment_one is None:
                moment_one, moment_two = -step_size * grad_one, -step_size * grad_two
            else:
                moment_one = momentum * moment_one - step_size * grad_one
                moment_two = momentum * moment_two - step_size * grad_two
            weight_one = (1.0 - forget) * weight_one + moment_one
            weight_two = (1.0 - forget) * weight_two + moment_two
            kept.update(
                key_rows=key_rows,
                hidden_pre=hidden_pre,
                hidden_act=hidden_act,
                mismatch=mismatch,
                through=through,
                blended=blended,
            )
        saved.append(kept)

    pers_unit, pers_inv = head_norm(persist_key.astype(f32))
    pers_low = pers_unit.astype(bf16)

    def block_scores(b):
        recalled = saved[b]["recalled"]
        mem_unit, mem_inv = head_norm(product(recalled, w_key))
        mem_value = product(recalled, w_value).astype(bf16)
        all_keys = jnp.concatenate(
            [pers_low, mem_unit.astype(bf16), rows_of(key_low, b)], axis=0
        ).reshape(-1, heads_here, HD)
        all_values = jnp.concatenate(
            [persist_value, mem_value, rows_of(value_low, b)], axis=0
        ).reshape(-1, heads_here, HD)
        query_heads = rows_of(query_low, b).reshape(STRETCH, heads_here, HD)
        scores = score_scale * jnp.einsum(
            "qhd,khd->hqk", query_heads, all_keys, preferred_element_type=f32
        )
        scores = jnp.where(visible(block_mask[b])[None], scores, -1e30)
        return (mem_unit, mem_inv, all_keys, all_values, query_heads, scores)

    mixed_list = []
    for b in range(blocks):
        mem_unit, mem_inv, all_keys, all_values, query_heads, scores = block_scores(b)
        row_peak = jnp.max(scores, axis=2, keepdims=True)
        exponent = jnp.exp(scores - row_peak)
        row_total = jnp.sum(exponent, axis=2, keepdims=True)
        prob_low = (exponent / row_total).astype(bf16)
        mixed_list.append(
            jnp.einsum(
                "hqk,khd->qhd", prob_low, all_values, preferred_element_type=f32
            ).reshape(STRETCH, local_width)
        )
        saved[b].update(
            log_total=row_peak + jnp.log(row_total),
            mem_unit=mem_unit,
            mem_inv=mem_inv,
            all_keys=all_keys,
            all_values=all_values,
            query_heads=query_heads,
        )
    mixed_all = jnp.concatenate(mixed_list, axis=0)
    gate_sig = jax.nn.sigmoid(gate_pre)
    gated = (mixed_all * gate_sig).astype(bf16)
    branch_here = scatter_columns(product(gated, w_out))
    branch_full = gather_columns(branch_here.astype(bf16)).astype(f32)
    middle = whole_x + branch_full
    middle_here = layer_input.astype(f32) + branch_here
    inv_two = lax.rsqrt(jnp.mean(middle * middle, axis=1, keepdims=True) + epsilon)
    unit_two = middle * inv_two
    normed_two = (unit_two * norm2_gain).astype(bf16)
    ffn_pre = product(normed_two, ffn_gate)
    up_pre = product(normed_two, ffn_up)
    ffn_sig = jax.nn.sigmoid(ffn_pre)
    hidden_low = (ffn_pre * ffn_sig * up_pre).astype(bf16)
    back_hidden = inner_right(whole_dy, ffn_down)
    back_up_low = (back_hidden * ffn_pre * ffn_sig).astype(bf16)
    back_ffn_low = (back_hidden * up_pre * silu_grad(ffn_pre)).astype(bf16)
    back_normed_two = inner_right(back_ffn_low, ffn_gate) + inner_right(back_up_low, ffn_up)
    gain_two_part = jnp.sum(back_normed_two * unit_two, axis=0)
    middle_part = norm_back(back_normed_two, unit_two, inv_two, norm2_gain)
    back_middle_here = scatter_columns(middle_part)
    grad_ffn_down = inner_left(hidden_low, whole_dy)
    grad_ffn_gate = inner_left(normed_two, back_ffn_low)
    grad_ffn_up = inner_left(normed_two, back_up_low)
    ffn_here = scatter_columns(product(hidden_low, ffn_down))
    layer_output = (middle_here + ffn_here).astype(bf16)
    back_middle_here = back_middle_here + out_grad.astype(f32)
    back_branch = gather_columns(back_middle_here.astype(bf16))
    grad_ffn_gate, grad_ffn_up, grad_ffn_down = sum_wide(
        [grad_ffn_gate, grad_ffn_up, grad_ffn_down]
    )
    grad_w_out = inner_left(gated, back_branch)
    back_gated = inner_right(back_branch, w_out)
    back_mixed_low = (back_gated * gate_sig).astype(bf16)
    back_gate_low = (back_gated * mixed_all * gate_sig * (1.0 - gate_sig)).astype(bf16)

    back_recalled_parts = []
    mem_key_grad = mem_value_grad = 0.0
    pers_key_acc = grad_persist_value = 0.0
    back_query_att, back_key_att, back_value_att = [], [], []
    for b in range(blocks):
        kept = saved[b]
        scores = score_scale * jnp.einsum(
            "qhd,khd->hqk", kept["query_heads"], kept["all_keys"], preferred_element_type=f32
        )
        scores = jnp.where(visible(block_mask[b])[None], scores, -1e30)
        prob_rows = jnp.exp(scores - kept["log_total"])
        prob_low = prob_rows.astype(bf16)
        back_heads = rows_of(back_mixed_low, b).reshape(STRETCH, heads_here, HD)
        back_all_values = jnp.einsum(
            "hqk,qhd->khd", prob_low, back_heads, preferred_element_type=f32
        )
        back_probs = jnp.einsum(
            "qhd,khd->hqk", back_heads, kept["all_values"], preferred_element_type=f32
        )
        back_scores = (
            prob_rows * (back_probs - jnp.sum(prob_rows * back_probs, axis=2, keepdims=True))
        ).astype(bf16)
        back_query = score_scale * jnp.einsum(
            "hqk,khd->qhd", back_scores, kept["all_keys"], preferred_element_type=f32
        )
        back_all_keys = score_scale * jnp.einsum(
            "hqk,qhd->khd", back_scores, kept["query_heads"], preferred_element_type=f32
        )
        back_all_keys = back_all_keys.reshape(-1, local_width)
        back_all_values = back_all_values.reshape(-1, local_width)
        back_mem_key = head_back(
            back_all_keys[NP : NP + STRETCH], kept["mem_unit"], kept["mem_inv"]
        ).astype(bf16)
        back_mem_value = back_all_values[NP : NP + STRETCH].astype(bf16)
        back_recalled_parts.append(
            inner_right(back_mem_key, w_key) + inner_right(back_mem_value, w_value)
        )
        mem_key_grad = mem_key_grad + inner_left(kept["recalled"], back_mem_key)
        mem_value_grad = mem_value_grad + inner_left(kept["recalled"], back_mem_value)
        pers_key_acc = pers_key_acc + back_all_keys[:NP]
        grad_persist_value = grad_persist_value + back_all_values[:NP]
        back_query_att.append(back_query.reshape(STRETCH, local_width))
        back_key_att.append(back_all_keys[NP + STRETCH :])
        back_value_att.append(back_all_values[NP + STRETCH :])
    grad_persist_key = head_back(pers_key_acc, pers_unit, pers_inv)

    cot_one = cot_two = mom_one = mom_two = None
    key_total, query_total, value_total = [None] * blocks, [None] * blocks, [None] * blocks
    for b in reversed(range(blocks)):
        kept = saved[b]
        step_size, momentum, forget = plan_rates(levels[b])
        first_low, second_low = kept["first"], kept["second"]
        back_recalled = gather_columns(scatter_columns(back_recalled_parts[b]).astype(bf16))
        new_one = new_two = None
        if cot_one is None:
            key_total[b], value_total[b] = back_key_att[b], back_value_att[b]
        else:
            key_rows, hidden_pre = kept["key_rows"], kept["hidden_pre"]
            hidden_slope = silu_grad(hidden_pre)
            total_one = cot_one if mom_one is None else mom_one + cot_one
            total_two = cot_two if mom_two is None else mom_two + cot_two
            back_g1 = (-step_size * total_one).astype(bf16)
            back_g2 = (-step_size * total_two).astype(bf16)
            back_blended = product(key_rows, back_g1)
            back_through = (back_blended * hidden_slope).astype(bf16)
            mismatch_part = product(kept["hidden_act"], back_g2) + product(
                back_through, second_low
            )
            mismatch_low = scatter_columns(mismatch_part).astype(bf16)
            back_mismatch = gather_columns(mismatch_low)
            key_part = inner_right(kept["blended"], back_g1)
            back_hidden_act = inner_right(kept["mismatch"], back_g2)
            extra_pre = back_blended * kept["through"] * silu_curve(hidden_pre)
            new_one = (1.0 - forget) * cot_one
            new_two = (1.0 - forget) * cot_two + inner_left(back_through, kept["mismatch"])
        back_query_act = inner_right(back_recalled, second_low)
        back_query_pre = (back_query_act * silu_grad(kept["query_mem"])).astype(bf16)
        query_part = inner_right(back_query_pre, first_low)
        one_term = inner_left(kept["query_rows"], back_query_pre)
        two_term = inner_left(kept["query_act"], back_recalled)
        new_one = one_term if new_one is None else new_one + one_term
        new_two = two_term if new_two is None else new_two + two_term
        if cot_one is not None:
            scale_rows = (block_mask[b] / STRETCH).astype(bf16)[:, None]
            back_pred = back_mismatch * scale_rows
            value_part = -(mismatch_low.astype(f32) * scale_rows.astype(f32))
            back_hidden_act = back_hidden_act + inner_right(back_pred, second_low)
            new_two = new_two + inner_left(kept["hidden_act"], back_pred)
            back_hidden_pre = (back_hidden_act * hidden_slope + extra_pre).astype(bf16)
            key_part = key_part + inner_right(back_hidden_pre, first_low)
            new_one = new_one + inner_left(key_rows, back_hidden_pre)
            key_total[b] = back_key_att[b] + scatter_columns(key_part)
            value_total[b] = back_value_att[b] + value_part
            mom_one, mom_two = momentum * total_one, momentum * total_two
        query_total[b] = back_query_att[b] + scatter_columns(query_part)
        cot_one, cot_two = new_one, new_two
    grad_mem_w1, grad_mem_w2 = cot_one, cot_two

    back_query_total = jnp.concatenate(query_total, axis=0)
    back_key_total = jnp.concatenate(key_total, axis=0)
    back_value_total = jnp.concatenate(value_total, axis=0)
    query_conv_back = head_back(back_query_total, query_unit, query_inv) * silu_grad(query_conv)
    key_conv_back = head_back(back_key_total, key_unit, key_inv) * silu_grad(key_conv)
    value_conv_back = back_value_total * silu_grad(value_conv)
    query_pre_back, grad_conv_query = conv_back(query_conv_back, query_pre, conv_query)
    key_pre_back, grad_conv_key = conv_back(key_conv_back, key_pre, conv_key)
    value_pre_back, grad_conv_value = conv_back(value_conv_back, value_pre, conv_value)
    query_pre_low = query_pre_back.astype(bf16)
    key_pre_low = key_pre_back.astype(bf16)
    value_pre_low = value_pre_back.astype(bf16)
    back_normed_one = (
        inner_right(back_gate_low, w_gate)
        + inner_right(query_pre_low, w_query)
        + inner_right(key_pre_low, w_key)
        + inner_right(value_pre_low, w_value)
    )
    gain_one_part = jnp.sum(back_normed_one * unit_one, axis=0)
    input_part = norm_back(back_normed_one, unit_one, inv_one, norm1_gain)
    back_input_here = scatter_columns(input_part)
    grad_w_gate = inner_left(normed_one, back_gate_low)
    grad_w_query = inner_left(normed_one, query_pre_low)
    grad_w_key = inner_left(normed_one, key_pre_low) + mem_key_grad
    grad_w_value = inner_left(normed_one, value_pre_low) + mem_value_grad
    input_grad = back_middle_here + back_input_here

    gains = lax.psum(
        jnp.concatenate([gain_one_part, gain_two_part]).astype(bf16), ("narrow", "wide")
    ).astype(f32)
    full_width = whole_x.shape[1]
    grad_norm1_gain = lax.dynamic_slice_in_dim(gains, column_start, local_width, 0)
    grad_norm2_gain = lax.dynamic_slice_in_dim(gains, full_width + column_start, local_width, 0)
    late = (
        grad_w_query, grad_w_key, grad_w_value, grad_w_gate, grad_conv_query, grad_conv_key,
        grad_conv_value, grad_persist_key, grad_persist_value, grad_mem_w1, grad_mem_w2, grad_w_out,
    )
    late, (grad_ffn_gate, grad_ffn_up, grad_ffn_down) = lax.optimization_barrier(
        (tuple(v.astype(bf16) for v in late), (grad_ffn_gate, grad_ffn_up, grad_ffn_down))
    )
    (
        grad_w_query, grad_w_key, grad_w_value, grad_w_gate, grad_conv_query, grad_conv_key,
        grad_conv_value, grad_persist_key, grad_persist_value, grad_mem_w1, grad_mem_w2, grad_w_out,
    ) = sum_wide(late)
    return (
        layer_output,
        input_grad,
        grad_norm1_gain,
        grad_w_query,
        grad_w_key,
        grad_w_value,
        grad_w_gate,
        grad_conv_query,
        grad_conv_key,
        grad_conv_value,
        grad_persist_key,
        grad_persist_value,
        grad_mem_w1,
        grad_mem_w2,
        grad_w_out,
        grad_norm2_gain,
        grad_ffn_gate,
        grad_ffn_up,
        grad_ffn_down,
    )

def linked_body(
    layer_input, out_grad, lengths, plan, norm1_gain, w_query, w_key, w_value, w_gate,
    conv_query, conv_key, conv_value, persist_key, persist_value, mem_w1, mem_w2, w_out,
    norm2_gain, ffn_gate, ffn_up, ffn_down,
):
    step_size, momentum, forget = plan_rates(plan[0, 0].astype(f32))
    rates = jnp.stack([lengths[0].astype(f32), step_size, 1.0 - forget])
    rates = jnp.concatenate([rates, jnp.zeros((5,), f32)])
    low_x = gather_columns(layer_input)
    whole_x = low_x.astype(f32)
    inv_one = lax.rsqrt(jnp.mean(whole_x * whole_x, axis=1, keepdims=True) + epsilon)
    unit_one = whole_x * inv_one
    normed_one = (unit_one * norm1_gain).astype(bf16)
    key_pre = product(normed_one, w_key)
    query_pre = product(normed_one, w_query)
    value_pre = product(normed_one, w_value)
    gate_pre = product(normed_one, w_gate).astype(bf16)
    key_conv = causal_conv(key_pre, conv_key)
    query_conv = causal_conv(query_pre, conv_query)
    value_conv = causal_conv(value_pre, conv_value)
    key_unit, key_inv = head_norm(jax.nn.silu(key_conv))
    query_unit, query_inv = head_norm(jax.nn.silu(query_conv))
    query_low = query_unit.astype(bf16)
    key_low = key_unit.astype(bf16)
    value_low = jax.nn.silu(value_conv).astype(bf16)
    pers_unit, pers_inv = head_norm(persist_key.astype(f32))
    pers_low = pers_unit.astype(bf16)

    keys, queries, pre, act, mis, thr, ble, qpre, qact, rec, next_one, next_two = run_memory_forward(
        key_low, query_low, value_low, mem_w1, mem_w2, rates
    )
    branch, branch_here, mixed, gated, whole_dy = run_attend_forward(
        query_low, key_low, value_low, rec, w_key, w_value, pers_low, persist_value, gate_pre,
        w_out, out_grad, rates,
    )
    taps = jnp.concatenate([conv_query, conv_key, conv_value], axis=0)
    (
        input_grad, layer_output, grad_ffn_gate, grad_ffn_up, grad_ffn_down, grad_mem_w1, grad_mem_w2, packed,
        extra,
    ) = run_backward_layer(
        query_low, key_low, value_low, rec, w_query, w_key, w_value, w_gate, persist_key, pers_low,
        persist_value, gate_pre, w_out, mixed, gated, keys, queries, pre, act, mis, thr,
        ble, qpre, qact, mem_w1, mem_w2, next_one, next_two, low_x, norm1_gain[None], taps, query_pre,
        key_pre, value_pre, norm2_gain[None], branch, branch_here, whole_dy, ffn_gate, ffn_up, ffn_down,
        rates,
    )
    local_width, start = w_query.shape[1], w_out.shape[0]
    parts = [packed[:, i * local_width : (i + 1) * local_width].astype(f32) for i in range(4)]
    small = extra[start : start + 16].astype(f32)
    pers_key, pers_value, convs, gains = [
        small[:, i * local_width : (i + 1) * local_width] for i in range(4)
    ]
    return (
        layer_output, input_grad, gains[0], *parts, convs[0:4], convs[4:8], convs[8:12], pers_key,
        pers_value, grad_mem_w1.astype(f32), grad_mem_w2.astype(f32), extra[:start].astype(f32),
        gains[1], grad_ffn_gate.astype(f32), grad_ffn_up.astype(f32), grad_ffn_down.astype(f32),
    )


def body(*arrays):
    tokens_here, local_width = arrays[0].shape
    width, units = arrays[14].shape
    linked = (
        (lax.axis_size("wide"), lax.axis_size("narrow")) == (8, 4)
        and local_width == 256
        and tokens_here == 2 * STRETCH
        and (width, units) == (1024, 1024)
        and arrays[18].shape == (1024, 1024)
    )
    return linked_body(*arrays) if linked else plain_body(*arrays)


def solution(mesh):
    return jax.shard_map(
        body,
        mesh=mesh,
        in_specs=(
            P("wide", "narrow"),
            P("wide", "narrow"),
            P("wide"),
            P("wide", None),
            P(),
            P(None, "narrow"),
            P(None, "narrow"),
            P(None, "narrow"),
            P(None, "narrow"),
            P(None, "narrow"),
            P(None, "narrow"),
            P(None, "narrow"),
            P(None, "narrow"),
            P(None, "narrow"),
            P(None, "narrow"),
            P("narrow", None),
            P("narrow", None),
            P(),
            P(None, "narrow"),
            P(None, "narrow"),
            P("narrow", None),
        ),
        out_specs=(
            P("wide", "narrow"),
            P("wide", "narrow"),
            P("narrow"),
            P(None, "narrow"),
            P(None, "narrow"),
            P(None, "narrow"),
            P(None, "narrow"),
            P(None, "narrow"),
            P(None, "narrow"),
            P(None, "narrow"),
            P(None, "narrow"),
            P(None, "narrow"),
            P(None, "narrow"),
            P("narrow", None),
            P("narrow", None),
            P("narrow"),
            P(None, "narrow"),
            P(None, "narrow"),
            P("narrow", None),
        ),
        check_vma=False,
    )
```

```python
import jax
import jax.numpy as jnp
from jax import lax
from jax.experimental import pallas as pl
from jax.experimental.pallas import tpu as pltpu
from jax.sharding import PartitionSpec as P

HD = 64
NP = 16
KW = 4
STRETCH = 512

epsilon = 1e-06
head_floor = 1.0
score_scale = 12.0
bf16 = jnp.bfloat16
f32 = jnp.float32


def product(left_side, right_side):
    return jnp.dot(left_side, right_side, preferred_element_type=f32)


def inner_left(left_side, right_side):
    return lax.dot_general(
        left_side, right_side, (((0,), (0,)), ((), ())), preferred_element_type=f32
    )


def inner_right(left_side, right_side):
    return lax.dot_general(
        left_side, right_side, (((1,), (1,)), ((), ())), preferred_element_type=f32
    )


def silu_grad(values):
    logistic = jax.nn.sigmoid(values)
    return logistic * (1.0 + values * (1.0 - logistic))


def silu_curve(values):
    logistic = jax.nn.sigmoid(values)
    logistic_slope = logistic * (1.0 - logistic)
    return logistic_slope * (1.0 + values * (1.0 - logistic)) + logistic * (
        1.0 - logistic - values * logistic_slope
    )


def plan_rates(level_now):
    return (0.1 * jnp.exp2(level_now), 0.9 - 0.2 * level_now, 0.02 + 0.05 * level_now)


def head_sums(values):
    width = values.shape[1]
    places = jnp.arange(width) // HD
    same_head = (places[:, None] == places[None, :]).astype(f32)
    return jnp.dot(
        values, same_head, precision=lax.Precision.HIGHEST, preferred_element_type=f32
    )


def head_norm(values):
    inv_norm = lax.rsqrt(head_sums(values * values) + head_floor)
    return (values * inv_norm, inv_norm)


def head_back(grad_rows, unit_rows, inv_norm):
    return (grad_rows - unit_rows * head_sums(grad_rows * unit_rows)) * inv_norm


def norm_back(grad_rows, unit_rows, inv_rows, gain_vec):
    scaled = grad_rows * gain_vec
    return inv_rows * (scaled - unit_rows * jnp.mean(scaled * unit_rows, axis=1, keepdims=True))


def shift_down(values, offset):
    return jnp.concatenate(
        [jnp.zeros((offset, values.shape[1]), values.dtype), values[:-offset]], axis=0
    )


def shift_up(values, offset):
    return jnp.concatenate(
        [values[offset:], jnp.zeros((offset, values.shape[1]), values.dtype)], axis=0
    )


def causal_conv(values, conv_taps):
    result = values * conv_taps[0]
    for offset in range(1, KW):
        result = result + shift_down(values, offset) * conv_taps[offset]
    return result


def conv_back(grad_rows, values, conv_taps):
    back_values = grad_rows * conv_taps[0]
    tap_grads = [jnp.sum(grad_rows * values, axis=0)]
    for offset in range(1, KW):
        back_values = back_values + shift_up(grad_rows, offset) * conv_taps[offset]
        tap_grads.append(jnp.sum(grad_rows * shift_down(values, offset), axis=0))
    return (back_values, jnp.stack(tap_grads, axis=0))


def visible(mask_rows):
    row_width = mask_rows.shape[0]
    places = jnp.arange(row_width)
    valid_keys = mask_rows[None, :] > 0.5
    causal = (places[None, :] <= places[:, None]) & valid_keys
    memory_seen = jnp.broadcast_to(valid_keys, (row_width, row_width))
    persistent = jnp.ones((row_width, NP), dtype=bool)
    return jnp.concatenate([persistent, memory_seen, causal], axis=1)


def gather_columns(values):
    return lax.all_gather(values, "narrow", axis=1, tiled=True)


def scatter_columns(values):
    return lax.psum_scatter(
        values.astype(bf16), "narrow", scatter_dimension=1, tiled=True
    ).astype(f32)


def sum_wide(values):
    return [lax.psum(v.astype(bf16), "wide").astype(f32) for v in values]


MESH = pl.DeviceIdType.MESH
ANY = pl.BlockSpec(memory_space=pl.ANY)
SCALARS = pl.BlockSpec(memory_space=pltpu.SMEM)
VMEM_LIMIT = 60 << 20


def group_places():
    me = lax.axis_index("narrow")
    core = lax.rem(me, 2)
    sib = me + 1 - 2 * core
    opp = lax.rem(me + 2, 4)
    diag = lax.rem(sib + 2, 4)
    return me, sib, opp, diag


def cols(index, width=256):
    return pl.ds(pl.multiple_of(index * width, width), width)


def enter_group(sib, opp):
    barrier = pltpu.get_barrier_semaphore()
    for peer in (sib, opp):
        pl.semaphore_signal(barrier, inc=1, device_id={"narrow": peer}, device_id_type=MESH)
    pl.semaphore_wait(barrier, 2)


class Wire:
    def __init__(self, send, recv):
        self.send, self.recv, self.used = send, recv, 0

    def to(self, source, target, device, axis="narrow"):
        k = self.used
        self.used += 1
        return pltpu.make_async_remote_copy(
            src_ref=source,
            dst_ref=target,
            send_sem=self.send.at[k],
            recv_sem=self.recv.at[k],
            device_id={axis: device},
            device_id_type=MESH,
        )


class Local:
    def __init__(self, sems):
        self.sems, self.used, self.open = sems, 0, []

    def start(self, source, target, late=False):
        copy = pltpu.make_async_copy(source, target, self.sems.at[self.used])
        self.used += 1
        copy.start()
        if late:
            self.open.append(copy)
        return copy

    def finish(self):
        for copy in self.open:
            copy.wait()
        self.open = []


class Gather:
    def __init__(self, wire, full, rows, places):
        me, sib, opp, diag = places
        own = full.at[rows, cols(me)]
        passed = full.at[rows, cols(opp)]
        self.far = wire.to(own, own, opp)
        self.near = wire.to(own, own, sib)
        self.relayed = wire.to(passed, passed, sib)

    def start(self):
        self.far.start()
        self.near.start()

    def relay(self):
        self.far.wait_recv()
        self.relayed.start()

    def end(self):
        self.near.wait_recv()
        self.relayed.wait_recv()

    def drain(self):
        self.far.wait_send()
        self.near.wait_send()
        self.relayed.wait_send()


class Scatter:
    def __init__(self, wire, part, rows, first, passed, last, places):
        me, sib, opp, diag = places
        self.part, self.rows, self.places = part, rows, places
        self.first, self.passed, self.last = first, passed, last
        self.pass_on = wire.to(part.at[rows, cols(diag)], first.at[1, rows], sib)
        self.keep = wire.to(part.at[rows, cols(sib)], first.at[0, rows], sib)
        self.far = wire.to(passed.at[rows], last.at[rows], opp)

    def start(self):
        self.pass_on.start()
        self.keep.start()

    def middle(self):
        me, sib, opp, diag = self.places
        self.pass_on.wait_recv()
        self.passed[self.rows] = (
            self.part[self.rows, cols(opp)].astype(f32) + self.first[1, self.rows].astype(f32)
        ).astype(bf16)
        self.far.start()

    def end(self):
        me, sib, opp, diag = self.places
        self.keep.wait_recv()
        near = self.part[self.rows, cols(me)].astype(f32) + self.first[0, self.rows].astype(f32)
        self.far.wait_recv()
        return near + self.last[self.rows].astype(f32)

    def drain(self):
        self.pass_on.wait_send()
        self.keep.wait_send()
        self.far.wait_send()


def scatter_room(rows):
    return [
        pltpu.VMEM((2, rows, 256), bf16),
        pltpu.VMEM((rows, 256), bf16),
        pltpu.VMEM((rows, 256), bf16),
    ]


def sems(count):
    return [
        pltpu.SemaphoreType.DMA((count,)),
        pltpu.SemaphoreType.DMA((count,)),
    ]


def shaped(shape, dtype=None):
    return jax.ShapeDtypeStruct(shape, bf16 if dtype is None else dtype)


def call(kernel, collective, outs, ins, scratch, flops, moved):
    return pl.pallas_call(
        kernel,
        out_shape=outs,
        in_specs=[SCALARS if s else ANY for s in ins],
        out_specs=[ANY] * len(outs),
        scratch_shapes=scratch,
        compiler_params=pltpu.CompilerParams(
            collective_id=collective, has_side_effects=True, vmem_limit_bytes=VMEM_LIMIT
        ),
        cost_estimate=pl.CostEstimate(flops=flops, bytes_accessed=moved, transcendentals=0),
        name=kernel.__name__,
    )


KEY_ROWS = 2 * STRETCH + 128


def silu(values):
    return values * jax.nn.sigmoid(values)


def head_ones():
    left = lax.broadcasted_iota(jnp.int32, (256, 256), 0) // HD
    right = lax.broadcasted_iota(jnp.int32, (256, 256), 1) // HD
    return (left == right).astype(f32).astype(bf16)


def split_sums(values, ones):
    high = values.astype(bf16)
    rest = (values - high.astype(f32)).astype(bf16)
    return jnp.dot(high, ones, preferred_element_type=f32) + jnp.dot(
        rest, ones, preferred_element_type=f32
    )


def head_only(values, head):
    lane_head = lax.broadcasted_iota(jnp.int32, values.shape, 1) // HD
    return jnp.where(lane_head == head, values.astype(f32), 0.0).astype(bf16)


def key_bias(first_row, rows, valid, flipped):
    shape = (KEY_ROWS, rows) if flipped else (rows, KEY_ROWS)
    slot = lax.broadcasted_iota(jnp.int32, shape, 0 if flipped else 1)
    row = lax.broadcasted_iota(jnp.int32, shape, 1 if flipped else 0) + first_row
    memory = (slot < STRETCH) & (slot.astype(f32) < valid)
    place = slot - STRETCH
    causal = (place >= 0) & (place <= row) & (place.astype(f32) < valid) & (slot < 2 * STRETCH)
    persistent = (slot >= 2 * STRETCH) & (slot < 2 * STRETCH + NP)
    return jnp.where(memory | causal | persistent, 0.0, -1e30)


def unit_rows(values, ones):
    wide_values = values.astype(f32)
    return wide_values * lax.rsqrt(split_sums(wide_values * wide_values, ones) + head_floor)


def nt(left, right):
    return lax.dot_general(left, right, (((1,), (1,)), ((), ())), preferred_element_type=f32)


def tn(left, right):
    return lax.dot_general(left, right, (((0,), (0,)), ((), ())), preferred_element_type=f32)


def slope_of(values):
    sig = jax.nn.sigmoid(values)
    return sig * (1.0 + values * (1.0 - sig))


def forward_layer(
    xl_in, dyl_in, gain_in, wq_in, wk_in, wv_in, wg_in, tq_in, tk_in, tv_in, pk_in, pv_in, one_in, two_in,
    wo_in, rates,
    x_out, qconv_out, kconv_out, vconv_out, qlow_out, klow_out, vlow_out, gate_out, key_out, query_out,
    pre_out, act_out, mis_out, thr_out, ble_out, qpre_out, qact_out, rec_out, one_out, two_out,
    branch_out, here_out, mixed_out, gated_out, dy_out,
    x, gain, weights, tq, tk, tv, qconv, kconv, vconv, qlow, klow, vlow, gate, pk, key, query, one, two,
    pre, act, part, mis, thr, ble, qpre, qact, qpart, rec, next_one, next_two, wo, keys, values, bias,
    mixed, gated, bpart, branch, here, dy,
    first, passed, last, q_first, q_passed, q_last, b_first, b_passed, b_last,
    send, recv, local_sems,
):
    places = group_places()
    me, sib, opp, diag = places
    wire, local = Wire(send, recv), Local(local_sems)
    half, block = STRETCH // 2, STRETCH
    lanes = [pl.ds(i * 256, 256) for i in range(4)]
    get_x = local.start(xl_in, x.at[:, cols(me)])
    loads = [
        local.start(s, t)
        for s, t in (
            (wq_in, weights.at[:, lanes[0]]), (wk_in, weights.at[:, lanes[1]]),
            (wv_in, weights.at[:, lanes[2]]), (wg_in, weights.at[:, lanes[3]]), (gain_in, gain),
            (tq_in, tq), (tk_in, tk), (tv_in, tv), (pk_in, pk),
            (pv_in, values.at[pl.ds(2 * block, NP)]),
        )
    ]
    later = [
        local.start(s, t)
        for s, t in ((one_in, one), (two_in, two), (wo_in, wo), (dyl_in, dy.at[:, cols(me)]))
    ]
    pieces = [pl.ds(c * half, half) for c in range(4)]
    blocks = [pl.ds(b * block, block) for b in range(2)]
    ones = head_ones()
    for pad in (qconv, kconv, vconv):
        pad[pl.ds(0, 8), :] = jnp.zeros((8, 256), f32)
    keys[pl.ds(2 * block + NP, 128 - NP), :] = jnp.zeros((128 - NP, 256), bf16)
    values[pl.ds(2 * block + NP, 128 - NP), :] = jnp.zeros((128 - NP, 256), bf16)
    enter_group(sib, opp)
    get_x.wait()
    rows_of_x = [Gather(wire, x, rows, places) for rows in pieces]
    key_joins = [Gather(wire, key, rows, places) for rows in pieces[:2]]
    query_joins = [Gather(wire, query, rows, places) for rows in blocks]
    sums = [Scatter(wire, part, rows, first, passed, last, places) for rows in pieces[:2]]
    misses = [Gather(wire, mis, rows, places) for rows in pieces[:2]]
    qsums = [Scatter(wire, qpart, rows, q_first, q_passed, q_last, places) for rows in blocks]
    reads = [Gather(wire, rec, rows, places) for rows in blocks]
    rows_of_dy = [Gather(wire, dy, rows, places) for rows in blocks]
    bsums = [Scatter(wire, bpart, rows, b_first, b_passed, b_last, places) for rows in pieces]
    joins = [Gather(wire, branch, rows, places) for rows in pieces]
    rows_of_x[0].start()
    rows_of_x[1].start()
    for item in loads:
        item.wait()
    keys[pl.ds(2 * block, NP), :] = unit_rows(pk[...], ones).astype(bf16)

    def project(c):
        rows = pieces[c]
        now = x[rows, :].astype(f32)
        inv = lax.rsqrt(jnp.mean(now * now, axis=1, keepdims=True) + epsilon)
        normed = (now * inv * gain[...]).astype(bf16)
        for at, (pad, low, taps) in enumerate(
            ((kconv, klow, tk), (qconv, qlow, tq), (vconv, vlow, tv))
        ):
            side = lanes[(1, 0, 2)[at]]
            start = 8 + c * half
            pad[pl.ds(start, half), :] = jnp.dot(
                normed, weights[:, side], preferred_element_type=f32
            )
            conv = pad[pl.ds(start, half), :] * taps[pl.ds(0, 1), :]
            for j in range(1, KW):
                conv = conv + pad[pl.ds(start - j, half), :] * taps[pl.ds(j, 1), :]
            conv = conv * jax.nn.sigmoid(conv)
            low[rows, :] = (unit_rows(conv, ones) if at < 2 else conv).astype(bf16)
            if at == 0 and c < 2:
                key[rows, cols(me)] = klow[rows, :]
                key_joins[c].start()
        query[rows, cols(me)] = qlow[rows, :]
        gate[rows, :] = jnp.dot(normed, weights[:, lanes[3]], preferred_element_type=f32).astype(bf16)

    def hide(c):
        rows = pieces[c]
        hidden = jnp.dot(key[rows, :], one[...], preferred_element_type=f32)
        pre[rows, :] = hidden.astype(bf16)
        act[rows, :] = silu(hidden).astype(bf16)
        part[rows, :] = jnp.dot(act[rows, :], two[...], preferred_element_type=f32).astype(bf16)
        sums[c].start()

    def read(b, weight_one, weight_two):
        rows = blocks[b]
        asked = jnp.dot(query[rows, :], weight_one[...], preferred_element_type=f32)
        qpre[rows, :] = asked.astype(bf16)
        qact[rows, :] = silu(asked).astype(bf16)
        qpart[rows, :] = jnp.dot(
            qact[rows, :], weight_two[...], preferred_element_type=f32
        ).astype(bf16)
        qsums[b].start()

    rows_of_x[0].relay()
    rows_of_x[0].end()
    project(0)
    rows_of_x[1].relay()
    rows_of_x[1].end()
    project(1)
    rows_of_x[2].start()
    for item in later:
        item.wait()
    key_joins[0].relay()
    key_joins[0].end()
    hide(0)
    key_joins[1].relay()
    sums[0].middle()
    key_joins[1].end()
    hide(1)
    rows_of_x[2].relay()
    sums[1].middle()
    rows_of_x[3].start()
    query_joins[0].start()
    for c in range(2):
        rows = pieces[c]
        predicted = sums[c].end()
        index = lax.broadcasted_iota(jnp.int32, (half, 1), 0) + c * half
        scale = jnp.where(index.astype(f32) < rates[0], 1.0 / STRETCH, 0.0)
        mis[rows, cols(me)] = ((predicted - vlow[rows, :].astype(f32)) * scale).astype(bf16)
        misses[c].start()
    for s, t in ((key, key_out), (pre, pre_out), (act, act_out)):
        local.start(s, t, late=True)
    rows_of_x[2].end()
    project(2)
    misses[0].relay()
    rows_of_x[3].relay()
    query_joins[0].relay()
    misses[1].relay()
    for c in range(2):
        rows = pieces[c]
        misses[c].end()
        through = nt(mis[rows, :], two[...])
        thr[rows, :] = through.astype(bf16)
        ble[rows, :] = (through * slope_of(pre[rows, :].astype(f32))).astype(bf16)
    rows_of_x[3].end()
    project(3)
    query_joins[1].start()
    for s, t in (
        (x, x_out), (qconv.at[pl.ds(8, 4 * half)], qconv_out), (kconv.at[pl.ds(8, 4 * half)], kconv_out),
        (vconv.at[pl.ds(8, 4 * half)], vconv_out), (qlow, qlow_out), (klow, klow_out),
        (vlow, vlow_out), (gate, gate_out), (mis, mis_out), (thr, thr_out), (ble, ble_out),
    ):
        local.start(s, t, late=True)
    step_size, keep = rates[1], rates[2]

    def update(c, carried):
        rows = pl.ds(pl.multiple_of(c * half, half), half)
        grad = tn(key[:, rows], ble[...])
        next_one[rows, :] = (keep * one[rows, :].astype(f32) - step_size * grad).astype(bf16)
        grad = tn(act[:, rows], mis[...])
        next_two[rows, :] = (keep * two[rows, :].astype(f32) - step_size * grad).astype(bf16)
        return carried

    query_joins[0].end()
    read(0, one, two)
    lax.fori_loop(0, 2, update, 0)
    qsums[0].middle()
    lax.fori_loop(2, 4, update, 0)
    for s, t in ((next_one, one_out), (next_two, two_out)):
        local.start(s, t, late=True)
    query_joins[1].relay()
    rec[blocks[0], cols(me)] = qsums[0].end().astype(bf16)
    reads[0].start()
    query_joins[1].end()
    read(1, next_one, next_two)
    reads[0].relay()
    qsums[1].middle()
    for s, t in ((query, query_out), (qpre, qpre_out), (qact, qact_out)):
        local.start(s, t, late=True)
    reads[0].end()
    rec[blocks[1], cols(me)] = qsums[1].end().astype(bf16)
    reads[1].start()
    rows_of_dy[0].start()

    def settle(c):
        rows = pieces[c]
        total = bsums[c].end()
        here[rows, :] = total
        branch[rows, cols(me)] = total.astype(bf16)
        joins[c].start()

    for c in range(4):
        b, rows = c // 2, pieces[c]
        if c % 2 == 0:
            if b == 1:
                reads[1].end()
            memory = rec[blocks[b], :]
            made = jnp.dot(memory, weights[:, lanes[1]], preferred_element_type=f32)
            keys[pl.ds(0, block), :] = unit_rows(made, ones).astype(bf16)
            values[pl.ds(0, block), :] = jnp.dot(
                memory, weights[:, lanes[2]], preferred_element_type=f32
            ).astype(bf16)
            keys[pl.ds(block, block), :] = klow[blocks[b], :]
            values[pl.ds(block, block), :] = vlow[blocks[b], :]
        bias[...] = key_bias((c % 2) * half, half, rates[0] - float(b * block), False)

        def one_head(head, total):
            asked = head_only(qlow[rows, :], head)
            scores = nt(asked, keys[...])
            chances = jnp.exp(score_scale * scores + bias[...])
            inv = 1.0 / jnp.sum(chances, axis=1, keepdims=True)
            got = jnp.dot((chances * inv).astype(bf16), values[...], preferred_element_type=f32)
            lane_head = lax.broadcasted_iota(jnp.int32, got.shape, 1) // HD
            return jnp.where(lane_head == head, got, total)

        total = lax.fori_loop(0, 4, one_head, jnp.zeros((half, 256), f32))
        mixed[rows, :] = total.astype(bf16)
        gated[rows, :] = (total * jax.nn.sigmoid(gate[rows, :].astype(f32))).astype(bf16)
        bpart[rows, :] = jnp.dot(gated[rows, :], wo[...], preferred_element_type=f32).astype(bf16)
        bsums[c].start()
        if c == 0:
            reads[1].relay()
            rows_of_dy[0].relay()
            bsums[0].middle()
        if c == 1:
            rows_of_dy[1].start()
            bsums[1].middle()
            settle(0)
        if c == 2:
            rows_of_dy[1].relay()
            bsums[2].middle()
            joins[0].relay()
            settle(1)
    for item in rows_of_dy:
        item.end()
    for s, t in ((rec, rec_out), (dy, dy_out), (mixed, mixed_out), (gated, gated_out)):
        local.start(s, t, late=True)
    bsums[3].middle()
    settle(2)
    joins[1].relay()
    settle(3)
    local.start(here, here_out, late=True)
    joins[2].relay()
    joins[3].relay()
    for item in joins:
        item.end()
    local.start(branch, branch_out, late=True)
    for item in (
        rows_of_x + key_joins + query_joins + sums + misses + qsums + reads + rows_of_dy + bsums + joins
    ):
        item.drain()
    local.finish()


def run_forward_layer(*arrays):
    tokens, lw = arrays[0].shape
    square, wo = arrays[12].shape, arrays[14].shape
    width = square[0]
    tall, full, flat, padded = (tokens, lw), (tokens, width), (STRETCH, width), (KEY_ROWS, lw)
    deep = (tokens + 8, lw)
    vm = lambda shape, dtype=None: pltpu.VMEM(shape, bf16 if dtype is None else dtype)
    return call(
        forward_layer, 1,
        [shaped(full), shaped(tall, f32), shaped(tall, f32), shaped(tall, f32)] + [shaped(tall)] * 4
        + [shaped(flat), shaped(full)] + [shaped(flat)] * 5 + [shaped(full)] * 3
        + [shaped(square)] * 2
        + [shaped(full), shaped(tall, f32), shaped(tall), shaped(tall), shaped(full)],
        (0,) * 15 + (1,),
        [vm(full), vm((1, width), f32), vm((width, width)), vm((KW, lw), f32), vm((KW, lw), f32),
         vm((KW, lw), f32), vm(deep, f32), vm(deep, f32), vm(deep, f32), vm(tall), vm(tall), vm(tall),
         vm(tall), vm((NP, lw)), vm(flat), vm(full), vm(square), vm(square)]
        + [vm(flat)] * 6 + [vm(full)] * 4 + [vm(square)] * 2
        + [vm(wo), vm(padded), vm(padded), vm((STRETCH // 2, KEY_ROWS), f32), vm(tall), vm(tall),
           vm(full), vm(full), vm(tall, f32), vm(full)]
        + scatter_room(STRETCH) + scatter_room(tokens) + scatter_room(tokens)
        + sems(100) + [pltpu.SemaphoreType.DMA((64,))],
        20 << 30, 40 << 20,
    )(*arrays)


def wide_places():
    at = lax.axis_index("wide")
    bits = (lax.rem(at, 2), lax.rem(lax.div(at, 2), 2), lax.div(at, 4))
    return bits, tuple(at + step * (1 - 2 * bit) for step, bit in zip((1, 2, 4), bits))


def enter_all(sib, opp, wide):
    barrier = pltpu.get_barrier_semaphore()
    for peer in (sib, opp):
        pl.semaphore_signal(barrier, inc=1, device_id={"narrow": peer}, device_id_type=MESH)
    for peer in wide[1]:
        pl.semaphore_signal(barrier, inc=1, device_id={"wide": peer}, device_id_type=MESH)
    pl.semaphore_wait(barrier, 5)


class WideSum:
    ahead = 2
    orders = ((0, 1, 2), (0, 1, 2), (1, 0, 2), (0, 1, 2))

    def __init__(self, wire, copy_sems, wide, chunks, room, ring):
        bits, peers = wide
        self.mine, self.got, self.more, self.rest, self.done = room
        self.items = []
        for k, (source, start, target, goal) in enumerate(chunks):
            slot = k % ring
            order = self.orders[k % len(self.orders)]
            a, b, c = [bits[d] for d in order]
            pa, pb, pc = [peers[d] for d in order]
            off = lambda bit, size: pl.multiple_of(bit * size, size)
            first = goal + off(a, 128)
            second = first + off(b, 64)
            third = second + off(c, 32)
            spots = [target.at[pl.ds(at, size)] for at, size in ((third, 32), (second, 64), (first, 128))]
            self.items.append({
                "slot": slot,
                "half": pl.ds(off(b, 64), 64),
                "quarter": pl.ds(off(c, 32), 32),
                "load": pltpu.make_async_copy(
                    source.at[pl.ds(start + off(a, 128), 128)], self.mine.at[slot], copy_sems.at[2 * k]
                ),
                "keep": pltpu.make_async_copy(self.done.at[slot], spots[0], copy_sems.at[2 * k + 1]),
                "one": wire.to(
                    source.at[pl.ds(start + off(1 - a, 128), 128)], self.got.at[slot], pa, "wide"
                ),
                "two": wire.to(
                    self.got.at[slot, pl.ds(off(1 - b, 64), 64)], self.more.at[slot], pb, "wide"
                ),
                "three": wire.to(
                    self.more.at[slot, pl.ds(off(1 - c, 32), 32)], self.rest.at[slot], pc, "wide"
                ),
                "four": wire.to(self.done.at[slot], spots[0], pc, "wide"),
                "five": wire.to(spots[1], spots[1], pb, "wide"),
                "six": wire.to(spots[2], spots[2], pa, "wide"),
            })
        count = len(self.items)
        self.steps, self.begun, self.ready, self.wanted, self.next = [], 0, count, 0, 0
        stages = ((self.last, 6), (self.halve, 0), (self.again, 1), (self.total, 2), (self.back, 3),
                  (self.most, 4))
        for i in range(count + 6):
            for stage, lag in stages:
                if 0 <= i - lag < count:
                    self.steps.append((stage, i - lag))

    def open(self, ready):
        self.ready = ready
        self.begin(self.wanted)

    def begin(self, upto):
        self.wanted = max(self.wanted, upto)
        while self.begun < min(upto, self.ready, len(self.items)):
            self.items[self.begun]["load"].start()
            self.items[self.begun]["one"].start()
            self.begun += 1

    def halve(self, i):
        item, slot = self.items[i], self.items[i]["slot"]
        self.begin(i + 1)
        item["one"].wait_recv()
        self.begin(i + 1 + self.ahead)
        item["load"].wait()
        self.got[slot] = (
            self.got[slot].astype(f32) + self.mine[slot].astype(f32)
        ).astype(bf16)
        item["two"].start()

    def again(self, i):
        item, slot = self.items[i], self.items[i]["slot"]
        item["two"].wait_recv()
        self.more[slot] = (
            self.more[slot].astype(f32) + self.got[slot, item["half"], :].astype(f32)
        ).astype(bf16)
        item["three"].start()

    def total(self, i):
        item, slot = self.items[i], self.items[i]["slot"]
        item["three"].wait_recv()
        self.done[slot] = (
            self.rest[slot].astype(f32) + self.more[slot, item["quarter"], :].astype(f32)
        ).astype(bf16)
        for name in ("one", "two", "three"):
            item[name].wait_send()
        item["four"].start()
        item["keep"].start()

    def back(self, i):
        item = self.items[i]
        item["four"].wait_recv()
        item["keep"].wait()
        item["four"].wait_send()
        item["five"].start()

    def most(self, i):
        item = self.items[i]
        item["five"].wait_recv()
        item["five"].wait_send()
        item["six"].start()

    def last(self, i):
        self.items[i]["six"].wait_recv()
        self.items[i]["six"].wait_send()

    def go(self, count=None):
        stop = len(self.steps) if count is None else min(self.next + count, len(self.steps))
        while self.next < stop:
            step, i = self.steps[self.next]
            if step == self.halve and i >= self.ready:
                break
            step(i)
            self.next += 1


def wide_room(ring):
    return [
        pltpu.VMEM((ring, rows, 1024), bf16) for rows in (128, 128, 64, 32, 32)
    ]


def moved_down(values, offset):
    row = lax.broadcasted_iota(jnp.int32, values.shape, 0)
    return jnp.where(row < offset, 0.0, pltpu.roll(values, offset, 0))


def moved_up(values, offset):
    rows = values.shape[0]
    row = lax.broadcasted_iota(jnp.int32, values.shape, 0)
    return jnp.where(row >= rows - offset, 0.0, pltpu.roll(values, rows - offset, 0))


RING = 8


def backward_layer(
    query_in, key_in, value_in, rec_in, wq_in, wk_in, wv_in, wg_in, pk_in, pv_in, gate_in, wo_in,
    mixed_in, gated_in, keys_in, queries_in, pre_in, act_in, mis_in, thr_in, ble_in, qpre_in,
    qact_in, one_in, two_in, next_one_in, next_two_in, x_in, gain_in, tq_in, tk_in, tv_in, cq_in, ck_in, cv_in,
    gaintwo_in, branch_in, here_in, dy_in, fgate_in, fup_in, fdown_in, rates,
    ig_out, lo_out, gg_out, gu_out, gd_out, gone_out, gtwo_out, packed_out, extra_out,
    gg_mid, gu_mid, gd_mid, bm_mid, gone_mid, gtwo_mid, packed_mid, extra_mid, bgate_mid, gmk_mid, gmv_mid, bq_mid, bk_mid, bv_mid,
    qpart_mid, kpart_mid, vpart_mid,
    brec, late, bb, gaintwo, pkacc, pvacc,
    a_first, a_passed, a_last, l_first, l_passed, l_last, m_first, m_passed, m_last,
    q_first, q_passed, q_last, k_first, k_passed, k_last, t_first, t_passed, t_last,
    mine, got, more, rest, done, send, recv, local_sems, copy_sems,
):
    places = group_places()
    me, sib, opp, diag = places
    wire, local = Wire(send, recv), Local(local_sems)
    wide = wide_places()
    half, block = STRETCH // 2, STRETCH
    tokens, width = x_in.shape
    slim = wo_in.shape[0]
    chunks = []
    for source, target in (
        (gg_mid, gg_out), (gu_mid, gu_out), (gd_mid, gd_out), (gone_mid, gone_out),
        (gtwo_mid, gtwo_out), (packed_mid, packed_out), (extra_mid, extra_out),
    ):
        chunks += [(source, i * 256, target, i * 256) for i in range(source.shape[0] // 256)]
    adds = WideSum(wire, copy_sems, wide, chunks, (mine, got, more, rest, done), RING)
    adds.ready = 0
    adds.begin(adds.ahead)
    pieces = [pl.ds(c * half, half) for c in range(2)]
    blocks = [pl.ds(b * block, block) for b in range(2)]
    whole = pl.ds(0, block)
    lanes = [pl.ds(i * 256, 256) for i in range(4)]
    early, bmis = bb.at[pl.ds(0, block)], bb.at[pl.ds(block, block)]
    early_join = Gather(wire, early, whole, places)
    misses = [Gather(wire, bmis, rows, places) for rows in pieces]
    recs = [Gather(wire, brec, rows, places) for rows in pieces]

    def feed(
        x, branch, here, dy, gain, gate, up, down, normed, hidden, bup, bffn, part, part_two, out, bm
    ):
        loads = [
            local.start(s, t)
            for s, t in (
                (x_in, x), (branch_in, branch), (gaintwo_in, gain), (fgate_in, gate), (fup_in, up),
                (dy_in, dy), (fdown_in, down), (here_in, here),
            )
        ]
        size = 256
        count = tokens // size
        parts_of = [pl.ds(c * size, size) for c in range(count)]
        enter_all(sib, opp, wide)
        for item in loads:
            item.wait()
        sums = [Scatter(wire, part, rows, t_first, t_passed, t_last, places) for rows in parts_of]
        outs = [Scatter(wire, part_two, rows, q_first, q_passed, q_last, places) for rows in parts_of]
        joins = [Gather(wire, bb, rows, places) for rows in parts_of]
        gaintwo[...] = jnp.zeros_like(gaintwo)

        def settle(c):
            rows = parts_of[c]
            back = sums[c].end().astype(bf16).astype(f32) + dy[rows, cols(me)].astype(f32)
            bm[rows, :] = back
            bb[rows, cols(me)] = back.astype(bf16)
            joins[c].start()

        for c in range(count):
            rows = parts_of[c]
            middle = x[rows, :].astype(f32) + branch[rows, :].astype(f32)
            inv = lax.rsqrt(jnp.mean(middle * middle, axis=1, keepdims=True) + epsilon)
            normed[rows, :] = (middle * inv * gain[...]).astype(bf16)
            pre = jnp.dot(normed[rows, :], gate[...], preferred_element_type=f32)
            lift = jnp.dot(normed[rows, :], up[...], preferred_element_type=f32)
            back = nt(dy[rows, :], down[...])
            sig = jax.nn.sigmoid(pre)
            act = pre * sig
            hidden[rows, :] = (act * lift).astype(bf16)
            bup[rows, :] = (back * act).astype(bf16)
            bffn[rows, :] = (back * lift * (sig * (1.0 + pre * (1.0 - sig)))).astype(bf16)
            back = nt(bffn[rows, :], gate[...]) + nt(bup[rows, :], up[...])
            middle = x[rows, :].astype(f32) + branch[rows, :].astype(f32)
            unit = middle * inv
            gaintwo[...] += jnp.sum(back * unit, axis=0, keepdims=True)
            back = back * gain[...]
            part[rows, :] = (
                inv * (back - unit * jnp.mean(back * unit, axis=1, keepdims=True))
            ).astype(bf16)
            sums[c].start()
            if c >= 1:
                sums[c - 1].middle()
            if c >= 2:
                settle(c - 2)
            if c >= 3:
                joins[c - 3].relay()

        def grads(left, right, keep, target, k):
            rows = parts_of[k]
            keep[rows, :] = tn(left[:, rows], right[...]).astype(bf16)
            return local.start(keep.at[rows], target.at[rows])

        copies = [grads(normed, bffn, gate, gg_mid, 0)]
        sums[3].middle()
        settle(2)
        joins[1].relay()
        for k in range(1, 4):
            copies.append(grads(normed, bffn, gate, gg_mid, k))
            copies.pop(0).wait()
            adds.open(adds.ready + 1)
            if k == 1:
                settle(3)
                joins[2].relay()
        for c, rows in enumerate(parts_of):
            part_two[rows, :] = jnp.dot(
                hidden[rows, :], down[...], preferred_element_type=f32
            ).astype(bf16)
            outs[c].start()
            if c == 1:
                joins[3].relay()
                copies.pop(0).wait()
                adds.open(adds.ready + 1)
                adds.go(2)
        for k in range(4):
            copies.append(grads(normed, bup, up, gu_mid, k))
            outs[k].middle()
        adds.go(3)
        for item in copies:
            item.wait()
        adds.open(adds.ready + 4)
        copies = [grads(hidden, dy, down, gd_mid, k) for k in range(4)]
        local.start(bm, bm_mid, late=True)
        adds.go(3)
        for c, rows in enumerate(parts_of):
            total = x[rows, cols(me)].astype(f32) + here[rows, :] + outs[c].end()
            out[rows, :] = total.astype(bf16)
        local.start(out, lo_out, late=True)
        for item in joins:
            item.end()
        for item in copies:
            item.wait()
        adds.open(adds.ready + 4)
        for item in sums + outs + joins:
            item.drain()
        local.finish()

    def attend(
        query, key, value, rec, wk, wv, gate, wo, mixed, gated, keys, values, bias, bmix, bgate,
        pk, gwo, gmk, gmv, bq, bk, bv, kacc, vacc, bmk, bmv, part,
    ):
        loads = [
            local.start(s, t)
            for s, t in (
                (wo_in, wo), (gate_in, gate), (mixed_in, mixed), (gated_in, gated),
                (rec_in, rec), (wk_in, wk), (wv_in, wv), (query_in, query), (key_in, key),
                (value_in, value), (pk_in, pk),
                (pv_in, values.at[pl.ds(2 * block, NP)]),
            )
        ]
        keys[pl.ds(2 * block + NP, 128 - NP), :] = jnp.zeros((128 - NP, 256), bf16)
        values[pl.ds(2 * block + NP, 128 - NP), :] = jnp.zeros((128 - NP, 256), bf16)
        pkacc[...] = jnp.zeros_like(pkacc)
        pvacc[...] = jnp.zeros_like(pvacc)
        gmk[...] = jnp.zeros_like(gmk)
        gmv[...] = jnp.zeros_like(gmv)
        for item in loads:
            item.wait()

        def through_gate(c, carried):
            rows = pl.ds(pl.multiple_of(c * half, half), half)
            back = nt(bb[rows, :], wo[...])
            sig = jax.nn.sigmoid(gate[rows, :].astype(f32))
            bmix[rows, :] = (back * sig).astype(bf16)
            bgate[rows, :] = (back * mixed[rows, :].astype(f32) * sig * (1.0 - sig)).astype(bf16)
            return carried

        lax.fori_loop(0, 4, through_gate, 0)
        local.start(bgate, bgate_mid, late=True)
        gwo[...] = tn(gated[...], bb[...]).astype(bf16)
        local.start(gwo, extra_mid.at[pl.ds(0, slim)], late=True)
        ones = head_ones()
        keys[pl.ds(2 * block, NP), :] = unit_rows(pk[...], ones).astype(bf16)
        sums = [Scatter(wire, part, rows, a_first, a_passed, a_last, places) for rows in pieces]
        adds.go(3)
        for b in (1, 0):
            rows = blocks[b]
            memory = rec[rows, :]
            made = jnp.dot(memory, wk[...], preferred_element_type=f32)
            inv = lax.rsqrt(split_sums(made * made, ones) + head_floor)
            keys[pl.ds(0, block), :] = (made * inv).astype(bf16)
            values[pl.ds(0, block), :] = jnp.dot(
                memory, wv[...], preferred_element_type=f32
            ).astype(bf16)
            keys[pl.ds(block, block), :] = key[rows, :]
            values[pl.ds(block, block), :] = value[rows, :]
            bias[...] = key_bias(0, block, rates[0] - float(b * block), True)
            kacc[...] = jnp.zeros_like(kacc)
            vacc[...] = jnp.zeros_like(vacc)

            def one_head(head, total):
                asked = head_only(query[rows, :], head)
                back = head_only(bmix[rows, :], head)
                weights = jnp.exp(score_scale * nt(keys[...], asked) + bias[...])
                weights = weights * (1.0 / jnp.sum(weights, axis=0, keepdims=True))
                vacc[...] += jnp.dot(weights.astype(bf16), back, preferred_element_type=f32)
                slope = nt(values[...], back)
                slope = (
                    weights * (slope - jnp.sum(weights * slope, axis=0, keepdims=True))
                ).astype(bf16)
                kacc[...] += jnp.dot(slope, asked, preferred_element_type=f32)
                read = tn(slope, keys[...])
                lane_head = lax.broadcasted_iota(jnp.int32, read.shape, 1) // HD
                return jnp.where(lane_head == head, read, total)

            asked_back = lax.fori_loop(0, 2, one_head, jnp.zeros((block, 256), f32))
            adds.go(5)
            bq[rows, :] = score_scale * lax.fori_loop(2, 4, one_head, asked_back)
            adds.go(5)
            bk[rows, :] = score_scale * kacc[pl.ds(block, block), :]
            bv[rows, :] = vacc[pl.ds(block, block), :]
            pkacc[...] += score_scale * kacc[pl.ds(2 * block, NP), :]
            pvacc[...] += vacc[pl.ds(2 * block, NP), :]
            unit = jnp.dot(memory, wk[...], preferred_element_type=f32) * inv
            back = score_scale * kacc[pl.ds(0, block), :]
            bmk[...] = ((back - unit * split_sums(back * unit, ones)) * inv).astype(bf16)
            bmv[...] = vacc[pl.ds(0, block), :].astype(bf16)
            for c in range(2):
                target = part if b == 1 else late
                target[pieces[c], :] = (
                    nt(bmk[pieces[c], :], wk[...]) + nt(bmv[pieces[c], :], wv[...])
                ).astype(bf16)
                if b == 1:
                    sums[c].start()
                else:
                    brec[pieces[c], cols(me)] = sums[c].end().astype(bf16)
                    recs[c].start()
            gmk[...] += tn(memory, bmk[...])
            if b == 1:
                sums[0].middle()
            gmv[...] += tn(memory, bmv[...])
            if b == 1:
                sums[1].middle()
            adds.go(3)
        for s, t in ((gmk, gmk_mid), (gmv, gmv_mid), (bq, bq_mid), (bk, bk_mid), (bv, bv_mid)):
            local.start(s, t, late=True)
        for item in recs:
            item.relay()
        for item in sums:
            item.drain()
        adds.go(2)
        local.finish()

    def remember(
        key, query, pre, act, mis, thr, ble, qpre, qact, one, two, next_one, next_two, cone, ctwo, bble,
        bthr, bqm, mpart, bpre, klow, qlow, kout, qout, vout,
    ):
        loads = [
            local.start(s, t)
            for s, t in (
                (next_two_in, next_two), (qpre_in, qpre), (next_one_in, next_one),
                (queries_in, query), (qact_in, qact), (keys_in, key), (pre_in, pre), (act_in, act),
                (two_in, two), (mis_in, mis), (one_in, one), (thr_in, thr), (ble_in, ble),
            )
        ]
        lates = Scatter(wire, late, whole, l_first, l_passed, l_last, places)
        sums = [Scatter(wire, mpart, rows, m_first, m_passed, m_last, places) for rows in pieces]
        asks = [Scatter(wire, qlow, rows, q_first, q_passed, q_last, places) for rows in blocks]
        tells = [Scatter(wire, klow, rows, k_first, k_passed, k_last, places) for rows in pieces]
        lates.start()
        for item in loads:
            item.wait()
        for item in recs:
            item.end()
            item.drain()
        step_size, keep = rates[1], rates[2]

        def ask_back(c, source, row_start, weight_one, weight_two):
            rows = pl.ds(row_start + c * half, half)
            back = nt(source[pieces[c], :], weight_two[...])
            bqm[pieces[c], :] = (back * slope_of(qpre[rows, :].astype(f32))).astype(bf16)
            qlow[rows, :] = nt(bqm[pieces[c], :], weight_one[...]).astype(bf16)

        for c in range(2):
            ask_back(c, brec, block, next_one, next_two)
            if c == 0:
                lates.middle()
        asks[1].start()
        early[:, cols(me)] = lates.end().astype(bf16)
        early_join.start()
        adds.go(3)

        def first_sums(c, carried):
            rows = pl.ds(pl.multiple_of(c * half, half), half)
            grad = tn(query[blocks[1], rows], bqm[...])
            cone[rows, :] = keep * grad
            next_one[rows, :] = (-step_size * grad).astype(bf16)
            grad = tn(qact[blocks[1], rows], brec[...])
            ctwo[rows, :] = keep * grad
            next_two[rows, :] = (-step_size * grad).astype(bf16)
            return carried

        lax.fori_loop(0, 4, first_sums, 0)
        adds.go(3)
        for c in range(2):
            rows = pieces[c]
            back = jnp.dot(key[rows, :], next_one[...], preferred_element_type=f32)
            bble[rows, :] = back.astype(bf16)
            bthr[rows, :] = (back * slope_of(pre[rows, :].astype(f32))).astype(bf16)
            mpart[rows, :] = (
                jnp.dot(act[rows, :], next_two[...], preferred_element_type=f32)
                + jnp.dot(bthr[rows, :], two[...], preferred_element_type=f32)
            ).astype(bf16)
            sums[c].start()
            if c == 0:
                early_join.relay()
        sums[0].middle()
        asks[1].middle()
        adds.go(3)
        sums[1].middle()
        early_join.end()
        for c in range(2):
            ask_back(c, early, 0, one, two)
        asks[0].start()
        adds.go(2)
        for c in range(2):
            rows = pieces[c]
            back = sums[c].end().astype(bf16)
            index = lax.broadcasted_iota(jnp.int32, (half, 1), 0) + c * half
            scale = jnp.where(index.astype(f32) < rates[0], 1.0 / STRETCH, 0.0)
            bmis[rows, cols(me)] = back
            misses[c].start()
            vout[rows, :] = -(back.astype(f32) * scale)
        local.start(vout, vpart_mid, late=True)

        def second_sums(c, carried):
            rows = pl.ds(pl.multiple_of(c * half, half), half)
            cone[rows, :] += tn(query[blocks[0], rows], bqm[...])
            ctwo[rows, :] += tn(bthr[:, rows], mis[...]) + tn(qact[blocks[0], rows], early[...])
            return carried

        lax.fori_loop(0, 2, second_sums, 0)
        misses[0].relay()
        asks[0].middle()
        adds.go(3)
        lax.fori_loop(2, 4, second_sums, 0)
        misses[1].relay()
        adds.go(2)
        for c in range(2):
            rows = pieces[c]
            misses[c].end()
            misses[c].drain()
            index = lax.broadcasted_iota(jnp.int32, (half, 1), 0) + c * half
            scale = jnp.where(index.astype(f32) < rates[0], 1.0 / STRETCH, 0.0)
            bmis[rows, :] = (bmis[rows, :].astype(f32) * scale).astype(bf16)
            values = pre[rows, :].astype(f32)
            sig = jax.nn.sigmoid(values)
            drop = 1.0 - sig
            slant = sig * drop
            curve = slant * (1.0 + values * drop) + sig * (drop - values * slant)
            back = nt(mis[rows, :], next_two[...]) + nt(bmis[rows, :], two[...])
            bpre[rows, :] = (
                back * (sig * (1.0 + values * drop))
                + bble[rows, :].astype(f32) * thr[rows, :].astype(f32) * curve
            ).astype(bf16)
            klow[rows, :] = (
                nt(ble[rows, :], next_one[...]) + nt(bpre[rows, :], one[...])
            ).astype(bf16)
            tells[c].start()
        adds.go(3)
        tells[0].middle()
        tells[1].middle()

        def last_sums(c, carried):
            rows = pl.ds(pl.multiple_of(c * half, half), half)
            next_one[rows, :] = (cone[rows, :] + tn(key[:, rows], bpre[...])).astype(bf16)
            next_two[rows, :] = (ctwo[rows, :] + tn(act[:, rows], bmis[...])).astype(bf16)
            return carried

        lax.fori_loop(0, 4, last_sums, 0)
        local.start(next_one, gone_mid, late=True)
        local.start(next_two, gtwo_mid, late=True)
        adds.go(3)
        for b in (1, 0):
            qout[blocks[b], :] = asks[b].end()
        local.start(qout, qpart_mid, late=True)
        for c in range(2):
            kout[pieces[c], :] = tells[c].end()
        local.start(kout, kpart_mid, late=True)
        for item in [lates, early_join] + sums + asks + tells:
            item.drain()
        local.finish()
        adds.open(adds.ready + 2 * width // 256)

    def finish(
        x, gain, weights, tq, tk, tv, qpre, kpre, vpre, bq, bk, bv, qpart, kpart, vpart, cot, gmk, gmv, pk,
        bm, extra, packed, normed, part, ig, conv_rows,
    ):
        loads = [
            local.start(s, t)
            for s, t in (
                (cq_in, qpre), (bq_mid, bq), (qpart_mid, qpart), (tq_in, tq), (tk_in, tk),
                (tv_in, tv), (ck_in, kpre),
                (bk_mid, bk), (kpart_mid, kpart), (cv_in, vpre), (bv_mid, bv), (vpart_mid, vpart),
                (x_in, x), (gain_in, gain), (wq_in, weights.at[:, lanes[0]]),
                (wk_in, weights.at[:, lanes[1]]), (wv_in, weights.at[:, lanes[2]]),
                (wg_in, weights.at[:, lanes[3]]), (bgate_mid, cot.at[:, lanes[3]]),
                (gmk_mid, gmk), (gmv_mid, gmv), (pk_in, pk), (bm_mid, bm),
            )
        ]
        adds.go(2)
        for item in loads:
            item.wait()
        ones = head_ones()

        def through_conv(pre, taps, at, back, normal):
            values = pre[...]
            conv = values * taps[pl.ds(0, 1), :]
            for j in range(1, KW):
                conv = conv + moved_down(values, j) * taps[pl.ds(j, 1), :]
            sig = jax.nn.sigmoid(conv)
            if normal:
                act = conv * sig
                inv = lax.rsqrt(split_sums(act * act, ones) + head_floor)
                unit = act * inv
                back = (back - unit * split_sums(back * unit, ones)) * inv
            back = back * (sig * (1.0 + conv * (1.0 - sig)))
            result = back * taps[pl.ds(0, 1), :]
            conv_rows[pl.ds(at, 1), :] = jnp.sum(back * values, axis=0, keepdims=True)
            for j in range(1, KW):
                conv_rows[pl.ds(at + j, 1), :] = jnp.sum(
                    back * moved_down(values, j), axis=0, keepdims=True
                )
                result = result + moved_up(back, j) * taps[pl.ds(j, 1), :]
            return result.astype(bf16)

        conv_rows[...] = jnp.zeros_like(conv_rows)
        cot[:, lanes[0]] = through_conv(qpre, tq, 0, bq[...] + qpart[...], True)
        adds.go(2)
        bk[whole, :] += kpart[...]
        cot[:, lanes[1]] = through_conv(kpre, tk, KW, bk[...], True)
        adds.go(2)
        bv[whole, :] += vpart[...]
        cot[:, lanes[2]] = through_conv(vpre, tv, 2 * KW, bv[...], False)
        adds.go(2)
        rows_of_x = [pl.ds(c * 256, 256) for c in range(tokens // 256)]
        sums = [Scatter(wire, part, rows, t_first, t_passed, t_last, places) for rows in rows_of_x]
        tail_rows = pl.ds(tokens, 16)
        gains = Scatter(wire, part, tail_rows, t_first, t_passed, t_last, places)
        gain_sum = jnp.zeros((1, width), f32)
        for c, rows in enumerate(rows_of_x):
            back = nt(cot[rows, :], weights[...])
            values = x[rows, :].astype(f32)
            inv = lax.rsqrt(jnp.mean(values * values, axis=1, keepdims=True) + epsilon)
            unit = values * inv
            normed[rows, :] = (unit * gain[...]).astype(bf16)
            gain_sum = gain_sum + jnp.sum(back * unit, axis=0, keepdims=True)
            back = back * gain[...]
            part[rows, :] = (
                inv * (back - unit * jnp.mean(back * unit, axis=1, keepdims=True))
            ).astype(bf16)
            sums[c].start()
            if c >= 1:
                sums[c - 1].middle()
            adds.go(2)
        row = lax.broadcasted_iota(jnp.int32, (16, width), 0)
        part[tail_rows, :] = jnp.where(
            row == 0, gain_sum, jnp.where(row == 1, gaintwo[...], 0.0)
        ).astype(bf16)
        gains.start()
        for c in range(width // 256):
            rows = rows_of_x[c]
            packed[rows, :] = tn(normed[:, rows], cot[...]).astype(bf16)
            if c % 2:
                adds.go(2)
        packed[:, lanes[1]] = (packed[:, lanes[1]].astype(f32) + gmk[...]).astype(bf16)
        packed[:, lanes[2]] = (packed[:, lanes[2]].astype(f32) + gmv[...]).astype(bf16)
        local.start(packed, packed_mid, late=True)
        sums[-1].middle()
        gains.middle()
        extra[...] = jnp.zeros_like(extra)
        start = pk[...].astype(f32)
        inv = lax.rsqrt(split_sums(start * start, ones) + head_floor)
        unit = start * inv
        back = pkacc[...]
        top = pl.ds(0, 16)
        extra[top, lanes[0]] = ((back - unit * split_sums(back * unit, ones)) * inv).astype(bf16)
        extra[top, lanes[1]] = pvacc[...].astype(bf16)
        extra[top, lanes[2]] = conv_rows[...].astype(bf16)
        adds.go(2)
        extra[top, lanes[3]] = gains.end().astype(bf16)
        local.start(extra, extra_mid.at[pl.ds(slim, 256)], late=True)
        for c, rows in enumerate(rows_of_x):
            ig[rows, :] = bm[rows, :] + sums[c].end()
        local.start(ig, ig_out, late=True)
        local.finish()
        adds.open(len(chunks))
        for item in sums + [gains]:
            item.drain()

    vm = lambda shape, dtype=None: pltpu.VMEM(shape, bf16 if dtype is None else dtype)
    lw = query_in.shape[1]
    tall, full, flat, weight = (tokens, lw), (tokens, width), (block, width), (width, lw)
    padded, small, square = (KEY_ROWS, lw), (block, lw), one_in.shape
    row = (1, width)
    pl.run_scoped(
        feed,
        vm(full), vm(full), vm(tall, f32), vm(full), vm(row, f32), vm(square), vm(square), vm(square),
        vm(full), vm(full), vm(full), vm(full), vm(full), vm(full), vm(tall), vm(tall, f32),
    )
    pl.run_scoped(
        attend,
        vm(tall), vm(tall), vm(tall), vm(full), vm(weight), vm(weight), vm(tall), vm((lw, width)),
        vm(tall), vm(tall), vm(padded), vm(padded), vm((KEY_ROWS, block), f32), vm(tall),
        vm(tall), vm((NP, lw)), vm((lw, width)), vm(weight, f32), vm(weight, f32), vm(tall, f32), vm(tall, f32),
        vm(tall, f32), vm(padded, f32), vm(padded, f32), vm(small), vm(small), vm(flat),
    )
    pl.run_scoped(
        remember,
        vm(flat), vm(full), vm(flat), vm(flat), vm(flat), vm(flat), vm(flat), vm(full), vm(full),
        vm(square), vm(square), vm(square), vm(square), vm(square, f32), vm(square, f32), vm(flat),
        vm(flat), vm(flat), vm(flat), vm(flat), vm(flat), vm(full), vm(small, f32), vm(tall, f32),
        vm(small, f32),
    )
    pl.run_scoped(
        finish,
        vm(full), vm(row, f32), vm((width, width)), vm((KW, lw), f32), vm((KW, lw), f32),
        vm((KW, lw), f32), vm(tall, f32),
        vm(tall, f32), vm(tall, f32), vm(tall, f32), vm(tall, f32), vm(tall, f32), vm(tall, f32),
        vm(small, f32), vm(small, f32), vm(full), vm(weight, f32), vm(weight, f32), vm((NP, lw)),
        vm(tall, f32), vm((256, width)), vm((width, width)), vm(full),
        vm((tokens + 16, width)), vm(tall, f32), vm((16, 256), f32),
    )
    adds.go()


def run_backward_layer(*arrays):
    query, wo, one, x = arrays[0], arrays[11], arrays[23], arrays[27]
    tokens, width = x.shape
    lw = query.shape[1]
    tall, flat, weight, square = (tokens, lw), (STRETCH, width), (width, lw), (width, width)
    small, extra = (STRETCH, lw), (wo.shape[0] + 256, width)
    count = (6 * width + extra[0]) // 256
    vm = lambda shape, dtype=None: pltpu.VMEM(shape, bf16 if dtype is None else dtype)
    sums = [shaped(square)] * 3 + [shaped(one.shape)] * 2 + [shaped(square), shaped(extra)]
    return call(
        backward_layer, 4,
        [shaped(tall, f32), shaped(tall)] + sums
        + [shaped(square)] * 3
        + [shaped(tall, f32), shaped(one.shape), shaped(one.shape), shaped(square), shaped(extra),
           shaped(tall), shaped(weight, f32), shaped(weight, f32), shaped(tall, f32),
           shaped(tall, f32), shaped(tall, f32), shaped(tall, f32), shaped(small, f32),
           shaped(small, f32)],
        (0,) * (len(arrays) - 1) + (1,),
        [vm(flat), vm(flat), vm((tokens, width)), vm((1, width), f32), vm((NP, lw), f32),
         vm((NP, lw), f32)]
        + scatter_room(STRETCH) * 3 + scatter_room(tokens) + scatter_room(STRETCH)
        + scatter_room(tokens + 16) + wide_room(RING)
        + sems(6 * count + 120)
        + [pltpu.SemaphoreType.DMA((160,)), pltpu.SemaphoreType.DMA((2 * count,))],
        65 << 30, 120 << 20,
    )(*arrays)[:9]


def plain_body(
    layer_input,
    out_grad,
    lengths,
    plan,
    norm1_gain,
    w_query,
    w_key,
    w_value,
    w_gate,
    conv_query,
    conv_key,
    conv_value,
    persist_key,
    persist_value,
    mem_w1,
    mem_w2,
    w_out,
    norm2_gain,
    ffn_gate,
    ffn_up,
    ffn_down,
):
    tokens_here = layer_input.shape[0]
    local_width = w_query.shape[1]
    heads_here = local_width // HD
    blocks = tokens_here // STRETCH
    places = jnp.arange(tokens_here)
    row_mask = (places < lengths[0]).astype(f32)
    block_mask = row_mask.reshape(blocks, STRETCH)
    levels = plan[0].astype(f32)
    column_start = lax.axis_index("narrow") * local_width

    def rows_of(values, b):
        return values[b * STRETCH : (b + 1) * STRETCH]

    whole_x = gather_columns(layer_input).astype(f32)
    whole_dy = gather_columns(out_grad)
    inv_one = lax.rsqrt(jnp.mean(whole_x * whole_x, axis=1, keepdims=True) + epsilon)
    unit_one = whole_x * inv_one
    normed_one = (unit_one * norm1_gain).astype(bf16)
    key_pre = product(normed_one, w_key)
    query_pre = product(normed_one, w_query)
    value_pre = product(normed_one, w_value)
    gate_pre = product(normed_one, w_gate)
    key_conv = causal_conv(key_pre, conv_key)
    query_conv = causal_conv(query_pre, conv_query)
    value_conv = causal_conv(value_pre, conv_value)
    key_unit, key_inv = head_norm(jax.nn.silu(key_conv))
    query_unit, query_inv = head_norm(jax.nn.silu(query_conv))
    query_low = query_unit.astype(bf16)
    key_low = key_unit.astype(bf16)
    value_low = jax.nn.silu(value_conv).astype(bf16)

    weight_one, weight_two = mem_w1.astype(f32), mem_w2.astype(f32)
    moment_one = moment_two = None
    saved = []
    for b in range(blocks):
        step_size, momentum, forget = plan_rates(levels[b])
        kept = {"first": weight_one.astype(bf16), "second": weight_two.astype(bf16)}
        mask_rows = block_mask[b][:, None]
        if b < blocks - 1:
            key_rows = gather_columns(rows_of(key_low, b))
            hidden_pre = product(key_rows, kept["first"])
            hidden_act = jax.nn.silu(hidden_pre).astype(bf16)
            predicted = scatter_columns(product(hidden_act, kept["second"]))
            mismatch_here = (
                (predicted - rows_of(value_low, b).astype(f32)) * (mask_rows / STRETCH)
            ).astype(bf16)
            mismatch = gather_columns(mismatch_here)
        query_rows = gather_columns(rows_of(query_low, b))
        query_mem = product(query_rows, kept["first"])
        query_act = jax.nn.silu(query_mem).astype(bf16)
        retrieved = scatter_columns(product(query_act, kept["second"]))
        kept["recalled"] = gather_columns(retrieved.astype(bf16))
        kept.update(query_rows=query_rows, query_mem=query_mem, query_act=query_act)
        if b < blocks - 1:
            through = inner_right(mismatch, kept["second"])
            blended = (through * silu_grad(hidden_pre)).astype(bf16)
            grad_one = inner_left(key_rows, blended)
            grad_two = inner_left(hidden_act, mismatch)
            if moment_one is None:
                moment_one, moment_two = -step_size * grad_one, -step_size * grad_two
            else:
                moment_one = momentum * moment_one - step_size * grad_one
                moment_two = momentum * moment_two - step_size * grad_two
            weight_one = (1.0 - forget) * weight_one + moment_one
            weight_two = (1.0 - forget) * weight_two + moment_two
            kept.update(
                key_rows=key_rows,
                hidden_pre=hidden_pre,
                hidden_act=hidden_act,
                mismatch=mismatch,
                through=through,
                blended=blended,
            )
        saved.append(kept)

    pers_unit, pers_inv = head_norm(persist_key.astype(f32))
    pers_low = pers_unit.astype(bf16)

    def block_scores(b):
        recalled = saved[b]["recalled"]
        mem_unit, mem_inv = head_norm(product(recalled, w_key))
        mem_value = product(recalled, w_value).astype(bf16)
        all_keys = jnp.concatenate(
            [pers_low, mem_unit.astype(bf16), rows_of(key_low, b)], axis=0
        ).reshape(-1, heads_here, HD)
        all_values = jnp.concatenate(
            [persist_value, mem_value, rows_of(value_low, b)], axis=0
        ).reshape(-1, heads_here, HD)
        query_heads = rows_of(query_low, b).reshape(STRETCH, heads_here, HD)
        scores = score_scale * jnp.einsum(
            "qhd,khd->hqk", query_heads, all_keys, preferred_element_type=f32
        )
        scores = jnp.where(visible(block_mask[b])[None], scores, -1e30)
        return (mem_unit, mem_inv, all_keys, all_values, query_heads, scores)

    mixed_list = []
    for b in range(blocks):
        mem_unit, mem_inv, all_keys, all_values, query_heads, scores = block_scores(b)
        row_peak = jnp.max(scores, axis=2, keepdims=True)
        exponent = jnp.exp(scores - row_peak)
        row_total = jnp.sum(exponent, axis=2, keepdims=True)
        prob_low = (exponent / row_total).astype(bf16)
        mixed_list.append(
            jnp.einsum(
                "hqk,khd->qhd", prob_low, all_values, preferred_element_type=f32
            ).reshape(STRETCH, local_width)
        )
        saved[b].update(
            log_total=row_peak + jnp.log(row_total),
            mem_unit=mem_unit,
            mem_inv=mem_inv,
            all_keys=all_keys,
            all_values=all_values,
            query_heads=query_heads,
        )
    mixed_all = jnp.concatenate(mixed_list, axis=0)
    gate_sig = jax.nn.sigmoid(gate_pre)
    gated = (mixed_all * gate_sig).astype(bf16)
    branch_here = scatter_columns(product(gated, w_out))
    branch_full = gather_columns(branch_here.astype(bf16)).astype(f32)
    middle = whole_x + branch_full
    middle_here = layer_input.astype(f32) + branch_here
    inv_two = lax.rsqrt(jnp.mean(middle * middle, axis=1, keepdims=True) + epsilon)
    unit_two = middle * inv_two
    normed_two = (unit_two * norm2_gain).astype(bf16)
    ffn_pre = product(normed_two, ffn_gate)
    up_pre = product(normed_two, ffn_up)
    ffn_sig = jax.nn.sigmoid(ffn_pre)
    hidden_low = (ffn_pre * ffn_sig * up_pre).astype(bf16)
    back_hidden = inner_right(whole_dy, ffn_down)
    back_up_low = (back_hidden * ffn_pre * ffn_sig).astype(bf16)
    back_ffn_low = (back_hidden * up_pre * silu_grad(ffn_pre)).astype(bf16)
    back_normed_two = inner_right(back_ffn_low, ffn_gate) + inner_right(back_up_low, ffn_up)
    gain_two_part = jnp.sum(back_normed_two * unit_two, axis=0)
    middle_part = norm_back(back_normed_two, unit_two, inv_two, norm2_gain)
    back_middle_here = scatter_columns(middle_part)
    grad_ffn_down = inner_left(hidden_low, whole_dy)
    grad_ffn_gate = inner_left(normed_two, back_ffn_low)
    grad_ffn_up = inner_left(normed_two, back_up_low)
    ffn_here = scatter_columns(product(hidden_low, ffn_down))
    layer_output = (middle_here + ffn_here).astype(bf16)
    back_middle_here = back_middle_here + out_grad.astype(f32)
    back_branch = gather_columns(back_middle_here.astype(bf16))
    grad_ffn_gate, grad_ffn_up, grad_ffn_down = sum_wide(
        [grad_ffn_gate, grad_ffn_up, grad_ffn_down]
    )
    grad_w_out = inner_left(gated, back_branch)
    back_gated = inner_right(back_branch, w_out)
    back_mixed_low = (back_gated * gate_sig).astype(bf16)
    back_gate_low = (back_gated * mixed_all * gate_sig * (1.0 - gate_sig)).astype(bf16)

    back_recalled_parts = []
    mem_key_grad = mem_value_grad = 0.0
    pers_key_acc = grad_persist_value = 0.0
    back_query_att, back_key_att, back_value_att = [], [], []
    for b in range(blocks):
        kept = saved[b]
        scores = score_scale * jnp.einsum(
            "qhd,khd->hqk", kept["query_heads"], kept["all_keys"], preferred_element_type=f32
        )
        scores = jnp.where(visible(block_mask[b])[None], scores, -1e30)
        prob_rows = jnp.exp(scores - kept["log_total"])
        prob_low = prob_rows.astype(bf16)
        back_heads = rows_of(back_mixed_low, b).reshape(STRETCH, heads_here, HD)
        back_all_values = jnp.einsum(
            "hqk,qhd->khd", prob_low, back_heads, preferred_element_type=f32
        )
        back_probs = jnp.einsum(
            "qhd,khd->hqk", back_heads, kept["all_values"], preferred_element_type=f32
        )
        back_scores = (
            prob_rows * (back_probs - jnp.sum(prob_rows * back_probs, axis=2, keepdims=True))
        ).astype(bf16)
        back_query = score_scale * jnp.einsum(
            "hqk,khd->qhd", back_scores, kept["all_keys"], preferred_element_type=f32
        )
        back_all_keys = score_scale * jnp.einsum(
            "hqk,qhd->khd", back_scores, kept["query_heads"], preferred_element_type=f32
        )
        back_all_keys = back_all_keys.reshape(-1, local_width)
        back_all_values = back_all_values.reshape(-1, local_width)
        back_mem_key = head_back(
            back_all_keys[NP : NP + STRETCH], kept["mem_unit"], kept["mem_inv"]
        ).astype(bf16)
        back_mem_value = back_all_values[NP : NP + STRETCH].astype(bf16)
        back_recalled_parts.append(
            inner_right(back_mem_key, w_key) + inner_right(back_mem_value, w_value)
        )
        mem_key_grad = mem_key_grad + inner_left(kept["recalled"], back_mem_key)
        mem_value_grad = mem_value_grad + inner_left(kept["recalled"], back_mem_value)
        pers_key_acc = pers_key_acc + back_all_keys[:NP]
        grad_persist_value = grad_persist_value + back_all_values[:NP]
        back_query_att.append(back_query.reshape(STRETCH, local_width))
        back_key_att.append(back_all_keys[NP + STRETCH :])
        back_value_att.append(back_all_values[NP + STRETCH :])
    grad_persist_key = head_back(pers_key_acc, pers_unit, pers_inv)

    cot_one = cot_two = mom_one = mom_two = None
    key_total, query_total, value_total = [None] * blocks, [None] * blocks, [None] * blocks
    for b in reversed(range(blocks)):
        kept = saved[b]
        step_size, momentum, forget = plan_rates(levels[b])
        first_low, second_low = kept["first"], kept["second"]
        back_recalled = gather_columns(scatter_columns(back_recalled_parts[b]).astype(bf16))
        new_one = new_two = None
        if cot_one is None:
            key_total[b], value_total[b] = back_key_att[b], back_value_att[b]
        else:
            key_rows, hidden_pre = kept["key_rows"], kept["hidden_pre"]
            hidden_slope = silu_grad(hidden_pre)
            total_one = cot_one if mom_one is None else mom_one + cot_one
            total_two = cot_two if mom_two is None else mom_two + cot_two
            back_g1 = (-step_size * total_one).astype(bf16)
            back_g2 = (-step_size * total_two).astype(bf16)
            back_blended = product(key_rows, back_g1)
            back_through = (back_blended * hidden_slope).astype(bf16)
            mismatch_part = product(kept["hidden_act"], back_g2) + product(
                back_through, second_low
            )
            mismatch_low = scatter_columns(mismatch_part).astype(bf16)
            back_mismatch = gather_columns(mismatch_low)
            key_part = inner_right(kept["blended"], back_g1)
            back_hidden_act = inner_right(kept["mismatch"], back_g2)
            extra_pre = back_blended * kept["through"] * silu_curve(hidden_pre)
            new_one = (1.0 - forget) * cot_one
            new_two = (1.0 - forget) * cot_two + inner_left(back_through, kept["mismatch"])
        back_query_act = inner_right(back_recalled, second_low)
        back_query_pre = (back_query_act * silu_grad(kept["query_mem"])).astype(bf16)
        query_part = inner_right(back_query_pre, first_low)
        one_term = inner_left(kept["query_rows"], back_query_pre)
        two_term = inner_left(kept["query_act"], back_recalled)
        new_one = one_term if new_one is None else new_one + one_term
        new_two = two_term if new_two is None else new_two + two_term
        if cot_one is not None:
            scale_rows = (block_mask[b] / STRETCH).astype(bf16)[:, None]
            back_pred = back_mismatch * scale_rows
            value_part = -(mismatch_low.astype(f32) * scale_rows.astype(f32))
            back_hidden_act = back_hidden_act + inner_right(back_pred, second_low)
            new_two = new_two + inner_left(kept["hidden_act"], back_pred)
            back_hidden_pre = (back_hidden_act * hidden_slope + extra_pre).astype(bf16)
            key_part = key_part + inner_right(back_hidden_pre, first_low)
            new_one = new_one + inner_left(key_rows, back_hidden_pre)
            key_total[b] = back_key_att[b] + scatter_columns(key_part)
            value_total[b] = back_value_att[b] + value_part
            mom_one, mom_two = momentum * total_one, momentum * total_two
        query_total[b] = back_query_att[b] + scatter_columns(query_part)
        cot_one, cot_two = new_one, new_two
    grad_mem_w1, grad_mem_w2 = cot_one, cot_two

    back_query_total = jnp.concatenate(query_total, axis=0)
    back_key_total = jnp.concatenate(key_total, axis=0)
    back_value_total = jnp.concatenate(value_total, axis=0)
    query_conv_back = head_back(back_query_total, query_unit, query_inv) * silu_grad(query_conv)
    key_conv_back = head_back(back_key_total, key_unit, key_inv) * silu_grad(key_conv)
    value_conv_back = back_value_total * silu_grad(value_conv)
    query_pre_back, grad_conv_query = conv_back(query_conv_back, query_pre, conv_query)
    key_pre_back, grad_conv_key = conv_back(key_conv_back, key_pre, conv_key)
    value_pre_back, grad_conv_value = conv_back(value_conv_back, value_pre, conv_value)
    query_pre_low = query_pre_back.astype(bf16)
    key_pre_low = key_pre_back.astype(bf16)
    value_pre_low = value_pre_back.astype(bf16)
    back_normed_one = (
        inner_right(back_gate_low, w_gate)
        + inner_right(query_pre_low, w_query)
        + inner_right(key_pre_low, w_key)
        + inner_right(value_pre_low, w_value)
    )
    gain_one_part = jnp.sum(back_normed_one * unit_one, axis=0)
    input_part = norm_back(back_normed_one, unit_one, inv_one, norm1_gain)
    back_input_here = scatter_columns(input_part)
    grad_w_gate = inner_left(normed_one, back_gate_low)
    grad_w_query = inner_left(normed_one, query_pre_low)
    grad_w_key = inner_left(normed_one, key_pre_low) + mem_key_grad
    grad_w_value = inner_left(normed_one, value_pre_low) + mem_value_grad
    input_grad = back_middle_here + back_input_here

    gains = lax.psum(
        jnp.concatenate([gain_one_part, gain_two_part]).astype(bf16), ("narrow", "wide")
    ).astype(f32)
    full_width = whole_x.shape[1]
    grad_norm1_gain = lax.dynamic_slice_in_dim(gains, column_start, local_width, 0)
    grad_norm2_gain = lax.dynamic_slice_in_dim(gains, full_width + column_start, local_width, 0)
    late = (
        grad_w_query, grad_w_key, grad_w_value, grad_w_gate, grad_conv_query, grad_conv_key,
        grad_conv_value, grad_persist_key, grad_persist_value, grad_mem_w1, grad_mem_w2, grad_w_out,
    )
    late, (grad_ffn_gate, grad_ffn_up, grad_ffn_down) = lax.optimization_barrier(
        (tuple(v.astype(bf16) for v in late), (grad_ffn_gate, grad_ffn_up, grad_ffn_down))
    )
    (
        grad_w_query, grad_w_key, grad_w_value, grad_w_gate, grad_conv_query, grad_conv_key,
        grad_conv_value, grad_persist_key, grad_persist_value, grad_mem_w1, grad_mem_w2, grad_w_out,
    ) = sum_wide(late)
    return (
        layer_output,
        input_grad,
        grad_norm1_gain,
        grad_w_query,
        grad_w_key,
        grad_w_value,
        grad_w_gate,
        grad_conv_query,
        grad_conv_key,
        grad_conv_value,
        grad_persist_key,
        grad_persist_value,
        grad_mem_w1,
        grad_mem_w2,
        grad_w_out,
        grad_norm2_gain,
        grad_ffn_gate,
        grad_ffn_up,
        grad_ffn_down,
    )

def linked_body(
    layer_input, out_grad, lengths, plan, norm1_gain, w_query, w_key, w_value, w_gate,
    conv_query, conv_key, conv_value, persist_key, persist_value, mem_w1, mem_w2, w_out,
    norm2_gain, ffn_gate, ffn_up, ffn_down,
):
    step_size, momentum, forget = plan_rates(plan[0, 0].astype(f32))
    rates = jnp.stack([lengths[0].astype(f32), step_size, 1.0 - forget])
    rates = jnp.concatenate([rates, jnp.zeros((5,), f32)])
    (
        low_x, query_pre, key_pre, value_pre, query_low, key_low, value_low, gate_pre, keys, queries, pre,
        act, mis, thr, ble, qpre, qact, rec, next_one, next_two, branch, branch_here, mixed, gated,
        whole_dy,
    ) = run_forward_layer(
        layer_input, out_grad, norm1_gain[None], w_query, w_key, w_value, w_gate, conv_query, conv_key,
        conv_value, persist_key, persist_value, mem_w1, mem_w2, w_out, rates,
    )
    (
        input_grad, layer_output, grad_ffn_gate, grad_ffn_up, grad_ffn_down, grad_mem_w1, grad_mem_w2,
        packed, extra,
    ) = run_backward_layer(
        query_low, key_low, value_low, rec, w_query, w_key, w_value, w_gate, persist_key,
        persist_value, gate_pre, w_out, mixed, gated, keys, queries, pre, act, mis, thr, ble, qpre,
        qact, mem_w1, mem_w2, next_one, next_two, low_x, norm1_gain[None], conv_query, conv_key,
        conv_value, query_pre, key_pre, value_pre, norm2_gain[None], branch, branch_here, whole_dy,
        ffn_gate, ffn_up, ffn_down, rates,
    )
    local_width, start = w_query.shape[1], w_out.shape[0]
    parts = [packed[:, i * local_width : (i + 1) * local_width].astype(f32) for i in range(4)]
    small = extra[start : start + 16].astype(f32)
    pers_key, pers_value, convs, gains = [
        small[:, i * local_width : (i + 1) * local_width] for i in range(4)
    ]
    return (
        layer_output, input_grad, gains[0], *parts, convs[0:4], convs[4:8], convs[8:12], pers_key,
        pers_value, grad_mem_w1.astype(f32), grad_mem_w2.astype(f32), extra[:start].astype(f32),
        gains[1], grad_ffn_gate.astype(f32), grad_ffn_up.astype(f32), grad_ffn_down.astype(f32),
    )


def body(*arrays):
    tokens_here, local_width = arrays[0].shape
    width, units = arrays[14].shape
    linked = (
        (lax.axis_size("wide"), lax.axis_size("narrow")) == (8, 4)
        and local_width == 256
        and tokens_here == 2 * STRETCH
        and (width, units) == (1024, 1024)
        and arrays[18].shape == (1024, 1024)
    )
    return linked_body(*arrays) if linked else plain_body(*arrays)


def solution(mesh):
    return jax.shard_map(
        body,
        mesh=mesh,
        in_specs=(
            P("wide", "narrow"),
            P("wide", "narrow"),
            P("wide"),
            P("wide", None),
            P(),
            P(None, "narrow"),
            P(None, "narrow"),
            P(None, "narrow"),
            P(None, "narrow"),
            P(None, "narrow"),
            P(None, "narrow"),
            P(None, "narrow"),
            P(None, "narrow"),
            P(None, "narrow"),
            P(None, "narrow"),
            P("narrow", None),
            P("narrow", None),
            P(),
            P(None, "narrow"),
            P(None, "narrow"),
            P("narrow", None),
        ),
        out_specs=(
            P("wide", "narrow"),
            P("wide", "narrow"),
            P("narrow"),
            P(None, "narrow"),
            P(None, "narrow"),
            P(None, "narrow"),
            P(None, "narrow"),
            P(None, "narrow"),
            P(None, "narrow"),
            P(None, "narrow"),
            P(None, "narrow"),
            P(None, "narrow"),
            P(None, "narrow"),
            P("narrow", None),
            P("narrow", None),
            P("narrow"),
            P(None, "narrow"),
            P(None, "narrow"),
            P("narrow", None),
        ),
        check_vma=False,
    )
```

```python
import jax
import jax.numpy as jnp
from jax import lax
from jax.experimental import pallas as pl
from jax.experimental.pallas import tpu as pltpu
from jax.sharding import PartitionSpec as P

HD = 64
NP = 16
KW = 4
STRETCH = 512

epsilon = 1e-06
head_floor = 1.0
score_scale = 12.0
bf16 = jnp.bfloat16
f32 = jnp.float32


def product(left_side, right_side):
    return jnp.dot(left_side, right_side, preferred_element_type=f32)


def inner_left(left_side, right_side):
    return lax.dot_general(
        left_side, right_side, (((0,), (0,)), ((), ())), preferred_element_type=f32
    )


def inner_right(left_side, right_side):
    return lax.dot_general(
        left_side, right_side, (((1,), (1,)), ((), ())), preferred_element_type=f32
    )


def silu_grad(values):
    logistic = jax.nn.sigmoid(values)
    return logistic * (1.0 + values * (1.0 - logistic))


def silu_curve(values):
    logistic = jax.nn.sigmoid(values)
    logistic_slope = logistic * (1.0 - logistic)
    return logistic_slope * (1.0 + values * (1.0 - logistic)) + logistic * (
        1.0 - logistic - values * logistic_slope
    )


def plan_rates(level_now):
    return (0.1 * jnp.exp2(level_now), 0.9 - 0.2 * level_now, 0.02 + 0.05 * level_now)


def head_sums(values):
    width = values.shape[1]
    places = jnp.arange(width) // HD
    same_head = (places[:, None] == places[None, :]).astype(f32)
    return jnp.dot(
        values, same_head, precision=lax.Precision.HIGHEST, preferred_element_type=f32
    )


def head_norm(values):
    inv_norm = lax.rsqrt(head_sums(values * values) + head_floor)
    return (values * inv_norm, inv_norm)


def head_back(grad_rows, unit_rows, inv_norm):
    return (grad_rows - unit_rows * head_sums(grad_rows * unit_rows)) * inv_norm


def norm_back(grad_rows, unit_rows, inv_rows, gain_vec):
    scaled = grad_rows * gain_vec
    return inv_rows * (scaled - unit_rows * jnp.mean(scaled * unit_rows, axis=1, keepdims=True))


def shift_down(values, offset):
    return jnp.concatenate(
        [jnp.zeros((offset, values.shape[1]), values.dtype), values[:-offset]], axis=0
    )


def shift_up(values, offset):
    return jnp.concatenate(
        [values[offset:], jnp.zeros((offset, values.shape[1]), values.dtype)], axis=0
    )


def causal_conv(values, conv_taps):
    result = values * conv_taps[0]
    for offset in range(1, KW):
        result = result + shift_down(values, offset) * conv_taps[offset]
    return result


def conv_back(grad_rows, values, conv_taps):
    back_values = grad_rows * conv_taps[0]
    tap_grads = [jnp.sum(grad_rows * values, axis=0)]
    for offset in range(1, KW):
        back_values = back_values + shift_up(grad_rows, offset) * conv_taps[offset]
        tap_grads.append(jnp.sum(grad_rows * shift_down(values, offset), axis=0))
    return (back_values, jnp.stack(tap_grads, axis=0))


def visible(mask_rows):
    row_width = mask_rows.shape[0]
    places = jnp.arange(row_width)
    valid_keys = mask_rows[None, :] > 0.5
    causal = (places[None, :] <= places[:, None]) & valid_keys
    memory_seen = jnp.broadcast_to(valid_keys, (row_width, row_width))
    persistent = jnp.ones((row_width, NP), dtype=bool)
    return jnp.concatenate([persistent, memory_seen, causal], axis=1)


def gather_columns(values):
    return lax.all_gather(values, "narrow", axis=1, tiled=True)


def scatter_columns(values):
    return lax.psum_scatter(
        values.astype(bf16), "narrow", scatter_dimension=1, tiled=True
    ).astype(f32)


def sum_wide(values):
    return [lax.psum(v.astype(bf16), "wide").astype(f32) for v in values]


MESH = pl.DeviceIdType.MESH
ANY = pl.BlockSpec(memory_space=pl.ANY)
SCALARS = pl.BlockSpec(memory_space=pltpu.SMEM)
VMEM_LIMIT = 60 << 20


def group_places():
    me = lax.axis_index("narrow")
    core = lax.rem(me, 2)
    sib = me + 1 - 2 * core
    opp = lax.rem(me + 2, 4)
    diag = lax.rem(sib + 2, 4)
    return me, sib, opp, diag


def cols(index, width=256):
    return pl.ds(pl.multiple_of(index * width, width), width)


def enter_group(sib, opp):
    barrier = pltpu.get_barrier_semaphore()
    for peer in (sib, opp):
        pl.semaphore_signal(barrier, inc=1, device_id={"narrow": peer}, device_id_type=MESH)
    pl.semaphore_wait(barrier, 2)


class Wire:
    def __init__(self, send, recv):
        self.send, self.recv, self.used = send, recv, 0

    def to(self, source, target, device, axis="narrow"):
        k = self.used
        self.used += 1
        return pltpu.make_async_remote_copy(
            src_ref=source,
            dst_ref=target,
            send_sem=self.send.at[k],
            recv_sem=self.recv.at[k],
            device_id={axis: device},
            device_id_type=MESH,
        )


class Local:
    def __init__(self, sems):
        self.sems, self.used, self.open = sems, 0, []

    def start(self, source, target, late=False):
        copy = pltpu.make_async_copy(source, target, self.sems.at[self.used])
        self.used += 1
        copy.start()
        if late:
            self.open.append(copy)
        return copy

    def finish(self):
        for copy in self.open:
            copy.wait()
        self.open = []


class Gather:
    def __init__(self, wire, full, rows, places):
        me, sib, opp, diag = places
        own = full.at[rows, cols(me)]
        passed = full.at[rows, cols(opp)]
        self.far = wire.to(own, own, opp)
        self.near = wire.to(own, own, sib)
        self.relayed = wire.to(passed, passed, sib)

    def start(self):
        self.far.start()
        self.near.start()

    def relay(self):
        self.far.wait_recv()
        self.relayed.start()

    def end(self):
        self.near.wait_recv()
        self.relayed.wait_recv()

    def drain(self):
        self.far.wait_send()
        self.near.wait_send()
        self.relayed.wait_send()


class Scatter:
    def __init__(self, wire, part, rows, first, passed, last, places):
        me, sib, opp, diag = places
        self.part, self.rows, self.places = part, rows, places
        self.first, self.passed, self.last = first, passed, last
        self.pass_on = wire.to(part.at[rows, cols(diag)], first.at[1, rows], sib)
        self.keep = wire.to(part.at[rows, cols(sib)], first.at[0, rows], sib)
        self.far = wire.to(passed.at[rows], last.at[rows], opp)

    def start(self):
        self.pass_on.start()
        self.keep.start()

    def middle(self):
        me, sib, opp, diag = self.places
        self.pass_on.wait_recv()
        self.passed[self.rows] = (
            self.part[self.rows, cols(opp)].astype(f32) + self.first[1, self.rows].astype(f32)
        ).astype(bf16)
        self.far.start()

    def end(self):
        me, sib, opp, diag = self.places
        self.keep.wait_recv()
        near = self.part[self.rows, cols(me)].astype(f32) + self.first[0, self.rows].astype(f32)
        self.far.wait_recv()
        return near + self.last[self.rows].astype(f32)

    def drain(self):
        self.pass_on.wait_send()
        self.keep.wait_send()
        self.far.wait_send()


def scatter_room(rows):
    return [
        pltpu.VMEM((2, rows, 256), bf16),
        pltpu.VMEM((rows, 256), bf16),
        pltpu.VMEM((rows, 256), bf16),
    ]


def sems(count):
    return [
        pltpu.SemaphoreType.DMA((count,)),
        pltpu.SemaphoreType.DMA((count,)),
    ]


def shaped(shape, dtype=None):
    return jax.ShapeDtypeStruct(shape, bf16 if dtype is None else dtype)


def call(kernel, collective, outs, ins, scratch, flops, moved):
    return pl.pallas_call(
        kernel,
        out_shape=outs,
        in_specs=[SCALARS if s else ANY for s in ins],
        out_specs=[ANY] * len(outs),
        scratch_shapes=scratch,
        compiler_params=pltpu.CompilerParams(
            collective_id=collective, has_side_effects=True, vmem_limit_bytes=VMEM_LIMIT
        ),
        cost_estimate=pl.CostEstimate(flops=flops, bytes_accessed=moved, transcendentals=0),
        name=kernel.__name__,
    )


KEY_ROWS = 2 * STRETCH + 128


def silu(values):
    return values * jax.nn.sigmoid(values)


def head_ones():
    left = lax.broadcasted_iota(jnp.int32, (256, 256), 0) // HD
    right = lax.broadcasted_iota(jnp.int32, (256, 256), 1) // HD
    return (left == right).astype(f32).astype(bf16)


def split_sums(values, ones):
    high = values.astype(bf16)
    rest = (values - high.astype(f32)).astype(bf16)
    return jnp.dot(high, ones, preferred_element_type=f32) + jnp.dot(
        rest, ones, preferred_element_type=f32
    )


def head_only(values, head):
    lane_head = lax.broadcasted_iota(jnp.int32, values.shape, 1) // HD
    return jnp.where(lane_head == head, values.astype(f32), 0.0).astype(bf16)


def key_bias(first_row, rows, valid, flipped):
    shape = (KEY_ROWS, rows) if flipped else (rows, KEY_ROWS)
    slot = lax.broadcasted_iota(jnp.int32, shape, 0 if flipped else 1)
    row = lax.broadcasted_iota(jnp.int32, shape, 1 if flipped else 0) + first_row
    memory = (slot < STRETCH) & (slot.astype(f32) < valid)
    place = slot - STRETCH
    causal = (place >= 0) & (place <= row) & (place.astype(f32) < valid) & (slot < 2 * STRETCH)
    persistent = (slot >= 2 * STRETCH) & (slot < 2 * STRETCH + NP)
    return jnp.where(memory | causal | persistent, 0.0, -1e30)


def unit_rows(values, ones):
    wide_values = values.astype(f32)
    return wide_values * lax.rsqrt(split_sums(wide_values * wide_values, ones) + head_floor)


def nt(left, right):
    return lax.dot_general(left, right, (((1,), (1,)), ((), ())), preferred_element_type=f32)


def tn(left, right):
    return lax.dot_general(left, right, (((0,), (0,)), ((), ())), preferred_element_type=f32)


def slope_of(values):
    sig = jax.nn.sigmoid(values)
    return sig * (1.0 + values * (1.0 - sig))


def forward_layer(
    xl_in, dyl_in, gain_in, wq_in, wk_in, wv_in, wg_in, tq_in, tk_in, tv_in, pk_in, pv_in, one_in, two_in,
    wo_in, rates,
    x_out, qconv_out, kconv_out, vconv_out, qlow_out, klow_out, vlow_out, gate_out, key_out, query_out,
    pre_out, act_out, mis_out, thr_out, ble_out, qpre_out, qact_out, rec_out, one_out, two_out,
    branch_out, here_out, mixed_out, gated_out, dy_out, normed_out,
    x, gain, weights, tq, tk, tv, qconv, kconv, vconv, qlow, klow, vlow, gate, pk, key, query, one, two,
    pre, act, part, mis, thr, ble, qpre, qact, qpart, rec, next_one, next_two, wo, keys, values, bias,
    mixed, gated, bpart, branch, here, dy, norms,
    first, passed, last, q_first, q_passed, q_last, b_first, b_passed, b_last,
    send, recv, local_sems,
):
    places = group_places()
    me, sib, opp, diag = places
    wire, local = Wire(send, recv), Local(local_sems)
    half, block = STRETCH // 2, STRETCH
    lanes = [pl.ds(i * 256, 256) for i in range(4)]
    get_x = local.start(xl_in, x.at[:, cols(me)])
    loads = [
        local.start(s, t)
        for s, t in (
            (wq_in, weights.at[:, lanes[0]]), (wk_in, weights.at[:, lanes[1]]),
            (wv_in, weights.at[:, lanes[2]]), (wg_in, weights.at[:, lanes[3]]), (gain_in, gain),
            (tq_in, tq), (tk_in, tk), (tv_in, tv), (pk_in, pk),
            (pv_in, values.at[pl.ds(2 * block, NP)]),
        )
    ]
    later = [
        local.start(s, t)
        for s, t in ((one_in, one), (two_in, two), (wo_in, wo), (dyl_in, dy.at[:, cols(me)]))
    ]
    pieces = [pl.ds(c * half, half) for c in range(4)]
    blocks = [pl.ds(b * block, block) for b in range(2)]
    ones = head_ones()
    for pad in (qconv, kconv, vconv):
        pad[pl.ds(0, 8), :] = jnp.zeros((8, 256), f32)
    keys[pl.ds(2 * block + NP, 128 - NP), :] = jnp.zeros((128 - NP, 256), bf16)
    values[pl.ds(2 * block + NP, 128 - NP), :] = jnp.zeros((128 - NP, 256), bf16)
    enter_group(sib, opp)
    get_x.wait()
    rows_of_x = [Gather(wire, x, rows, places) for rows in pieces]
    key_joins = [Gather(wire, key, rows, places) for rows in pieces[:2]]
    query_joins = [Gather(wire, query, rows, places) for rows in blocks]
    sums = [Scatter(wire, part, rows, first, passed, last, places) for rows in pieces[:2]]
    misses = [Gather(wire, mis, rows, places) for rows in pieces[:2]]
    qsums = [Scatter(wire, qpart, rows, q_first, q_passed, q_last, places) for rows in blocks]
    reads = [Gather(wire, rec, rows, places) for rows in blocks]
    rows_of_dy = [Gather(wire, dy, rows, places) for rows in blocks]
    bsums = [Scatter(wire, bpart, rows, b_first, b_passed, b_last, places) for rows in pieces]
    joins = [Gather(wire, branch, rows, places) for rows in pieces]
    rows_of_x[0].start()
    rows_of_x[1].start()
    for item in loads:
        item.wait()
    keys[pl.ds(2 * block, NP), :] = unit_rows(pk[...], ones).astype(bf16)

    def project(c):
        rows = pieces[c]
        now = x[rows, :].astype(f32)
        inv = lax.rsqrt(jnp.mean(now * now, axis=1, keepdims=True) + epsilon)
        normed = (now * inv * gain[...]).astype(bf16)
        norms[rows, :] = normed
        for at, (pad, low, taps) in enumerate(
            ((kconv, klow, tk), (qconv, qlow, tq), (vconv, vlow, tv))
        ):
            side = lanes[(1, 0, 2)[at]]
            start = 8 + c * half
            pad[pl.ds(start, half), :] = jnp.dot(
                normed, weights[:, side], preferred_element_type=f32
            )
            conv = pad[pl.ds(start, half), :] * taps[pl.ds(0, 1), :]
            for j in range(1, KW):
                conv = conv + pad[pl.ds(start - j, half), :] * taps[pl.ds(j, 1), :]
            conv = conv * jax.nn.sigmoid(conv)
            low[rows, :] = (unit_rows(conv, ones) if at < 2 else conv).astype(bf16)
            if at == 0 and c < 2:
                key[rows, cols(me)] = klow[rows, :]
                key_joins[c].start()
        query[rows, cols(me)] = qlow[rows, :]
        gate[rows, :] = jnp.dot(normed, weights[:, lanes[3]], preferred_element_type=f32).astype(bf16)

    def hide(c):
        rows = pieces[c]
        hidden = jnp.dot(key[rows, :], one[...], preferred_element_type=f32)
        pre[rows, :] = hidden.astype(bf16)
        act[rows, :] = silu(hidden).astype(bf16)
        part[rows, :] = jnp.dot(act[rows, :], two[...], preferred_element_type=f32).astype(bf16)
        sums[c].start()

    def read(b, weight_one, weight_two):
        rows = blocks[b]
        asked = jnp.dot(query[rows, :], weight_one[...], preferred_element_type=f32)
        qpre[rows, :] = asked.astype(bf16)
        qact[rows, :] = silu(asked).astype(bf16)
        qpart[rows, :] = jnp.dot(
            qact[rows, :], weight_two[...], preferred_element_type=f32
        ).astype(bf16)
        qsums[b].start()

    rows_of_x[0].relay()
    rows_of_x[0].end()
    project(0)
    rows_of_x[1].relay()
    rows_of_x[1].end()
    project(1)
    rows_of_x[2].start()
    for item in later:
        item.wait()
    key_joins[0].relay()
    key_joins[0].end()
    hide(0)
    key_joins[1].relay()
    sums[0].middle()
    key_joins[1].end()
    hide(1)
    rows_of_x[2].relay()
    sums[1].middle()
    rows_of_x[3].start()
    query_joins[0].start()
    for c in range(2):
        rows = pieces[c]
        predicted = sums[c].end()
        index = lax.broadcasted_iota(jnp.int32, (half, 1), 0) + c * half
        scale = jnp.where(index.astype(f32) < rates[0], 1.0 / STRETCH, 0.0)
        mis[rows, cols(me)] = ((predicted - vlow[rows, :].astype(f32)) * scale).astype(bf16)
        misses[c].start()
    for s, t in ((key, key_out), (pre, pre_out), (act, act_out)):
        local.start(s, t, late=True)
    rows_of_x[2].end()
    project(2)
    misses[0].relay()
    rows_of_x[3].relay()
    query_joins[0].relay()
    misses[1].relay()
    for c in range(2):
        rows = pieces[c]
        misses[c].end()
        through = nt(mis[rows, :], two[...])
        thr[rows, :] = through.astype(bf16)
        ble[rows, :] = (through * slope_of(pre[rows, :].astype(f32))).astype(bf16)
    rows_of_x[3].end()
    project(3)
    query_joins[1].start()
    for s, t in (
        (x, x_out), (norms, normed_out), (qconv.at[pl.ds(8, 4 * half)], qconv_out), (kconv.at[pl.ds(8, 4 * half)], kconv_out),
        (vconv.at[pl.ds(8, 4 * half)], vconv_out), (qlow, qlow_out), (klow, klow_out),
        (vlow, vlow_out), (gate, gate_out), (mis, mis_out), (thr, thr_out), (ble, ble_out),
    ):
        local.start(s, t, late=True)
    step_size, keep = rates[1], rates[2]

    def update(c, carried):
        rows = pl.ds(pl.multiple_of(c * half, half), half)
        grad = tn(key[:, rows], ble[...])
        next_one[rows, :] = (keep * one[rows, :].astype(f32) - step_size * grad).astype(bf16)
        grad = tn(act[:, rows], mis[...])
        next_two[rows, :] = (keep * two[rows, :].astype(f32) - step_size * grad).astype(bf16)
        return carried

    query_joins[0].end()
    read(0, one, two)
    lax.fori_loop(0, 2, update, 0)
    qsums[0].middle()
    lax.fori_loop(2, 4, update, 0)
    for s, t in ((next_one, one_out), (next_two, two_out)):
        local.start(s, t, late=True)
    query_joins[1].relay()
    rec[blocks[0], cols(me)] = qsums[0].end().astype(bf16)
    reads[0].start()
    query_joins[1].end()
    read(1, next_one, next_two)
    reads[0].relay()
    qsums[1].middle()
    for s, t in ((query, query_out), (qpre, qpre_out), (qact, qact_out)):
        local.start(s, t, late=True)
    reads[0].end()
    rec[blocks[1], cols(me)] = qsums[1].end().astype(bf16)
    reads[1].start()
    rows_of_dy[0].start()

    def settle(c):
        rows = pieces[c]
        total = bsums[c].end()
        here[rows, :] = total
        branch[rows, cols(me)] = total.astype(bf16)
        joins[c].start()

    for c in range(4):
        b, rows = c // 2, pieces[c]
        if c % 2 == 0:
            if b == 1:
                reads[1].end()
            memory = rec[blocks[b], :]
            made = jnp.dot(memory, weights[:, lanes[1]], preferred_element_type=f32)
            keys[pl.ds(0, block), :] = unit_rows(made, ones).astype(bf16)
            values[pl.ds(0, block), :] = jnp.dot(
                memory, weights[:, lanes[2]], preferred_element_type=f32
            ).astype(bf16)
            keys[pl.ds(block, block), :] = klow[blocks[b], :]
            values[pl.ds(block, block), :] = vlow[blocks[b], :]
        bias[...] = key_bias((c % 2) * half, half, rates[0] - float(b * block), False)

        def one_head(head, total):
            asked = head_only(qlow[rows, :], head)
            scores = nt(asked, keys[...])
            chances = jnp.exp(score_scale * scores + bias[...])
            inv = 1.0 / jnp.sum(chances, axis=1, keepdims=True)
            got = jnp.dot((chances * inv).astype(bf16), values[...], preferred_element_type=f32)
            lane_head = lax.broadcasted_iota(jnp.int32, got.shape, 1) // HD
            return jnp.where(lane_head == head, got, total)

        total = lax.fori_loop(0, 4, one_head, jnp.zeros((half, 256), f32))
        mixed[rows, :] = total.astype(bf16)
        gated[rows, :] = (total * jax.nn.sigmoid(gate[rows, :].astype(f32))).astype(bf16)
        bpart[rows, :] = jnp.dot(gated[rows, :], wo[...], preferred_element_type=f32).astype(bf16)
        bsums[c].start()
        if c == 0:
            reads[1].relay()
            rows_of_dy[0].relay()
            bsums[0].middle()
        if c == 1:
            rows_of_dy[1].start()
            bsums[1].middle()
            settle(0)
        if c == 2:
            rows_of_dy[1].relay()
            bsums[2].middle()
            joins[0].relay()
            settle(1)
    for item in rows_of_dy:
        item.end()
    for s, t in ((rec, rec_out), (dy, dy_out), (mixed, mixed_out), (gated, gated_out)):
        local.start(s, t, late=True)
    bsums[3].middle()
    settle(2)
    joins[1].relay()
    settle(3)
    local.start(here, here_out, late=True)
    joins[2].relay()
    joins[3].relay()
    for item in joins:
        item.end()
    local.start(branch, branch_out, late=True)
    for item in (
        rows_of_x + key_joins + query_joins + sums + misses + qsums + reads + rows_of_dy + bsums + joins
    ):
        item.drain()
    local.finish()


def run_forward_layer(*arrays):
    tokens, lw = arrays[0].shape
    square, wo = arrays[12].shape, arrays[14].shape
    width = square[0]
    tall, full, flat, padded = (tokens, lw), (tokens, width), (STRETCH, width), (KEY_ROWS, lw)
    deep = (tokens + 8, lw)
    vm = lambda shape, dtype=None: pltpu.VMEM(shape, bf16 if dtype is None else dtype)
    return call(
        forward_layer, 1,
        [shaped(full), shaped(tall, f32), shaped(tall, f32), shaped(tall, f32)] + [shaped(tall)] * 4
        + [shaped(flat), shaped(full)] + [shaped(flat)] * 5 + [shaped(full)] * 3
        + [shaped(square)] * 2
        + [shaped(full), shaped(tall, f32), shaped(tall), shaped(tall), shaped(full), shaped(full)],
        (0,) * 15 + (1,),
        [vm(full), vm((1, width), f32), vm((width, width)), vm((KW, lw), f32), vm((KW, lw), f32),
         vm((KW, lw), f32), vm(deep, f32), vm(deep, f32), vm(deep, f32), vm(tall), vm(tall), vm(tall),
         vm(tall), vm((NP, lw)), vm(flat), vm(full), vm(square), vm(square)]
        + [vm(flat)] * 6 + [vm(full)] * 4 + [vm(square)] * 2
        + [vm(wo), vm(padded), vm(padded), vm((STRETCH // 2, KEY_ROWS), f32), vm(tall), vm(tall),
           vm(full), vm(full), vm(tall, f32), vm(full), vm(full)]
        + scatter_room(STRETCH) + scatter_room(tokens) + scatter_room(tokens)
        + sems(100) + [pltpu.SemaphoreType.DMA((64,))],
        20 << 30, 40 << 20,
    )(*arrays)


def wide_places():
    at = lax.axis_index("wide")
    bits = (lax.rem(at, 2), lax.rem(lax.div(at, 2), 2), lax.div(at, 4))
    return bits, tuple(at + step * (1 - 2 * bit) for step, bit in zip((1, 2, 4), bits))


def enter_all(sib, opp, wide):
    barrier = pltpu.get_barrier_semaphore()
    for peer in (sib, opp):
        pl.semaphore_signal(barrier, inc=1, device_id={"narrow": peer}, device_id_type=MESH)
    for peer in wide[1]:
        pl.semaphore_signal(barrier, inc=1, device_id={"wide": peer}, device_id_type=MESH)
    pl.semaphore_wait(barrier, 5)


class WideSum:
    ahead = 2
    orders = ((0, 1, 2), (0, 1, 2), (1, 0, 2), (0, 1, 2))

    def __init__(self, wire, copy_sems, wide, chunks, room, ring):
        bits, peers = wide
        self.mine, self.got, self.more, self.rest, self.done = room
        self.items = []
        for k, (source, start, target, goal, rows) in enumerate(chunks):
            slot = k % ring
            order = self.orders[k % len(self.orders)]
            a, b, c = [bits[d] for d in order]
            pa, pb, pc = [peers[d] for d in order]
            off = lambda bit, size: pl.multiple_of(bit * size, size)
            n, h, q = rows // 2, rows // 4, rows // 8
            first = goal + off(a, n)
            second = first + off(b, h)
            third = second + off(c, q)
            spots = [target.at[pl.ds(at, size)] for at, size in ((third, q), (second, h), (first, n))]
            mine, got = self.mine.at[slot, pl.ds(0, n)], self.got.at[slot, pl.ds(0, n)]
            more, rest = self.more.at[slot, pl.ds(0, h)], self.rest.at[slot, pl.ds(0, q)]
            done = self.done.at[slot, pl.ds(0, q)]
            self.items.append({
                "mine": mine, "got": got, "more": more, "rest": rest, "done": done,
                "kept": self.got.at[slot, pl.ds(off(b, h), h)],
                "left": self.more.at[slot, pl.ds(off(c, q), q)],
                "load": pltpu.make_async_copy(
                    source.at[pl.ds(start + off(a, n), n)], mine, copy_sems.at[2 * k]
                ),
                "keep": pltpu.make_async_copy(done, spots[0], copy_sems.at[2 * k + 1]),
                "one": wire.to(source.at[pl.ds(start + off(1 - a, n), n)], got, pa, "wide"),
                "two": wire.to(self.got.at[slot, pl.ds(off(1 - b, h), h)], more, pb, "wide"),
                "three": wire.to(self.more.at[slot, pl.ds(off(1 - c, q), q)], rest, pc, "wide"),
                "four": wire.to(done, spots[0], pc, "wide"),
                "five": wire.to(spots[1], spots[1], pb, "wide"),
                "six": wire.to(spots[2], spots[2], pa, "wide"),
            })
        count = len(self.items)
        self.steps, self.begun, self.ready, self.wanted, self.next = [], 0, count, 0, 0
        stages = ((self.last, 6), (self.halve, 0), (self.again, 1), (self.total, 2), (self.back, 3),
                  (self.most, 4))
        for i in range(count + 6):
            for stage, lag in stages:
                if 0 <= i - lag < count:
                    self.steps.append((stage, i - lag))

    def open(self, ready):
        self.ready = ready
        self.begin(self.wanted)

    def begin(self, upto):
        self.wanted = max(self.wanted, upto)
        while self.begun < min(upto, self.ready, len(self.items)):
            self.items[self.begun]["load"].start()
            self.items[self.begun]["one"].start()
            self.begun += 1

    def halve(self, i):
        item = self.items[i]
        self.begin(i + 1)
        item["one"].wait_recv()
        self.begin(i + 1 + self.ahead)
        item["load"].wait()
        item["got"][...] = (
            item["got"][...].astype(f32) + item["mine"][...].astype(f32)
        ).astype(bf16)
        item["two"].start()

    def again(self, i):
        item = self.items[i]
        item["two"].wait_recv()
        item["more"][...] = (
            item["more"][...].astype(f32) + item["kept"][...].astype(f32)
        ).astype(bf16)
        item["three"].start()

    def total(self, i):
        item = self.items[i]
        item["three"].wait_recv()
        item["done"][...] = (
            item["rest"][...].astype(f32) + item["left"][...].astype(f32)
        ).astype(bf16)
        for name in ("one", "two", "three"):
            item[name].wait_send()
        item["four"].start()
        item["keep"].start()

    def back(self, i):
        item = self.items[i]
        item["four"].wait_recv()
        item["keep"].wait()
        item["four"].wait_send()
        item["five"].start()

    def most(self, i):
        item = self.items[i]
        item["five"].wait_recv()
        item["five"].wait_send()
        item["six"].start()

    def last(self, i):
        self.items[i]["six"].wait_recv()
        self.items[i]["six"].wait_send()

    def go(self, count=None):
        stop = len(self.steps) if count is None else min(self.next + count, len(self.steps))
        while self.next < stop:
            step, i = self.steps[self.next]
            if step == self.halve and i >= self.ready:
                break
            step(i)
            self.next += 1


def wide_room(ring):
    return [
        pltpu.VMEM((ring, rows, 1024), bf16) for rows in (128, 128, 64, 32, 32)
    ]


def moved_down(values, offset):
    row = lax.broadcasted_iota(jnp.int32, values.shape, 0)
    return jnp.where(row < offset, 0.0, pltpu.roll(values, offset, 0))


def moved_up(values, offset):
    rows = values.shape[0]
    row = lax.broadcasted_iota(jnp.int32, values.shape, 0)
    return jnp.where(row >= rows - offset, 0.0, pltpu.roll(values, rows - offset, 0))


RING = 8


def backward_layer(
    query_in, key_in, value_in, rec_in, wq_in, wk_in, wv_in, wg_in, pk_in, pv_in, gate_in, wo_in,
    mixed_in, gated_in, keys_in, queries_in, pre_in, act_in, mis_in, thr_in, ble_in, qpre_in,
    qact_in, one_in, two_in, next_one_in, next_two_in, x_in, gain_in, tq_in, tk_in, tv_in, cq_in, ck_in, cv_in,
    gaintwo_in, branch_in, here_in, dy_in, fgate_in, fup_in, fdown_in, normed_in, rates,
    ig_out, lo_out, gg_out, gu_out, gd_out, gwo_out, gwg_out, gone_out, gtwo_out, packed_out,
    extra_out,
    gg_mid, gu_mid, gd_mid, bm_mid, gwo_mid, gwg_mid, gone_mid, gtwo_mid, packed_mid, extra_mid, bgate_mid, gmk_mid, gmv_mid, bq_mid, bk_mid, bv_mid,
    qpart_mid, kpart_mid, vpart_mid,
    brec, late, bb, gaintwo, pkacc, pvacc,
    a_first, a_passed, a_last, l_first, l_passed, l_last, m_first, m_passed, m_last,
    q_first, q_passed, q_last, k_first, k_passed, k_last, t_first, t_passed, t_last,
    mine, got, more, rest, done, send, recv, local_sems, copy_sems,
):
    places = group_places()
    me, sib, opp, diag = places
    wire, local = Wire(send, recv), Local(local_sems)
    wide = wide_places()
    half, block = STRETCH // 2, STRETCH
    tokens, width = x_in.shape
    slim = wo_in.shape[0]
    chunks = []
    for source, target in (
        (gg_mid, gg_out), (gu_mid, gu_out), (gd_mid, gd_out), (gwo_mid, gwo_out), (gwg_mid, gwg_out),
        (gone_mid, gone_out), (gtwo_mid, gtwo_out), (packed_mid, packed_out),
    ):
        chunks += [(source, i * 256, target, i * 256, 256) for i in range(source.shape[0] // 256)]
    chunks += [(extra_mid, 0, extra_out, 0, 128)]
    adds = WideSum(wire, copy_sems, wide, chunks, (mine, got, more, rest, done), RING)
    adds.ready = 0
    adds.begin(adds.ahead)
    pieces = [pl.ds(c * half, half) for c in range(2)]
    blocks = [pl.ds(b * block, block) for b in range(2)]
    whole = pl.ds(0, block)
    lanes = [pl.ds(i * 256, 256) for i in range(4)]
    early, bmis = bb.at[pl.ds(0, block)], bb.at[pl.ds(block, block)]
    early_join = Gather(wire, early, whole, places)
    misses = [Gather(wire, bmis, rows, places) for rows in pieces]
    recs = [Gather(wire, brec, rows, places) for rows in pieces]

    def feed(
        x, branch, here, dy, gain, gate, up, down, normed, hidden, bup, bffn, part, part_two, out, bm,
        first_sum,
    ):
        loads = [
            local.start(s, t)
            for s, t in (
                (x_in, x), (branch_in, branch), (gaintwo_in, gain), (fgate_in, gate), (fup_in, up),
                (dy_in, dy), (fdown_in, down), (here_in, here),
            )
        ]
        size = 256
        count = tokens // size
        parts_of = [pl.ds(c * size, size) for c in range(count)]
        enter_all(sib, opp, wide)
        for item in loads:
            item.wait()
        sums = [Scatter(wire, part, rows, t_first, t_passed, t_last, places) for rows in parts_of]
        outs = [Scatter(wire, part_two, rows, q_first, q_passed, q_last, places) for rows in parts_of]
        joins = [Gather(wire, bb, rows, places) for rows in parts_of]
        gaintwo[...] = jnp.zeros_like(gaintwo)

        def settle(c):
            rows = parts_of[c]
            back = sums[c].end().astype(bf16).astype(f32) + dy[rows, cols(me)].astype(f32)
            bm[rows, :] = back
            bb[rows, cols(me)] = back.astype(bf16)
            joins[c].start()

        for c in range(count):
            rows = parts_of[c]
            middle = x[rows, :].astype(f32) + branch[rows, :].astype(f32)
            inv = lax.rsqrt(jnp.mean(middle * middle, axis=1, keepdims=True) + epsilon)
            normed[rows, :] = (middle * inv * gain[...]).astype(bf16)
            pre = jnp.dot(normed[rows, :], gate[...], preferred_element_type=f32)
            lift = jnp.dot(normed[rows, :], up[...], preferred_element_type=f32)
            back = nt(dy[rows, :], down[...])
            sig = jax.nn.sigmoid(pre)
            act = pre * sig
            hidden[rows, :] = (act * lift).astype(bf16)
            bup[rows, :] = (back * act).astype(bf16)
            bffn[rows, :] = (back * lift * (sig * (1.0 + pre * (1.0 - sig)))).astype(bf16)

        def grads(left, right, keep, target, k):
            rows = parts_of[k]
            keep[rows, :] = tn(left[:, rows], right[...]).astype(bf16)
            return local.start(keep.at[rows], target.at[rows])

        copies = []
        for c in range(count):
            rows = parts_of[c]
            copies.append(grads(normed, bffn, first_sum, gg_mid, c))
            back = nt(bffn[rows, :], gate[...]) + nt(bup[rows, :], up[...])
            middle = x[rows, :].astype(f32) + branch[rows, :].astype(f32)
            inv = lax.rsqrt(jnp.mean(middle * middle, axis=1, keepdims=True) + epsilon)
            unit = middle * inv
            gaintwo[...] += jnp.sum(back * unit, axis=0, keepdims=True)
            back = back * gain[...]
            part[rows, :] = (
                inv * (back - unit * jnp.mean(back * unit, axis=1, keepdims=True))
            ).astype(bf16)
            sums[c].start()
            copies.pop(0).wait()
            adds.open(adds.ready + 1)
            if c >= 1:
                sums[c - 1].middle()
                adds.go(1)
            if c >= 2:
                settle(c - 2)
            if c >= 3:
                joins[c - 3].relay()
        copies = [grads(normed, bup, gate, gu_mid, 0)]
        sums[3].middle()
        settle(2)
        joins[1].relay()
        for k in range(1, 4):
            copies.append(grads(normed, bup, gate, gu_mid, k))
            if k == 2:
                settle(3)
                joins[2].relay()
        adds.go(1)
        for c, rows in enumerate(parts_of):
            part_two[rows, :] = jnp.dot(
                hidden[rows, :], down[...], preferred_element_type=f32
            ).astype(bf16)
            outs[c].start()
        for item in copies:
            item.wait()
        adds.open(adds.ready + 4)
        joins[3].relay()
        adds.go(2)
        copies = []
        for k in range(4):
            copies.append(grads(hidden, dy, up, gd_mid, k))
            outs[k].middle()
        local.start(bm, bm_mid, late=True)
        adds.go(2)
        for c, rows in enumerate(parts_of):
            total = x[rows, cols(me)].astype(f32) + here[rows, :] + outs[c].end()
            out[rows, :] = total.astype(bf16)
        local.start(out, lo_out, late=True)
        for item in joins:
            item.end()
        for item in copies:
            item.wait()
        adds.open(adds.ready + 4)
        for item in sums + outs + joins:
            item.drain()
        local.finish()

    def attend(
        query, key, value, rec, wk, wv, gate, wo, mixed, gated, keys, values, bias, bmix, bgate,
        pk, gwo, gmk, gmv, bq, bk, bv, kacc, vacc, bmk, bmv, part,
        normed, gwg,
    ):
        loads = [
            local.start(s, t)
            for s, t in (
                (normed_in, normed), (wo_in, wo), (gate_in, gate), (mixed_in, mixed), (gated_in, gated),
                (rec_in, rec), (wk_in, wk), (wv_in, wv), (query_in, query), (key_in, key),
                (value_in, value), (pk_in, pk),
                (pv_in, values.at[pl.ds(2 * block, NP)]),
            )
        ]
        keys[pl.ds(2 * block + NP, 128 - NP), :] = jnp.zeros((128 - NP, 256), bf16)
        values[pl.ds(2 * block + NP, 128 - NP), :] = jnp.zeros((128 - NP, 256), bf16)
        pkacc[...] = jnp.zeros_like(pkacc)
        pvacc[...] = jnp.zeros_like(pvacc)
        gmk[...] = jnp.zeros_like(gmk)
        gmv[...] = jnp.zeros_like(gmv)
        for item in loads:
            item.wait()

        def through_gate(c, carried):
            rows = pl.ds(pl.multiple_of(c * half, half), half)
            back = nt(bb[rows, :], wo[...])
            sig = jax.nn.sigmoid(gate[rows, :].astype(f32))
            bmix[rows, :] = (back * sig).astype(bf16)
            bgate[rows, :] = (back * mixed[rows, :].astype(f32) * sig * (1.0 - sig)).astype(bf16)
            return carried

        lax.fori_loop(0, 4, through_gate, 0)
        local.start(bgate, bgate_mid, late=True)
        gwo[...] = tn(gated[...], bb[...]).astype(bf16)
        out_copy = local.start(gwo, gwo_mid)
        for i, side in enumerate(lanes):
            gwg[:, side] = tn(normed[:, side], bgate[...]).astype(bf16)
        gate_copy = local.start(gwg, gwg_mid)
        ones = head_ones()
        keys[pl.ds(2 * block, NP), :] = unit_rows(pk[...], ones).astype(bf16)
        sums = [Scatter(wire, part, rows, a_first, a_passed, a_last, places) for rows in pieces]
        adds.go(3)
        out_copy.wait()
        gate_copy.wait()
        adds.open(adds.ready + 2)
        for b in (1, 0):
            rows = blocks[b]
            memory = rec[rows, :]
            made = jnp.dot(memory, wk[...], preferred_element_type=f32)
            inv = lax.rsqrt(split_sums(made * made, ones) + head_floor)
            keys[pl.ds(0, block), :] = (made * inv).astype(bf16)
            values[pl.ds(0, block), :] = jnp.dot(
                memory, wv[...], preferred_element_type=f32
            ).astype(bf16)
            keys[pl.ds(block, block), :] = key[rows, :]
            values[pl.ds(block, block), :] = value[rows, :]
            bias[...] = key_bias(0, block, rates[0] - float(b * block), True)
            kacc[...] = jnp.zeros_like(kacc)
            vacc[...] = jnp.zeros_like(vacc)

            def one_head(head, total):
                asked = head_only(query[rows, :], head)
                back = head_only(bmix[rows, :], head)
                weights = jnp.exp(score_scale * nt(keys[...], asked) + bias[...])
                weights = weights * (1.0 / jnp.sum(weights, axis=0, keepdims=True))
                vacc[...] += jnp.dot(weights.astype(bf16), back, preferred_element_type=f32)
                slope = nt(values[...], back)
                slope = (
                    weights * (slope - jnp.sum(weights * slope, axis=0, keepdims=True))
                ).astype(bf16)
                kacc[...] += jnp.dot(slope, asked, preferred_element_type=f32)
                read = tn(slope, keys[...])
                lane_head = lax.broadcasted_iota(jnp.int32, read.shape, 1) // HD
                return jnp.where(lane_head == head, read, total)

            asked_back = lax.fori_loop(0, 2, one_head, jnp.zeros((block, 256), f32))
            adds.go(3)
            bq[rows, :] = score_scale * lax.fori_loop(2, 4, one_head, asked_back)
            adds.go(3)
            bk[rows, :] = score_scale * kacc[pl.ds(block, block), :]
            bv[rows, :] = vacc[pl.ds(block, block), :]
            pkacc[...] += score_scale * kacc[pl.ds(2 * block, NP), :]
            pvacc[...] += vacc[pl.ds(2 * block, NP), :]
            unit = jnp.dot(memory, wk[...], preferred_element_type=f32) * inv
            back = score_scale * kacc[pl.ds(0, block), :]
            bmk[...] = ((back - unit * split_sums(back * unit, ones)) * inv).astype(bf16)
            bmv[...] = vacc[pl.ds(0, block), :].astype(bf16)
            for c in range(2):
                target = part if b == 1 else late
                target[pieces[c], :] = (
                    nt(bmk[pieces[c], :], wk[...]) + nt(bmv[pieces[c], :], wv[...])
                ).astype(bf16)
                if b == 1:
                    sums[c].start()
                else:
                    brec[pieces[c], cols(me)] = sums[c].end().astype(bf16)
                    recs[c].start()
            gmk[...] += tn(memory, bmk[...])
            if b == 1:
                sums[0].middle()
            gmv[...] += tn(memory, bmv[...])
            if b == 1:
                sums[1].middle()
            adds.go(2)
        for s, t in ((gmk, gmk_mid), (gmv, gmv_mid), (bq, bq_mid), (bk, bk_mid), (bv, bv_mid)):
            local.start(s, t, late=True)
        for item in recs:
            item.relay()
        for item in sums:
            item.drain()
        adds.go(2)
        local.finish()

    def remember(
        key, query, pre, act, mis, thr, ble, qpre, qact, one, two, next_one, next_two, cone, ctwo, bble,
        bthr, bqm, mpart, bpre, klow, qlow, kout, qout, vout,
    ):
        loads = [
            local.start(s, t)
            for s, t in (
                (next_two_in, next_two), (qpre_in, qpre), (next_one_in, next_one),
                (queries_in, query), (qact_in, qact), (keys_in, key), (pre_in, pre), (act_in, act),
                (two_in, two), (mis_in, mis), (one_in, one), (thr_in, thr), (ble_in, ble),
            )
        ]
        lates = Scatter(wire, late, whole, l_first, l_passed, l_last, places)
        sums = [Scatter(wire, mpart, rows, m_first, m_passed, m_last, places) for rows in pieces]
        asks = [Scatter(wire, qlow, rows, q_first, q_passed, q_last, places) for rows in blocks]
        tells = [Scatter(wire, klow, rows, k_first, k_passed, k_last, places) for rows in pieces]
        lates.start()
        for item in loads:
            item.wait()
        for item in recs:
            item.end()
            item.drain()
        step_size, keep = rates[1], rates[2]

        def ask_back(c, source, row_start, weight_one, weight_two):
            rows = pl.ds(row_start + c * half, half)
            back = nt(source[pieces[c], :], weight_two[...])
            bqm[pieces[c], :] = (back * slope_of(qpre[rows, :].astype(f32))).astype(bf16)
            qlow[rows, :] = nt(bqm[pieces[c], :], weight_one[...]).astype(bf16)

        for c in range(2):
            ask_back(c, brec, block, next_one, next_two)
            if c == 0:
                lates.middle()
        asks[1].start()
        early[:, cols(me)] = lates.end().astype(bf16)
        early_join.start()
        adds.go(4)

        def first_sums(c, carried):
            rows = pl.ds(pl.multiple_of(c * half, half), half)
            grad = tn(query[blocks[1], rows], bqm[...])
            cone[rows, :] = keep * grad
            next_one[rows, :] = (-step_size * grad).astype(bf16)
            grad = tn(qact[blocks[1], rows], brec[...])
            ctwo[rows, :] = keep * grad
            next_two[rows, :] = (-step_size * grad).astype(bf16)
            return carried

        lax.fori_loop(0, 4, first_sums, 0)
        adds.go(5)
        for c in range(2):
            rows = pieces[c]
            back = jnp.dot(key[rows, :], next_one[...], preferred_element_type=f32)
            bble[rows, :] = back.astype(bf16)
            bthr[rows, :] = (back * slope_of(pre[rows, :].astype(f32))).astype(bf16)
            mpart[rows, :] = (
                jnp.dot(act[rows, :], next_two[...], preferred_element_type=f32)
                + jnp.dot(bthr[rows, :], two[...], preferred_element_type=f32)
            ).astype(bf16)
            sums[c].start()
            if c == 0:
                early_join.relay()
        sums[0].middle()
        asks[1].middle()
        adds.go(5)
        sums[1].middle()
        early_join.end()
        for c in range(2):
            ask_back(c, early, 0, one, two)
        asks[0].start()
        adds.go(4)
        for c in range(2):
            rows = pieces[c]
            back = sums[c].end().astype(bf16)
            index = lax.broadcasted_iota(jnp.int32, (half, 1), 0) + c * half
            scale = jnp.where(index.astype(f32) < rates[0], 1.0 / STRETCH, 0.0)
            bmis[rows, cols(me)] = back
            misses[c].start()
            vout[rows, :] = -(back.astype(f32) * scale)
        local.start(vout, vpart_mid, late=True)

        def second_sums(c, carried):
            rows = pl.ds(pl.multiple_of(c * half, half), half)
            cone[rows, :] += tn(query[blocks[0], rows], bqm[...])
            ctwo[rows, :] += tn(bthr[:, rows], mis[...]) + tn(qact[blocks[0], rows], early[...])
            return carried

        lax.fori_loop(0, 2, second_sums, 0)
        misses[0].relay()
        asks[0].middle()
        adds.go(5)
        lax.fori_loop(2, 4, second_sums, 0)
        misses[1].relay()
        adds.go(4)
        for c in range(2):
            rows = pieces[c]
            misses[c].end()
            misses[c].drain()
            index = lax.broadcasted_iota(jnp.int32, (half, 1), 0) + c * half
            scale = jnp.where(index.astype(f32) < rates[0], 1.0 / STRETCH, 0.0)
            bmis[rows, :] = (bmis[rows, :].astype(f32) * scale).astype(bf16)
            values = pre[rows, :].astype(f32)
            sig = jax.nn.sigmoid(values)
            drop = 1.0 - sig
            slant = sig * drop
            curve = slant * (1.0 + values * drop) + sig * (drop - values * slant)
            back = nt(mis[rows, :], next_two[...]) + nt(bmis[rows, :], two[...])
            bpre[rows, :] = (
                back * (sig * (1.0 + values * drop))
                + bble[rows, :].astype(f32) * thr[rows, :].astype(f32) * curve
            ).astype(bf16)
            klow[rows, :] = (
                nt(ble[rows, :], next_one[...]) + nt(bpre[rows, :], one[...])
            ).astype(bf16)
            tells[c].start()
        adds.go(5)
        tells[0].middle()
        tells[1].middle()

        def last_sums(c, carried):
            rows = pl.ds(pl.multiple_of(c * half, half), half)
            next_one[rows, :] = (cone[rows, :] + tn(key[:, rows], bpre[...])).astype(bf16)
            next_two[rows, :] = (ctwo[rows, :] + tn(act[:, rows], bmis[...])).astype(bf16)
            return carried

        lax.fori_loop(0, 4, last_sums, 0)
        local.start(next_one, gone_mid, late=True)
        local.start(next_two, gtwo_mid, late=True)
        adds.go(5)
        for b in (1, 0):
            qout[blocks[b], :] = asks[b].end()
        local.start(qout, qpart_mid, late=True)
        for c in range(2):
            kout[pieces[c], :] = tells[c].end()
        local.start(kout, kpart_mid, late=True)
        for item in [lates, early_join] + sums + asks + tells:
            item.drain()
        local.finish()
        adds.open(adds.ready + 2 * width // 256)

    def finish(
        x, gain, weights, tq, tk, tv, qpre, kpre, vpre, bq, bk, bv, qpart, kpart, vpart, cot, gmk, gmv, pk,
        bm, extra, packed, normed, part, ig, conv_rows,
    ):
        loads = [
            local.start(s, t)
            for s, t in (
                (cq_in, qpre), (bq_mid, bq), (qpart_mid, qpart), (tq_in, tq), (tk_in, tk),
                (tv_in, tv), (ck_in, kpre),
                (bk_mid, bk), (kpart_mid, kpart), (cv_in, vpre), (bv_mid, bv), (vpart_mid, vpart),
                (x_in, x), (gain_in, gain), (wq_in, weights.at[:, lanes[0]]),
                (wk_in, weights.at[:, lanes[1]]), (wv_in, weights.at[:, lanes[2]]),
                (wg_in, weights.at[:, lanes[3]]), (bgate_mid, cot.at[:, lanes[3]]),
                (gmk_mid, gmk), (gmv_mid, gmv), (pk_in, pk), (bm_mid, bm),
            )
        ]
        adds.go(2)
        for item in loads:
            item.wait()
        ones = head_ones()

        def through_conv(pre, taps, at, back, normal):
            values = pre[...]
            conv = values * taps[pl.ds(0, 1), :]
            for j in range(1, KW):
                conv = conv + moved_down(values, j) * taps[pl.ds(j, 1), :]
            sig = jax.nn.sigmoid(conv)
            if normal:
                act = conv * sig
                inv = lax.rsqrt(split_sums(act * act, ones) + head_floor)
                unit = act * inv
                back = (back - unit * split_sums(back * unit, ones)) * inv
            back = back * (sig * (1.0 + conv * (1.0 - sig)))
            result = back * taps[pl.ds(0, 1), :]
            conv_rows[pl.ds(at, 1), :] = jnp.sum(back * values, axis=0, keepdims=True)
            for j in range(1, KW):
                conv_rows[pl.ds(at + j, 1), :] = jnp.sum(
                    back * moved_down(values, j), axis=0, keepdims=True
                )
                result = result + moved_up(back, j) * taps[pl.ds(j, 1), :]
            return result.astype(bf16)

        conv_rows[...] = jnp.zeros_like(conv_rows)
        cot[:, lanes[0]] = through_conv(qpre, tq, 0, bq[...] + qpart[...], True)
        adds.go(2)
        bk[whole, :] += kpart[...]
        cot[:, lanes[1]] = through_conv(kpre, tk, KW, bk[...], True)
        adds.go(2)
        bv[whole, :] += vpart[...]
        cot[:, lanes[2]] = through_conv(vpre, tv, 2 * KW, bv[...], False)
        adds.go(2)
        rows_of_x = [pl.ds(c * 256, 256) for c in range(tokens // 256)]
        sums = [Scatter(wire, part, rows, t_first, t_passed, t_last, places) for rows in rows_of_x]
        tail_rows = pl.ds(tokens, 16)
        gains = Scatter(wire, part, tail_rows, t_first, t_passed, t_last, places)
        gain_sum = jnp.zeros((1, width), f32)
        for c, rows in enumerate(rows_of_x):
            back = nt(cot[rows, :], weights[...])
            values = x[rows, :].astype(f32)
            inv = lax.rsqrt(jnp.mean(values * values, axis=1, keepdims=True) + epsilon)
            unit = values * inv
            normed[rows, :] = (unit * gain[...]).astype(bf16)
            gain_sum = gain_sum + jnp.sum(back * unit, axis=0, keepdims=True)
            back = back * gain[...]
            part[rows, :] = (
                inv * (back - unit * jnp.mean(back * unit, axis=1, keepdims=True))
            ).astype(bf16)
            sums[c].start()
            if c >= 1:
                sums[c - 1].middle()
            adds.go(2)
        row = lax.broadcasted_iota(jnp.int32, (16, width), 0)
        part[tail_rows, :] = jnp.where(
            row == 0, gain_sum, jnp.where(row == 1, gaintwo[...], 0.0)
        ).astype(bf16)
        gains.start()
        for c in range(width // 256):
            made = tn(normed[:, rows_of_x[c]], cot[:, pl.ds(0, 768)])
            packed[pl.ds(0, 256), lanes[c]] = made[:, 0:256].astype(bf16)
            packed[pl.ds(256, 256), lanes[c]] = (made[:, 256:512] + gmk[rows_of_x[c], :]).astype(bf16)
            packed[pl.ds(512, 256), lanes[c]] = (made[:, 512:768] + gmv[rows_of_x[c], :]).astype(bf16)
            if c % 2:
                adds.go(2)
        pack_copy = local.start(packed, packed_mid)
        sums[-1].middle()
        gains.middle()
        extra[...] = jnp.zeros_like(extra)
        start = pk[...].astype(f32)
        inv = lax.rsqrt(split_sums(start * start, ones) + head_floor)
        unit = start * inv
        back = pkacc[...]
        top = pl.ds(0, 16)
        extra[top, lanes[0]] = ((back - unit * split_sums(back * unit, ones)) * inv).astype(bf16)
        extra[top, lanes[1]] = pvacc[...].astype(bf16)
        extra[top, lanes[2]] = conv_rows[...].astype(bf16)
        pack_copy.wait()
        adds.open(adds.ready + 3)
        adds.go(2)
        extra[top, lanes[3]] = gains.end().astype(bf16)
        local.start(extra, extra_mid, late=True)
        for c, rows in enumerate(rows_of_x):
            ig[rows, :] = bm[rows, :] + sums[c].end()
        local.start(ig, ig_out, late=True)
        local.finish()
        adds.open(len(chunks))
        for item in sums + [gains]:
            item.drain()

    vm = lambda shape, dtype=None: pltpu.VMEM(shape, bf16 if dtype is None else dtype)
    lw = query_in.shape[1]
    tall, full, flat, weight = (tokens, lw), (tokens, width), (block, width), (width, lw)
    padded, small, square = (KEY_ROWS, lw), (block, lw), one_in.shape
    row = (1, width)
    pl.run_scoped(
        feed,
        vm(full), vm(full), vm(tall, f32), vm(full), vm(row, f32), vm(square), vm(square), vm(square),
        vm(full), vm(full), vm(full), vm(full), vm(full), vm(full), vm(tall), vm(tall, f32), vm(square),
    )
    pl.run_scoped(
        attend,
        vm(tall), vm(tall), vm(tall), vm(full), vm(weight), vm(weight), vm(tall), vm((lw, width)),
        vm(tall), vm(tall), vm(padded), vm(padded), vm((KEY_ROWS, block), f32), vm(tall),
        vm(tall), vm((NP, lw)), vm((lw, width)), vm(weight, f32), vm(weight, f32), vm(tall, f32), vm(tall, f32),
        vm(tall, f32), vm(padded, f32), vm(padded, f32), vm(small), vm(small), vm(flat), vm(full), vm((256, width)),
    )
    pl.run_scoped(
        remember,
        vm(flat), vm(full), vm(flat), vm(flat), vm(flat), vm(flat), vm(flat), vm(full), vm(full),
        vm(square), vm(square), vm(square), vm(square), vm(square, f32), vm(square, f32), vm(flat),
        vm(flat), vm(flat), vm(flat), vm(flat), vm(flat), vm(full), vm(small, f32), vm(tall, f32),
        vm(small, f32),
    )
    pl.run_scoped(
        finish,
        vm(full), vm(row, f32), vm((width, width)), vm((KW, lw), f32), vm((KW, lw), f32),
        vm((KW, lw), f32), vm(tall, f32),
        vm(tall, f32), vm(tall, f32), vm(tall, f32), vm(tall, f32), vm(tall, f32), vm(tall, f32),
        vm(small, f32), vm(small, f32), vm(full), vm(weight, f32), vm(weight, f32), vm((NP, lw)),
        vm(tall, f32), vm((128, width)), vm((768, width)), vm(full),
        vm((tokens + 16, width)), vm(tall, f32), vm((16, 256), f32),
    )
    adds.go()


def run_backward_layer(*arrays):
    query, wo, one, x = arrays[0], arrays[11], arrays[23], arrays[27]
    tokens, width = x.shape
    lw = query.shape[1]
    tall, flat, weight, square = (tokens, lw), (STRETCH, width), (width, lw), (width, width)
    small, packed, extra = (STRETCH, lw), (3 * lw, width), (128, width)
    count = (5 * width + 5 * lw) // 256 + 1
    vm = lambda shape, dtype=None: pltpu.VMEM(shape, bf16 if dtype is None else dtype)
    sums = [shaped(square)] * 3 + [shaped((lw, width))] * 2 + [shaped(one.shape)] * 2
    sums += [shaped(packed), shaped(extra)]
    return call(
        backward_layer, 4,
        [shaped(tall, f32), shaped(tall)] + sums
        + [shaped(square)] * 3 + [shaped(tall, f32)] + sums[3:]
        + [shaped(tall), shaped(weight, f32), shaped(weight, f32), shaped(tall, f32),
           shaped(tall, f32), shaped(tall, f32), shaped(tall, f32), shaped(small, f32),
           shaped(small, f32)],
        (0,) * (len(arrays) - 1) + (1,),
        [vm(flat), vm(flat), vm((tokens, width)), vm((1, width), f32), vm((NP, lw), f32),
         vm((NP, lw), f32)]
        + scatter_room(STRETCH) * 3 + scatter_room(tokens) + scatter_room(STRETCH)
        + scatter_room(tokens + 16) + wide_room(RING)
        + sems(6 * count + 120)
        + [pltpu.SemaphoreType.DMA((160,)), pltpu.SemaphoreType.DMA((2 * count,))],
        65 << 30, 120 << 20,
    )(*arrays)[:11]


def widen(*refs):
    count = len(refs) // 2
    for source, target in zip(refs[:count], refs[count:]):
        target[...] = source[...].astype(target.dtype)


def run_widen(flat, quarter, same):
    steps = 8
    ins, outs, shapes = [], [], []
    for v in flat:
        spec = pl.BlockSpec((v.shape[0] // steps, v.shape[1]), lambda i: (i, 0))
        ins.append(spec)
        outs.append(spec)
        shapes.append(shaped(v.shape, f32))
    for v, place in quarter:
        ins.append(pl.BlockSpec((128, 256), lambda i, place=place: (2 * place + i % 2, i // 2)))
        outs.append(pl.BlockSpec((128, 256), lambda i: (i, 0)))
        shapes.append(shaped((1024, 256), f32))
    for v in same:
        spec = pl.BlockSpec((v.shape[0] // steps, v.shape[1]), lambda i: (i, 0))
        ins.append(spec)
        outs.append(spec)
        shapes.append(shaped(v.shape, v.dtype))
    return pl.pallas_call(
        widen, out_shape=shapes, grid=(steps,), in_specs=ins, out_specs=outs,
        compiler_params=pltpu.CompilerParams(vmem_limit_bytes=VMEM_LIMIT), name="widen",
    )(*flat, *(v for v, place in quarter), *same)


def plain_body(
    layer_input,
    out_grad,
    lengths,
    plan,
    norm1_gain,
    w_query,
    w_key,
    w_value,
    w_gate,
    conv_query,
    conv_key,
    conv_value,
    persist_key,
    persist_value,
    mem_w1,
    mem_w2,
    w_out,
    norm2_gain,
    ffn_gate,
    ffn_up,
    ffn_down,
):
    tokens_here = layer_input.shape[0]
    local_width = w_query.shape[1]
    heads_here = local_width // HD
    blocks = tokens_here // STRETCH
    places = jnp.arange(tokens_here)
    row_mask = (places < lengths[0]).astype(f32)
    block_mask = row_mask.reshape(blocks, STRETCH)
    levels = plan[0].astype(f32)
    column_start = lax.axis_index("narrow") * local_width

    def rows_of(values, b):
        return values[b * STRETCH : (b + 1) * STRETCH]

    whole_x = gather_columns(layer_input).astype(f32)
    whole_dy = gather_columns(out_grad)
    inv_one = lax.rsqrt(jnp.mean(whole_x * whole_x, axis=1, keepdims=True) + epsilon)
    unit_one = whole_x * inv_one
    normed_one = (unit_one * norm1_gain).astype(bf16)
    key_pre = product(normed_one, w_key)
    query_pre = product(normed_one, w_query)
    value_pre = product(normed_one, w_value)
    gate_pre = product(normed_one, w_gate)
    key_conv = causal_conv(key_pre, conv_key)
    query_conv = causal_conv(query_pre, conv_query)
    value_conv = causal_conv(value_pre, conv_value)
    key_unit, key_inv = head_norm(jax.nn.silu(key_conv))
    query_unit, query_inv = head_norm(jax.nn.silu(query_conv))
    query_low = query_unit.astype(bf16)
    key_low = key_unit.astype(bf16)
    value_low = jax.nn.silu(value_conv).astype(bf16)

    weight_one, weight_two = mem_w1.astype(f32), mem_w2.astype(f32)
    moment_one = moment_two = None
    saved = []
    for b in range(blocks):
        step_size, momentum, forget = plan_rates(levels[b])
        kept = {"first": weight_one.astype(bf16), "second": weight_two.astype(bf16)}
        mask_rows = block_mask[b][:, None]
        if b < blocks - 1:
            key_rows = gather_columns(rows_of(key_low, b))
            hidden_pre = product(key_rows, kept["first"])
            hidden_act = jax.nn.silu(hidden_pre).astype(bf16)
            predicted = scatter_columns(product(hidden_act, kept["second"]))
            mismatch_here = (
                (predicted - rows_of(value_low, b).astype(f32)) * (mask_rows / STRETCH)
            ).astype(bf16)
            mismatch = gather_columns(mismatch_here)
        query_rows = gather_columns(rows_of(query_low, b))
        query_mem = product(query_rows, kept["first"])
        query_act = jax.nn.silu(query_mem).astype(bf16)
        retrieved = scatter_columns(product(query_act, kept["second"]))
        kept["recalled"] = gather_columns(retrieved.astype(bf16))
        kept.update(query_rows=query_rows, query_mem=query_mem, query_act=query_act)
        if b < blocks - 1:
            through = inner_right(mismatch, kept["second"])
            blended = (through * silu_grad(hidden_pre)).astype(bf16)
            grad_one = inner_left(key_rows, blended)
            grad_two = inner_left(hidden_act, mismatch)
            if moment_one is None:
                moment_one, moment_two = -step_size * grad_one, -step_size * grad_two
            else:
                moment_one = momentum * moment_one - step_size * grad_one
                moment_two = momentum * moment_two - step_size * grad_two
            weight_one = (1.0 - forget) * weight_one + moment_one
            weight_two = (1.0 - forget) * weight_two + moment_two
            kept.update(
                key_rows=key_rows,
                hidden_pre=hidden_pre,
                hidden_act=hidden_act,
                mismatch=mismatch,
                through=through,
                blended=blended,
            )
        saved.append(kept)

    pers_unit, pers_inv = head_norm(persist_key.astype(f32))
    pers_low = pers_unit.astype(bf16)

    def block_scores(b):
        recalled = saved[b]["recalled"]
        mem_unit, mem_inv = head_norm(product(recalled, w_key))
        mem_value = product(recalled, w_value).astype(bf16)
        all_keys = jnp.concatenate(
            [pers_low, mem_unit.astype(bf16), rows_of(key_low, b)], axis=0
        ).reshape(-1, heads_here, HD)
        all_values = jnp.concatenate(
            [persist_value, mem_value, rows_of(value_low, b)], axis=0
        ).reshape(-1, heads_here, HD)
        query_heads = rows_of(query_low, b).reshape(STRETCH, heads_here, HD)
        scores = score_scale * jnp.einsum(
            "qhd,khd->hqk", query_heads, all_keys, preferred_element_type=f32
        )
        scores = jnp.where(visible(block_mask[b])[None], scores, -1e30)
        return (mem_unit, mem_inv, all_keys, all_values, query_heads, scores)

    mixed_list = []
    for b in range(blocks):
        mem_unit, mem_inv, all_keys, all_values, query_heads, scores = block_scores(b)
        row_peak = jnp.max(scores, axis=2, keepdims=True)
        exponent = jnp.exp(scores - row_peak)
        row_total = jnp.sum(exponent, axis=2, keepdims=True)
        prob_low = (exponent / row_total).astype(bf16)
        mixed_list.append(
            jnp.einsum(
                "hqk,khd->qhd", prob_low, all_values, preferred_element_type=f32
            ).reshape(STRETCH, local_width)
        )
        saved[b].update(
            log_total=row_peak + jnp.log(row_total),
            mem_unit=mem_unit,
            mem_inv=mem_inv,
            all_keys=all_keys,
            all_values=all_values,
            query_heads=query_heads,
        )
    mixed_all = jnp.concatenate(mixed_list, axis=0)
    gate_sig = jax.nn.sigmoid(gate_pre)
    gated = (mixed_all * gate_sig).astype(bf16)
    branch_here = scatter_columns(product(gated, w_out))
    branch_full = gather_columns(branch_here.astype(bf16)).astype(f32)
    middle = whole_x + branch_full
    middle_here = layer_input.astype(f32) + branch_here
    inv_two = lax.rsqrt(jnp.mean(middle * middle, axis=1, keepdims=True) + epsilon)
    unit_two = middle * inv_two
    normed_two = (unit_two * norm2_gain).astype(bf16)
    ffn_pre = product(normed_two, ffn_gate)
    up_pre = product(normed_two, ffn_up)
    ffn_sig = jax.nn.sigmoid(ffn_pre)
    hidden_low = (ffn_pre * ffn_sig * up_pre).astype(bf16)
    back_hidden = inner_right(whole_dy, ffn_down)
    back_up_low = (back_hidden * ffn_pre * ffn_sig).astype(bf16)
    back_ffn_low = (back_hidden * up_pre * silu_grad(ffn_pre)).astype(bf16)
    back_normed_two = inner_right(back_ffn_low, ffn_gate) + inner_right(back_up_low, ffn_up)
    gain_two_part = jnp.sum(back_normed_two * unit_two, axis=0)
    middle_part = norm_back(back_normed_two, unit_two, inv_two, norm2_gain)
    back_middle_here = scatter_columns(middle_part)
    grad_ffn_down = inner_left(hidden_low, whole_dy)
    grad_ffn_gate = inner_left(normed_two, back_ffn_low)
    grad_ffn_up = inner_left(normed_two, back_up_low)
    ffn_here = scatter_columns(product(hidden_low, ffn_down))
    layer_output = (middle_here + ffn_here).astype(bf16)
    back_middle_here = back_middle_here + out_grad.astype(f32)
    back_branch = gather_columns(back_middle_here.astype(bf16))
    grad_ffn_gate, grad_ffn_up, grad_ffn_down = sum_wide(
        [grad_ffn_gate, grad_ffn_up, grad_ffn_down]
    )
    grad_w_out = inner_left(gated, back_branch)
    back_gated = inner_right(back_branch, w_out)
    back_mixed_low = (back_gated * gate_sig).astype(bf16)
    back_gate_low = (back_gated * mixed_all * gate_sig * (1.0 - gate_sig)).astype(bf16)

    back_recalled_parts = []
    mem_key_grad = mem_value_grad = 0.0
    pers_key_acc = grad_persist_value = 0.0
    back_query_att, back_key_att, back_value_att = [], [], []
    for b in range(blocks):
        kept = saved[b]
        scores = score_scale * jnp.einsum(
            "qhd,khd->hqk", kept["query_heads"], kept["all_keys"], preferred_element_type=f32
        )
        scores = jnp.where(visible(block_mask[b])[None], scores, -1e30)
        prob_rows = jnp.exp(scores - kept["log_total"])
        prob_low = prob_rows.astype(bf16)
        back_heads = rows_of(back_mixed_low, b).reshape(STRETCH, heads_here, HD)
        back_all_values = jnp.einsum(
            "hqk,qhd->khd", prob_low, back_heads, preferred_element_type=f32
        )
        back_probs = jnp.einsum(
            "qhd,khd->hqk", back_heads, kept["all_values"], preferred_element_type=f32
        )
        back_scores = (
            prob_rows * (back_probs - jnp.sum(prob_rows * back_probs, axis=2, keepdims=True))
        ).astype(bf16)
        back_query = score_scale * jnp.einsum(
            "hqk,khd->qhd", back_scores, kept["all_keys"], preferred_element_type=f32
        )
        back_all_keys = score_scale * jnp.einsum(
            "hqk,qhd->khd", back_scores, kept["query_heads"], preferred_element_type=f32
        )
        back_all_keys = back_all_keys.reshape(-1, local_width)
        back_all_values = back_all_values.reshape(-1, local_width)
        back_mem_key = head_back(
            back_all_keys[NP : NP + STRETCH], kept["mem_unit"], kept["mem_inv"]
        ).astype(bf16)
        back_mem_value = back_all_values[NP : NP + STRETCH].astype(bf16)
        back_recalled_parts.append(
            inner_right(back_mem_key, w_key) + inner_right(back_mem_value, w_value)
        )
        mem_key_grad = mem_key_grad + inner_left(kept["recalled"], back_mem_key)
        mem_value_grad = mem_value_grad + inner_left(kept["recalled"], back_mem_value)
        pers_key_acc = pers_key_acc + back_all_keys[:NP]
        grad_persist_value = grad_persist_value + back_all_values[:NP]
        back_query_att.append(back_query.reshape(STRETCH, local_width))
        back_key_att.append(back_all_keys[NP + STRETCH :])
        back_value_att.append(back_all_values[NP + STRETCH :])
    grad_persist_key = head_back(pers_key_acc, pers_unit, pers_inv)

    cot_one = cot_two = mom_one = mom_two = None
    key_total, query_total, value_total = [None] * blocks, [None] * blocks, [None] * blocks
    for b in reversed(range(blocks)):
        kept = saved[b]
        step_size, momentum, forget = plan_rates(levels[b])
        first_low, second_low = kept["first"], kept["second"]
        back_recalled = gather_columns(scatter_columns(back_recalled_parts[b]).astype(bf16))
        new_one = new_two = None
        if cot_one is None:
            key_total[b], value_total[b] = back_key_att[b], back_value_att[b]
        else:
            key_rows, hidden_pre = kept["key_rows"], kept["hidden_pre"]
            hidden_slope = silu_grad(hidden_pre)
            total_one = cot_one if mom_one is None else mom_one + cot_one
            total_two = cot_two if mom_two is None else mom_two + cot_two
            back_g1 = (-step_size * total_one).astype(bf16)
            back_g2 = (-step_size * total_two).astype(bf16)
            back_blended = product(key_rows, back_g1)
            back_through = (back_blended * hidden_slope).astype(bf16)
            mismatch_part = product(kept["hidden_act"], back_g2) + product(
                back_through, second_low
            )
            mismatch_low = scatter_columns(mismatch_part).astype(bf16)
            back_mismatch = gather_columns(mismatch_low)
            key_part = inner_right(kept["blended"], back_g1)
            back_hidden_act = inner_right(kept["mismatch"], back_g2)
            extra_pre = back_blended * kept["through"] * silu_curve(hidden_pre)
            new_one = (1.0 - forget) * cot_one
            new_two = (1.0 - forget) * cot_two + inner_left(back_through, kept["mismatch"])
        back_query_act = inner_right(back_recalled, second_low)
        back_query_pre = (back_query_act * silu_grad(kept["query_mem"])).astype(bf16)
        query_part = inner_right(back_query_pre, first_low)
        one_term = inner_left(kept["query_rows"], back_query_pre)
        two_term = inner_left(kept["query_act"], back_recalled)
        new_one = one_term if new_one is None else new_one + one_term
        new_two = two_term if new_two is None else new_two + two_term
        if cot_one is not None:
            scale_rows = (block_mask[b] / STRETCH).astype(bf16)[:, None]
            back_pred = back_mismatch * scale_rows
            value_part = -(mismatch_low.astype(f32) * scale_rows.astype(f32))
            back_hidden_act = back_hidden_act + inner_right(back_pred, second_low)
            new_two = new_two + inner_left(kept["hidden_act"], back_pred)
            back_hidden_pre = (back_hidden_act * hidden_slope + extra_pre).astype(bf16)
            key_part = key_part + inner_right(back_hidden_pre, first_low)
            new_one = new_one + inner_left(key_rows, back_hidden_pre)
            key_total[b] = back_key_att[b] + scatter_columns(key_part)
            value_total[b] = back_value_att[b] + value_part
            mom_one, mom_two = momentum * total_one, momentum * total_two
        query_total[b] = back_query_att[b] + scatter_columns(query_part)
        cot_one, cot_two = new_one, new_two
    grad_mem_w1, grad_mem_w2 = cot_one, cot_two

    back_query_total = jnp.concatenate(query_total, axis=0)
    back_key_total = jnp.concatenate(key_total, axis=0)
    back_value_total = jnp.concatenate(value_total, axis=0)
    query_conv_back = head_back(back_query_total, query_unit, query_inv) * silu_grad(query_conv)
    key_conv_back = head_back(back_key_total, key_unit, key_inv) * silu_grad(key_conv)
    value_conv_back = back_value_total * silu_grad(value_conv)
    query_pre_back, grad_conv_query = conv_back(query_conv_back, query_pre, conv_query)
    key_pre_back, grad_conv_key = conv_back(key_conv_back, key_pre, conv_key)
    value_pre_back, grad_conv_value = conv_back(value_conv_back, value_pre, conv_value)
    query_pre_low = query_pre_back.astype(bf16)
    key_pre_low = key_pre_back.astype(bf16)
    value_pre_low = value_pre_back.astype(bf16)
    back_normed_one = (
        inner_right(back_gate_low, w_gate)
        + inner_right(query_pre_low, w_query)
        + inner_right(key_pre_low, w_key)
        + inner_right(value_pre_low, w_value)
    )
    gain_one_part = jnp.sum(back_normed_one * unit_one, axis=0)
    input_part = norm_back(back_normed_one, unit_one, inv_one, norm1_gain)
    back_input_here = scatter_columns(input_part)
    grad_w_gate = inner_left(normed_one, back_gate_low)
    grad_w_query = inner_left(normed_one, query_pre_low)
    grad_w_key = inner_left(normed_one, key_pre_low) + mem_key_grad
    grad_w_value = inner_left(normed_one, value_pre_low) + mem_value_grad
    input_grad = back_middle_here + back_input_here

    gains = lax.psum(
        jnp.concatenate([gain_one_part, gain_two_part]).astype(bf16), ("narrow", "wide")
    ).astype(f32)
    full_width = whole_x.shape[1]
    grad_norm1_gain = lax.dynamic_slice_in_dim(gains, column_start, local_width, 0)
    grad_norm2_gain = lax.dynamic_slice_in_dim(gains, full_width + column_start, local_width, 0)
    late = (
        grad_w_query, grad_w_key, grad_w_value, grad_w_gate, grad_conv_query, grad_conv_key,
        grad_conv_value, grad_persist_key, grad_persist_value, grad_mem_w1, grad_mem_w2, grad_w_out,
    )
    late, (grad_ffn_gate, grad_ffn_up, grad_ffn_down) = lax.optimization_barrier(
        (tuple(v.astype(bf16) for v in late), (grad_ffn_gate, grad_ffn_up, grad_ffn_down))
    )
    (
        grad_w_query, grad_w_key, grad_w_value, grad_w_gate, grad_conv_query, grad_conv_key,
        grad_conv_value, grad_persist_key, grad_persist_value, grad_mem_w1, grad_mem_w2, grad_w_out,
    ) = sum_wide(late)
    return (
        layer_output,
        input_grad,
        grad_norm1_gain,
        grad_w_query,
        grad_w_key,
        grad_w_value,
        grad_w_gate,
        grad_conv_query,
        grad_conv_key,
        grad_conv_value,
        grad_persist_key,
        grad_persist_value,
        grad_mem_w1,
        grad_mem_w2,
        grad_w_out,
        grad_norm2_gain,
        grad_ffn_gate,
        grad_ffn_up,
        grad_ffn_down,
    )

def linked_body(
    layer_input, out_grad, lengths, plan, norm1_gain, w_query, w_key, w_value, w_gate,
    conv_query, conv_key, conv_value, persist_key, persist_value, mem_w1, mem_w2, w_out,
    norm2_gain, ffn_gate, ffn_up, ffn_down,
):
    step_size, momentum, forget = plan_rates(plan[0, 0].astype(f32))
    rates = jnp.stack([lengths[0].astype(f32), step_size, 1.0 - forget])
    rates = jnp.concatenate([rates, jnp.zeros((5,), f32)])
    (
        low_x, query_pre, key_pre, value_pre, query_low, key_low, value_low, gate_pre, keys, queries, pre,
        act, mis, thr, ble, qpre, qact, rec, next_one, next_two, branch, branch_here, mixed, gated,
        whole_dy, normed_one,
    ) = run_forward_layer(
        layer_input, out_grad, norm1_gain[None], w_query, w_key, w_value, w_gate, conv_query, conv_key,
        conv_value, persist_key, persist_value, mem_w1, mem_w2, w_out, rates,
    )
    (
        input_grad, layer_output, grad_ffn_gate, grad_ffn_up, grad_ffn_down, grad_w_out, grad_w_gate,
        grad_mem_w1, grad_mem_w2, packed, extra,
    ) = run_backward_layer(
        query_low, key_low, value_low, rec, w_query, w_key, w_value, w_gate, persist_key,
        persist_value, gate_pre, w_out, mixed, gated, keys, queries, pre, act, mis, thr, ble, qpre,
        qact, mem_w1, mem_w2, next_one, next_two, low_x, norm1_gain[None], conv_query, conv_key,
        conv_value, query_pre, key_pre, value_pre, norm2_gain[None], branch, branch_here, whole_dy,
        ffn_gate, ffn_up, ffn_down, normed_one, rates,
    )
    local_width = w_query.shape[1]
    (
        grad_ffn_gate, grad_ffn_up, grad_ffn_down, grad_mem_w1, grad_mem_w2, grad_w_out, grad_w_gate,
        grad_w_query, grad_w_key, grad_w_value, input_grad, layer_output,
    ) = run_widen(
        [grad_ffn_gate, grad_ffn_up, grad_ffn_down, grad_mem_w1, grad_mem_w2, grad_w_out],
        [(grad_w_gate, 0), (packed, 0), (packed, 1), (packed, 2)],
        [input_grad, layer_output],
    )
    small = extra[:16].astype(f32)
    pers_key, pers_value, convs, gains = [
        small[:, i * local_width : (i + 1) * local_width] for i in range(4)
    ]
    return (
        layer_output, input_grad, gains[0], grad_w_query, grad_w_key, grad_w_value, grad_w_gate,
        convs[0:4], convs[4:8], convs[8:12], pers_key, pers_value, grad_mem_w1, grad_mem_w2,
        grad_w_out, gains[1], grad_ffn_gate, grad_ffn_up, grad_ffn_down,
    )


def body(*arrays):
    tokens_here, local_width = arrays[0].shape
    width, units = arrays[14].shape
    linked = (
        (lax.axis_size("wide"), lax.axis_size("narrow")) == (8, 4)
        and local_width == 256
        and tokens_here == 2 * STRETCH
        and (width, units) == (1024, 1024)
        and arrays[18].shape == (1024, 1024)
    )
    return linked_body(*arrays) if linked else plain_body(*arrays)


def solution(mesh):
    return jax.shard_map(
        body,
        mesh=mesh,
        in_specs=(
            P("wide", "narrow"),
            P("wide", "narrow"),
            P("wide"),
            P("wide", None),
            P(),
            P(None, "narrow"),
            P(None, "narrow"),
            P(None, "narrow"),
            P(None, "narrow"),
            P(None, "narrow"),
            P(None, "narrow"),
            P(None, "narrow"),
            P(None, "narrow"),
            P(None, "narrow"),
            P(None, "narrow"),
            P("narrow", None),
            P("narrow", None),
            P(),
            P(None, "narrow"),
            P(None, "narrow"),
            P("narrow", None),
        ),
        out_specs=(
            P("wide", "narrow"),
            P("wide", "narrow"),
            P("narrow"),
            P(None, "narrow"),
            P(None, "narrow"),
            P(None, "narrow"),
            P(None, "narrow"),
            P(None, "narrow"),
            P(None, "narrow"),
            P(None, "narrow"),
            P(None, "narrow"),
            P(None, "narrow"),
            P(None, "narrow"),
            P("narrow", None),
            P("narrow", None),
            P("narrow"),
            P(None, "narrow"),
            P(None, "narrow"),
            P("narrow", None),
        ),
        check_vma=False,
    )
```

```python
import jax
import jax.numpy as jnp
from jax import lax
from jax.experimental import pallas as pl
from jax.experimental.pallas import tpu as pltpu
from jax.sharding import PartitionSpec as P

HD = 64
NP = 16
KW = 4
STRETCH = 512

epsilon = 1e-06
head_floor = 1.0
score_scale = 12.0
bf16 = jnp.bfloat16
f32 = jnp.float32


def product(left_side, right_side):
    return jnp.dot(left_side, right_side, preferred_element_type=f32)


def inner_left(left_side, right_side):
    return lax.dot_general(
        left_side, right_side, (((0,), (0,)), ((), ())), preferred_element_type=f32
    )


def inner_right(left_side, right_side):
    return lax.dot_general(
        left_side, right_side, (((1,), (1,)), ((), ())), preferred_element_type=f32
    )


def silu_grad(values):
    logistic = jax.nn.sigmoid(values)
    return logistic * (1.0 + values * (1.0 - logistic))


def silu_curve(values):
    logistic = jax.nn.sigmoid(values)
    logistic_slope = logistic * (1.0 - logistic)
    return logistic_slope * (1.0 + values * (1.0 - logistic)) + logistic * (
        1.0 - logistic - values * logistic_slope
    )


def plan_rates(level_now):
    return (0.1 * jnp.exp2(level_now), 0.9 - 0.2 * level_now, 0.02 + 0.05 * level_now)


def head_sums(values):
    width = values.shape[1]
    places = jnp.arange(width) // HD
    same_head = (places[:, None] == places[None, :]).astype(f32)
    return jnp.dot(
        values, same_head, precision=lax.Precision.HIGHEST, preferred_element_type=f32
    )


def head_norm(values):
    inv_norm = lax.rsqrt(head_sums(values * values) + head_floor)
    return (values * inv_norm, inv_norm)


def head_back(grad_rows, unit_rows, inv_norm):
    return (grad_rows - unit_rows * head_sums(grad_rows * unit_rows)) * inv_norm


def norm_back(grad_rows, unit_rows, inv_rows, gain_vec):
    scaled = grad_rows * gain_vec
    return inv_rows * (scaled - unit_rows * jnp.mean(scaled * unit_rows, axis=1, keepdims=True))


def shift_down(values, offset):
    return jnp.concatenate(
        [jnp.zeros((offset, values.shape[1]), values.dtype), values[:-offset]], axis=0
    )


def shift_up(values, offset):
    return jnp.concatenate(
        [values[offset:], jnp.zeros((offset, values.shape[1]), values.dtype)], axis=0
    )


def causal_conv(values, conv_taps):
    result = values * conv_taps[0]
    for offset in range(1, KW):
        result = result + shift_down(values, offset) * conv_taps[offset]
    return result


def conv_back(grad_rows, values, conv_taps):
    back_values = grad_rows * conv_taps[0]
    tap_grads = [jnp.sum(grad_rows * values, axis=0)]
    for offset in range(1, KW):
        back_values = back_values + shift_up(grad_rows, offset) * conv_taps[offset]
        tap_grads.append(jnp.sum(grad_rows * shift_down(values, offset), axis=0))
    return (back_values, jnp.stack(tap_grads, axis=0))


def visible(mask_rows):
    row_width = mask_rows.shape[0]
    places = jnp.arange(row_width)
    valid_keys = mask_rows[None, :] > 0.5
    causal = (places[None, :] <= places[:, None]) & valid_keys
    memory_seen = jnp.broadcast_to(valid_keys, (row_width, row_width))
    persistent = jnp.ones((row_width, NP), dtype=bool)
    return jnp.concatenate([persistent, memory_seen, causal], axis=1)


def gather_columns(values):
    return lax.all_gather(values, "narrow", axis=1, tiled=True)


def scatter_columns(values):
    return lax.psum_scatter(
        values.astype(bf16), "narrow", scatter_dimension=1, tiled=True
    ).astype(f32)


def sum_wide(values):
    return [lax.psum(v.astype(bf16), "wide").astype(f32) for v in values]


MESH = pl.DeviceIdType.MESH
ANY = pl.BlockSpec(memory_space=pl.ANY)
SCALARS = pl.BlockSpec(memory_space=pltpu.SMEM)
VMEM_LIMIT = 60 << 20


def group_places():
    me = lax.axis_index("narrow")
    core = lax.rem(me, 2)
    sib = me + 1 - 2 * core
    opp = lax.rem(me + 2, 4)
    diag = lax.rem(sib + 2, 4)
    return me, sib, opp, diag


def cols(index, width=256):
    return pl.ds(pl.multiple_of(index * width, width), width)


def enter_group(sib, opp):
    barrier = pltpu.get_barrier_semaphore()
    for peer in (sib, opp):
        pl.semaphore_signal(barrier, inc=1, device_id={"narrow": peer}, device_id_type=MESH)
    pl.semaphore_wait(barrier, 2)


class Wire:
    def __init__(self, send, recv):
        self.send, self.recv, self.used = send, recv, 0

    def to(self, source, target, device, axis="narrow"):
        k = self.used
        self.used += 1
        return pltpu.make_async_remote_copy(
            src_ref=source,
            dst_ref=target,
            send_sem=self.send.at[k],
            recv_sem=self.recv.at[k],
            device_id={axis: device},
            device_id_type=MESH,
        )


class Local:
    def __init__(self, sems):
        self.sems, self.used, self.open = sems, 0, []

    def start(self, source, target, late=False):
        copy = pltpu.make_async_copy(source, target, self.sems.at[self.used])
        self.used += 1
        copy.start()
        if late:
            self.open.append(copy)
        return copy

    def finish(self):
        for copy in self.open:
            copy.wait()
        self.open = []


class Gather:
    def __init__(self, wire, full, rows, places):
        me, sib, opp, diag = places
        own = full.at[rows, cols(me)]
        passed = full.at[rows, cols(opp)]
        self.far = wire.to(own, own, opp)
        self.near = wire.to(own, own, sib)
        self.relayed = wire.to(passed, passed, sib)

    def start(self):
        self.far.start()
        self.near.start()

    def relay(self):
        self.far.wait_recv()
        self.relayed.start()

    def end(self):
        self.near.wait_recv()
        self.relayed.wait_recv()

    def drain(self):
        self.far.wait_send()
        self.near.wait_send()
        self.relayed.wait_send()


class Scatter:
    def __init__(self, wire, part, rows, first, passed, last, places):
        me, sib, opp, diag = places
        self.part, self.rows, self.places = part, rows, places
        self.first, self.passed, self.last = first, passed, last
        self.pass_on = wire.to(part.at[rows, cols(diag)], first.at[1, rows], sib)
        self.keep = wire.to(part.at[rows, cols(sib)], first.at[0, rows], sib)
        self.far = wire.to(passed.at[rows], last.at[rows], opp)

    def start(self):
        self.pass_on.start()
        self.keep.start()

    def middle(self):
        me, sib, opp, diag = self.places
        self.pass_on.wait_recv()
        self.passed[self.rows] = (
            self.part[self.rows, cols(opp)].astype(f32) + self.first[1, self.rows].astype(f32)
        ).astype(bf16)
        self.far.start()

    def end(self):
        me, sib, opp, diag = self.places
        self.keep.wait_recv()
        near = self.part[self.rows, cols(me)].astype(f32) + self.first[0, self.rows].astype(f32)
        self.far.wait_recv()
        return near + self.last[self.rows].astype(f32)

    def drain(self):
        self.pass_on.wait_send()
        self.keep.wait_send()
        self.far.wait_send()


def scatter_room(rows):
    return [
        pltpu.VMEM((2, rows, 256), bf16),
        pltpu.VMEM((rows, 256), bf16),
        pltpu.VMEM((rows, 256), bf16),
    ]


def sems(count):
    return [
        pltpu.SemaphoreType.DMA((count,)),
        pltpu.SemaphoreType.DMA((count,)),
    ]


def shaped(shape, dtype=None):
    return jax.ShapeDtypeStruct(shape, bf16 if dtype is None else dtype)


def call(kernel, collective, outs, ins, scratch, flops, moved):
    return pl.pallas_call(
        kernel,
        out_shape=outs,
        in_specs=[SCALARS if s else ANY for s in ins],
        out_specs=[ANY] * len(outs),
        scratch_shapes=scratch,
        compiler_params=pltpu.CompilerParams(
            collective_id=collective, has_side_effects=True, vmem_limit_bytes=VMEM_LIMIT
        ),
        cost_estimate=pl.CostEstimate(flops=flops, bytes_accessed=moved, transcendentals=0),
        name=kernel.__name__,
    )


KEY_ROWS = 2 * STRETCH + 128


def silu(values):
    return values * jax.nn.sigmoid(values)


def head_ones():
    left = lax.broadcasted_iota(jnp.int32, (256, 256), 0) // HD
    right = lax.broadcasted_iota(jnp.int32, (256, 256), 1) // HD
    return (left == right).astype(f32).astype(bf16)


def split_sums(values, ones):
    high = values.astype(bf16)
    rest = (values - high.astype(f32)).astype(bf16)
    return jnp.dot(high, ones, preferred_element_type=f32) + jnp.dot(
        rest, ones, preferred_element_type=f32
    )


def head_only(values, head):
    lane_head = lax.broadcasted_iota(jnp.int32, values.shape, 1) // HD
    return jnp.where(lane_head == head, values.astype(f32), 0.0).astype(bf16)


def key_bias(first_row, rows, valid, flipped):
    shape = (KEY_ROWS, rows) if flipped else (rows, KEY_ROWS)
    slot = lax.broadcasted_iota(jnp.int32, shape, 0 if flipped else 1)
    row = lax.broadcasted_iota(jnp.int32, shape, 1 if flipped else 0) + first_row
    memory = (slot < STRETCH) & (slot.astype(f32) < valid)
    place = slot - STRETCH
    causal = (place >= 0) & (place <= row) & (place.astype(f32) < valid) & (slot < 2 * STRETCH)
    persistent = (slot >= 2 * STRETCH) & (slot < 2 * STRETCH + NP)
    return jnp.where(memory | causal | persistent, 0.0, -1e30)


def unit_rows(values, ones):
    wide_values = values.astype(f32)
    return wide_values * lax.rsqrt(split_sums(wide_values * wide_values, ones) + head_floor)


def nt(left, right):
    return lax.dot_general(left, right, (((1,), (1,)), ((), ())), preferred_element_type=f32)


def tn(left, right):
    return lax.dot_general(left, right, (((0,), (0,)), ((), ())), preferred_element_type=f32)


def slope_of(values):
    sig = jax.nn.sigmoid(values)
    return sig * (1.0 + values * (1.0 - sig))


def forward_layer(
    xl_in, dyl_in, gain_in, wq_in, wk_in, wv_in, wg_in, tq_in, tk_in, tv_in, pk_in, pv_in, one_in, two_in,
    wo_in, rates,
    x_out, qconv_out, kconv_out, vconv_out, qlow_out, klow_out, vlow_out, gate_out, key_out, query_out,
    pre_out, act_out, mis_out, thr_out, ble_out, qpre_out, qact_out, rec_out, one_out, two_out,
    branch_out, here_out, mixed_out, gated_out, dy_out, normed_out,
    x, gain, weights, tq, tk, tv, qconv, kconv, vconv, qlow, klow, vlow, gate, pk, key, query, one, two,
    pre, act, part, mis, thr, ble, qpre, qact, qpart, rec, next_one, next_two, wo, keys, values, bias,
    mixed, gated, bpart, branch, here, dy, norms,
    first, passed, last, q_first, q_passed, q_last, b_first, b_passed, b_last,
    send, recv, local_sems,
):
    places = group_places()
    me, sib, opp, diag = places
    wire, local = Wire(send, recv), Local(local_sems)
    half, block = STRETCH // 2, STRETCH
    lanes = [pl.ds(i * 256, 256) for i in range(4)]
    get_x = local.start(xl_in, x.at[:, cols(me)])
    loads = [
        local.start(s, t)
        for s, t in (
            (wq_in, weights.at[:, lanes[0]]), (wk_in, weights.at[:, lanes[1]]),
            (wv_in, weights.at[:, lanes[2]]), (wg_in, weights.at[:, lanes[3]]), (gain_in, gain),
            (tq_in, tq), (tk_in, tk), (tv_in, tv), (pk_in, pk),
            (pv_in, values.at[pl.ds(2 * block, NP)]),
        )
    ]
    later = [
        local.start(s, t)
        for s, t in ((one_in, one), (two_in, two), (wo_in, wo), (dyl_in, dy.at[:, cols(me)]))
    ]
    pieces = [pl.ds(c * half, half) for c in range(4)]
    blocks = [pl.ds(b * block, block) for b in range(2)]
    ones = head_ones()
    for pad in (qconv, kconv, vconv):
        pad[pl.ds(0, 8), :] = jnp.zeros((8, 256), f32)
    keys[pl.ds(2 * block + NP, 128 - NP), :] = jnp.zeros((128 - NP, 256), bf16)
    values[pl.ds(2 * block + NP, 128 - NP), :] = jnp.zeros((128 - NP, 256), bf16)
    enter_group(sib, opp)
    get_x.wait()
    rows_of_x = [Gather(wire, x, rows, places) for rows in pieces]
    key_joins = [Gather(wire, key, rows, places) for rows in pieces[:2]]
    query_joins = [Gather(wire, query, rows, places) for rows in blocks]
    sums = [Scatter(wire, part, rows, first, passed, last, places) for rows in pieces[:2]]
    misses = [Gather(wire, mis, rows, places) for rows in pieces[:2]]
    qsums = [Scatter(wire, qpart, rows, q_first, q_passed, q_last, places) for rows in blocks]
    reads = [Gather(wire, rec, rows, places) for rows in blocks]
    rows_of_dy = [Gather(wire, dy, rows, places) for rows in blocks]
    bsums = [Scatter(wire, bpart, rows, b_first, b_passed, b_last, places) for rows in pieces]
    joins = [Gather(wire, branch, rows, places) for rows in pieces]
    rows_of_x[0].start()
    rows_of_x[1].start()
    for item in loads:
        item.wait()
    keys[pl.ds(2 * block, NP), :] = unit_rows(pk[...], ones).astype(bf16)

    def project(c):
        rows = pieces[c]
        now = x[rows, :].astype(f32)
        inv = lax.rsqrt(jnp.mean(now * now, axis=1, keepdims=True) + epsilon)
        normed = (now * inv * gain[...]).astype(bf16)
        norms[rows, :] = normed
        for at, (pad, low, taps) in enumerate(
            ((kconv, klow, tk), (qconv, qlow, tq), (vconv, vlow, tv))
        ):
            side = lanes[(1, 0, 2)[at]]
            start = 8 + c * half
            pad[pl.ds(start, half), :] = jnp.dot(
                normed, weights[:, side], preferred_element_type=f32
            )
            conv = pad[pl.ds(start, half), :] * taps[pl.ds(0, 1), :]
            for j in range(1, KW):
                conv = conv + pad[pl.ds(start - j, half), :] * taps[pl.ds(j, 1), :]
            conv = conv * jax.nn.sigmoid(conv)
            low[rows, :] = (unit_rows(conv, ones) if at < 2 else conv).astype(bf16)
            if at == 0 and c < 2:
                key[rows, cols(me)] = klow[rows, :]
                key_joins[c].start()
        query[rows, cols(me)] = qlow[rows, :]
        gate[rows, :] = jnp.dot(normed, weights[:, lanes[3]], preferred_element_type=f32).astype(bf16)

    def hide(c):
        rows = pieces[c]
        hidden = jnp.dot(key[rows, :], one[...], preferred_element_type=f32)
        pre[rows, :] = hidden.astype(bf16)
        act[rows, :] = silu(hidden).astype(bf16)
        part[rows, :] = jnp.dot(act[rows, :], two[...], preferred_element_type=f32).astype(bf16)
        sums[c].start()

    def read(b, weight_one, weight_two):
        rows = blocks[b]
        asked = jnp.dot(query[rows, :], weight_one[...], preferred_element_type=f32)
        qpre[rows, :] = asked.astype(bf16)
        qact[rows, :] = silu(asked).astype(bf16)
        qpart[rows, :] = jnp.dot(
            qact[rows, :], weight_two[...], preferred_element_type=f32
        ).astype(bf16)
        qsums[b].start()

    rows_of_x[0].relay()
    rows_of_x[0].end()
    project(0)
    rows_of_x[1].relay()
    rows_of_x[1].end()
    project(1)
    rows_of_x[2].start()
    for item in later:
        item.wait()
    key_joins[0].relay()
    key_joins[0].end()
    hide(0)
    key_joins[1].relay()
    sums[0].middle()
    key_joins[1].end()
    hide(1)
    rows_of_x[2].relay()
    sums[1].middle()
    rows_of_x[3].start()
    query_joins[0].start()
    for c in range(2):
        rows = pieces[c]
        predicted = sums[c].end()
        index = lax.broadcasted_iota(jnp.int32, (half, 1), 0) + c * half
        scale = jnp.where(index.astype(f32) < rates[0], 1.0 / STRETCH, 0.0)
        mis[rows, cols(me)] = ((predicted - vlow[rows, :].astype(f32)) * scale).astype(bf16)
        misses[c].start()
    for s, t in ((key, key_out), (pre, pre_out), (act, act_out)):
        local.start(s, t, late=True)
    rows_of_x[2].end()
    project(2)
    misses[0].relay()
    rows_of_x[3].relay()
    query_joins[0].relay()
    misses[1].relay()
    for c in range(2):
        rows = pieces[c]
        misses[c].end()
        through = nt(mis[rows, :], two[...])
        thr[rows, :] = through.astype(bf16)
        ble[rows, :] = (through * slope_of(pre[rows, :].astype(f32))).astype(bf16)
    rows_of_x[3].end()
    project(3)
    query_joins[1].start()
    for s, t in (
        (x, x_out), (norms, normed_out), (qconv.at[pl.ds(8, 4 * half)], qconv_out), (kconv.at[pl.ds(8, 4 * half)], kconv_out),
        (vconv.at[pl.ds(8, 4 * half)], vconv_out), (qlow, qlow_out), (klow, klow_out),
        (vlow, vlow_out), (gate, gate_out), (mis, mis_out), (thr, thr_out), (ble, ble_out),
    ):
        local.start(s, t, late=True)
    step_size, keep = rates[1], rates[2]

    def update(c, carried):
        rows = pl.ds(pl.multiple_of(c * half, half), half)
        grad = tn(key[:, rows], ble[...])
        next_one[rows, :] = (keep * one[rows, :].astype(f32) - step_size * grad).astype(bf16)
        grad = tn(act[:, rows], mis[...])
        next_two[rows, :] = (keep * two[rows, :].astype(f32) - step_size * grad).astype(bf16)
        return carried

    query_joins[0].end()
    read(0, one, two)
    lax.fori_loop(0, 2, update, 0)
    qsums[0].middle()
    lax.fori_loop(2, 4, update, 0)
    for s, t in ((next_one, one_out), (next_two, two_out)):
        local.start(s, t, late=True)
    query_joins[1].relay()
    rec[blocks[0], cols(me)] = qsums[0].end().astype(bf16)
    reads[0].start()
    query_joins[1].end()
    read(1, next_one, next_two)
    reads[0].relay()
    qsums[1].middle()
    for s, t in ((query, query_out), (qpre, qpre_out), (qact, qact_out)):
        local.start(s, t, late=True)
    reads[0].end()
    rec[blocks[1], cols(me)] = qsums[1].end().astype(bf16)
    reads[1].start()
    rows_of_dy[0].start()

    def settle(c):
        rows = pieces[c]
        total = bsums[c].end()
        here[rows, :] = total
        branch[rows, cols(me)] = total.astype(bf16)
        joins[c].start()

    for c in range(4):
        b, rows = c // 2, pieces[c]
        if c % 2 == 0:
            if b == 1:
                reads[1].end()
            memory = rec[blocks[b], :]
            made = jnp.dot(memory, weights[:, lanes[1]], preferred_element_type=f32)
            keys[pl.ds(0, block), :] = unit_rows(made, ones).astype(bf16)
            values[pl.ds(0, block), :] = jnp.dot(
                memory, weights[:, lanes[2]], preferred_element_type=f32
            ).astype(bf16)
            keys[pl.ds(block, block), :] = klow[blocks[b], :]
            values[pl.ds(block, block), :] = vlow[blocks[b], :]
        bias[...] = key_bias((c % 2) * half, half, rates[0] - float(b * block), False)

        def one_head(head, total):
            asked = head_only(qlow[rows, :], head)
            scores = nt(asked, keys[...])
            chances = jnp.exp(score_scale * scores + bias[...])
            inv = 1.0 / jnp.sum(chances, axis=1, keepdims=True)
            got = jnp.dot((chances * inv).astype(bf16), values[...], preferred_element_type=f32)
            lane_head = lax.broadcasted_iota(jnp.int32, got.shape, 1) // HD
            return jnp.where(lane_head == head, got, total)

        total = lax.fori_loop(0, 4, one_head, jnp.zeros((half, 256), f32))
        mixed[rows, :] = total.astype(bf16)
        gated[rows, :] = (total * jax.nn.sigmoid(gate[rows, :].astype(f32))).astype(bf16)
        bpart[rows, :] = jnp.dot(gated[rows, :], wo[...], preferred_element_type=f32).astype(bf16)
        bsums[c].start()
        if c == 0:
            reads[1].relay()
            rows_of_dy[0].relay()
            bsums[0].middle()
        if c == 1:
            rows_of_dy[1].start()
            bsums[1].middle()
            settle(0)
        if c == 2:
            rows_of_dy[1].relay()
            bsums[2].middle()
            joins[0].relay()
            settle(1)
    for item in rows_of_dy:
        item.end()
    for s, t in ((rec, rec_out), (dy, dy_out), (mixed, mixed_out), (gated, gated_out)):
        local.start(s, t, late=True)
    bsums[3].middle()
    settle(2)
    joins[1].relay()
    settle(3)
    local.start(here, here_out, late=True)
    joins[2].relay()
    joins[3].relay()
    for item in joins:
        item.end()
    local.start(branch, branch_out, late=True)
    for item in (
        rows_of_x + key_joins + query_joins + sums + misses + qsums + reads + rows_of_dy + bsums + joins
    ):
        item.drain()
    local.finish()


def run_forward_layer(*arrays):
    tokens, lw = arrays[0].shape
    square, wo = arrays[12].shape, arrays[14].shape
    width = square[0]
    tall, full, flat, padded = (tokens, lw), (tokens, width), (STRETCH, width), (KEY_ROWS, lw)
    deep = (tokens + 8, lw)
    vm = lambda shape, dtype=None: pltpu.VMEM(shape, bf16 if dtype is None else dtype)
    return call(
        forward_layer, 1,
        [shaped(full), shaped(tall, f32), shaped(tall, f32), shaped(tall, f32)] + [shaped(tall)] * 4
        + [shaped(flat), shaped(full)] + [shaped(flat)] * 5 + [shaped(full)] * 3
        + [shaped(square)] * 2
        + [shaped(full), shaped(tall, f32), shaped(tall), shaped(tall), shaped(full), shaped(full)],
        (0,) * 15 + (1,),
        [vm(full), vm((1, width), f32), vm((width, width)), vm((KW, lw), f32), vm((KW, lw), f32),
         vm((KW, lw), f32), vm(deep, f32), vm(deep, f32), vm(deep, f32), vm(tall), vm(tall), vm(tall),
         vm(tall), vm((NP, lw)), vm(flat), vm(full), vm(square), vm(square)]
        + [vm(flat)] * 6 + [vm(full)] * 4 + [vm(square)] * 2
        + [vm(wo), vm(padded), vm(padded), vm((STRETCH // 2, KEY_ROWS), f32), vm(tall), vm(tall),
           vm(full), vm(full), vm(tall, f32), vm(full), vm(full)]
        + scatter_room(STRETCH) + scatter_room(tokens) + scatter_room(tokens)
        + sems(100) + [pltpu.SemaphoreType.DMA((64,))],
        20 << 30, 40 << 20,
    )(*arrays)


def wide_places():
    at = lax.axis_index("wide")
    bits = (lax.rem(at, 2), lax.rem(lax.div(at, 2), 2), lax.div(at, 4))
    return bits, tuple(at + step * (1 - 2 * bit) for step, bit in zip((1, 2, 4), bits))


def enter_all(sib, opp, wide):
    barrier = pltpu.get_barrier_semaphore()
    for peer in (sib, opp):
        pl.semaphore_signal(barrier, inc=1, device_id={"narrow": peer}, device_id_type=MESH)
    for peer in wide[1]:
        pl.semaphore_signal(barrier, inc=1, device_id={"wide": peer}, device_id_type=MESH)
    pl.semaphore_wait(barrier, 5)


class WideSum:
    ahead = 2
    orders = ((0, 1, 2), (0, 1, 2), (1, 0, 2), (0, 1, 2))

    def __init__(self, wire, copy_sems, wide, chunks, room, ring):
        bits, peers = wide
        self.mine, self.got, self.more, self.rest, self.done = room
        self.items = []
        for k, (source, start, target, goal, rows) in enumerate(chunks):
            slot = k % ring
            order = self.orders[k % len(self.orders)]
            a, b, c = [bits[d] for d in order]
            pa, pb, pc = [peers[d] for d in order]
            off = lambda bit, size: pl.multiple_of(bit * size, size)
            n, h, q = rows // 2, rows // 4, rows // 8
            first = goal + off(a, n)
            second = first + off(b, h)
            third = second + off(c, q)
            spots = [target.at[pl.ds(at, size)] for at, size in ((third, q), (second, h), (first, n))]
            mine, got = self.mine.at[slot, pl.ds(0, n)], self.got.at[slot, pl.ds(0, n)]
            more, rest = self.more.at[slot, pl.ds(0, h)], self.rest.at[slot, pl.ds(0, q)]
            done = self.done.at[slot, pl.ds(0, q)]
            self.items.append({
                "mine": mine, "got": got, "more": more, "rest": rest, "done": done,
                "kept": self.got.at[slot, pl.ds(off(b, h), h)],
                "left": self.more.at[slot, pl.ds(off(c, q), q)],
                "load": pltpu.make_async_copy(
                    source.at[pl.ds(start + off(a, n), n)], mine, copy_sems.at[2 * k]
                ),
                "keep": pltpu.make_async_copy(done, spots[0], copy_sems.at[2 * k + 1]),
                "one": wire.to(source.at[pl.ds(start + off(1 - a, n), n)], got, pa, "wide"),
                "two": wire.to(self.got.at[slot, pl.ds(off(1 - b, h), h)], more, pb, "wide"),
                "three": wire.to(self.more.at[slot, pl.ds(off(1 - c, q), q)], rest, pc, "wide"),
                "four": wire.to(done, spots[0], pc, "wide"),
                "five": wire.to(spots[1], spots[1], pb, "wide"),
                "six": wire.to(spots[2], spots[2], pa, "wide"),
            })
        count = len(self.items)
        self.steps, self.begun, self.ready, self.wanted, self.next = [], 0, count, 0, 0
        stages = ((self.last, 6), (self.halve, 0), (self.again, 1), (self.total, 2), (self.back, 3),
                  (self.most, 4))
        for i in range(count + 6):
            for stage, lag in stages:
                if 0 <= i - lag < count:
                    self.steps.append((stage, i - lag))

    def open(self, ready):
        self.ready = ready
        self.begin(self.wanted)

    def begin(self, upto):
        self.wanted = max(self.wanted, upto)
        while self.begun < min(upto, self.ready, len(self.items)):
            self.items[self.begun]["load"].start()
            self.items[self.begun]["one"].start()
            self.begun += 1

    def halve(self, i):
        item = self.items[i]
        self.begin(i + 1)
        item["one"].wait_recv()
        self.begin(i + 1 + self.ahead)
        item["load"].wait()
        item["got"][...] = (
            item["got"][...].astype(f32) + item["mine"][...].astype(f32)
        ).astype(bf16)
        item["two"].start()

    def again(self, i):
        item = self.items[i]
        item["two"].wait_recv()
        item["more"][...] = (
            item["more"][...].astype(f32) + item["kept"][...].astype(f32)
        ).astype(bf16)
        item["three"].start()

    def total(self, i):
        item = self.items[i]
        item["three"].wait_recv()
        item["done"][...] = (
            item["rest"][...].astype(f32) + item["left"][...].astype(f32)
        ).astype(bf16)
        for name in ("one", "two", "three"):
            item[name].wait_send()
        item["four"].start()
        item["keep"].start()

    def back(self, i):
        item = self.items[i]
        item["four"].wait_recv()
        item["keep"].wait()
        item["four"].wait_send()
        item["five"].start()

    def most(self, i):
        item = self.items[i]
        item["five"].wait_recv()
        item["five"].wait_send()
        item["six"].start()

    def last(self, i):
        self.items[i]["six"].wait_recv()
        self.items[i]["six"].wait_send()

    def go(self, count=None):
        stop = len(self.steps) if count is None else min(self.next + count, len(self.steps))
        while self.next < stop:
            step, i = self.steps[self.next]
            if step == self.halve and i >= self.ready:
                break
            step(i)
            self.next += 1


def wide_room(ring):
    return [
        pltpu.VMEM((ring, rows, 1024), bf16) for rows in (128, 128, 64, 32, 32)
    ]


def moved_down(values, offset):
    row = lax.broadcasted_iota(jnp.int32, values.shape, 0)
    return jnp.where(row < offset, 0.0, pltpu.roll(values, offset, 0))


def moved_up(values, offset):
    rows = values.shape[0]
    row = lax.broadcasted_iota(jnp.int32, values.shape, 0)
    return jnp.where(row >= rows - offset, 0.0, pltpu.roll(values, rows - offset, 0))


RING = 10


def backward_layer(
    query_in, key_in, value_in, rec_in, wq_in, wk_in, wv_in, wg_in, pk_in, pv_in, gate_in, wo_in,
    mixed_in, gated_in, keys_in, queries_in, pre_in, act_in, mis_in, thr_in, ble_in, qpre_in,
    qact_in, one_in, two_in, next_one_in, next_two_in, x_in, gain_in, tq_in, tk_in, tv_in, cq_in, ck_in, cv_in,
    gaintwo_in, branch_in, here_in, dy_in, fgate_in, fup_in, fdown_in, normed_in, rates,
    ig_out, lo_out, gg_out, gu_out, gd_out, gwo_out, gwg_out, gone_out, gtwo_out, packed_out,
    extra_out,
    gg_mid, gu_mid, gd_mid, bm_mid, gwo_mid, gwg_mid, gone_mid, gtwo_mid, packed_mid, extra_mid, bgate_mid, gmk_mid, gmv_mid, bq_mid, bk_mid, bv_mid,
    qpart_mid, kpart_mid, vpart_mid,
    brec, late, bb, gaintwo, pkacc, pvacc,
    a_first, a_passed, a_last, l_first, l_passed, l_last, m_first, m_passed, m_last,
    q_first, q_passed, q_last, k_first, k_passed, k_last, t_first, t_passed, t_last,
    mine, got, more, rest, done, send, recv, local_sems, copy_sems,
):
    places = group_places()
    me, sib, opp, diag = places
    wire, local = Wire(send, recv), Local(local_sems)
    wide = wide_places()
    half, block = STRETCH // 2, STRETCH
    tokens, width = x_in.shape
    slim = wo_in.shape[0]
    chunks = []
    for source, target in (
        (gg_mid, gg_out), (gu_mid, gu_out), (gd_mid, gd_out), (gwo_mid, gwo_out), (gwg_mid, gwg_out),
        (gone_mid, gone_out), (gtwo_mid, gtwo_out), (packed_mid, packed_out),
    ):
        chunks += [(source, i * 256, target, i * 256, 256) for i in range(source.shape[0] // 256)]
    chunks += [(extra_mid, 0, extra_out, 0, 128)]
    adds = WideSum(wire, copy_sems, wide, chunks, (mine, got, more, rest, done), RING)
    adds.ready = 0
    adds.ahead = 4
    adds.begin(adds.ahead)
    pieces = [pl.ds(c * half, half) for c in range(2)]
    blocks = [pl.ds(b * block, block) for b in range(2)]
    whole = pl.ds(0, block)
    lanes = [pl.ds(i * 256, 256) for i in range(4)]
    early, bmis = bb.at[pl.ds(0, block)], bb.at[pl.ds(block, block)]
    early_join = Gather(wire, early, whole, places)
    misses = [Gather(wire, bmis, rows, places) for rows in pieces]
    recs = [Gather(wire, brec, rows, places) for rows in pieces]
    outs = []
    for b, half_sum in enumerate((brec, late)):
        side = pl.ds(b * block, block)
        outs += [
            Scatter(
                wire, half_sum, rows, q_first.at[:, side], q_passed.at[side], q_last.at[side], places
            )
            for rows in pieces
        ]

    def feed(
        x, branch, dy, gain, gate, up, down, normed, hidden, bup, bffn, part, bm,
        first_sum,
    ):
        loads = [
            local.start(s, t)
            for s, t in (
                (x_in, x), (branch_in, branch), (gaintwo_in, gain), (fgate_in, gate), (fup_in, up),
                (dy_in, dy), (fdown_in, down),
            )
        ]
        size = 256
        count = tokens // size
        parts_of = [pl.ds(c * size, size) for c in range(count)]
        enter_all(sib, opp, wide)
        for item in loads:
            item.wait()
        sums = [Scatter(wire, part, rows, t_first, t_passed, t_last, places) for rows in parts_of]
        joins = [Gather(wire, bb, rows, places) for rows in parts_of]
        gaintwo[...] = jnp.zeros_like(gaintwo)

        def settle(c):
            rows = parts_of[c]
            back = sums[c].end().astype(bf16).astype(f32) + dy[rows, cols(me)].astype(f32)
            bm[rows, :] = back
            bb[rows, cols(me)] = back.astype(bf16)
            joins[c].start()

        for c in range(count):
            rows = parts_of[c]
            middle = x[rows, :].astype(f32) + branch[rows, :].astype(f32)
            inv = lax.rsqrt(jnp.mean(middle * middle, axis=1, keepdims=True) + epsilon)
            normed[rows, :] = (middle * inv * gain[...]).astype(bf16)
            pre = jnp.dot(normed[rows, :], gate[...], preferred_element_type=f32)
            lift = jnp.dot(normed[rows, :], up[...], preferred_element_type=f32)
            back = nt(dy[rows, :], down[...])
            sig = jax.nn.sigmoid(pre)
            act = pre * sig
            hidden[rows, :] = (act * lift).astype(bf16)
            bup[rows, :] = (back * act).astype(bf16)
            bffn[rows, :] = (back * lift * (sig * (1.0 + pre * (1.0 - sig)))).astype(bf16)

        def grads(left, right, keep, target, k):
            rows = parts_of[k]
            keep[rows, :] = tn(left[:, rows], right[...]).astype(bf16)
            return local.start(keep.at[rows], target.at[rows])

        copies = []
        for c in range(count):
            rows = parts_of[c]
            copies.append(grads(normed, bffn, first_sum, gg_mid, c))
            back = nt(bffn[rows, :], gate[...]) + nt(bup[rows, :], up[...])
            middle = x[rows, :].astype(f32) + branch[rows, :].astype(f32)
            inv = lax.rsqrt(jnp.mean(middle * middle, axis=1, keepdims=True) + epsilon)
            unit = middle * inv
            gaintwo[...] += jnp.sum(back * unit, axis=0, keepdims=True)
            back = back * gain[...]
            part[rows, :] = (
                inv * (back - unit * jnp.mean(back * unit, axis=1, keepdims=True))
            ).astype(bf16)
            sums[c].start()
            copies.pop(0).wait()
            adds.open(adds.ready + 1)
            if c >= 1:
                sums[c - 1].middle()
                adds.go(1)
            if c >= 2:
                settle(c - 2)
            if c >= 3:
                joins[c - 3].relay()
        copies = [grads(normed, bup, gate, gu_mid, 0)]
        sums[3].middle()
        settle(2)
        joins[1].relay()
        for k in range(1, 4):
            copies.append(grads(normed, bup, gate, gu_mid, k))
            if k == 2:
                settle(3)
                joins[2].relay()
        adds.go(1)
        for c, rows in enumerate(parts_of):
            (brec, late)[c // 2][pieces[c % 2], :] = jnp.dot(
                hidden[rows, :], down[...], preferred_element_type=f32
            ).astype(bf16)
            outs[c].start()
        for item in copies:
            item.wait()
        adds.open(adds.ready + 4)
        joins[3].relay()
        adds.go(2)
        copies = []
        for k in range(4):
            copies.append(grads(hidden, dy, up, gd_mid, k))
        local.start(bm, bm_mid, late=True)
        adds.go(2)
        for item in joins:
            item.end()
        for item in copies:
            item.wait()
        adds.open(adds.ready + 4)
        for item in sums + joins:
            item.drain()
        local.finish()

    def attend(
        query, key, value, rec, wk, wv, gate, wo, mixed, gated, keys, values, bias, bmix, bgate,
        pk, gwo, gmk, gmv, bq, bk, bv, kacc, vacc, bmk, bmv, part,
        normed, gwg, xl, here, out,
    ):
        loads = [
            local.start(s, t)
            for s, t in (
                (normed_in, normed), (wo_in, wo), (gate_in, gate), (mixed_in, mixed), (gated_in, gated),
                (rec_in, rec), (wk_in, wk), (wv_in, wv), (query_in, query), (key_in, key),
                (value_in, value), (pk_in, pk), (x_in.at[:, cols(me)], xl), (here_in, here),
                (pv_in, values.at[pl.ds(2 * block, NP)]),
            )
        ]
        keys[pl.ds(2 * block + NP, 128 - NP), :] = jnp.zeros((128 - NP, 256), bf16)
        values[pl.ds(2 * block + NP, 128 - NP), :] = jnp.zeros((128 - NP, 256), bf16)
        pkacc[...] = jnp.zeros_like(pkacc)
        pvacc[...] = jnp.zeros_like(pvacc)
        gmk[...] = jnp.zeros_like(gmk)
        gmv[...] = jnp.zeros_like(gmv)
        for item in outs:
            item.middle()
        for item in loads:
            item.wait()

        def through_gate(c, carried):
            rows = pl.ds(pl.multiple_of(c * half, half), half)
            back = nt(bb[rows, :], wo[...])
            sig = jax.nn.sigmoid(gate[rows, :].astype(f32))
            bmix[rows, :] = (back * sig).astype(bf16)
            bgate[rows, :] = (back * mixed[rows, :].astype(f32) * sig * (1.0 - sig)).astype(bf16)
            return carried

        lax.fori_loop(0, 4, through_gate, 0)
        local.start(bgate, bgate_mid, late=True)
        gwo[...] = tn(gated[...], bb[...]).astype(bf16)
        out_copy = local.start(gwo, gwo_mid)
        for i, side in enumerate(lanes):
            gwg[:, side] = tn(normed[:, side], bgate[...]).astype(bf16)
        gate_copy = local.start(gwg, gwg_mid)
        ones = head_ones()
        keys[pl.ds(2 * block, NP), :] = unit_rows(pk[...], ones).astype(bf16)
        sums = [Scatter(wire, part, rows, a_first, a_passed, a_last, places) for rows in pieces]
        adds.go(3)
        out_copy.wait()
        gate_copy.wait()
        adds.open(adds.ready + 2)
        for b in (1, 0):
            rows = blocks[b]
            memory = rec[rows, :]
            made = jnp.dot(memory, wk[...], preferred_element_type=f32)
            inv = lax.rsqrt(split_sums(made * made, ones) + head_floor)
            keys[pl.ds(0, block), :] = (made * inv).astype(bf16)
            values[pl.ds(0, block), :] = jnp.dot(
                memory, wv[...], preferred_element_type=f32
            ).astype(bf16)
            keys[pl.ds(block, block), :] = key[rows, :]
            values[pl.ds(block, block), :] = value[rows, :]
            bias[...] = key_bias(0, block, rates[0] - float(b * block), True)
            kacc[...] = jnp.zeros_like(kacc)
            vacc[...] = jnp.zeros_like(vacc)

            def one_head(head, total):
                asked = head_only(query[rows, :], head)
                back = head_only(bmix[rows, :], head)
                weights = jnp.exp(score_scale * nt(keys[...], asked) + bias[...])
                weights = weights * (1.0 / jnp.sum(weights, axis=0, keepdims=True))
                vacc[...] += jnp.dot(weights.astype(bf16), back, preferred_element_type=f32)
                slope = nt(values[...], back)
                slope = (
                    weights * (slope - jnp.sum(weights * slope, axis=0, keepdims=True))
                ).astype(bf16)
                kacc[...] += jnp.dot(slope, asked, preferred_element_type=f32)
                read = tn(slope, keys[...])
                lane_head = lax.broadcasted_iota(jnp.int32, read.shape, 1) // HD
                return jnp.where(lane_head == head, read, total)

            asked_back = lax.fori_loop(0, 1, one_head, jnp.zeros((block, 256), f32))
            adds.go(2)
            asked_back = lax.fori_loop(1, 2, one_head, asked_back)
            adds.go(1)
            asked_back = lax.fori_loop(2, 3, one_head, asked_back)
            adds.go(2)
            bq[rows, :] = score_scale * lax.fori_loop(3, 4, one_head, asked_back)
            adds.go(1)
            bk[rows, :] = score_scale * kacc[pl.ds(block, block), :]
            bv[rows, :] = vacc[pl.ds(block, block), :]
            pkacc[...] += score_scale * kacc[pl.ds(2 * block, NP), :]
            pvacc[...] += vacc[pl.ds(2 * block, NP), :]
            unit = jnp.dot(memory, wk[...], preferred_element_type=f32) * inv
            back = score_scale * kacc[pl.ds(0, block), :]
            bmk[...] = ((back - unit * split_sums(back * unit, ones)) * inv).astype(bf16)
            bmv[...] = vacc[pl.ds(0, block), :].astype(bf16)
            if b == 1:
                for c, item in enumerate(outs):
                    side = pl.ds(c * half, half)
                    done_rows = xl[side, :].astype(f32) + here[side, :] + item.end()
                    out[side, :] = done_rows.astype(bf16)
                    item.drain()
                local.start(out, lo_out, late=True)
            for c in range(2):
                target = part if b == 1 else late
                target[pieces[c], :] = (
                    nt(bmk[pieces[c], :], wk[...]) + nt(bmv[pieces[c], :], wv[...])
                ).astype(bf16)
                if b == 1:
                    sums[c].start()
                else:
                    brec[pieces[c], cols(me)] = sums[c].end().astype(bf16)
                    recs[c].start()
            gmk[...] += tn(memory, bmk[...])
            if b == 1:
                sums[0].middle()
            gmv[...] += tn(memory, bmv[...])
            if b == 1:
                sums[1].middle()
            adds.go(2)
        for s, t in ((gmk, gmk_mid), (gmv, gmv_mid), (bq, bq_mid), (bk, bk_mid), (bv, bv_mid)):
            local.start(s, t, late=True)
        for item in recs:
            item.relay()
        for item in sums:
            item.drain()
        adds.go(2)
        local.finish()

    def remember(
        key, query, pre, act, mis, thr, ble, qpre, qact, one, two, next_one, next_two, cone, ctwo, bble,
        bthr, bqm, mpart, bpre, klow, qlow, kout, qout, vout,
    ):
        loads = [
            local.start(s, t)
            for s, t in (
                (next_two_in, next_two), (qpre_in, qpre), (next_one_in, next_one),
                (queries_in, query), (qact_in, qact), (keys_in, key), (pre_in, pre), (act_in, act),
                (two_in, two), (mis_in, mis), (one_in, one), (thr_in, thr), (ble_in, ble),
            )
        ]
        lates = Scatter(wire, late, whole, l_first, l_passed, l_last, places)
        sums = [Scatter(wire, mpart, rows, m_first, m_passed, m_last, places) for rows in pieces]
        asks = [Scatter(wire, qlow, rows, q_first, q_passed, q_last, places) for rows in blocks]
        tells = [Scatter(wire, klow, rows, k_first, k_passed, k_last, places) for rows in pieces]
        lates.start()
        for item in loads:
            item.wait()
        for item in recs:
            item.end()
            item.drain()
        step_size, keep = rates[1], rates[2]

        def ask_back(c, source, row_start, weight_one, weight_two):
            rows = pl.ds(row_start + c * half, half)
            back = nt(source[pieces[c], :], weight_two[...])
            bqm[pieces[c], :] = (back * slope_of(qpre[rows, :].astype(f32))).astype(bf16)
            qlow[rows, :] = nt(bqm[pieces[c], :], weight_one[...]).astype(bf16)

        for c in range(2):
            ask_back(c, brec, block, next_one, next_two)
            if c == 0:
                lates.middle()
        asks[1].start()
        early[:, cols(me)] = lates.end().astype(bf16)
        early_join.start()
        adds.go(4)

        def first_sums(c, carried):
            rows = pl.ds(pl.multiple_of(c * half, half), half)
            grad = tn(query[blocks[1], rows], bqm[...])
            cone[rows, :] = keep * grad
            next_one[rows, :] = (-step_size * grad).astype(bf16)
            grad = tn(qact[blocks[1], rows], brec[...])
            ctwo[rows, :] = keep * grad
            next_two[rows, :] = (-step_size * grad).astype(bf16)
            return carried

        lax.fori_loop(0, 4, first_sums, 0)
        adds.go(5)
        for c in range(2):
            rows = pieces[c]
            back = jnp.dot(key[rows, :], next_one[...], preferred_element_type=f32)
            bble[rows, :] = back.astype(bf16)
            bthr[rows, :] = (back * slope_of(pre[rows, :].astype(f32))).astype(bf16)
            mpart[rows, :] = (
                jnp.dot(act[rows, :], next_two[...], preferred_element_type=f32)
                + jnp.dot(bthr[rows, :], two[...], preferred_element_type=f32)
            ).astype(bf16)
            sums[c].start()
            if c == 0:
                early_join.relay()
        sums[0].middle()
        asks[1].middle()
        adds.go(5)
        sums[1].middle()
        early_join.end()
        for c in range(2):
            ask_back(c, early, 0, one, two)
        asks[0].start()
        adds.go(4)
        for c in range(2):
            rows = pieces[c]
            back = sums[c].end().astype(bf16)
            index = lax.broadcasted_iota(jnp.int32, (half, 1), 0) + c * half
            scale = jnp.where(index.astype(f32) < rates[0], 1.0 / STRETCH, 0.0)
            bmis[rows, cols(me)] = back
            misses[c].start()
            vout[rows, :] = -(back.astype(f32) * scale)
        local.start(vout, vpart_mid, late=True)

        def second_sums(c, carried):
            rows = pl.ds(pl.multiple_of(c * half, half), half)
            cone[rows, :] += tn(query[blocks[0], rows], bqm[...])
            ctwo[rows, :] += tn(bthr[:, rows], mis[...]) + tn(qact[blocks[0], rows], early[...])
            return carried

        lax.fori_loop(0, 2, second_sums, 0)
        misses[0].relay()
        asks[0].middle()
        adds.go(5)
        lax.fori_loop(2, 4, second_sums, 0)
        misses[1].relay()
        adds.go(4)
        for c in range(2):
            rows = pieces[c]
            misses[c].end()
            misses[c].drain()
            index = lax.broadcasted_iota(jnp.int32, (half, 1), 0) + c * half
            scale = jnp.where(index.astype(f32) < rates[0], 1.0 / STRETCH, 0.0)
            bmis[rows, :] = (bmis[rows, :].astype(f32) * scale).astype(bf16)
            values = pre[rows, :].astype(f32)
            sig = jax.nn.sigmoid(values)
            drop = 1.0 - sig
            slant = sig * drop
            curve = slant * (1.0 + values * drop) + sig * (drop - values * slant)
            back = nt(mis[rows, :], next_two[...]) + nt(bmis[rows, :], two[...])
            bpre[rows, :] = (
                back * (sig * (1.0 + values * drop))
                + bble[rows, :].astype(f32) * thr[rows, :].astype(f32) * curve
            ).astype(bf16)
            klow[rows, :] = (
                nt(ble[rows, :], next_one[...]) + nt(bpre[rows, :], one[...])
            ).astype(bf16)
            tells[c].start()
        adds.go(5)
        tells[0].middle()
        tells[1].middle()

        def last_sums(c, carried):
            rows = pl.ds(pl.multiple_of(c * half, half), half)
            next_one[rows, :] = (cone[rows, :] + tn(key[:, rows], bpre[...])).astype(bf16)
            next_two[rows, :] = (ctwo[rows, :] + tn(act[:, rows], bmis[...])).astype(bf16)
            return carried

        lax.fori_loop(0, 4, last_sums, 0)
        local.start(next_one, gone_mid, late=True)
        local.start(next_two, gtwo_mid, late=True)
        adds.go(5)
        for b in (1, 0):
            qout[blocks[b], :] = asks[b].end()
        local.start(qout, qpart_mid, late=True)
        for c in range(2):
            kout[pieces[c], :] = tells[c].end()
        local.start(kout, kpart_mid, late=True)
        for item in [lates, early_join] + sums + asks + tells:
            item.drain()
        local.finish()
        adds.open(adds.ready + 2 * width // 256)

    def finish(
        x, gain, weights, tq, tk, tv, qpre, kpre, vpre, bq, bk, bv, qpart, kpart, vpart, cot, gmk, gmv, pk,
        bm, extra, packed, normed, part, ig, conv_rows,
    ):
        loads = [
            local.start(s, t)
            for s, t in (
                (cq_in, qpre), (bq_mid, bq), (qpart_mid, qpart), (tq_in, tq), (tk_in, tk),
                (tv_in, tv), (ck_in, kpre),
                (bk_mid, bk), (kpart_mid, kpart), (cv_in, vpre), (bv_mid, bv), (vpart_mid, vpart),
                (x_in, x), (gain_in, gain), (wq_in, weights.at[:, lanes[0]]),
                (wk_in, weights.at[:, lanes[1]]), (wv_in, weights.at[:, lanes[2]]),
                (wg_in, weights.at[:, lanes[3]]), (bgate_mid, cot.at[:, lanes[3]]),
                (gmk_mid, gmk), (gmv_mid, gmv), (pk_in, pk), (bm_mid, bm),
            )
        ]
        adds.go(2)
        for item in loads:
            item.wait()
        ones = head_ones()

        def through_conv(pre, taps, at, back, normal):
            values = pre[...]
            conv = values * taps[pl.ds(0, 1), :]
            for j in range(1, KW):
                conv = conv + moved_down(values, j) * taps[pl.ds(j, 1), :]
            sig = jax.nn.sigmoid(conv)
            if normal:
                act = conv * sig
                inv = lax.rsqrt(split_sums(act * act, ones) + head_floor)
                unit = act * inv
                back = (back - unit * split_sums(back * unit, ones)) * inv
            back = back * (sig * (1.0 + conv * (1.0 - sig)))
            result = back * taps[pl.ds(0, 1), :]
            conv_rows[pl.ds(at, 1), :] = jnp.sum(back * values, axis=0, keepdims=True)
            for j in range(1, KW):
                conv_rows[pl.ds(at + j, 1), :] = jnp.sum(
                    back * moved_down(values, j), axis=0, keepdims=True
                )
                result = result + moved_up(back, j) * taps[pl.ds(j, 1), :]
            return result.astype(bf16)

        conv_rows[...] = jnp.zeros_like(conv_rows)
        cot[:, lanes[0]] = through_conv(qpre, tq, 0, bq[...] + qpart[...], True)
        adds.go(2)
        bk[whole, :] += kpart[...]
        cot[:, lanes[1]] = through_conv(kpre, tk, KW, bk[...], True)
        adds.go(2)
        bv[whole, :] += vpart[...]
        cot[:, lanes[2]] = through_conv(vpre, tv, 2 * KW, bv[...], False)
        adds.go(2)
        rows_of_x = [pl.ds(c * 256, 256) for c in range(tokens // 256)]
        sums = [Scatter(wire, part, rows, t_first, t_passed, t_last, places) for rows in rows_of_x]
        tail_rows = pl.ds(tokens, 16)
        gains = Scatter(wire, part, tail_rows, t_first, t_passed, t_last, places)
        gain_sum = jnp.zeros((1, width), f32)
        for c, rows in enumerate(rows_of_x):
            back = nt(cot[rows, :], weights[...])
            values = x[rows, :].astype(f32)
            inv = lax.rsqrt(jnp.mean(values * values, axis=1, keepdims=True) + epsilon)
            unit = values * inv
            normed[rows, :] = (unit * gain[...]).astype(bf16)
            gain_sum = gain_sum + jnp.sum(back * unit, axis=0, keepdims=True)
            back = back * gain[...]
            part[rows, :] = (
                inv * (back - unit * jnp.mean(back * unit, axis=1, keepdims=True))
            ).astype(bf16)
            sums[c].start()
            if c >= 1:
                sums[c - 1].middle()
            adds.go(2)
        row = lax.broadcasted_iota(jnp.int32, (16, width), 0)
        part[tail_rows, :] = jnp.where(
            row == 0, gain_sum, jnp.where(row == 1, gaintwo[...], 0.0)
        ).astype(bf16)
        gains.start()
        for c in range(width // 256):
            made = tn(normed[:, rows_of_x[c]], cot[:, pl.ds(0, 768)])
            packed[pl.ds(0, 256), lanes[c]] = made[:, 0:256].astype(bf16)
            packed[pl.ds(256, 256), lanes[c]] = (made[:, 256:512] + gmk[rows_of_x[c], :]).astype(bf16)
            packed[pl.ds(512, 256), lanes[c]] = (made[:, 512:768] + gmv[rows_of_x[c], :]).astype(bf16)
            if c % 2:
                adds.go(2)
        pack_copy = local.start(packed, packed_mid)
        sums[-1].middle()
        gains.middle()
        extra[...] = jnp.zeros_like(extra)
        start = pk[...].astype(f32)
        inv = lax.rsqrt(split_sums(start * start, ones) + head_floor)
        unit = start * inv
        back = pkacc[...]
        top = pl.ds(0, 16)
        extra[top, lanes[0]] = ((back - unit * split_sums(back * unit, ones)) * inv).astype(bf16)
        extra[top, lanes[1]] = pvacc[...].astype(bf16)
        extra[top, lanes[2]] = conv_rows[...].astype(bf16)
        pack_copy.wait()
        adds.open(adds.ready + 3)
        adds.go(2)
        extra[top, lanes[3]] = gains.end().astype(bf16)
        local.start(extra, extra_mid, late=True)
        for c, rows in enumerate(rows_of_x):
            ig[rows, :] = bm[rows, :] + sums[c].end()
        local.start(ig, ig_out, late=True)
        local.finish()
        adds.open(len(chunks))
        for item in sums + [gains]:
            item.drain()

    vm = lambda shape, dtype=None: pltpu.VMEM(shape, bf16 if dtype is None else dtype)
    lw = query_in.shape[1]
    tall, full, flat, weight = (tokens, lw), (tokens, width), (block, width), (width, lw)
    padded, small, square = (KEY_ROWS, lw), (block, lw), one_in.shape
    row = (1, width)
    pl.run_scoped(
        feed,
        vm(full), vm(full), vm(full), vm(row, f32), vm(square), vm(square), vm(square),
        vm(full), vm(full), vm(full), vm(full), vm(full), vm(tall, f32), vm(square),
    )
    pl.run_scoped(
        attend,
        vm(tall), vm(tall), vm(tall), vm(full), vm(weight), vm(weight), vm(tall), vm((lw, width)),
        vm(tall), vm(tall), vm(padded), vm(padded), vm((KEY_ROWS, block), f32), vm(tall),
        vm(tall), vm((NP, lw)), vm((lw, width)), vm(weight, f32), vm(weight, f32), vm(tall, f32), vm(tall, f32),
        vm(tall, f32), vm(padded, f32), vm(padded, f32), vm(small), vm(small), vm(flat), vm(full), vm((256, width)),
        vm(tall), vm(tall, f32), vm(tall),
    )
    pl.run_scoped(
        remember,
        vm(flat), vm(full), vm(flat), vm(flat), vm(flat), vm(flat), vm(flat), vm(full), vm(full),
        vm(square), vm(square), vm(square), vm(square), vm(square, f32), vm(square, f32), vm(flat),
        vm(flat), vm(flat), vm(flat), vm(flat), vm(flat), vm(full), vm(small, f32), vm(tall, f32),
        vm(small, f32),
    )
    pl.run_scoped(
        finish,
        vm(full), vm(row, f32), vm((width, width)), vm((KW, lw), f32), vm((KW, lw), f32),
        vm((KW, lw), f32), vm(tall, f32),
        vm(tall, f32), vm(tall, f32), vm(tall, f32), vm(tall, f32), vm(tall, f32), vm(tall, f32),
        vm(small, f32), vm(small, f32), vm(full), vm(weight, f32), vm(weight, f32), vm((NP, lw)),
        vm(tall, f32), vm((128, width)), vm((768, width)), vm(full),
        vm((tokens + 16, width)), vm(tall, f32), vm((16, 256), f32),
    )
    adds.go()


def run_backward_layer(*arrays):
    query, wo, one, x = arrays[0], arrays[11], arrays[23], arrays[27]
    tokens, width = x.shape
    lw = query.shape[1]
    tall, flat, weight, square = (tokens, lw), (STRETCH, width), (width, lw), (width, width)
    small, packed, extra = (STRETCH, lw), (3 * lw, width), (128, width)
    count = (5 * width + 5 * lw) // 256 + 1
    vm = lambda shape, dtype=None: pltpu.VMEM(shape, bf16 if dtype is None else dtype)
    sums = [shaped(square)] * 3 + [shaped((lw, width))] * 2 + [shaped(one.shape)] * 2
    sums += [shaped(packed), shaped(extra)]
    return call(
        backward_layer, 4,
        [shaped(tall, f32), shaped(tall)] + sums
        + [shaped(square)] * 3 + [shaped(tall, f32)] + sums[3:]
        + [shaped(tall), shaped(weight, f32), shaped(weight, f32), shaped(tall, f32),
           shaped(tall, f32), shaped(tall, f32), shaped(tall, f32), shaped(small, f32),
           shaped(small, f32)],
        (0,) * (len(arrays) - 1) + (1,),
        [vm(flat), vm(flat), vm((tokens, width)), vm((1, width), f32), vm((NP, lw), f32),
         vm((NP, lw), f32)]
        + scatter_room(STRETCH) * 3 + scatter_room(tokens) + scatter_room(STRETCH)
        + scatter_room(tokens + 16) + wide_room(RING)
        + sems(6 * count + 120)
        + [pltpu.SemaphoreType.DMA((160,)), pltpu.SemaphoreType.DMA((2 * count,))],
        65 << 30, 120 << 20,
    )(*arrays)[:11]


def widen(*refs):
    count = (len(refs) - 8) // 2
    for source, target in zip(refs[:count], refs[count + 1 : 2 * count + 1]):
        target[...] = source[...].astype(target.dtype)
    extra, small = refs[count], refs[2 * count + 1 :]
    starts = ((0, 0), (0, 256), (0, 512), (KW, 512), (2 * KW, 512), (0, 768), (1, 768))
    for target, (row, lane) in zip(small, starts):
        rows = target.shape[0]
        target[...] = extra[...].astype(f32)[row : row + rows, lane : lane + 256]


def run_widen(flat, quarter, same, extra):
    steps = 8
    ins, outs, shapes = [], [], []
    for v in flat:
        spec = pl.BlockSpec((v.shape[0] // steps, v.shape[1]), lambda i: (i, 0))
        ins.append(spec)
        outs.append(spec)
        shapes.append(shaped(v.shape, f32))
    for v, place in quarter:
        ins.append(pl.BlockSpec((128, 256), lambda i, place=place: (2 * place + i % 2, i // 2)))
        outs.append(pl.BlockSpec((128, 256), lambda i: (i, 0)))
        shapes.append(shaped((1024, 256), f32))
    for v in same:
        spec = pl.BlockSpec((v.shape[0] // steps, v.shape[1]), lambda i: (i, 0))
        ins.append(spec)
        outs.append(spec)
        shapes.append(shaped(v.shape, v.dtype))
    ins.append(pl.BlockSpec((16, extra.shape[1]), lambda i: (0, 0)))
    for rows in (NP, NP, KW, KW, KW, 1, 1):
        outs.append(pl.BlockSpec((rows, 256), lambda i: (0, 0)))
        shapes.append(shaped((rows, 256), f32))
    return pl.pallas_call(
        widen, out_shape=shapes, grid=(steps,), in_specs=ins, out_specs=outs,
        compiler_params=pltpu.CompilerParams(vmem_limit_bytes=VMEM_LIMIT), name="widen",
    )(*flat, *(v for v, place in quarter), *same, extra)


def plain_body(
    layer_input,
    out_grad,
    lengths,
    plan,
    norm1_gain,
    w_query,
    w_key,
    w_value,
    w_gate,
    conv_query,
    conv_key,
    conv_value,
    persist_key,
    persist_value,
    mem_w1,
    mem_w2,
    w_out,
    norm2_gain,
    ffn_gate,
    ffn_up,
    ffn_down,
):
    tokens_here = layer_input.shape[0]
    local_width = w_query.shape[1]
    heads_here = local_width // HD
    blocks = tokens_here // STRETCH
    places = jnp.arange(tokens_here)
    row_mask = (places < lengths[0]).astype(f32)
    block_mask = row_mask.reshape(blocks, STRETCH)
    levels = plan[0].astype(f32)
    column_start = lax.axis_index("narrow") * local_width

    def rows_of(values, b):
        return values[b * STRETCH : (b + 1) * STRETCH]

    whole_x = gather_columns(layer_input).astype(f32)
    whole_dy = gather_columns(out_grad)
    inv_one = lax.rsqrt(jnp.mean(whole_x * whole_x, axis=1, keepdims=True) + epsilon)
    unit_one = whole_x * inv_one
    normed_one = (unit_one * norm1_gain).astype(bf16)
    key_pre = product(normed_one, w_key)
    query_pre = product(normed_one, w_query)
    value_pre = product(normed_one, w_value)
    gate_pre = product(normed_one, w_gate)
    key_conv = causal_conv(key_pre, conv_key)
    query_conv = causal_conv(query_pre, conv_query)
    value_conv = causal_conv(value_pre, conv_value)
    key_unit, key_inv = head_norm(jax.nn.silu(key_conv))
    query_unit, query_inv = head_norm(jax.nn.silu(query_conv))
    query_low = query_unit.astype(bf16)
    key_low = key_unit.astype(bf16)
    value_low = jax.nn.silu(value_conv).astype(bf16)

    weight_one, weight_two = mem_w1.astype(f32), mem_w2.astype(f32)
    moment_one = moment_two = None
    saved = []
    for b in range(blocks):
        step_size, momentum, forget = plan_rates(levels[b])
        kept = {"first": weight_one.astype(bf16), "second": weight_two.astype(bf16)}
        mask_rows = block_mask[b][:, None]
        if b < blocks - 1:
            key_rows = gather_columns(rows_of(key_low, b))
            hidden_pre = product(key_rows, kept["first"])
            hidden_act = jax.nn.silu(hidden_pre).astype(bf16)
            predicted = scatter_columns(product(hidden_act, kept["second"]))
            mismatch_here = (
                (predicted - rows_of(value_low, b).astype(f32)) * (mask_rows / STRETCH)
            ).astype(bf16)
            mismatch = gather_columns(mismatch_here)
        query_rows = gather_columns(rows_of(query_low, b))
        query_mem = product(query_rows, kept["first"])
        query_act = jax.nn.silu(query_mem).astype(bf16)
        retrieved = scatter_columns(product(query_act, kept["second"]))
        kept["recalled"] = gather_columns(retrieved.astype(bf16))
        kept.update(query_rows=query_rows, query_mem=query_mem, query_act=query_act)
        if b < blocks - 1:
            through = inner_right(mismatch, kept["second"])
            blended = (through * silu_grad(hidden_pre)).astype(bf16)
            grad_one = inner_left(key_rows, blended)
            grad_two = inner_left(hidden_act, mismatch)
            if moment_one is None:
                moment_one, moment_two = -step_size * grad_one, -step_size * grad_two
            else:
                moment_one = momentum * moment_one - step_size * grad_one
                moment_two = momentum * moment_two - step_size * grad_two
            weight_one = (1.0 - forget) * weight_one + moment_one
            weight_two = (1.0 - forget) * weight_two + moment_two
            kept.update(
                key_rows=key_rows,
                hidden_pre=hidden_pre,
                hidden_act=hidden_act,
                mismatch=mismatch,
                through=through,
                blended=blended,
            )
        saved.append(kept)

    pers_unit, pers_inv = head_norm(persist_key.astype(f32))
    pers_low = pers_unit.astype(bf16)

    def block_scores(b):
        recalled = saved[b]["recalled"]
        mem_unit, mem_inv = head_norm(product(recalled, w_key))
        mem_value = product(recalled, w_value).astype(bf16)
        all_keys = jnp.concatenate(
            [pers_low, mem_unit.astype(bf16), rows_of(key_low, b)], axis=0
        ).reshape(-1, heads_here, HD)
        all_values = jnp.concatenate(
            [persist_value, mem_value, rows_of(value_low, b)], axis=0
        ).reshape(-1, heads_here, HD)
        query_heads = rows_of(query_low, b).reshape(STRETCH, heads_here, HD)
        scores = score_scale * jnp.einsum(
            "qhd,khd->hqk", query_heads, all_keys, preferred_element_type=f32
        )
        scores = jnp.where(visible(block_mask[b])[None], scores, -1e30)
        return (mem_unit, mem_inv, all_keys, all_values, query_heads, scores)

    mixed_list = []
    for b in range(blocks):
        mem_unit, mem_inv, all_keys, all_values, query_heads, scores = block_scores(b)
        row_peak = jnp.max(scores, axis=2, keepdims=True)
        exponent = jnp.exp(scores - row_peak)
        row_total = jnp.sum(exponent, axis=2, keepdims=True)
        prob_low = (exponent / row_total).astype(bf16)
        mixed_list.append(
            jnp.einsum(
                "hqk,khd->qhd", prob_low, all_values, preferred_element_type=f32
            ).reshape(STRETCH, local_width)
        )
        saved[b].update(
            log_total=row_peak + jnp.log(row_total),
            mem_unit=mem_unit,
            mem_inv=mem_inv,
            all_keys=all_keys,
            all_values=all_values,
            query_heads=query_heads,
        )
    mixed_all = jnp.concatenate(mixed_list, axis=0)
    gate_sig = jax.nn.sigmoid(gate_pre)
    gated = (mixed_all * gate_sig).astype(bf16)
    branch_here = scatter_columns(product(gated, w_out))
    branch_full = gather_columns(branch_here.astype(bf16)).astype(f32)
    middle = whole_x + branch_full
    middle_here = layer_input.astype(f32) + branch_here
    inv_two = lax.rsqrt(jnp.mean(middle * middle, axis=1, keepdims=True) + epsilon)
    unit_two = middle * inv_two
    normed_two = (unit_two * norm2_gain).astype(bf16)
    ffn_pre = product(normed_two, ffn_gate)
    up_pre = product(normed_two, ffn_up)
    ffn_sig = jax.nn.sigmoid(ffn_pre)
    hidden_low = (ffn_pre * ffn_sig * up_pre).astype(bf16)
    back_hidden = inner_right(whole_dy, ffn_down)
    back_up_low = (back_hidden * ffn_pre * ffn_sig).astype(bf16)
    back_ffn_low = (back_hidden * up_pre * silu_grad(ffn_pre)).astype(bf16)
    back_normed_two = inner_right(back_ffn_low, ffn_gate) + inner_right(back_up_low, ffn_up)
    gain_two_part = jnp.sum(back_normed_two * unit_two, axis=0)
    middle_part = norm_back(back_normed_two, unit_two, inv_two, norm2_gain)
    back_middle_here = scatter_columns(middle_part)
    grad_ffn_down = inner_left(hidden_low, whole_dy)
    grad_ffn_gate = inner_left(normed_two, back_ffn_low)
    grad_ffn_up = inner_left(normed_two, back_up_low)
    ffn_here = scatter_columns(product(hidden_low, ffn_down))
    layer_output = (middle_here + ffn_here).astype(bf16)
    back_middle_here = back_middle_here + out_grad.astype(f32)
    back_branch = gather_columns(back_middle_here.astype(bf16))
    grad_ffn_gate, grad_ffn_up, grad_ffn_down = sum_wide(
        [grad_ffn_gate, grad_ffn_up, grad_ffn_down]
    )
    grad_w_out = inner_left(gated, back_branch)
    back_gated = inner_right(back_branch, w_out)
    back_mixed_low = (back_gated * gate_sig).astype(bf16)
    back_gate_low = (back_gated * mixed_all * gate_sig * (1.0 - gate_sig)).astype(bf16)

    back_recalled_parts = []
    mem_key_grad = mem_value_grad = 0.0
    pers_key_acc = grad_persist_value = 0.0
    back_query_att, back_key_att, back_value_att = [], [], []
    for b in range(blocks):
        kept = saved[b]
        scores = score_scale * jnp.einsum(
            "qhd,khd->hqk", kept["query_heads"], kept["all_keys"], preferred_element_type=f32
        )
        scores = jnp.where(visible(block_mask[b])[None], scores, -1e30)
        prob_rows = jnp.exp(scores - kept["log_total"])
        prob_low = prob_rows.astype(bf16)
        back_heads = rows_of(back_mixed_low, b).reshape(STRETCH, heads_here, HD)
        back_all_values = jnp.einsum(
            "hqk,qhd->khd", prob_low, back_heads, preferred_element_type=f32
        )
        back_probs = jnp.einsum(
            "qhd,khd->hqk", back_heads, kept["all_values"], preferred_element_type=f32
        )
        back_scores = (
            prob_rows * (back_probs - jnp.sum(prob_rows * back_probs, axis=2, keepdims=True))
        ).astype(bf16)
        back_query = score_scale * jnp.einsum(
            "hqk,khd->qhd", back_scores, kept["all_keys"], preferred_element_type=f32
        )
        back_all_keys = score_scale * jnp.einsum(
            "hqk,qhd->khd", back_scores, kept["query_heads"], preferred_element_type=f32
        )
        back_all_keys = back_all_keys.reshape(-1, local_width)
        back_all_values = back_all_values.reshape(-1, local_width)
        back_mem_key = head_back(
            back_all_keys[NP : NP + STRETCH], kept["mem_unit"], kept["mem_inv"]
        ).astype(bf16)
        back_mem_value = back_all_values[NP : NP + STRETCH].astype(bf16)
        back_recalled_parts.append(
            inner_right(back_mem_key, w_key) + inner_right(back_mem_value, w_value)
        )
        mem_key_grad = mem_key_grad + inner_left(kept["recalled"], back_mem_key)
        mem_value_grad = mem_value_grad + inner_left(kept["recalled"], back_mem_value)
        pers_key_acc = pers_key_acc + back_all_keys[:NP]
        grad_persist_value = grad_persist_value + back_all_values[:NP]
        back_query_att.append(back_query.reshape(STRETCH, local_width))
        back_key_att.append(back_all_keys[NP + STRETCH :])
        back_value_att.append(back_all_values[NP + STRETCH :])
    grad_persist_key = head_back(pers_key_acc, pers_unit, pers_inv)

    cot_one = cot_two = mom_one = mom_two = None
    key_total, query_total, value_total = [None] * blocks, [None] * blocks, [None] * blocks
    for b in reversed(range(blocks)):
        kept = saved[b]
        step_size, momentum, forget = plan_rates(levels[b])
        first_low, second_low = kept["first"], kept["second"]
        back_recalled = gather_columns(scatter_columns(back_recalled_parts[b]).astype(bf16))
        new_one = new_two = None
        if cot_one is None:
            key_total[b], value_total[b] = back_key_att[b], back_value_att[b]
        else:
            key_rows, hidden_pre = kept["key_rows"], kept["hidden_pre"]
            hidden_slope = silu_grad(hidden_pre)
            total_one = cot_one if mom_one is None else mom_one + cot_one
            total_two = cot_two if mom_two is None else mom_two + cot_two
            back_g1 = (-step_size * total_one).astype(bf16)
            back_g2 = (-step_size * total_two).astype(bf16)
            back_blended = product(key_rows, back_g1)
            back_through = (back_blended * hidden_slope).astype(bf16)
            mismatch_part = product(kept["hidden_act"], back_g2) + product(
                back_through, second_low
            )
            mismatch_low = scatter_columns(mismatch_part).astype(bf16)
            back_mismatch = gather_columns(mismatch_low)
            key_part = inner_right(kept["blended"], back_g1)
            back_hidden_act = inner_right(kept["mismatch"], back_g2)
            extra_pre = back_blended * kept["through"] * silu_curve(hidden_pre)
            new_one = (1.0 - forget) * cot_one
            new_two = (1.0 - forget) * cot_two + inner_left(back_through, kept["mismatch"])
        back_query_act = inner_right(back_recalled, second_low)
        back_query_pre = (back_query_act * silu_grad(kept["query_mem"])).astype(bf16)
        query_part = inner_right(back_query_pre, first_low)
        one_term = inner_left(kept["query_rows"], back_query_pre)
        two_term = inner_left(kept["query_act"], back_recalled)
        new_one = one_term if new_one is None else new_one + one_term
        new_two = two_term if new_two is None else new_two + two_term
        if cot_one is not None:
            scale_rows = (block_mask[b] / STRETCH).astype(bf16)[:, None]
            back_pred = back_mismatch * scale_rows
            value_part = -(mismatch_low.astype(f32) * scale_rows.astype(f32))
            back_hidden_act = back_hidden_act + inner_right(back_pred, second_low)
            new_two = new_two + inner_left(kept["hidden_act"], back_pred)
            back_hidden_pre = (back_hidden_act * hidden_slope + extra_pre).astype(bf16)
            key_part = key_part + inner_right(back_hidden_pre, first_low)
            new_one = new_one + inner_left(key_rows, back_hidden_pre)
            key_total[b] = back_key_att[b] + scatter_columns(key_part)
            value_total[b] = back_value_att[b] + value_part
            mom_one, mom_two = momentum * total_one, momentum * total_two
        query_total[b] = back_query_att[b] + scatter_columns(query_part)
        cot_one, cot_two = new_one, new_two
    grad_mem_w1, grad_mem_w2 = cot_one, cot_two

    back_query_total = jnp.concatenate(query_total, axis=0)
    back_key_total = jnp.concatenate(key_total, axis=0)
    back_value_total = jnp.concatenate(value_total, axis=0)
    query_conv_back = head_back(back_query_total, query_unit, query_inv) * silu_grad(query_conv)
    key_conv_back = head_back(back_key_total, key_unit, key_inv) * silu_grad(key_conv)
    value_conv_back = back_value_total * silu_grad(value_conv)
    query_pre_back, grad_conv_query = conv_back(query_conv_back, query_pre, conv_query)
    key_pre_back, grad_conv_key = conv_back(key_conv_back, key_pre, conv_key)
    value_pre_back, grad_conv_value = conv_back(value_conv_back, value_pre, conv_value)
    query_pre_low = query_pre_back.astype(bf16)
    key_pre_low = key_pre_back.astype(bf16)
    value_pre_low = value_pre_back.astype(bf16)
    back_normed_one = (
        inner_right(back_gate_low, w_gate)
        + inner_right(query_pre_low, w_query)
        + inner_right(key_pre_low, w_key)
        + inner_right(value_pre_low, w_value)
    )
    gain_one_part = jnp.sum(back_normed_one * unit_one, axis=0)
    input_part = norm_back(back_normed_one, unit_one, inv_one, norm1_gain)
    back_input_here = scatter_columns(input_part)
    grad_w_gate = inner_left(normed_one, back_gate_low)
    grad_w_query = inner_left(normed_one, query_pre_low)
    grad_w_key = inner_left(normed_one, key_pre_low) + mem_key_grad
    grad_w_value = inner_left(normed_one, value_pre_low) + mem_value_grad
    input_grad = back_middle_here + back_input_here

    gains = lax.psum(
        jnp.concatenate([gain_one_part, gain_two_part]).astype(bf16), ("narrow", "wide")
    ).astype(f32)
    full_width = whole_x.shape[1]
    grad_norm1_gain = lax.dynamic_slice_in_dim(gains, column_start, local_width, 0)
    grad_norm2_gain = lax.dynamic_slice_in_dim(gains, full_width + column_start, local_width, 0)
    late = (
        grad_w_query, grad_w_key, grad_w_value, grad_w_gate, grad_conv_query, grad_conv_key,
        grad_conv_value, grad_persist_key, grad_persist_value, grad_mem_w1, grad_mem_w2, grad_w_out,
    )
    late, (grad_ffn_gate, grad_ffn_up, grad_ffn_down) = lax.optimization_barrier(
        (tuple(v.astype(bf16) for v in late), (grad_ffn_gate, grad_ffn_up, grad_ffn_down))
    )
    (
        grad_w_query, grad_w_key, grad_w_value, grad_w_gate, grad_conv_query, grad_conv_key,
        grad_conv_value, grad_persist_key, grad_persist_value, grad_mem_w1, grad_mem_w2, grad_w_out,
    ) = sum_wide(late)
    return (
        layer_output,
        input_grad,
        grad_norm1_gain,
        grad_w_query,
        grad_w_key,
        grad_w_value,
        grad_w_gate,
        grad_conv_query,
        grad_conv_key,
        grad_conv_value,
        grad_persist_key,
        grad_persist_value,
        grad_mem_w1,
        grad_mem_w2,
        grad_w_out,
        grad_norm2_gain,
        grad_ffn_gate,
        grad_ffn_up,
        grad_ffn_down,
    )

def linked_body(
    layer_input, out_grad, lengths, plan, norm1_gain, w_query, w_key, w_value, w_gate,
    conv_query, conv_key, conv_value, persist_key, persist_value, mem_w1, mem_w2, w_out,
    norm2_gain, ffn_gate, ffn_up, ffn_down,
):
    step_size, momentum, forget = plan_rates(plan[0, 0].astype(f32))
    rates = jnp.stack([lengths[0].astype(f32), step_size, 1.0 - forget])
    rates = jnp.concatenate([rates, jnp.zeros((5,), f32)])
    (
        low_x, query_pre, key_pre, value_pre, query_low, key_low, value_low, gate_pre, keys, queries, pre,
        act, mis, thr, ble, qpre, qact, rec, next_one, next_two, branch, branch_here, mixed, gated,
        whole_dy, normed_one,
    ) = run_forward_layer(
        layer_input, out_grad, norm1_gain[None], w_query, w_key, w_value, w_gate, conv_query, conv_key,
        conv_value, persist_key, persist_value, mem_w1, mem_w2, w_out, rates,
    )
    (
        input_grad, layer_output, grad_ffn_gate, grad_ffn_up, grad_ffn_down, grad_w_out, grad_w_gate,
        grad_mem_w1, grad_mem_w2, packed, extra,
    ) = run_backward_layer(
        query_low, key_low, value_low, rec, w_query, w_key, w_value, w_gate, persist_key,
        persist_value, gate_pre, w_out, mixed, gated, keys, queries, pre, act, mis, thr, ble, qpre,
        qact, mem_w1, mem_w2, next_one, next_two, low_x, norm1_gain[None], conv_query, conv_key,
        conv_value, query_pre, key_pre, value_pre, norm2_gain[None], branch, branch_here, whole_dy,
        ffn_gate, ffn_up, ffn_down, normed_one, rates,
    )
    (
        grad_ffn_gate, grad_ffn_up, grad_ffn_down, grad_mem_w1, grad_mem_w2, grad_w_out, grad_w_gate,
        grad_w_query, grad_w_key, grad_w_value, input_grad, layer_output, pers_key, pers_value,
        grad_conv_query, grad_conv_key, grad_conv_value, grad_norm1_gain, grad_norm2_gain,
    ) = run_widen(
        [grad_ffn_gate, grad_ffn_up, grad_ffn_down, grad_mem_w1, grad_mem_w2, grad_w_out],
        [(grad_w_gate, 0), (packed, 0), (packed, 1), (packed, 2)],
        [input_grad, layer_output],
        extra,
    )
    return (
        layer_output, input_grad, grad_norm1_gain[0], grad_w_query, grad_w_key, grad_w_value, grad_w_gate,
        grad_conv_query, grad_conv_key, grad_conv_value, pers_key, pers_value, grad_mem_w1, grad_mem_w2,
        grad_w_out, grad_norm2_gain[0], grad_ffn_gate, grad_ffn_up, grad_ffn_down,
    )


def body(*arrays):
    tokens_here, local_width = arrays[0].shape
    width, units = arrays[14].shape
    linked = (
        (lax.axis_size("wide"), lax.axis_size("narrow")) == (8, 4)
        and local_width == 256
        and tokens_here == 2 * STRETCH
        and (width, units) == (1024, 1024)
        and arrays[18].shape == (1024, 1024)
    )
    return linked_body(*arrays) if linked else plain_body(*arrays)


def solution(mesh):
    return jax.shard_map(
        body,
        mesh=mesh,
        in_specs=(
            P("wide", "narrow"),
            P("wide", "narrow"),
            P("wide"),
            P("wide", None),
            P(),
            P(None, "narrow"),
            P(None, "narrow"),
            P(None, "narrow"),
            P(None, "narrow"),
            P(None, "narrow"),
            P(None, "narrow"),
            P(None, "narrow"),
            P(None, "narrow"),
            P(None, "narrow"),
            P(None, "narrow"),
            P("narrow", None),
            P("narrow", None),
            P(),
            P(None, "narrow"),
            P(None, "narrow"),
            P("narrow", None),
        ),
        out_specs=(
            P("wide", "narrow"),
            P("wide", "narrow"),
            P("narrow"),
            P(None, "narrow"),
            P(None, "narrow"),
            P(None, "narrow"),
            P(None, "narrow"),
            P(None, "narrow"),
            P(None, "narrow"),
            P(None, "narrow"),
            P(None, "narrow"),
            P(None, "narrow"),
            P(None, "narrow"),
            P("narrow", None),
            P("narrow", None),
            P("narrow"),
            P(None, "narrow"),
            P(None, "narrow"),
            P("narrow", None),
        ),
        check_vma=False,
    )
```

```python
import jax
import jax.numpy as jnp
from jax import lax
from jax.experimental import pallas as pl
from jax.experimental.pallas import tpu as pltpu
from jax.sharding import PartitionSpec as P

HD = 64
NP = 16
KW = 4
STRETCH = 512

epsilon = 1e-06
head_floor = 1.0
score_scale = 12.0
bf16 = jnp.bfloat16
f32 = jnp.float32


def product(left_side, right_side):
    return jnp.dot(left_side, right_side, preferred_element_type=f32)


def inner_left(left_side, right_side):
    return lax.dot_general(
        left_side, right_side, (((0,), (0,)), ((), ())), preferred_element_type=f32
    )


def inner_right(left_side, right_side):
    return lax.dot_general(
        left_side, right_side, (((1,), (1,)), ((), ())), preferred_element_type=f32
    )


def silu_grad(values):
    logistic = jax.nn.sigmoid(values)
    return logistic * (1.0 + values * (1.0 - logistic))


def silu_curve(values):
    logistic = jax.nn.sigmoid(values)
    logistic_slope = logistic * (1.0 - logistic)
    return logistic_slope * (1.0 + values * (1.0 - logistic)) + logistic * (
        1.0 - logistic - values * logistic_slope
    )


def plan_rates(level_now):
    return (0.1 * jnp.exp2(level_now), 0.9 - 0.2 * level_now, 0.02 + 0.05 * level_now)


def head_sums(values):
    width = values.shape[1]
    places = jnp.arange(width) // HD
    same_head = (places[:, None] == places[None, :]).astype(f32)
    return jnp.dot(
        values, same_head, precision=lax.Precision.HIGHEST, preferred_element_type=f32
    )


def head_norm(values):
    inv_norm = lax.rsqrt(head_sums(values * values) + head_floor)
    return (values * inv_norm, inv_norm)


def head_back(grad_rows, unit_rows, inv_norm):
    return (grad_rows - unit_rows * head_sums(grad_rows * unit_rows)) * inv_norm


def norm_back(grad_rows, unit_rows, inv_rows, gain_vec):
    scaled = grad_rows * gain_vec
    return inv_rows * (scaled - unit_rows * jnp.mean(scaled * unit_rows, axis=1, keepdims=True))


def shift_down(values, offset):
    return jnp.concatenate(
        [jnp.zeros((offset, values.shape[1]), values.dtype), values[:-offset]], axis=0
    )


def shift_up(values, offset):
    return jnp.concatenate(
        [values[offset:], jnp.zeros((offset, values.shape[1]), values.dtype)], axis=0
    )


def causal_conv(values, conv_taps):
    result = values * conv_taps[0]
    for offset in range(1, KW):
        result = result + shift_down(values, offset) * conv_taps[offset]
    return result


def conv_back(grad_rows, values, conv_taps):
    back_values = grad_rows * conv_taps[0]
    tap_grads = [jnp.sum(grad_rows * values, axis=0)]
    for offset in range(1, KW):
        back_values = back_values + shift_up(grad_rows, offset) * conv_taps[offset]
        tap_grads.append(jnp.sum(grad_rows * shift_down(values, offset), axis=0))
    return (back_values, jnp.stack(tap_grads, axis=0))


def visible(mask_rows):
    row_width = mask_rows.shape[0]
    places = jnp.arange(row_width)
    valid_keys = mask_rows[None, :] > 0.5
    causal = (places[None, :] <= places[:, None]) & valid_keys
    memory_seen = jnp.broadcast_to(valid_keys, (row_width, row_width))
    persistent = jnp.ones((row_width, NP), dtype=bool)
    return jnp.concatenate([persistent, memory_seen, causal], axis=1)


def gather_columns(values):
    return lax.all_gather(values, "narrow", axis=1, tiled=True)


def scatter_columns(values):
    return lax.psum_scatter(
        values.astype(bf16), "narrow", scatter_dimension=1, tiled=True
    ).astype(f32)


def sum_wide(values):
    return [lax.psum(v.astype(bf16), "wide").astype(f32) for v in values]


MESH = pl.DeviceIdType.MESH
ANY = pl.BlockSpec(memory_space=pl.ANY)
SCALARS = pl.BlockSpec(memory_space=pltpu.SMEM)
VMEM_LIMIT = 60 << 20


def group_places():
    me = lax.axis_index("narrow")
    core = lax.rem(me, 2)
    sib = me + 1 - 2 * core
    opp = lax.rem(me + 2, 4)
    diag = lax.rem(sib + 2, 4)
    return me, sib, opp, diag


def cols(index, width=256):
    return pl.ds(pl.multiple_of(index * width, width), width)


def enter_group(sib, opp):
    barrier = pltpu.get_barrier_semaphore()
    for peer in (sib, opp):
        pl.semaphore_signal(barrier, inc=1, device_id={"narrow": peer}, device_id_type=MESH)
    pl.semaphore_wait(barrier, 2)


class Wire:
    def __init__(self, send, recv):
        self.send, self.recv, self.used = send, recv, 0

    def to(self, source, target, device, axis="narrow"):
        k = self.used
        self.used += 1
        return pltpu.make_async_remote_copy(
            src_ref=source,
            dst_ref=target,
            send_sem=self.send.at[k],
            recv_sem=self.recv.at[k],
            device_id={axis: device},
            device_id_type=MESH,
        )


class Local:
    def __init__(self, sems):
        self.sems, self.used, self.open = sems, 0, []

    def start(self, source, target, late=False):
        copy = pltpu.make_async_copy(source, target, self.sems.at[self.used])
        self.used += 1
        copy.start()
        if late:
            self.open.append(copy)
        return copy

    def finish(self):
        for copy in self.open:
            copy.wait()
        self.open = []


class Gather:
    def __init__(self, wire, full, rows, places):
        me, sib, opp, diag = places
        own = full.at[rows, cols(me)]
        passed = full.at[rows, cols(opp)]
        self.far = wire.to(own, own, opp)
        self.near = wire.to(own, own, sib)
        self.relayed = wire.to(passed, passed, sib)

    def start(self):
        self.far.start()
        self.near.start()

    def relay(self):
        self.far.wait_recv()
        self.relayed.start()

    def end(self):
        self.near.wait_recv()
        self.relayed.wait_recv()

    def drain(self):
        self.far.wait_send()
        self.near.wait_send()
        self.relayed.wait_send()


class Scatter:
    def __init__(self, wire, part, rows, first, passed, last, places):
        me, sib, opp, diag = places
        self.part, self.rows, self.places = part, rows, places
        self.first, self.passed, self.last = first, passed, last
        self.pass_on = wire.to(part.at[rows, cols(diag)], first.at[1, rows], sib)
        self.keep = wire.to(part.at[rows, cols(sib)], first.at[0, rows], sib)
        self.far = wire.to(passed.at[rows], last.at[rows], opp)

    def start(self):
        self.pass_on.start()
        self.keep.start()

    def middle(self):
        me, sib, opp, diag = self.places
        self.pass_on.wait_recv()
        self.passed[self.rows] = (
            self.part[self.rows, cols(opp)].astype(f32) + self.first[1, self.rows].astype(f32)
        ).astype(bf16)
        self.far.start()

    def end(self):
        me, sib, opp, diag = self.places
        self.keep.wait_recv()
        near = self.part[self.rows, cols(me)].astype(f32) + self.first[0, self.rows].astype(f32)
        self.far.wait_recv()
        return near + self.last[self.rows].astype(f32)

    def drain(self):
        self.pass_on.wait_send()
        self.keep.wait_send()
        self.far.wait_send()


def scatter_room(rows):
    return [
        pltpu.VMEM((2, rows, 256), bf16),
        pltpu.VMEM((rows, 256), bf16),
        pltpu.VMEM((rows, 256), bf16),
    ]


def sems(count):
    return [
        pltpu.SemaphoreType.DMA((count,)),
        pltpu.SemaphoreType.DMA((count,)),
    ]


def shaped(shape, dtype=None):
    return jax.ShapeDtypeStruct(shape, bf16 if dtype is None else dtype)


def call(kernel, collective, outs, ins, scratch, flops, moved):
    return pl.pallas_call(
        kernel,
        out_shape=outs,
        in_specs=[SCALARS if s else ANY for s in ins],
        out_specs=[ANY] * len(outs),
        scratch_shapes=scratch,
        compiler_params=pltpu.CompilerParams(
            collective_id=collective, has_side_effects=True, vmem_limit_bytes=VMEM_LIMIT
        ),
        cost_estimate=pl.CostEstimate(flops=flops, bytes_accessed=moved, transcendentals=0),
        name=kernel.__name__,
    )


KEY_ROWS = 2 * STRETCH + 128


def silu(values):
    return values * jax.nn.sigmoid(values)


def head_ones():
    left = lax.broadcasted_iota(jnp.int32, (256, 256), 0) // HD
    right = lax.broadcasted_iota(jnp.int32, (256, 256), 1) // HD
    return (left == right).astype(f32).astype(bf16)


def split_sums(values, ones):
    high = values.astype(bf16)
    rest = (values - high.astype(f32)).astype(bf16)
    return jnp.dot(high, ones, preferred_element_type=f32) + jnp.dot(
        rest, ones, preferred_element_type=f32
    )


def head_only(values, head):
    lane_head = lax.broadcasted_iota(jnp.int32, values.shape, 1) // HD
    return jnp.where(lane_head == head, values.astype(f32), 0.0).astype(bf16)


def key_bias(first_row, rows, valid, flipped):
    shape = (KEY_ROWS, rows) if flipped else (rows, KEY_ROWS)
    slot = lax.broadcasted_iota(jnp.int32, shape, 0 if flipped else 1)
    row = lax.broadcasted_iota(jnp.int32, shape, 1 if flipped else 0) + first_row
    memory = (slot < STRETCH) & (slot.astype(f32) < valid)
    place = slot - STRETCH
    causal = (place >= 0) & (place <= row) & (place.astype(f32) < valid) & (slot < 2 * STRETCH)
    persistent = (slot >= 2 * STRETCH) & (slot < 2 * STRETCH + NP)
    return jnp.where(memory | causal | persistent, 0.0, -1e30)


def unit_rows(values, ones):
    wide_values = values.astype(f32)
    return wide_values * lax.rsqrt(split_sums(wide_values * wide_values, ones) + head_floor)


def nt(left, right):
    return lax.dot_general(left, right, (((1,), (1,)), ((), ())), preferred_element_type=f32)


def tn(left, right):
    return lax.dot_general(left, right, (((0,), (0,)), ((), ())), preferred_element_type=f32)


def slope_of(values):
    sig = jax.nn.sigmoid(values)
    return sig * (1.0 + values * (1.0 - sig))


def forward_layer(
    xl_in, dyl_in, gain_in, wq_in, wk_in, wv_in, wg_in, tq_in, tk_in, tv_in, pk_in, pv_in, one_in, two_in,
    wo_in, rates,
    x_out, qconv_out, kconv_out, vconv_out, qlow_out, klow_out, vlow_out, gate_out, key_out, query_out,
    pre_out, act_out, mis_out, thr_out, ble_out, qpre_out, qact_out, rec_out, one_out, two_out,
    branch_out, here_out, mixed_out, gated_out, dy_out, normed_out,
    x, gain, weights, tq, tk, tv, qconv, kconv, vconv, qlow, klow, vlow, gate, pk, key, query, one, two,
    pre, act, part, mis, thr, ble, qpre, qact, qpart, rec, next_one, next_two, wo, keys, values, bias,
    mixed, gated, bpart, branch, here, dy, norms,
    first, passed, last, q_first, q_passed, q_last, b_first, b_passed, b_last,
    send, recv, local_sems,
):
    places = group_places()
    me, sib, opp, diag = places
    wire, local = Wire(send, recv), Local(local_sems)
    half, block = STRETCH // 2, STRETCH
    lanes = [pl.ds(i * 256, 256) for i in range(4)]
    get_x = local.start(xl_in, x.at[:, cols(me)])
    loads = [
        local.start(s, t)
        for s, t in (
            (wq_in, weights.at[:, lanes[0]]), (wk_in, weights.at[:, lanes[1]]),
            (wv_in, weights.at[:, lanes[2]]), (wg_in, weights.at[:, lanes[3]]), (gain_in, gain),
            (tq_in, tq), (tk_in, tk), (tv_in, tv), (pk_in, pk),
            (pv_in, values.at[pl.ds(2 * block, NP)]),
        )
    ]
    later = [
        local.start(s, t)
        for s, t in ((one_in, one), (two_in, two), (wo_in, wo), (dyl_in, dy.at[:, cols(me)]))
    ]
    pieces = [pl.ds(c * half, half) for c in range(4)]
    blocks = [pl.ds(b * block, block) for b in range(2)]
    ones = head_ones()
    for pad in (qconv, kconv, vconv):
        pad[pl.ds(0, 8), :] = jnp.zeros((8, 256), f32)
    keys[pl.ds(2 * block + NP, 128 - NP), :] = jnp.zeros((128 - NP, 256), bf16)
    values[pl.ds(2 * block + NP, 128 - NP), :] = jnp.zeros((128 - NP, 256), bf16)
    enter_group(sib, opp)
    get_x.wait()
    rows_of_x = [Gather(wire, x, rows, places) for rows in pieces]
    key_joins = [Gather(wire, key, rows, places) for rows in pieces[:2]]
    query_joins = [Gather(wire, query, rows, places) for rows in blocks]
    sums = [Scatter(wire, part, rows, first, passed, last, places) for rows in pieces[:2]]
    misses = [Gather(wire, mis, rows, places) for rows in pieces[:2]]
    qsums = [Scatter(wire, qpart, rows, q_first, q_passed, q_last, places) for rows in blocks]
    reads = [Gather(wire, rec, rows, places) for rows in blocks]
    rows_of_dy = [Gather(wire, dy, rows, places) for rows in blocks]
    bsums = [Scatter(wire, bpart, rows, b_first, b_passed, b_last, places) for rows in pieces]
    joins = [Gather(wire, branch, rows, places) for rows in pieces]
    rows_of_x[0].start()
    rows_of_x[1].start()
    for item in loads:
        item.wait()
    keys[pl.ds(2 * block, NP), :] = unit_rows(pk[...], ones).astype(bf16)

    def project(c):
        rows = pieces[c]
        now = x[rows, :].astype(f32)
        inv = lax.rsqrt(jnp.mean(now * now, axis=1, keepdims=True) + epsilon)
        normed = (now * inv * gain[...]).astype(bf16)
        norms[rows, :] = normed
        for at, (pad, low, taps) in enumerate(
            ((kconv, klow, tk), (qconv, qlow, tq), (vconv, vlow, tv))
        ):
            side = lanes[(1, 0, 2)[at]]
            start = 8 + c * half
            pad[pl.ds(start, half), :] = jnp.dot(
                normed, weights[:, side], preferred_element_type=f32
            )
            conv = pad[pl.ds(start, half), :] * taps[pl.ds(0, 1), :]
            for j in range(1, KW):
                conv = conv + pad[pl.ds(start - j, half), :] * taps[pl.ds(j, 1), :]
            conv = conv * jax.nn.sigmoid(conv)
            low[rows, :] = (unit_rows(conv, ones) if at < 2 else conv).astype(bf16)
            if at == 0 and c < 2:
                key[rows, cols(me)] = klow[rows, :]
                key_joins[c].start()
        query[rows, cols(me)] = qlow[rows, :]
        gate[rows, :] = jnp.dot(normed, weights[:, lanes[3]], preferred_element_type=f32).astype(bf16)

    def hide(c):
        rows = pieces[c]
        hidden = jnp.dot(key[rows, :], one[...], preferred_element_type=f32)
        pre[rows, :] = hidden.astype(bf16)
        act[rows, :] = silu(hidden).astype(bf16)
        part[rows, :] = jnp.dot(act[rows, :], two[...], preferred_element_type=f32).astype(bf16)
        sums[c].start()

    def read(b, weight_one, weight_two):
        rows = blocks[b]
        asked = jnp.dot(query[rows, :], weight_one[...], preferred_element_type=f32)
        qpre[rows, :] = asked.astype(bf16)
        qact[rows, :] = silu(asked).astype(bf16)
        qpart[rows, :] = jnp.dot(
            qact[rows, :], weight_two[...], preferred_element_type=f32
        ).astype(bf16)
        qsums[b].start()

    rows_of_x[0].relay()
    rows_of_x[0].end()
    project(0)
    rows_of_x[1].relay()
    rows_of_x[1].end()
    project(1)
    rows_of_x[2].start()
    for item in later:
        item.wait()
    key_joins[0].relay()
    key_joins[0].end()
    hide(0)
    key_joins[1].relay()
    sums[0].middle()
    key_joins[1].end()
    hide(1)
    rows_of_x[2].relay()
    sums[1].middle()
    rows_of_x[3].start()
    query_joins[0].start()
    for c in range(2):
        rows = pieces[c]
        predicted = sums[c].end()
        index = lax.broadcasted_iota(jnp.int32, (half, 1), 0) + c * half
        scale = jnp.where(index.astype(f32) < rates[0], 1.0 / STRETCH, 0.0)
        mis[rows, cols(me)] = ((predicted - vlow[rows, :].astype(f32)) * scale).astype(bf16)
        misses[c].start()
    for s, t in ((key, key_out), (pre, pre_out), (act, act_out)):
        local.start(s, t, late=True)
    rows_of_x[2].end()
    project(2)
    misses[0].relay()
    rows_of_x[3].relay()
    query_joins[0].relay()
    misses[1].relay()
    for c in range(2):
        rows = pieces[c]
        misses[c].end()
        through = nt(mis[rows, :], two[...])
        thr[rows, :] = through.astype(bf16)
        ble[rows, :] = (through * slope_of(pre[rows, :].astype(f32))).astype(bf16)
    rows_of_x[3].end()
    project(3)
    query_joins[1].start()
    for s, t in (
        (x, x_out), (norms, normed_out), (qconv.at[pl.ds(8, 4 * half)], qconv_out), (kconv.at[pl.ds(8, 4 * half)], kconv_out),
        (vconv.at[pl.ds(8, 4 * half)], vconv_out), (qlow, qlow_out), (klow, klow_out),
        (vlow, vlow_out), (gate, gate_out), (mis, mis_out), (thr, thr_out), (ble, ble_out),
    ):
        local.start(s, t, late=True)
    step_size, keep = rates[1], rates[2]

    def update(c, carried):
        rows = pl.ds(pl.multiple_of(c * half, half), half)
        grad = tn(key[:, rows], ble[...])
        next_one[rows, :] = (keep * one[rows, :].astype(f32) - step_size * grad).astype(bf16)
        grad = tn(act[:, rows], mis[...])
        next_two[rows, :] = (keep * two[rows, :].astype(f32) - step_size * grad).astype(bf16)
        return carried

    query_joins[0].end()
    read(0, one, two)
    lax.fori_loop(0, 2, update, 0)
    qsums[0].middle()
    lax.fori_loop(2, 4, update, 0)
    for s, t in ((next_one, one_out), (next_two, two_out)):
        local.start(s, t, late=True)
    query_joins[1].relay()
    rec[blocks[0], cols(me)] = qsums[0].end().astype(bf16)
    reads[0].start()
    query_joins[1].end()
    read(1, next_one, next_two)
    reads[0].relay()
    qsums[1].middle()
    for s, t in ((query, query_out), (qpre, qpre_out), (qact, qact_out)):
        local.start(s, t, late=True)
    reads[0].end()
    rec[blocks[1], cols(me)] = qsums[1].end().astype(bf16)
    reads[1].start()
    rows_of_dy[0].start()

    def settle(c):
        rows = pieces[c]
        total = bsums[c].end()
        here[rows, :] = total
        branch[rows, cols(me)] = total.astype(bf16)
        joins[c].start()

    for c in range(4):
        b, rows = c // 2, pieces[c]
        if c % 2 == 0:
            if b == 1:
                reads[1].end()
            memory = rec[blocks[b], :]
            made = jnp.dot(memory, weights[:, lanes[1]], preferred_element_type=f32)
            keys[pl.ds(0, block), :] = unit_rows(made, ones).astype(bf16)
            values[pl.ds(0, block), :] = jnp.dot(
                memory, weights[:, lanes[2]], preferred_element_type=f32
            ).astype(bf16)
            keys[pl.ds(block, block), :] = klow[blocks[b], :]
            values[pl.ds(block, block), :] = vlow[blocks[b], :]
        bias[...] = key_bias((c % 2) * half, half, rates[0] - float(b * block), False)

        def one_head(head, total):
            asked = head_only(qlow[rows, :], head)
            scores = nt(asked, keys[...])
            chances = jnp.exp(score_scale * scores + bias[...])
            inv = 1.0 / jnp.sum(chances, axis=1, keepdims=True)
            got = jnp.dot((chances * inv).astype(bf16), values[...], preferred_element_type=f32)
            lane_head = lax.broadcasted_iota(jnp.int32, got.shape, 1) // HD
            return jnp.where(lane_head == head, got, total)

        total = lax.fori_loop(0, 4, one_head, jnp.zeros((half, 256), f32))
        mixed[rows, :] = total.astype(bf16)
        gated[rows, :] = (total * jax.nn.sigmoid(gate[rows, :].astype(f32))).astype(bf16)
        bpart[rows, :] = jnp.dot(gated[rows, :], wo[...], preferred_element_type=f32).astype(bf16)
        bsums[c].start()
        if c == 0:
            reads[1].relay()
            rows_of_dy[0].relay()
            bsums[0].middle()
        if c == 1:
            rows_of_dy[1].start()
            bsums[1].middle()
            settle(0)
        if c == 2:
            rows_of_dy[1].relay()
            bsums[2].middle()
            joins[0].relay()
            settle(1)
    for item in rows_of_dy:
        item.end()
    for s, t in ((rec, rec_out), (dy, dy_out), (mixed, mixed_out), (gated, gated_out)):
        local.start(s, t, late=True)
    bsums[3].middle()
    settle(2)
    joins[1].relay()
    settle(3)
    local.start(here, here_out, late=True)
    joins[2].relay()
    joins[3].relay()
    for item in joins:
        item.end()
    local.start(branch, branch_out, late=True)
    for item in (
        rows_of_x + key_joins + query_joins + sums + misses + qsums + reads + rows_of_dy + bsums + joins
    ):
        item.drain()
    local.finish()


def run_forward_layer(*arrays):
    tokens, lw = arrays[0].shape
    square, wo = arrays[12].shape, arrays[14].shape
    width = square[0]
    tall, full, flat, padded = (tokens, lw), (tokens, width), (STRETCH, width), (KEY_ROWS, lw)
    deep = (tokens + 8, lw)
    vm = lambda shape, dtype=None: pltpu.VMEM(shape, bf16 if dtype is None else dtype)
    return call(
        forward_layer, 1,
        [shaped(full), shaped(tall, f32), shaped(tall, f32), shaped(tall, f32)] + [shaped(tall)] * 4
        + [shaped(flat), shaped(full)] + [shaped(flat)] * 5 + [shaped(full)] * 3
        + [shaped(square)] * 2
        + [shaped(full), shaped(tall, f32), shaped(tall), shaped(tall), shaped(full), shaped(full)],
        (0,) * 15 + (1,),
        [vm(full), vm((1, width), f32), vm((width, width)), vm((KW, lw), f32), vm((KW, lw), f32),
         vm((KW, lw), f32), vm(deep, f32), vm(deep, f32), vm(deep, f32), vm(tall), vm(tall), vm(tall),
         vm(tall), vm((NP, lw)), vm(flat), vm(full), vm(square), vm(square)]
        + [vm(flat)] * 6 + [vm(full)] * 4 + [vm(square)] * 2
        + [vm(wo), vm(padded), vm(padded), vm((STRETCH // 2, KEY_ROWS), f32), vm(tall), vm(tall),
           vm(full), vm(full), vm(tall, f32), vm(full), vm(full)]
        + scatter_room(STRETCH) + scatter_room(tokens) + scatter_room(tokens)
        + sems(100) + [pltpu.SemaphoreType.DMA((64,))],
        20 << 30, 40 << 20,
    )(*arrays)


def wide_places():
    at = lax.axis_index("wide")
    bits = (lax.rem(at, 2), lax.rem(lax.div(at, 2), 2), lax.div(at, 4))
    return bits, tuple(at + step * (1 - 2 * bit) for step, bit in zip((1, 2, 4), bits))


def enter_all(sib, opp, wide):
    barrier = pltpu.get_barrier_semaphore()
    for peer in (sib, opp):
        pl.semaphore_signal(barrier, inc=1, device_id={"narrow": peer}, device_id_type=MESH)
    for peer in wide[1]:
        pl.semaphore_signal(barrier, inc=1, device_id={"wide": peer}, device_id_type=MESH)
    pl.semaphore_wait(barrier, 5)


class WideSum:
    ahead = 2
    orders = ((0, 1, 2), (0, 1, 2), (1, 0, 2), (0, 1, 2))

    def __init__(self, wire, copy_sems, wide, chunks, room, ring):
        bits, peers = wide
        self.mine, self.got, self.more, self.rest, self.done = room
        self.items = []
        for k, (source, start, target, goal, rows) in enumerate(chunks):
            slot = k % ring
            order = self.orders[k % len(self.orders)]
            a, b, c = [bits[d] for d in order]
            pa, pb, pc = [peers[d] for d in order]
            off = lambda bit, size: pl.multiple_of(bit * size, size)
            n, h, q = rows // 2, rows // 4, rows // 8
            first = goal + off(a, n)
            second = first + off(b, h)
            third = second + off(c, q)
            spots = [target.at[pl.ds(at, size)] for at, size in ((third, q), (second, h), (first, n))]
            mine, got = self.mine.at[slot, pl.ds(0, n)], self.got.at[slot, pl.ds(0, n)]
            more, rest = self.more.at[slot, pl.ds(0, h)], self.rest.at[slot, pl.ds(0, q)]
            done = self.done.at[slot, pl.ds(0, q)]
            self.items.append({
                "mine": mine, "got": got, "more": more, "rest": rest, "done": done,
                "kept": self.got.at[slot, pl.ds(off(b, h), h)],
                "left": self.more.at[slot, pl.ds(off(c, q), q)],
                "load": pltpu.make_async_copy(
                    source.at[pl.ds(start + off(a, n), n)], mine, copy_sems.at[2 * k]
                ),
                "keep": pltpu.make_async_copy(done, spots[0], copy_sems.at[2 * k + 1]),
                "one": wire.to(source.at[pl.ds(start + off(1 - a, n), n)], got, pa, "wide"),
                "two": wire.to(self.got.at[slot, pl.ds(off(1 - b, h), h)], more, pb, "wide"),
                "three": wire.to(self.more.at[slot, pl.ds(off(1 - c, q), q)], rest, pc, "wide"),
                "four": wire.to(done, spots[0], pc, "wide"),
                "five": wire.to(spots[1], spots[1], pb, "wide"),
                "six": wire.to(spots[2], spots[2], pa, "wide"),
            })
        count = len(self.items)
        self.steps, self.begun, self.ready, self.wanted, self.next = [], 0, count, 0, 0
        stages = ((self.last, 6), (self.halve, 0), (self.again, 1), (self.total, 2), (self.back, 3),
                  (self.most, 4))
        for i in range(count + 6):
            for stage, lag in stages:
                if 0 <= i - lag < count:
                    self.steps.append((stage, i - lag))

    def open(self, ready):
        self.ready = ready
        self.begin(self.wanted)

    def begin(self, upto):
        self.wanted = max(self.wanted, upto)
        while self.begun < min(upto, self.ready, len(self.items)):
            self.items[self.begun]["load"].start()
            self.items[self.begun]["one"].start()
            self.begun += 1

    def halve(self, i):
        item = self.items[i]
        self.begin(i + 1)
        item["one"].wait_recv()
        self.begin(i + 1 + self.ahead)
        item["load"].wait()
        item["got"][...] = (
            item["got"][...].astype(f32) + item["mine"][...].astype(f32)
        ).astype(bf16)
        item["two"].start()

    def again(self, i):
        item = self.items[i]
        item["two"].wait_recv()
        item["more"][...] = (
            item["more"][...].astype(f32) + item["kept"][...].astype(f32)
        ).astype(bf16)
        item["three"].start()

    def total(self, i):
        item = self.items[i]
        item["three"].wait_recv()
        item["done"][...] = (
            item["rest"][...].astype(f32) + item["left"][...].astype(f32)
        ).astype(bf16)
        for name in ("one", "two", "three"):
            item[name].wait_send()
        item["four"].start()
        item["keep"].start()

    def back(self, i):
        item = self.items[i]
        item["four"].wait_recv()
        item["keep"].wait()
        item["four"].wait_send()
        item["five"].start()

    def most(self, i):
        item = self.items[i]
        item["five"].wait_recv()
        item["five"].wait_send()
        item["six"].start()

    def last(self, i):
        self.items[i]["six"].wait_recv()
        self.items[i]["six"].wait_send()

    def go(self, count=None):
        stop = len(self.steps) if count is None else min(self.next + count, len(self.steps))
        while self.next < stop:
            step, i = self.steps[self.next]
            if step == self.halve and i >= self.ready:
                break
            step(i)
            self.next += 1


def wide_room(ring):
    return [
        pltpu.VMEM((ring, rows, 1024), bf16) for rows in (128, 128, 64, 32, 32)
    ]


def moved_down(values, offset):
    row = lax.broadcasted_iota(jnp.int32, values.shape, 0)
    return jnp.where(row < offset, 0.0, pltpu.roll(values, offset, 0))


def moved_up(values, offset):
    rows = values.shape[0]
    row = lax.broadcasted_iota(jnp.int32, values.shape, 0)
    return jnp.where(row >= rows - offset, 0.0, pltpu.roll(values, rows - offset, 0))


RING = 10


def backward_layer(
    query_in, key_in, value_in, rec_in, wq_in, wk_in, wv_in, wg_in, pk_in, pv_in, gate_in, wo_in,
    mixed_in, gated_in, keys_in, queries_in, pre_in, act_in, mis_in, thr_in, ble_in, qpre_in,
    qact_in, one_in, two_in, next_one_in, next_two_in, x_in, gain_in, tq_in, tk_in, tv_in, cq_in, ck_in, cv_in,
    gaintwo_in, branch_in, here_in, dy_in, fgate_in, fup_in, fdown_in, normed_in, rates,
    ig_out, lo_out, gg_out, gu_out, gd_out, gwo_out, gwg_out, gone_out, gtwo_out, packed_out,
    extra_out,
    gg_mid, gu_mid, gd_mid, bm_mid, gwo_mid, gwg_mid, gone_mid, gtwo_mid, packed_mid, extra_mid, bgate_mid, gmk_mid, gmv_mid, bq_mid, bk_mid, bv_mid,
    qpart_mid, kpart_mid, vpart_mid,
    brec, late, bb, gaintwo, pkacc, pvacc,
    a_first, a_passed, a_last, l_first, l_passed, l_last, m_first, m_passed, m_last,
    q_first, q_passed, q_last, k_first, k_passed, k_last, t_first, t_passed, t_last,
    mine, got, more, rest, done, send, recv, local_sems, copy_sems,
):
    places = group_places()
    me, sib, opp, diag = places
    wire, local = Wire(send, recv), Local(local_sems)
    wide = wide_places()
    half, block = STRETCH // 2, STRETCH
    tokens, width = x_in.shape
    slim = wo_in.shape[0]
    chunks = []
    for source, target in (
        (gg_mid, gg_out), (gu_mid, gu_out), (gd_mid, gd_out), (gwo_mid, gwo_out), (gwg_mid, gwg_out),
        (gone_mid, gone_out), (gtwo_mid, gtwo_out), (packed_mid, packed_out),
    ):
        chunks += [(source, i * 256, target, i * 256, 256) for i in range(source.shape[0] // 256)]
    chunks += [(extra_mid, 0, extra_out, 0, 128)]
    adds = WideSum(wire, copy_sems, wide, chunks, (mine, got, more, rest, done), RING)
    adds.ready = 0
    adds.ahead = 4
    adds.begin(adds.ahead)
    pieces = [pl.ds(c * half, half) for c in range(2)]
    blocks = [pl.ds(b * block, block) for b in range(2)]
    whole = pl.ds(0, block)
    lanes = [pl.ds(i * 256, 256) for i in range(4)]
    early, bmis = bb.at[pl.ds(0, block)], bb.at[pl.ds(block, block)]
    early_join = Gather(wire, early, whole, places)
    misses = [Gather(wire, bmis, rows, places) for rows in pieces]
    recs = [Gather(wire, brec, rows, places) for rows in pieces]
    outs = []
    for b, half_sum in enumerate((brec, late)):
        side = pl.ds(b * block, block)
        outs += [
            Scatter(
                wire, half_sum, rows, q_first.at[:, side], q_passed.at[side], q_last.at[side], places
            )
            for rows in pieces
        ]

    def feed(
        x, branch, dy, gain, gate, up, down, normed, hidden, bup, bffn, part, bm,
        first_sum,
    ):
        loads = [
            local.start(s, t)
            for s, t in (
                (x_in, x), (branch_in, branch), (gaintwo_in, gain), (fgate_in, gate), (fup_in, up),
                (dy_in, dy), (fdown_in, down),
            )
        ]
        size = 256
        count = tokens // size
        parts_of = [pl.ds(c * size, size) for c in range(count)]
        enter_all(sib, opp, wide)
        for item in loads:
            item.wait()
        sums = [Scatter(wire, part, rows, t_first, t_passed, t_last, places) for rows in parts_of]
        joins = [Gather(wire, bb, rows, places) for rows in parts_of]
        gaintwo[...] = jnp.zeros_like(gaintwo)

        def settle(c):
            rows = parts_of[c]
            back = sums[c].end().astype(bf16).astype(f32) + dy[rows, cols(me)].astype(f32)
            bm[rows, :] = back
            bb[rows, cols(me)] = back.astype(bf16)
            joins[c].start()

        for c in range(count):
            rows = parts_of[c]
            middle = x[rows, :].astype(f32) + branch[rows, :].astype(f32)
            inv = lax.rsqrt(jnp.mean(middle * middle, axis=1, keepdims=True) + epsilon)
            normed[rows, :] = (middle * inv * gain[...]).astype(bf16)
            pre = jnp.dot(normed[rows, :], gate[...], preferred_element_type=f32)
            lift = jnp.dot(normed[rows, :], up[...], preferred_element_type=f32)
            back = nt(dy[rows, :], down[...])
            sig = jax.nn.sigmoid(pre)
            act = pre * sig
            hidden[rows, :] = (act * lift).astype(bf16)
            bup[rows, :] = (back * act).astype(bf16)
            bffn[rows, :] = (back * lift * (sig * (1.0 + pre * (1.0 - sig)))).astype(bf16)

        def grads(left, right, keep, target, k):
            rows = parts_of[k]
            keep[rows, :] = tn(left[:, rows], right[...]).astype(bf16)
            return local.start(keep.at[rows], target.at[rows])

        copies = []
        for c in range(count):
            rows = parts_of[c]
            copies.append(grads(normed, bffn, first_sum, gg_mid, c))
            back = nt(bffn[rows, :], gate[...]) + nt(bup[rows, :], up[...])
            middle = x[rows, :].astype(f32) + branch[rows, :].astype(f32)
            inv = lax.rsqrt(jnp.mean(middle * middle, axis=1, keepdims=True) + epsilon)
            unit = middle * inv
            gaintwo[...] += jnp.sum(back * unit, axis=0, keepdims=True)
            back = back * gain[...]
            part[rows, :] = (
                inv * (back - unit * jnp.mean(back * unit, axis=1, keepdims=True))
            ).astype(bf16)
            sums[c].start()
            copies.pop(0).wait()
            adds.open(adds.ready + 1)
            if c >= 1:
                sums[c - 1].middle()
                adds.go(1)
            if c >= 2:
                settle(c - 2)
            if c >= 3:
                joins[c - 3].relay()
        copies = [grads(normed, bup, gate, gu_mid, 0)]
        sums[3].middle()
        settle(2)
        joins[1].relay()
        for k in range(1, 4):
            copies.append(grads(normed, bup, gate, gu_mid, k))
            if k == 2:
                settle(3)
                joins[2].relay()
        adds.go(1)
        for c, rows in enumerate(parts_of):
            (brec, late)[c // 2][pieces[c % 2], :] = jnp.dot(
                hidden[rows, :], down[...], preferred_element_type=f32
            ).astype(bf16)
            outs[c].start()
        for item in copies:
            item.wait()
        adds.open(adds.ready + 4)
        joins[3].relay()
        adds.go(2)
        copies = []
        for k in range(4):
            copies.append(grads(hidden, dy, up, gd_mid, k))
        local.start(bm, bm_mid, late=True)
        adds.go(2)
        for item in joins:
            item.end()
        for item in copies:
            item.wait()
        adds.open(adds.ready + 4)
        for item in sums + joins:
            item.drain()
        local.finish()

    def attend(
        query, key, value, rec, wk, wv, gate, wo, mixed, gated, keys, values, bias, bmix, bgate,
        pk, gwo, gmk, gmv, bq, bk, bv, kacc, vacc, bmk, bmv, part,
        normed, gwg, xl, here, out,
    ):
        loads = [
            local.start(s, t)
            for s, t in (
                (normed_in, normed), (wo_in, wo), (gate_in, gate), (mixed_in, mixed), (gated_in, gated),
                (rec_in, rec), (wk_in, wk), (wv_in, wv), (query_in, query), (key_in, key),
                (value_in, value), (pk_in, pk), (x_in.at[:, cols(me)], xl), (here_in, here),
                (pv_in, values.at[pl.ds(2 * block, NP)]),
            )
        ]
        keys[pl.ds(2 * block + NP, 128 - NP), :] = jnp.zeros((128 - NP, 256), bf16)
        values[pl.ds(2 * block + NP, 128 - NP), :] = jnp.zeros((128 - NP, 256), bf16)
        pkacc[...] = jnp.zeros_like(pkacc)
        pvacc[...] = jnp.zeros_like(pvacc)
        gmk[...] = jnp.zeros_like(gmk)
        gmv[...] = jnp.zeros_like(gmv)
        for item in outs:
            item.middle()
        for item in loads:
            item.wait()

        def through_gate(c, carried):
            rows = pl.ds(pl.multiple_of(c * half, half), half)
            back = nt(bb[rows, :], wo[...])
            sig = jax.nn.sigmoid(gate[rows, :].astype(f32))
            bmix[rows, :] = (back * sig).astype(bf16)
            bgate[rows, :] = (back * mixed[rows, :].astype(f32) * sig * (1.0 - sig)).astype(bf16)
            return carried

        lax.fori_loop(0, 4, through_gate, 0)
        local.start(bgate, bgate_mid, late=True)
        gwo[...] = tn(gated[...], bb[...]).astype(bf16)
        out_copy = local.start(gwo, gwo_mid)
        for i, side in enumerate(lanes):
            gwg[:, side] = tn(normed[:, side], bgate[...]).astype(bf16)
        gate_copy = local.start(gwg, gwg_mid)
        ones = head_ones()
        keys[pl.ds(2 * block, NP), :] = unit_rows(pk[...], ones).astype(bf16)
        sums = [Scatter(wire, part, rows, a_first, a_passed, a_last, places) for rows in pieces]
        adds.go(3)
        out_copy.wait()
        gate_copy.wait()
        adds.open(adds.ready + 2)
        for b in (1, 0):
            rows = blocks[b]
            memory = rec[rows, :]
            made = jnp.dot(memory, wk[...], preferred_element_type=f32)
            inv = lax.rsqrt(split_sums(made * made, ones) + head_floor)
            keys[pl.ds(0, block), :] = (made * inv).astype(bf16)
            values[pl.ds(0, block), :] = jnp.dot(
                memory, wv[...], preferred_element_type=f32
            ).astype(bf16)
            keys[pl.ds(block, block), :] = key[rows, :]
            values[pl.ds(block, block), :] = value[rows, :]
            bias[...] = key_bias(0, block, rates[0] - float(b * block), True)
            kacc[...] = jnp.zeros_like(kacc)
            vacc[...] = jnp.zeros_like(vacc)

            def one_head(head, total):
                asked = head_only(query[rows, :], head)
                back = head_only(bmix[rows, :], head)
                weights = jnp.exp(score_scale * nt(keys[...], asked) + bias[...])
                weights = weights * (1.0 / jnp.sum(weights, axis=0, keepdims=True))
                vacc[...] += jnp.dot(weights.astype(bf16), back, preferred_element_type=f32)
                slope = nt(values[...], back)
                slope = (
                    weights * (slope - jnp.sum(weights * slope, axis=0, keepdims=True))
                ).astype(bf16)
                kacc[...] += jnp.dot(slope, asked, preferred_element_type=f32)
                read = tn(slope, keys[...])
                lane_head = lax.broadcasted_iota(jnp.int32, read.shape, 1) // HD
                return jnp.where(lane_head == head, read, total)

            asked_back = lax.fori_loop(0, 1, one_head, jnp.zeros((block, 256), f32))
            adds.go(2)
            asked_back = lax.fori_loop(1, 2, one_head, asked_back)
            adds.go(1)
            asked_back = lax.fori_loop(2, 3, one_head, asked_back)
            adds.go(2)
            bq[rows, :] = score_scale * lax.fori_loop(3, 4, one_head, asked_back)
            adds.go(1)
            bk[rows, :] = score_scale * kacc[pl.ds(block, block), :]
            bv[rows, :] = vacc[pl.ds(block, block), :]
            pkacc[...] += score_scale * kacc[pl.ds(2 * block, NP), :]
            pvacc[...] += vacc[pl.ds(2 * block, NP), :]
            unit = jnp.dot(memory, wk[...], preferred_element_type=f32) * inv
            back = score_scale * kacc[pl.ds(0, block), :]
            bmk[...] = ((back - unit * split_sums(back * unit, ones)) * inv).astype(bf16)
            bmv[...] = vacc[pl.ds(0, block), :].astype(bf16)
            if b == 1:
                for c, item in enumerate(outs):
                    side = pl.ds(c * half, half)
                    done_rows = xl[side, :].astype(f32) + here[side, :] + item.end()
                    out[side, :] = done_rows.astype(bf16)
                    item.drain()
                local.start(out, lo_out, late=True)
            for c in range(2):
                target = part if b == 1 else late
                target[pieces[c], :] = (
                    nt(bmk[pieces[c], :], wk[...]) + nt(bmv[pieces[c], :], wv[...])
                ).astype(bf16)
                if b == 1:
                    sums[c].start()
                else:
                    brec[pieces[c], cols(me)] = sums[c].end().astype(bf16)
                    recs[c].start()
            gmk[...] += tn(memory, bmk[...])
            if b == 1:
                sums[0].middle()
            gmv[...] += tn(memory, bmv[...])
            if b == 1:
                sums[1].middle()
            adds.go(2)
        for s, t in ((gmk, gmk_mid), (gmv, gmv_mid), (bq, bq_mid), (bk, bk_mid), (bv, bv_mid)):
            local.start(s, t, late=True)
        for item in recs:
            item.relay()
        for item in sums:
            item.drain()
        adds.go(2)
        local.finish()

    def remember(
        key, query, pre, act, mis, thr, ble, qpre, qact, one, two, next_one, next_two, cone, ctwo, bble,
        bthr, bqm, mpart, bpre, klow, qlow, kout, qout, vout,
    ):
        loads = [
            local.start(s, t)
            for s, t in (
                (next_two_in, next_two), (qpre_in, qpre), (next_one_in, next_one),
                (queries_in, query), (qact_in, qact), (keys_in, key), (pre_in, pre), (act_in, act),
                (two_in, two), (mis_in, mis), (one_in, one), (thr_in, thr), (ble_in, ble),
            )
        ]
        lates = Scatter(wire, late, whole, l_first, l_passed, l_last, places)
        sums = [Scatter(wire, mpart, rows, m_first, m_passed, m_last, places) for rows in pieces]
        asks = [Scatter(wire, qlow, rows, q_first, q_passed, q_last, places) for rows in blocks]
        tells = [Scatter(wire, klow, rows, k_first, k_passed, k_last, places) for rows in pieces]
        lates.start()
        for item in loads:
            item.wait()
        for item in recs:
            item.end()
            item.drain()
        step_size, keep = rates[1], rates[2]

        def ask_back(c, source, row_start, weight_one, weight_two):
            rows = pl.ds(row_start + c * half, half)
            back = nt(source[pieces[c], :], weight_two[...])
            bqm[pieces[c], :] = (back * slope_of(qpre[rows, :].astype(f32))).astype(bf16)
            qlow[rows, :] = nt(bqm[pieces[c], :], weight_one[...]).astype(bf16)

        for c in range(2):
            ask_back(c, brec, block, next_one, next_two)
            if c == 0:
                lates.middle()
                adds.go(2)
        asks[1].start()
        early[:, cols(me)] = lates.end().astype(bf16)
        early_join.start()
        adds.go(2)

        def first_sums(c, carried):
            rows = pl.ds(pl.multiple_of(c * half, half), half)
            grad = tn(query[blocks[1], rows], bqm[...])
            cone[rows, :] = keep * grad
            next_one[rows, :] = (-step_size * grad).astype(bf16)
            grad = tn(qact[blocks[1], rows], brec[...])
            ctwo[rows, :] = keep * grad
            next_two[rows, :] = (-step_size * grad).astype(bf16)
            return carried

        for c in range(0, 4, 2):
            lax.fori_loop(c, c + 2, first_sums, 0)
            adds.go(3 if c else 2)
        for c in range(2):
            rows = pieces[c]
            back = jnp.dot(key[rows, :], next_one[...], preferred_element_type=f32)
            bble[rows, :] = back.astype(bf16)
            bthr[rows, :] = (back * slope_of(pre[rows, :].astype(f32))).astype(bf16)
            mpart[rows, :] = (
                jnp.dot(act[rows, :], next_two[...], preferred_element_type=f32)
                + jnp.dot(bthr[rows, :], two[...], preferred_element_type=f32)
            ).astype(bf16)
            sums[c].start()
            if c == 0:
                early_join.relay()
                adds.go(2)
        sums[0].middle()
        asks[1].middle()
        adds.go(3)
        sums[1].middle()
        early_join.end()
        for c in range(2):
            ask_back(c, early, 0, one, two)
            adds.go(2)
        asks[0].start()
        for c in range(2):
            rows = pieces[c]
            back = sums[c].end().astype(bf16)
            index = lax.broadcasted_iota(jnp.int32, (half, 1), 0) + c * half
            scale = jnp.where(index.astype(f32) < rates[0], 1.0 / STRETCH, 0.0)
            bmis[rows, cols(me)] = back
            misses[c].start()
            vout[rows, :] = -(back.astype(f32) * scale)
        local.start(vout, vpart_mid, late=True)

        def second_sums(c, carried):
            rows = pl.ds(pl.multiple_of(c * half, half), half)
            cone[rows, :] += tn(query[blocks[0], rows], bqm[...])
            ctwo[rows, :] += tn(bthr[:, rows], mis[...]) + tn(qact[blocks[0], rows], early[...])
            return carried

        lax.fori_loop(0, 1, second_sums, 0)
        adds.go(2)
        lax.fori_loop(1, 2, second_sums, 0)
        misses[0].relay()
        asks[0].middle()
        adds.go(3)
        lax.fori_loop(2, 3, second_sums, 0)
        misses[1].relay()
        adds.go(2)
        lax.fori_loop(3, 4, second_sums, 0)
        adds.go(2)
        for c in range(2):
            rows = pieces[c]
            misses[c].end()
            misses[c].drain()
            index = lax.broadcasted_iota(jnp.int32, (half, 1), 0) + c * half
            scale = jnp.where(index.astype(f32) < rates[0], 1.0 / STRETCH, 0.0)
            bmis[rows, :] = (bmis[rows, :].astype(f32) * scale).astype(bf16)
            values = pre[rows, :].astype(f32)
            sig = jax.nn.sigmoid(values)
            drop = 1.0 - sig
            slant = sig * drop
            curve = slant * (1.0 + values * drop) + sig * (drop - values * slant)
            back = nt(mis[rows, :], next_two[...]) + nt(bmis[rows, :], two[...])
            bpre[rows, :] = (
                back * (sig * (1.0 + values * drop))
                + bble[rows, :].astype(f32) * thr[rows, :].astype(f32) * curve
            ).astype(bf16)
            klow[rows, :] = (
                nt(ble[rows, :], next_one[...]) + nt(bpre[rows, :], one[...])
            ).astype(bf16)
            tells[c].start()
            adds.go(3 if c else 2)
        tells[0].middle()
        tells[1].middle()

        def last_sums(c, carried):
            rows = pl.ds(pl.multiple_of(c * half, half), half)
            next_one[rows, :] = (cone[rows, :] + tn(key[:, rows], bpre[...])).astype(bf16)
            next_two[rows, :] = (ctwo[rows, :] + tn(act[:, rows], bmis[...])).astype(bf16)
            return carried

        for c in range(0, 4, 2):
            lax.fori_loop(c, c + 2, last_sums, 0)
            if c == 0:
                adds.go(2)
        local.start(next_one, gone_mid, late=True)
        local.start(next_two, gtwo_mid, late=True)
        adds.go(3)
        for b in (1, 0):
            qout[blocks[b], :] = asks[b].end()
        local.start(qout, qpart_mid, late=True)
        for c in range(2):
            kout[pieces[c], :] = tells[c].end()
        local.start(kout, kpart_mid, late=True)
        for item in [lates, early_join] + sums + asks + tells:
            item.drain()
        local.finish()
        adds.open(adds.ready + 2 * width // 256)

    def finish(
        x, gain, weights, tq, tk, tv, qpre, kpre, vpre, bq, bk, bv, qpart, kpart, vpart, cot, gmk, gmv, pk,
        bm, extra, packed, normed, part, ig, conv_rows,
    ):
        loads = [
            local.start(s, t)
            for s, t in (
                (cq_in, qpre), (bq_mid, bq), (qpart_mid, qpart), (tq_in, tq), (tk_in, tk),
                (tv_in, tv), (ck_in, kpre),
                (bk_mid, bk), (kpart_mid, kpart), (cv_in, vpre), (bv_mid, bv), (vpart_mid, vpart),
                (x_in, x), (gain_in, gain), (wq_in, weights.at[:, lanes[0]]),
                (wk_in, weights.at[:, lanes[1]]), (wv_in, weights.at[:, lanes[2]]),
                (wg_in, weights.at[:, lanes[3]]), (bgate_mid, cot.at[:, lanes[3]]),
                (gmk_mid, gmk), (gmv_mid, gmv), (pk_in, pk), (bm_mid, bm),
            )
        ]
        adds.go(2)
        for item in loads:
            item.wait()
        ones = head_ones()

        def through_conv(pre, taps, at, back, normal):
            values = pre[...]
            conv = values * taps[pl.ds(0, 1), :]
            for j in range(1, KW):
                conv = conv + moved_down(values, j) * taps[pl.ds(j, 1), :]
            sig = jax.nn.sigmoid(conv)
            if normal:
                act = conv * sig
                inv = lax.rsqrt(split_sums(act * act, ones) + head_floor)
                unit = act * inv
                back = (back - unit * split_sums(back * unit, ones)) * inv
            back = back * (sig * (1.0 + conv * (1.0 - sig)))
            result = back * taps[pl.ds(0, 1), :]
            conv_rows[pl.ds(at, 1), :] = jnp.sum(back * values, axis=0, keepdims=True)
            for j in range(1, KW):
                conv_rows[pl.ds(at + j, 1), :] = jnp.sum(
                    back * moved_down(values, j), axis=0, keepdims=True
                )
                result = result + moved_up(back, j) * taps[pl.ds(j, 1), :]
            return result.astype(bf16)

        conv_rows[...] = jnp.zeros_like(conv_rows)
        cot[:, lanes[0]] = through_conv(qpre, tq, 0, bq[...] + qpart[...], True)
        adds.go(2)
        bk[whole, :] += kpart[...]
        cot[:, lanes[1]] = through_conv(kpre, tk, KW, bk[...], True)
        adds.go(2)
        bv[whole, :] += vpart[...]
        cot[:, lanes[2]] = through_conv(vpre, tv, 2 * KW, bv[...], False)
        adds.go(2)
        rows_of_x = [pl.ds(c * 256, 256) for c in range(tokens // 256)]
        sums = [Scatter(wire, part, rows, t_first, t_passed, t_last, places) for rows in rows_of_x]
        tail_rows = pl.ds(tokens, 16)
        gains = Scatter(wire, part, tail_rows, t_first, t_passed, t_last, places)
        gain_sum = jnp.zeros((1, width), f32)
        for c, rows in enumerate(rows_of_x):
            back = nt(cot[rows, :], weights[...])
            values = x[rows, :].astype(f32)
            inv = lax.rsqrt(jnp.mean(values * values, axis=1, keepdims=True) + epsilon)
            unit = values * inv
            normed[rows, :] = (unit * gain[...]).astype(bf16)
            gain_sum = gain_sum + jnp.sum(back * unit, axis=0, keepdims=True)
            back = back * gain[...]
            part[rows, :] = (
                inv * (back - unit * jnp.mean(back * unit, axis=1, keepdims=True))
            ).astype(bf16)
            sums[c].start()
            if c >= 1:
                sums[c - 1].middle()
            adds.go(2)
        row = lax.broadcasted_iota(jnp.int32, (16, width), 0)
        part[tail_rows, :] = jnp.where(
            row == 0, gain_sum, jnp.where(row == 1, gaintwo[...], 0.0)
        ).astype(bf16)
        gains.start()
        for c in range(width // 256):
            made = tn(normed[:, rows_of_x[c]], cot[:, pl.ds(0, 768)])
            packed[pl.ds(0, 256), lanes[c]] = made[:, 0:256].astype(bf16)
            packed[pl.ds(256, 256), lanes[c]] = (made[:, 256:512] + gmk[rows_of_x[c], :]).astype(bf16)
            packed[pl.ds(512, 256), lanes[c]] = (made[:, 512:768] + gmv[rows_of_x[c], :]).astype(bf16)
            if c % 2:
                adds.go(2)
        pack_copy = local.start(packed, packed_mid)
        sums[-1].middle()
        gains.middle()
        extra[...] = jnp.zeros_like(extra)
        start = pk[...].astype(f32)
        inv = lax.rsqrt(split_sums(start * start, ones) + head_floor)
        unit = start * inv
        back = pkacc[...]
        top = pl.ds(0, 16)
        extra[top, lanes[0]] = ((back - unit * split_sums(back * unit, ones)) * inv).astype(bf16)
        extra[top, lanes[1]] = pvacc[...].astype(bf16)
        extra[top, lanes[2]] = conv_rows[...].astype(bf16)
        pack_copy.wait()
        adds.open(adds.ready + 3)
        adds.go(2)
        extra[top, lanes[3]] = gains.end().astype(bf16)
        local.start(extra, extra_mid, late=True)
        for c, rows in enumerate(rows_of_x):
            ig[rows, :] = bm[rows, :] + sums[c].end()
        local.start(ig, ig_out, late=True)
        local.finish()
        adds.open(len(chunks))
        for item in sums + [gains]:
            item.drain()

    vm = lambda shape, dtype=None: pltpu.VMEM(shape, bf16 if dtype is None else dtype)
    lw = query_in.shape[1]
    tall, full, flat, weight = (tokens, lw), (tokens, width), (block, width), (width, lw)
    padded, small, square = (KEY_ROWS, lw), (block, lw), one_in.shape
    row = (1, width)
    pl.run_scoped(
        feed,
        vm(full), vm(full), vm(full), vm(row, f32), vm(square), vm(square), vm(square),
        vm(full), vm(full), vm(full), vm(full), vm(full), vm(tall, f32), vm(square),
    )
    pl.run_scoped(
        attend,
        vm(tall), vm(tall), vm(tall), vm(full), vm(weight), vm(weight), vm(tall), vm((lw, width)),
        vm(tall), vm(tall), vm(padded), vm(padded), vm((KEY_ROWS, block), f32), vm(tall),
        vm(tall), vm((NP, lw)), vm((lw, width)), vm(weight, f32), vm(weight, f32), vm(tall, f32), vm(tall, f32),
        vm(tall, f32), vm(padded, f32), vm(padded, f32), vm(small), vm(small), vm(flat), vm(full), vm((256, width)),
        vm(tall), vm(tall, f32), vm(tall),
    )
    pl.run_scoped(
        remember,
        vm(flat), vm(full), vm(flat), vm(flat), vm(flat), vm(flat), vm(flat), vm(full), vm(full),
        vm(square), vm(square), vm(square), vm(square), vm(square, f32), vm(square, f32), vm(flat),
        vm(flat), vm(flat), vm(flat), vm(flat), vm(flat), vm(full), vm(small, f32), vm(tall, f32),
        vm(small, f32),
    )
    pl.run_scoped(
        finish,
        vm(full), vm(row, f32), vm((width, width)), vm((KW, lw), f32), vm((KW, lw), f32),
        vm((KW, lw), f32), vm(tall, f32),
        vm(tall, f32), vm(tall, f32), vm(tall, f32), vm(tall, f32), vm(tall, f32), vm(tall, f32),
        vm(small, f32), vm(small, f32), vm(full), vm(weight, f32), vm(weight, f32), vm((NP, lw)),
        vm(tall, f32), vm((128, width)), vm((768, width)), vm(full),
        vm((tokens + 16, width)), vm(tall, f32), vm((16, 256), f32),
    )
    adds.go()


def run_backward_layer(*arrays):
    query, wo, one, x = arrays[0], arrays[11], arrays[23], arrays[27]
    tokens, width = x.shape
    lw = query.shape[1]
    tall, flat, weight, square = (tokens, lw), (STRETCH, width), (width, lw), (width, width)
    small, packed, extra = (STRETCH, lw), (3 * lw, width), (128, width)
    count = (5 * width + 5 * lw) // 256 + 1
    vm = lambda shape, dtype=None: pltpu.VMEM(shape, bf16 if dtype is None else dtype)
    sums = [shaped(square)] * 3 + [shaped((lw, width))] * 2 + [shaped(one.shape)] * 2
    sums += [shaped(packed), shaped(extra)]
    return call(
        backward_layer, 4,
        [shaped(tall, f32), shaped(tall)] + sums
        + [shaped(square)] * 3 + [shaped(tall, f32)] + sums[3:]
        + [shaped(tall), shaped(weight, f32), shaped(weight, f32), shaped(tall, f32),
           shaped(tall, f32), shaped(tall, f32), shaped(tall, f32), shaped(small, f32),
           shaped(small, f32)],
        (0,) * (len(arrays) - 1) + (1,),
        [vm(flat), vm(flat), vm((tokens, width)), vm((1, width), f32), vm((NP, lw), f32),
         vm((NP, lw), f32)]
        + scatter_room(STRETCH) * 3 + scatter_room(tokens) + scatter_room(STRETCH)
        + scatter_room(tokens + 16) + wide_room(RING)
        + sems(6 * count + 120)
        + [pltpu.SemaphoreType.DMA((160,)), pltpu.SemaphoreType.DMA((2 * count,))],
        65 << 30, 120 << 20,
    )(*arrays)[:11]


def widen(*refs):
    count = (len(refs) - 8) // 2
    for source, target in zip(refs[:count], refs[count + 1 : 2 * count + 1]):
        target[...] = source[...].astype(target.dtype)
    extra, small = refs[count], refs[2 * count + 1 :]
    starts = ((0, 0), (0, 256), (0, 512), (KW, 512), (2 * KW, 512), (0, 768), (1, 768))
    for target, (row, lane) in zip(small, starts):
        rows = target.shape[0]
        target[...] = extra[...].astype(f32)[row : row + rows, lane : lane + 256]


def run_widen(flat, quarter, same, extra):
    steps = 4
    ins, outs, shapes = [], [], []
    for v in flat:
        spec = pl.BlockSpec((v.shape[0] // steps, v.shape[1]), lambda i: (i, 0))
        ins.append(spec)
        outs.append(spec)
        shapes.append(shaped(v.shape, f32))
    for v, place in quarter:
        ins.append(pl.BlockSpec((256, 256), lambda i, place=place: (place, i)))
        outs.append(pl.BlockSpec((256, 256), lambda i: (i, 0)))
        shapes.append(shaped((1024, 256), f32))
    for v in same:
        spec = pl.BlockSpec((v.shape[0] // steps, v.shape[1]), lambda i: (i, 0))
        ins.append(spec)
        outs.append(spec)
        shapes.append(shaped(v.shape, v.dtype))
    ins.append(pl.BlockSpec((16, extra.shape[1]), lambda i: (0, 0)))
    for rows in (NP, NP, KW, KW, KW, 1, 1):
        outs.append(pl.BlockSpec((rows, 256), lambda i: (0, 0)))
        shapes.append(shaped((rows, 256), f32))
    return pl.pallas_call(
        widen, out_shape=shapes, grid=(steps,), in_specs=ins, out_specs=outs,
        compiler_params=pltpu.CompilerParams(vmem_limit_bytes=VMEM_LIMIT), name="widen",
    )(*flat, *(v for v, place in quarter), *same, extra)


def plain_body(
    layer_input,
    out_grad,
    lengths,
    plan,
    norm1_gain,
    w_query,
    w_key,
    w_value,
    w_gate,
    conv_query,
    conv_key,
    conv_value,
    persist_key,
    persist_value,
    mem_w1,
    mem_w2,
    w_out,
    norm2_gain,
    ffn_gate,
    ffn_up,
    ffn_down,
):
    tokens_here = layer_input.shape[0]
    local_width = w_query.shape[1]
    heads_here = local_width // HD
    blocks = tokens_here // STRETCH
    places = jnp.arange(tokens_here)
    row_mask = (places < lengths[0]).astype(f32)
    block_mask = row_mask.reshape(blocks, STRETCH)
    levels = plan[0].astype(f32)
    column_start = lax.axis_index("narrow") * local_width

    def rows_of(values, b):
        return values[b * STRETCH : (b + 1) * STRETCH]

    whole_x = gather_columns(layer_input).astype(f32)
    whole_dy = gather_columns(out_grad)
    inv_one = lax.rsqrt(jnp.mean(whole_x * whole_x, axis=1, keepdims=True) + epsilon)
    unit_one = whole_x * inv_one
    normed_one = (unit_one * norm1_gain).astype(bf16)
    key_pre = product(normed_one, w_key)
    query_pre = product(normed_one, w_query)
    value_pre = product(normed_one, w_value)
    gate_pre = product(normed_one, w_gate)
    key_conv = causal_conv(key_pre, conv_key)
    query_conv = causal_conv(query_pre, conv_query)
    value_conv = causal_conv(value_pre, conv_value)
    key_unit, key_inv = head_norm(jax.nn.silu(key_conv))
    query_unit, query_inv = head_norm(jax.nn.silu(query_conv))
    query_low = query_unit.astype(bf16)
    key_low = key_unit.astype(bf16)
    value_low = jax.nn.silu(value_conv).astype(bf16)

    weight_one, weight_two = mem_w1.astype(f32), mem_w2.astype(f32)
    moment_one = moment_two = None
    saved = []
    for b in range(blocks):
        step_size, momentum, forget = plan_rates(levels[b])
        kept = {"first": weight_one.astype(bf16), "second": weight_two.astype(bf16)}
        mask_rows = block_mask[b][:, None]
        if b < blocks - 1:
            key_rows = gather_columns(rows_of(key_low, b))
            hidden_pre = product(key_rows, kept["first"])
            hidden_act = jax.nn.silu(hidden_pre).astype(bf16)
            predicted = scatter_columns(product(hidden_act, kept["second"]))
            mismatch_here = (
                (predicted - rows_of(value_low, b).astype(f32)) * (mask_rows / STRETCH)
            ).astype(bf16)
            mismatch = gather_columns(mismatch_here)
        query_rows = gather_columns(rows_of(query_low, b))
        query_mem = product(query_rows, kept["first"])
        query_act = jax.nn.silu(query_mem).astype(bf16)
        retrieved = scatter_columns(product(query_act, kept["second"]))
        kept["recalled"] = gather_columns(retrieved.astype(bf16))
        kept.update(query_rows=query_rows, query_mem=query_mem, query_act=query_act)
        if b < blocks - 1:
            through = inner_right(mismatch, kept["second"])
            blended = (through * silu_grad(hidden_pre)).astype(bf16)
            grad_one = inner_left(key_rows, blended)
            grad_two = inner_left(hidden_act, mismatch)
            if moment_one is None:
                moment_one, moment_two = -step_size * grad_one, -step_size * grad_two
            else:
                moment_one = momentum * moment_one - step_size * grad_one
                moment_two = momentum * moment_two - step_size * grad_two
            weight_one = (1.0 - forget) * weight_one + moment_one
            weight_two = (1.0 - forget) * weight_two + moment_two
            kept.update(
                key_rows=key_rows,
                hidden_pre=hidden_pre,
                hidden_act=hidden_act,
                mismatch=mismatch,
                through=through,
                blended=blended,
            )
        saved.append(kept)

    pers_unit, pers_inv = head_norm(persist_key.astype(f32))
    pers_low = pers_unit.astype(bf16)

    def block_scores(b):
        recalled = saved[b]["recalled"]
        mem_unit, mem_inv = head_norm(product(recalled, w_key))
        mem_value = product(recalled, w_value).astype(bf16)
        all_keys = jnp.concatenate(
            [pers_low, mem_unit.astype(bf16), rows_of(key_low, b)], axis=0
        ).reshape(-1, heads_here, HD)
        all_values = jnp.concatenate(
            [persist_value, mem_value, rows_of(value_low, b)], axis=0
        ).reshape(-1, heads_here, HD)
        query_heads = rows_of(query_low, b).reshape(STRETCH, heads_here, HD)
        scores = score_scale * jnp.einsum(
            "qhd,khd->hqk", query_heads, all_keys, preferred_element_type=f32
        )
        scores = jnp.where(visible(block_mask[b])[None], scores, -1e30)
        return (mem_unit, mem_inv, all_keys, all_values, query_heads, scores)

    mixed_list = []
    for b in range(blocks):
        mem_unit, mem_inv, all_keys, all_values, query_heads, scores = block_scores(b)
        row_peak = jnp.max(scores, axis=2, keepdims=True)
        exponent = jnp.exp(scores - row_peak)
        row_total = jnp.sum(exponent, axis=2, keepdims=True)
        prob_low = (exponent / row_total).astype(bf16)
        mixed_list.append(
            jnp.einsum(
                "hqk,khd->qhd", prob_low, all_values, preferred_element_type=f32
            ).reshape(STRETCH, local_width)
        )
        saved[b].update(
            log_total=row_peak + jnp.log(row_total),
            mem_unit=mem_unit,
            mem_inv=mem_inv,
            all_keys=all_keys,
            all_values=all_values,
            query_heads=query_heads,
        )
    mixed_all = jnp.concatenate(mixed_list, axis=0)
    gate_sig = jax.nn.sigmoid(gate_pre)
    gated = (mixed_all * gate_sig).astype(bf16)
    branch_here = scatter_columns(product(gated, w_out))
    branch_full = gather_columns(branch_here.astype(bf16)).astype(f32)
    middle = whole_x + branch_full
    middle_here = layer_input.astype(f32) + branch_here
    inv_two = lax.rsqrt(jnp.mean(middle * middle, axis=1, keepdims=True) + epsilon)
    unit_two = middle * inv_two
    normed_two = (unit_two * norm2_gain).astype(bf16)
    ffn_pre = product(normed_two, ffn_gate)
    up_pre = product(normed_two, ffn_up)
    ffn_sig = jax.nn.sigmoid(ffn_pre)
    hidden_low = (ffn_pre * ffn_sig * up_pre).astype(bf16)
    back_hidden = inner_right(whole_dy, ffn_down)
    back_up_low = (back_hidden * ffn_pre * ffn_sig).astype(bf16)
    back_ffn_low = (back_hidden * up_pre * silu_grad(ffn_pre)).astype(bf16)
    back_normed_two = inner_right(back_ffn_low, ffn_gate) + inner_right(back_up_low, ffn_up)
    gain_two_part = jnp.sum(back_normed_two * unit_two, axis=0)
    middle_part = norm_back(back_normed_two, unit_two, inv_two, norm2_gain)
    back_middle_here = scatter_columns(middle_part)
    grad_ffn_down = inner_left(hidden_low, whole_dy)
    grad_ffn_gate = inner_left(normed_two, back_ffn_low)
    grad_ffn_up = inner_left(normed_two, back_up_low)
    ffn_here = scatter_columns(product(hidden_low, ffn_down))
    layer_output = (middle_here + ffn_here).astype(bf16)
    back_middle_here = back_middle_here + out_grad.astype(f32)
    back_branch = gather_columns(back_middle_here.astype(bf16))
    grad_ffn_gate, grad_ffn_up, grad_ffn_down = sum_wide(
        [grad_ffn_gate, grad_ffn_up, grad_ffn_down]
    )
    grad_w_out = inner_left(gated, back_branch)
    back_gated = inner_right(back_branch, w_out)
    back_mixed_low = (back_gated * gate_sig).astype(bf16)
    back_gate_low = (back_gated * mixed_all * gate_sig * (1.0 - gate_sig)).astype(bf16)

    back_recalled_parts = []
    mem_key_grad = mem_value_grad = 0.0
    pers_key_acc = grad_persist_value = 0.0
    back_query_att, back_key_att, back_value_att = [], [], []
    for b in range(blocks):
        kept = saved[b]
        scores = score_scale * jnp.einsum(
            "qhd,khd->hqk", kept["query_heads"], kept["all_keys"], preferred_element_type=f32
        )
        scores = jnp.where(visible(block_mask[b])[None], scores, -1e30)
        prob_rows = jnp.exp(scores - kept["log_total"])
        prob_low = prob_rows.astype(bf16)
        back_heads = rows_of(back_mixed_low, b).reshape(STRETCH, heads_here, HD)
        back_all_values = jnp.einsum(
            "hqk,qhd->khd", prob_low, back_heads, preferred_element_type=f32
        )
        back_probs = jnp.einsum(
            "qhd,khd->hqk", back_heads, kept["all_values"], preferred_element_type=f32
        )
        back_scores = (
            prob_rows * (back_probs - jnp.sum(prob_rows * back_probs, axis=2, keepdims=True))
        ).astype(bf16)
        back_query = score_scale * jnp.einsum(
            "hqk,khd->qhd", back_scores, kept["all_keys"], preferred_element_type=f32
        )
        back_all_keys = score_scale * jnp.einsum(
            "hqk,qhd->khd", back_scores, kept["query_heads"], preferred_element_type=f32
        )
        back_all_keys = back_all_keys.reshape(-1, local_width)
        back_all_values = back_all_values.reshape(-1, local_width)
        back_mem_key = head_back(
            back_all_keys[NP : NP + STRETCH], kept["mem_unit"], kept["mem_inv"]
        ).astype(bf16)
        back_mem_value = back_all_values[NP : NP + STRETCH].astype(bf16)
        back_recalled_parts.append(
            inner_right(back_mem_key, w_key) + inner_right(back_mem_value, w_value)
        )
        mem_key_grad = mem_key_grad + inner_left(kept["recalled"], back_mem_key)
        mem_value_grad = mem_value_grad + inner_left(kept["recalled"], back_mem_value)
        pers_key_acc = pers_key_acc + back_all_keys[:NP]
        grad_persist_value = grad_persist_value + back_all_values[:NP]
        back_query_att.append(back_query.reshape(STRETCH, local_width))
        back_key_att.append(back_all_keys[NP + STRETCH :])
        back_value_att.append(back_all_values[NP + STRETCH :])
    grad_persist_key = head_back(pers_key_acc, pers_unit, pers_inv)

    cot_one = cot_two = mom_one = mom_two = None
    key_total, query_total, value_total = [None] * blocks, [None] * blocks, [None] * blocks
    for b in reversed(range(blocks)):
        kept = saved[b]
        step_size, momentum, forget = plan_rates(levels[b])
        first_low, second_low = kept["first"], kept["second"]
        back_recalled = gather_columns(scatter_columns(back_recalled_parts[b]).astype(bf16))
        new_one = new_two = None
        if cot_one is None:
            key_total[b], value_total[b] = back_key_att[b], back_value_att[b]
        else:
            key_rows, hidden_pre = kept["key_rows"], kept["hidden_pre"]
            hidden_slope = silu_grad(hidden_pre)
            total_one = cot_one if mom_one is None else mom_one + cot_one
            total_two = cot_two if mom_two is None else mom_two + cot_two
            back_g1 = (-step_size * total_one).astype(bf16)
            back_g2 = (-step_size * total_two).astype(bf16)
            back_blended = product(key_rows, back_g1)
            back_through = (back_blended * hidden_slope).astype(bf16)
            mismatch_part = product(kept["hidden_act"], back_g2) + product(
                back_through, second_low
            )
            mismatch_low = scatter_columns(mismatch_part).astype(bf16)
            back_mismatch = gather_columns(mismatch_low)
            key_part = inner_right(kept["blended"], back_g1)
            back_hidden_act = inner_right(kept["mismatch"], back_g2)
            extra_pre = back_blended * kept["through"] * silu_curve(hidden_pre)
            new_one = (1.0 - forget) * cot_one
            new_two = (1.0 - forget) * cot_two + inner_left(back_through, kept["mismatch"])
        back_query_act = inner_right(back_recalled, second_low)
        back_query_pre = (back_query_act * silu_grad(kept["query_mem"])).astype(bf16)
        query_part = inner_right(back_query_pre, first_low)
        one_term = inner_left(kept["query_rows"], back_query_pre)
        two_term = inner_left(kept["query_act"], back_recalled)
        new_one = one_term if new_one is None else new_one + one_term
        new_two = two_term if new_two is None else new_two + two_term
        if cot_one is not None:
            scale_rows = (block_mask[b] / STRETCH).astype(bf16)[:, None]
            back_pred = back_mismatch * scale_rows
            value_part = -(mismatch_low.astype(f32) * scale_rows.astype(f32))
            back_hidden_act = back_hidden_act + inner_right(back_pred, second_low)
            new_two = new_two + inner_left(kept["hidden_act"], back_pred)
            back_hidden_pre = (back_hidden_act * hidden_slope + extra_pre).astype(bf16)
            key_part = key_part + inner_right(back_hidden_pre, first_low)
            new_one = new_one + inner_left(key_rows, back_hidden_pre)
            key_total[b] = back_key_att[b] + scatter_columns(key_part)
            value_total[b] = back_value_att[b] + value_part
            mom_one, mom_two = momentum * total_one, momentum * total_two
        query_total[b] = back_query_att[b] + scatter_columns(query_part)
        cot_one, cot_two = new_one, new_two
    grad_mem_w1, grad_mem_w2 = cot_one, cot_two

    back_query_total = jnp.concatenate(query_total, axis=0)
    back_key_total = jnp.concatenate(key_total, axis=0)
    back_value_total = jnp.concatenate(value_total, axis=0)
    query_conv_back = head_back(back_query_total, query_unit, query_inv) * silu_grad(query_conv)
    key_conv_back = head_back(back_key_total, key_unit, key_inv) * silu_grad(key_conv)
    value_conv_back = back_value_total * silu_grad(value_conv)
    query_pre_back, grad_conv_query = conv_back(query_conv_back, query_pre, conv_query)
    key_pre_back, grad_conv_key = conv_back(key_conv_back, key_pre, conv_key)
    value_pre_back, grad_conv_value = conv_back(value_conv_back, value_pre, conv_value)
    query_pre_low = query_pre_back.astype(bf16)
    key_pre_low = key_pre_back.astype(bf16)
    value_pre_low = value_pre_back.astype(bf16)
    back_normed_one = (
        inner_right(back_gate_low, w_gate)
        + inner_right(query_pre_low, w_query)
        + inner_right(key_pre_low, w_key)
        + inner_right(value_pre_low, w_value)
    )
    gain_one_part = jnp.sum(back_normed_one * unit_one, axis=0)
    input_part = norm_back(back_normed_one, unit_one, inv_one, norm1_gain)
    back_input_here = scatter_columns(input_part)
    grad_w_gate = inner_left(normed_one, back_gate_low)
    grad_w_query = inner_left(normed_one, query_pre_low)
    grad_w_key = inner_left(normed_one, key_pre_low) + mem_key_grad
    grad_w_value = inner_left(normed_one, value_pre_low) + mem_value_grad
    input_grad = back_middle_here + back_input_here

    gains = lax.psum(
        jnp.concatenate([gain_one_part, gain_two_part]).astype(bf16), ("narrow", "wide")
    ).astype(f32)
    full_width = whole_x.shape[1]
    grad_norm1_gain = lax.dynamic_slice_in_dim(gains, column_start, local_width, 0)
    grad_norm2_gain = lax.dynamic_slice_in_dim(gains, full_width + column_start, local_width, 0)
    late = (
        grad_w_query, grad_w_key, grad_w_value, grad_w_gate, grad_conv_query, grad_conv_key,
        grad_conv_value, grad_persist_key, grad_persist_value, grad_mem_w1, grad_mem_w2, grad_w_out,
    )
    late, (grad_ffn_gate, grad_ffn_up, grad_ffn_down) = lax.optimization_barrier(
        (tuple(v.astype(bf16) for v in late), (grad_ffn_gate, grad_ffn_up, grad_ffn_down))
    )
    (
        grad_w_query, grad_w_key, grad_w_value, grad_w_gate, grad_conv_query, grad_conv_key,
        grad_conv_value, grad_persist_key, grad_persist_value, grad_mem_w1, grad_mem_w2, grad_w_out,
    ) = sum_wide(late)
    return (
        layer_output,
        input_grad,
        grad_norm1_gain,
        grad_w_query,
        grad_w_key,
        grad_w_value,
        grad_w_gate,
        grad_conv_query,
        grad_conv_key,
        grad_conv_value,
        grad_persist_key,
        grad_persist_value,
        grad_mem_w1,
        grad_mem_w2,
        grad_w_out,
        grad_norm2_gain,
        grad_ffn_gate,
        grad_ffn_up,
        grad_ffn_down,
    )

def linked_body(
    layer_input, out_grad, lengths, plan, norm1_gain, w_query, w_key, w_value, w_gate,
    conv_query, conv_key, conv_value, persist_key, persist_value, mem_w1, mem_w2, w_out,
    norm2_gain, ffn_gate, ffn_up, ffn_down,
):
    step_size, momentum, forget = plan_rates(plan[0, 0].astype(f32))
    rates = jnp.stack([lengths[0].astype(f32), step_size, 1.0 - forget])
    rates = jnp.concatenate([rates, jnp.zeros((5,), f32)])
    (
        low_x, query_pre, key_pre, value_pre, query_low, key_low, value_low, gate_pre, keys, queries, pre,
        act, mis, thr, ble, qpre, qact, rec, next_one, next_two, branch, branch_here, mixed, gated,
        whole_dy, normed_one,
    ) = run_forward_layer(
        layer_input, out_grad, norm1_gain[None], w_query, w_key, w_value, w_gate, conv_query, conv_key,
        conv_value, persist_key, persist_value, mem_w1, mem_w2, w_out, rates,
    )
    (
        input_grad, layer_output, grad_ffn_gate, grad_ffn_up, grad_ffn_down, grad_w_out, grad_w_gate,
        grad_mem_w1, grad_mem_w2, packed, extra,
    ) = run_backward_layer(
        query_low, key_low, value_low, rec, w_query, w_key, w_value, w_gate, persist_key,
        persist_value, gate_pre, w_out, mixed, gated, keys, queries, pre, act, mis, thr, ble, qpre,
        qact, mem_w1, mem_w2, next_one, next_two, low_x, norm1_gain[None], conv_query, conv_key,
        conv_value, query_pre, key_pre, value_pre, norm2_gain[None], branch, branch_here, whole_dy,
        ffn_gate, ffn_up, ffn_down, normed_one, rates,
    )
    (
        grad_ffn_gate, grad_ffn_up, grad_ffn_down, grad_mem_w1, grad_mem_w2, grad_w_out, grad_w_gate,
        grad_w_query, grad_w_key, grad_w_value, input_grad, layer_output, pers_key, pers_value,
        grad_conv_query, grad_conv_key, grad_conv_value, grad_norm1_gain, grad_norm2_gain,
    ) = run_widen(
        [grad_ffn_gate, grad_ffn_up, grad_ffn_down, grad_mem_w1, grad_mem_w2, grad_w_out],
        [(grad_w_gate, 0), (packed, 0), (packed, 1), (packed, 2)],
        [input_grad, layer_output],
        extra,
    )
    return (
        layer_output, input_grad, grad_norm1_gain[0], grad_w_query, grad_w_key, grad_w_value, grad_w_gate,
        grad_conv_query, grad_conv_key, grad_conv_value, pers_key, pers_value, grad_mem_w1, grad_mem_w2,
        grad_w_out, grad_norm2_gain[0], grad_ffn_gate, grad_ffn_up, grad_ffn_down,
    )


def body(*arrays):
    tokens_here, local_width = arrays[0].shape
    width, units = arrays[14].shape
    linked = (
        (lax.axis_size("wide"), lax.axis_size("narrow")) == (8, 4)
        and local_width == 256
        and tokens_here == 2 * STRETCH
        and (width, units) == (1024, 1024)
        and arrays[18].shape == (1024, 1024)
    )
    return linked_body(*arrays) if linked else plain_body(*arrays)


def solution(mesh):
    return jax.shard_map(
        body,
        mesh=mesh,
        in_specs=(
            P("wide", "narrow"),
            P("wide", "narrow"),
            P("wide"),
            P("wide", None),
            P(),
            P(None, "narrow"),
            P(None, "narrow"),
            P(None, "narrow"),
            P(None, "narrow"),
            P(None, "narrow"),
            P(None, "narrow"),
            P(None, "narrow"),
            P(None, "narrow"),
            P(None, "narrow"),
            P(None, "narrow"),
            P("narrow", None),
            P("narrow", None),
            P(),
            P(None, "narrow"),
            P(None, "narrow"),
            P("narrow", None),
        ),
        out_specs=(
            P("wide", "narrow"),
            P("wide", "narrow"),
            P("narrow"),
            P(None, "narrow"),
            P(None, "narrow"),
            P(None, "narrow"),
            P(None, "narrow"),
            P(None, "narrow"),
            P(None, "narrow"),
            P(None, "narrow"),
            P(None, "narrow"),
            P(None, "narrow"),
            P(None, "narrow"),
            P("narrow", None),
            P("narrow", None),
            P("narrow"),
            P(None, "narrow"),
            P(None, "narrow"),
            P("narrow", None),
        ),
        check_vma=False,
    )
```

```python
import jax
import jax.numpy as jnp
from jax import lax
from jax.experimental import pallas as pl
from jax.experimental.pallas import tpu as pltpu
from jax.sharding import PartitionSpec as P

HD = 64
NP = 16
KW = 4
STRETCH = 512

epsilon = 1e-06
head_floor = 1.0
score_scale = 12.0
bf16 = jnp.bfloat16
f32 = jnp.float32


def product(left_side, right_side):
    return jnp.dot(left_side, right_side, preferred_element_type=f32)


def inner_left(left_side, right_side):
    return lax.dot_general(
        left_side, right_side, (((0,), (0,)), ((), ())), preferred_element_type=f32
    )


def inner_right(left_side, right_side):
    return lax.dot_general(
        left_side, right_side, (((1,), (1,)), ((), ())), preferred_element_type=f32
    )


def silu_grad(values):
    logistic = jax.nn.sigmoid(values)
    return logistic * (1.0 + values * (1.0 - logistic))


def silu_curve(values):
    logistic = jax.nn.sigmoid(values)
    logistic_slope = logistic * (1.0 - logistic)
    return logistic_slope * (1.0 + values * (1.0 - logistic)) + logistic * (
        1.0 - logistic - values * logistic_slope
    )


def plan_rates(level_now):
    return (0.1 * jnp.exp2(level_now), 0.9 - 0.2 * level_now, 0.02 + 0.05 * level_now)


def head_sums(values):
    width = values.shape[1]
    places = jnp.arange(width) // HD
    same_head = (places[:, None] == places[None, :]).astype(f32)
    return jnp.dot(
        values, same_head, precision=lax.Precision.HIGHEST, preferred_element_type=f32
    )


def head_norm(values):
    inv_norm = lax.rsqrt(head_sums(values * values) + head_floor)
    return (values * inv_norm, inv_norm)


def head_back(grad_rows, unit_rows, inv_norm):
    return (grad_rows - unit_rows * head_sums(grad_rows * unit_rows)) * inv_norm


def norm_back(grad_rows, unit_rows, inv_rows, gain_vec):
    scaled = grad_rows * gain_vec
    return inv_rows * (scaled - unit_rows * jnp.mean(scaled * unit_rows, axis=1, keepdims=True))


def shift_down(values, offset):
    return jnp.concatenate(
        [jnp.zeros((offset, values.shape[1]), values.dtype), values[:-offset]], axis=0
    )


def shift_up(values, offset):
    return jnp.concatenate(
        [values[offset:], jnp.zeros((offset, values.shape[1]), values.dtype)], axis=0
    )


def causal_conv(values, conv_taps):
    result = values * conv_taps[0]
    for offset in range(1, KW):
        result = result + shift_down(values, offset) * conv_taps[offset]
    return result


def conv_back(grad_rows, values, conv_taps):
    back_values = grad_rows * conv_taps[0]
    tap_grads = [jnp.sum(grad_rows * values, axis=0)]
    for offset in range(1, KW):
        back_values = back_values + shift_up(grad_rows, offset) * conv_taps[offset]
        tap_grads.append(jnp.sum(grad_rows * shift_down(values, offset), axis=0))
    return (back_values, jnp.stack(tap_grads, axis=0))


def visible(mask_rows):
    row_width = mask_rows.shape[0]
    places = jnp.arange(row_width)
    valid_keys = mask_rows[None, :] > 0.5
    causal = (places[None, :] <= places[:, None]) & valid_keys
    memory_seen = jnp.broadcast_to(valid_keys, (row_width, row_width))
    persistent = jnp.ones((row_width, NP), dtype=bool)
    return jnp.concatenate([persistent, memory_seen, causal], axis=1)


def gather_columns(values):
    return lax.all_gather(values, "narrow", axis=1, tiled=True)


def scatter_columns(values):
    return lax.psum_scatter(
        values.astype(bf16), "narrow", scatter_dimension=1, tiled=True
    ).astype(f32)


def sum_wide(values):
    return [lax.psum(v.astype(bf16), "wide").astype(f32) for v in values]


MESH = pl.DeviceIdType.MESH
ANY = pl.BlockSpec(memory_space=pl.ANY)
SCALARS = pl.BlockSpec(memory_space=pltpu.SMEM)
VMEM_LIMIT = 60 << 20


def group_places():
    me = lax.axis_index("narrow")
    core = lax.rem(me, 2)
    sib = me + 1 - 2 * core
    opp = lax.rem(me + 2, 4)
    diag = lax.rem(sib + 2, 4)
    return me, sib, opp, diag


def cols(index, width=256):
    return pl.ds(pl.multiple_of(index * width, width), width)


def enter_group(sib, opp):
    barrier = pltpu.get_barrier_semaphore()
    for peer in (sib, opp):
        pl.semaphore_signal(barrier, inc=1, device_id={"narrow": peer}, device_id_type=MESH)
    pl.semaphore_wait(barrier, 2)


class Wire:
    def __init__(self, send, recv):
        self.send, self.recv, self.used = send, recv, 0

    def to(self, source, target, device, axis="narrow"):
        k = self.used
        self.used += 1
        return pltpu.make_async_remote_copy(
            src_ref=source,
            dst_ref=target,
            send_sem=self.send.at[k],
            recv_sem=self.recv.at[k],
            device_id={axis: device},
            device_id_type=MESH,
        )


class Local:
    def __init__(self, sems):
        self.sems, self.used, self.open = sems, 0, []

    def start(self, source, target, late=False):
        copy = pltpu.make_async_copy(source, target, self.sems.at[self.used])
        self.used += 1
        copy.start()
        if late:
            self.open.append(copy)
        return copy

    def finish(self):
        for copy in self.open:
            copy.wait()
        self.open = []


class Gather:
    def __init__(self, wire, full, rows, places):
        me, sib, opp, diag = places
        own = full.at[rows, cols(me)]
        passed = full.at[rows, cols(opp)]
        self.far = wire.to(own, own, opp)
        self.near = wire.to(own, own, sib)
        self.relayed = wire.to(passed, passed, sib)

    def start(self):
        self.far.start()
        self.near.start()

    def relay(self):
        self.far.wait_recv()
        self.relayed.start()

    def end(self):
        self.near.wait_recv()
        self.relayed.wait_recv()

    def drain(self):
        self.far.wait_send()
        self.near.wait_send()
        self.relayed.wait_send()


class Scatter:
    def __init__(self, wire, part, rows, first, passed, last, places):
        me, sib, opp, diag = places
        self.part, self.rows, self.places = part, rows, places
        self.first, self.passed, self.last = first, passed, last
        self.pass_on = wire.to(part.at[rows, cols(diag)], first.at[1, rows], sib)
        self.keep = wire.to(part.at[rows, cols(sib)], first.at[0, rows], sib)
        self.far = wire.to(passed.at[rows], last.at[rows], opp)

    def start(self):
        self.pass_on.start()
        self.keep.start()

    def middle(self):
        me, sib, opp, diag = self.places
        self.pass_on.wait_recv()
        self.passed[self.rows] = (
            self.part[self.rows, cols(opp)].astype(f32) + self.first[1, self.rows].astype(f32)
        ).astype(bf16)
        self.far.start()

    def end(self):
        me, sib, opp, diag = self.places
        self.keep.wait_recv()
        near = self.part[self.rows, cols(me)].astype(f32) + self.first[0, self.rows].astype(f32)
        self.far.wait_recv()
        return near + self.last[self.rows].astype(f32)

    def drain(self):
        self.pass_on.wait_send()
        self.keep.wait_send()
        self.far.wait_send()


def scatter_room(rows):
    return [
        pltpu.VMEM((2, rows, 256), bf16),
        pltpu.VMEM((rows, 256), bf16),
        pltpu.VMEM((rows, 256), bf16),
    ]


def sems(count):
    return [
        pltpu.SemaphoreType.DMA((count,)),
        pltpu.SemaphoreType.DMA((count,)),
    ]


def shaped(shape, dtype=None):
    return jax.ShapeDtypeStruct(shape, bf16 if dtype is None else dtype)


def call(kernel, collective, outs, ins, scratch, flops, moved):
    return pl.pallas_call(
        kernel,
        out_shape=outs,
        in_specs=[SCALARS if s else ANY for s in ins],
        out_specs=[ANY] * len(outs),
        scratch_shapes=scratch,
        compiler_params=pltpu.CompilerParams(
            collective_id=collective, has_side_effects=True, vmem_limit_bytes=VMEM_LIMIT
        ),
        cost_estimate=pl.CostEstimate(flops=flops, bytes_accessed=moved, transcendentals=0),
        name=kernel.__name__,
    )


KEY_ROWS = 2 * STRETCH + 128


def silu(values):
    return values * jax.nn.sigmoid(values)


def head_ones():
    left = lax.broadcasted_iota(jnp.int32, (256, 256), 0) // HD
    right = lax.broadcasted_iota(jnp.int32, (256, 256), 1) // HD
    return (left == right).astype(f32).astype(bf16)


def split_sums(values, ones):
    high = values.astype(bf16)
    rest = (values - high.astype(f32)).astype(bf16)
    return jnp.dot(high, ones, preferred_element_type=f32) + jnp.dot(
        rest, ones, preferred_element_type=f32
    )


def head_only(values, head):
    lane_head = lax.broadcasted_iota(jnp.int32, values.shape, 1) // HD
    return jnp.where(lane_head == head, values.astype(f32), 0.0).astype(bf16)


def key_bias(first_row, rows, valid, flipped):
    shape = (KEY_ROWS, rows) if flipped else (rows, KEY_ROWS)
    slot = lax.broadcasted_iota(jnp.int32, shape, 0 if flipped else 1)
    row = lax.broadcasted_iota(jnp.int32, shape, 1 if flipped else 0) + first_row
    memory = (slot < STRETCH) & (slot.astype(f32) < valid)
    place = slot - STRETCH
    causal = (place >= 0) & (place <= row) & (place.astype(f32) < valid) & (slot < 2 * STRETCH)
    persistent = (slot >= 2 * STRETCH) & (slot < 2 * STRETCH + NP)
    return jnp.where(memory | causal | persistent, 0.0, -1e30)


def unit_rows(values, ones):
    wide_values = values.astype(f32)
    return wide_values * lax.rsqrt(split_sums(wide_values * wide_values, ones) + head_floor)


def nt(left, right):
    return lax.dot_general(left, right, (((1,), (1,)), ((), ())), preferred_element_type=f32)


def tn(left, right):
    return lax.dot_general(left, right, (((0,), (0,)), ((), ())), preferred_element_type=f32)


def slope_of(values):
    sig = jax.nn.sigmoid(values)
    return sig * (1.0 + values * (1.0 - sig))


def forward_layer(
    xl_in, dyl_in, gain_in, wq_in, wk_in, wv_in, wg_in, tq_in, tk_in, tv_in, pk_in, pv_in, one_in, two_in,
    wo_in, rates,
    x_out, qconv_out, kconv_out, vconv_out, qlow_out, klow_out, vlow_out, gate_out, key_out, query_out,
    pre_out, act_out, mis_out, thr_out, ble_out, qpre_out, qact_out, rec_out, one_out, two_out,
    branch_out, here_out, mixed_out, gated_out, dy_out, normed_out,
    x, gain, weights, tq, tk, tv, qconv, kconv, vconv, qlow, klow, vlow, gate, pk, key, query, one, two,
    pre, act, part, mis, thr, ble, qpre, qact, qpart, rec, next_one, next_two, wo, keys, values, bias,
    mixed, gated, bpart, branch, here, dy, norms,
    first, passed, last, q_first, q_passed, q_last, b_first, b_passed, b_last,
    send, recv, local_sems,
):
    places = group_places()
    me, sib, opp, diag = places
    wire, local = Wire(send, recv), Local(local_sems)
    half, block = STRETCH // 2, STRETCH
    lanes = [pl.ds(i * 256, 256) for i in range(4)]
    get_x = local.start(xl_in, x.at[:, cols(me)])
    loads = [
        local.start(s, t)
        for s, t in (
            (wq_in, weights.at[:, lanes[0]]), (wk_in, weights.at[:, lanes[1]]),
            (wv_in, weights.at[:, lanes[2]]), (wg_in, weights.at[:, lanes[3]]), (gain_in, gain),
            (tq_in, tq), (tk_in, tk), (tv_in, tv), (pk_in, pk),
            (pv_in, values.at[pl.ds(2 * block, NP)]),
        )
    ]
    later = [
        local.start(s, t)
        for s, t in ((one_in, one), (two_in, two), (wo_in, wo), (dyl_in, dy.at[:, cols(me)]))
    ]
    pieces = [pl.ds(c * half, half) for c in range(4)]
    blocks = [pl.ds(b * block, block) for b in range(2)]
    ones = head_ones()
    for pad in (qconv, kconv, vconv):
        pad[pl.ds(0, 8), :] = jnp.zeros((8, 256), f32)
    keys[pl.ds(2 * block + NP, 128 - NP), :] = jnp.zeros((128 - NP, 256), bf16)
    values[pl.ds(2 * block + NP, 128 - NP), :] = jnp.zeros((128 - NP, 256), bf16)
    enter_group(sib, opp)
    get_x.wait()
    rows_of_x = [Gather(wire, x, rows, places) for rows in pieces]
    key_joins = [Gather(wire, key, rows, places) for rows in pieces[:2]]
    query_joins = [Gather(wire, query, rows, places) for rows in blocks]
    sums = [Scatter(wire, part, rows, first, passed, last, places) for rows in pieces[:2]]
    misses = [Gather(wire, mis, rows, places) for rows in pieces[:2]]
    qsums = [Scatter(wire, qpart, rows, q_first, q_passed, q_last, places) for rows in blocks]
    reads = [Gather(wire, rec, rows, places) for rows in blocks]
    rows_of_dy = [Gather(wire, dy, rows, places) for rows in blocks]
    bsums = [Scatter(wire, bpart, rows, b_first, b_passed, b_last, places) for rows in pieces]
    joins = [Gather(wire, branch, rows, places) for rows in pieces]
    rows_of_x[0].start()
    rows_of_x[1].start()
    for item in loads:
        item.wait()
    keys[pl.ds(2 * block, NP), :] = unit_rows(pk[...], ones).astype(bf16)

    def project(c):
        rows = pieces[c]
        now = x[rows, :].astype(f32)
        inv = lax.rsqrt(jnp.mean(now * now, axis=1, keepdims=True) + epsilon)
        normed = (now * inv * gain[...]).astype(bf16)
        norms[rows, :] = normed
        for at, (pad, low, taps) in enumerate(
            ((kconv, klow, tk), (qconv, qlow, tq), (vconv, vlow, tv))
        ):
            side = lanes[(1, 0, 2)[at]]
            start = 8 + c * half
            pad[pl.ds(start, half), :] = jnp.dot(
                normed, weights[:, side], preferred_element_type=f32
            )
            conv = pad[pl.ds(start, half), :] * taps[pl.ds(0, 1), :]
            for j in range(1, KW):
                conv = conv + pad[pl.ds(start - j, half), :] * taps[pl.ds(j, 1), :]
            conv = conv * jax.nn.sigmoid(conv)
            low[rows, :] = (unit_rows(conv, ones) if at < 2 else conv).astype(bf16)
            if at == 0 and c < 2:
                key[rows, cols(me)] = klow[rows, :]
                key_joins[c].start()
        query[rows, cols(me)] = qlow[rows, :]
        gate[rows, :] = jnp.dot(normed, weights[:, lanes[3]], preferred_element_type=f32).astype(bf16)

    def hide(c):
        rows = pieces[c]
        hidden = jnp.dot(key[rows, :], one[...], preferred_element_type=f32)
        pre[rows, :] = hidden.astype(bf16)
        act[rows, :] = silu(hidden).astype(bf16)
        part[rows, :] = jnp.dot(act[rows, :], two[...], preferred_element_type=f32).astype(bf16)
        sums[c].start()

    def read(b, weight_one, weight_two):
        rows = blocks[b]
        asked = jnp.dot(query[rows, :], weight_one[...], preferred_element_type=f32)
        qpre[rows, :] = asked.astype(bf16)
        qact[rows, :] = silu(asked).astype(bf16)
        qpart[rows, :] = jnp.dot(
            qact[rows, :], weight_two[...], preferred_element_type=f32
        ).astype(bf16)
        qsums[b].start()

    rows_of_x[0].relay()
    rows_of_x[0].end()
    project(0)
    rows_of_x[1].relay()
    rows_of_x[1].end()
    project(1)
    rows_of_x[2].start()
    for item in later:
        item.wait()
    key_joins[0].relay()
    key_joins[0].end()
    hide(0)
    key_joins[1].relay()
    sums[0].middle()
    key_joins[1].end()
    hide(1)
    rows_of_x[2].relay()
    sums[1].middle()
    rows_of_x[3].start()
    query_joins[0].start()
    for c in range(2):
        rows = pieces[c]
        predicted = sums[c].end()
        index = lax.broadcasted_iota(jnp.int32, (half, 1), 0) + c * half
        scale = jnp.where(index.astype(f32) < rates[0], 1.0 / STRETCH, 0.0)
        mis[rows, cols(me)] = ((predicted - vlow[rows, :].astype(f32)) * scale).astype(bf16)
        misses[c].start()
    for s, t in ((key, key_out), (pre, pre_out), (act, act_out)):
        local.start(s, t, late=True)
    rows_of_x[2].end()
    project(2)
    misses[0].relay()
    rows_of_x[3].relay()
    query_joins[0].relay()
    misses[1].relay()
    for c in range(2):
        rows = pieces[c]
        misses[c].end()
        through = nt(mis[rows, :], two[...])
        thr[rows, :] = through.astype(bf16)
        ble[rows, :] = (through * slope_of(pre[rows, :].astype(f32))).astype(bf16)
    rows_of_x[3].end()
    project(3)
    query_joins[1].start()
    for s, t in (
        (x, x_out), (norms, normed_out), (qconv.at[pl.ds(8, 4 * half)], qconv_out), (kconv.at[pl.ds(8, 4 * half)], kconv_out),
        (vconv.at[pl.ds(8, 4 * half)], vconv_out), (qlow, qlow_out), (klow, klow_out),
        (vlow, vlow_out), (gate, gate_out), (mis, mis_out), (thr, thr_out), (ble, ble_out),
    ):
        local.start(s, t, late=True)
    step_size, keep = rates[1], rates[2]

    def update(c, carried):
        rows = pl.ds(pl.multiple_of(c * half, half), half)
        grad = tn(key[:, rows], ble[...])
        next_one[rows, :] = (keep * one[rows, :].astype(f32) - step_size * grad).astype(bf16)
        grad = tn(act[:, rows], mis[...])
        next_two[rows, :] = (keep * two[rows, :].astype(f32) - step_size * grad).astype(bf16)
        return carried

    query_joins[0].end()
    read(0, one, two)
    lax.fori_loop(0, 2, update, 0)
    qsums[0].middle()
    lax.fori_loop(2, 4, update, 0)
    for s, t in ((next_one, one_out), (next_two, two_out)):
        local.start(s, t, late=True)
    query_joins[1].relay()
    rec[blocks[0], cols(me)] = qsums[0].end().astype(bf16)
    reads[0].start()
    query_joins[1].end()
    read(1, next_one, next_two)
    reads[0].relay()
    qsums[1].middle()
    for s, t in ((query, query_out), (qpre, qpre_out), (qact, qact_out)):
        local.start(s, t, late=True)
    reads[0].end()
    rec[blocks[1], cols(me)] = qsums[1].end().astype(bf16)
    reads[1].start()
    rows_of_dy[0].start()

    def settle(c):
        rows = pieces[c]
        total = bsums[c].end()
        here[rows, :] = total
        branch[rows, cols(me)] = total.astype(bf16)
        joins[c].start()

    for c in range(4):
        b, rows = c // 2, pieces[c]
        if c % 2 == 0:
            if b == 1:
                reads[1].end()
            memory = rec[blocks[b], :]
            made = jnp.dot(memory, weights[:, lanes[1]], preferred_element_type=f32)
            keys[pl.ds(0, block), :] = unit_rows(made, ones).astype(bf16)
            values[pl.ds(0, block), :] = jnp.dot(
                memory, weights[:, lanes[2]], preferred_element_type=f32
            ).astype(bf16)
            keys[pl.ds(block, block), :] = klow[blocks[b], :]
            values[pl.ds(block, block), :] = vlow[blocks[b], :]
        bias[...] = key_bias((c % 2) * half, half, rates[0] - float(b * block), False)

        def one_head(head, total):
            asked = head_only(qlow[rows, :], head)
            scores = nt(asked, keys[...])
            chances = jnp.exp(score_scale * scores + bias[...])
            inv = 1.0 / jnp.sum(chances, axis=1, keepdims=True)
            got = jnp.dot((chances * inv).astype(bf16), values[...], preferred_element_type=f32)
            lane_head = lax.broadcasted_iota(jnp.int32, got.shape, 1) // HD
            return jnp.where(lane_head == head, got, total)

        total = lax.fori_loop(0, 4, one_head, jnp.zeros((half, 256), f32))
        mixed[rows, :] = total.astype(bf16)
        gated[rows, :] = (total * jax.nn.sigmoid(gate[rows, :].astype(f32))).astype(bf16)
        bpart[rows, :] = jnp.dot(gated[rows, :], wo[...], preferred_element_type=f32).astype(bf16)
        bsums[c].start()
        if c == 0:
            reads[1].relay()
            rows_of_dy[0].relay()
            bsums[0].middle()
        if c == 1:
            rows_of_dy[1].start()
            bsums[1].middle()
            settle(0)
        if c == 2:
            rows_of_dy[1].relay()
            bsums[2].middle()
            joins[0].relay()
            settle(1)
    for item in rows_of_dy:
        item.end()
    for s, t in ((rec, rec_out), (dy, dy_out), (mixed, mixed_out), (gated, gated_out)):
        local.start(s, t, late=True)
    bsums[3].middle()
    settle(2)
    joins[1].relay()
    settle(3)
    local.start(here, here_out, late=True)
    joins[2].relay()
    joins[3].relay()
    for item in joins:
        item.end()
    local.start(branch, branch_out, late=True)
    for item in (
        rows_of_x + key_joins + query_joins + sums + misses + qsums + reads + rows_of_dy + bsums + joins
    ):
        item.drain()
    local.finish()


def run_forward_layer(*arrays):
    tokens, lw = arrays[0].shape
    square, wo = arrays[12].shape, arrays[14].shape
    width = square[0]
    tall, full, flat, padded = (tokens, lw), (tokens, width), (STRETCH, width), (KEY_ROWS, lw)
    deep = (tokens + 8, lw)
    vm = lambda shape, dtype=None: pltpu.VMEM(shape, bf16 if dtype is None else dtype)
    return call(
        forward_layer, 1,
        [shaped(full), shaped(tall, f32), shaped(tall, f32), shaped(tall, f32)] + [shaped(tall)] * 4
        + [shaped(flat), shaped(full)] + [shaped(flat)] * 5 + [shaped(full)] * 3
        + [shaped(square)] * 2
        + [shaped(full), shaped(tall, f32), shaped(tall), shaped(tall), shaped(full), shaped(full)],
        (0,) * 15 + (1,),
        [vm(full), vm((1, width), f32), vm((width, width)), vm((KW, lw), f32), vm((KW, lw), f32),
         vm((KW, lw), f32), vm(deep, f32), vm(deep, f32), vm(deep, f32), vm(tall), vm(tall), vm(tall),
         vm(tall), vm((NP, lw)), vm(flat), vm(full), vm(square), vm(square)]
        + [vm(flat)] * 6 + [vm(full)] * 4 + [vm(square)] * 2
        + [vm(wo), vm(padded), vm(padded), vm((STRETCH // 2, KEY_ROWS), f32), vm(tall), vm(tall),
           vm(full), vm(full), vm(tall, f32), vm(full), vm(full)]
        + scatter_room(STRETCH) + scatter_room(tokens) + scatter_room(tokens)
        + sems(100) + [pltpu.SemaphoreType.DMA((64,))],
        20 << 30, 40 << 20,
    )(*arrays)


def wide_places():
    at = lax.axis_index("wide")
    bits = (lax.rem(at, 2), lax.rem(lax.div(at, 2), 2), lax.div(at, 4))
    return bits, tuple(at + step * (1 - 2 * bit) for step, bit in zip((1, 2, 4), bits))


def enter_all(sib, opp, wide):
    barrier = pltpu.get_barrier_semaphore()
    for peer in (sib, opp):
        pl.semaphore_signal(barrier, inc=1, device_id={"narrow": peer}, device_id_type=MESH)
    for peer in wide[1]:
        pl.semaphore_signal(barrier, inc=1, device_id={"wide": peer}, device_id_type=MESH)
    pl.semaphore_wait(barrier, 5)


class WideSum:
    ahead = 2
    orders = ((0, 1, 2), (0, 1, 2), (1, 0, 2), (0, 1, 2))

    def __init__(self, wire, copy_sems, wide, chunks, room, ring):
        bits, peers = wide
        self.mine, self.got, self.more, self.rest, self.done = room
        self.items = []
        for k, (source, start, target, goal, rows) in enumerate(chunks):
            slot = k % ring
            order = self.orders[k % len(self.orders)]
            a, b, c = [bits[d] for d in order]
            pa, pb, pc = [peers[d] for d in order]
            off = lambda bit, size: pl.multiple_of(bit * size, size)
            n, h, q = rows // 2, rows // 4, rows // 8
            first = goal + off(a, n)
            second = first + off(b, h)
            third = second + off(c, q)
            spots = [target.at[pl.ds(at, size)] for at, size in ((third, q), (second, h), (first, n))]
            mine, got = self.mine.at[slot, pl.ds(0, n)], self.got.at[slot, pl.ds(0, n)]
            more, rest = self.more.at[slot, pl.ds(0, h)], self.rest.at[slot, pl.ds(0, q)]
            done = self.done.at[slot, pl.ds(0, q)]
            self.items.append({
                "mine": mine, "got": got, "more": more, "rest": rest, "done": done,
                "kept": self.got.at[slot, pl.ds(off(b, h), h)],
                "left": self.more.at[slot, pl.ds(off(c, q), q)],
                "load": pltpu.make_async_copy(
                    source.at[pl.ds(start + off(a, n), n)], mine, copy_sems.at[2 * k]
                ),
                "keep": pltpu.make_async_copy(done, spots[0], copy_sems.at[2 * k + 1]),
                "one": wire.to(source.at[pl.ds(start + off(1 - a, n), n)], got, pa, "wide"),
                "two": wire.to(self.got.at[slot, pl.ds(off(1 - b, h), h)], more, pb, "wide"),
                "three": wire.to(self.more.at[slot, pl.ds(off(1 - c, q), q)], rest, pc, "wide"),
                "four": wire.to(done, spots[0], pc, "wide"),
                "five": wire.to(spots[1], spots[1], pb, "wide"),
                "six": wire.to(spots[2], spots[2], pa, "wide"),
            })
        count = len(self.items)
        self.steps, self.begun, self.ready, self.wanted, self.next = [], 0, count, 0, 0
        stages = ((self.last, 6), (self.halve, 0), (self.again, 1), (self.total, 2), (self.back, 3),
                  (self.most, 4))
        for i in range(count + 6):
            for stage, lag in stages:
                if 0 <= i - lag < count:
                    self.steps.append((stage, i - lag))

    def open(self, ready):
        self.ready = ready
        self.begin(self.wanted)

    def begin(self, upto):
        self.wanted = max(self.wanted, upto)
        while self.begun < min(upto, self.ready, len(self.items)):
            self.items[self.begun]["load"].start()
            self.items[self.begun]["one"].start()
            self.begun += 1

    def halve(self, i):
        item = self.items[i]
        self.begin(i + 1)
        item["one"].wait_recv()
        self.begin(i + 1 + self.ahead)
        item["load"].wait()
        item["got"][...] = (
            item["got"][...].astype(f32) + item["mine"][...].astype(f32)
        ).astype(bf16)
        item["two"].start()

    def again(self, i):
        item = self.items[i]
        item["two"].wait_recv()
        item["more"][...] = (
            item["more"][...].astype(f32) + item["kept"][...].astype(f32)
        ).astype(bf16)
        item["three"].start()

    def total(self, i):
        item = self.items[i]
        item["three"].wait_recv()
        item["done"][...] = (
            item["rest"][...].astype(f32) + item["left"][...].astype(f32)
        ).astype(bf16)
        for name in ("one", "two", "three"):
            item[name].wait_send()
        item["four"].start()
        item["keep"].start()

    def back(self, i):
        item = self.items[i]
        item["four"].wait_recv()
        item["keep"].wait()
        item["four"].wait_send()
        item["five"].start()

    def most(self, i):
        item = self.items[i]
        item["five"].wait_recv()
        item["five"].wait_send()
        item["six"].start()

    def last(self, i):
        self.items[i]["six"].wait_recv()
        self.items[i]["six"].wait_send()

    def go(self, count=None):
        stop = len(self.steps) if count is None else min(self.next + count, len(self.steps))
        while self.next < stop:
            step, i = self.steps[self.next]
            if step == self.halve and i >= self.ready:
                break
            step(i)
            self.next += 1


def wide_room(ring):
    return [
        pltpu.VMEM((ring, rows, 1024), bf16) for rows in (128, 128, 64, 32, 32)
    ]


def moved_down(values, offset):
    row = lax.broadcasted_iota(jnp.int32, values.shape, 0)
    return jnp.where(row < offset, 0.0, pltpu.roll(values, offset, 0))


def moved_up(values, offset):
    rows = values.shape[0]
    row = lax.broadcasted_iota(jnp.int32, values.shape, 0)
    return jnp.where(row >= rows - offset, 0.0, pltpu.roll(values, rows - offset, 0))


RING = 11


def backward_layer(
    query_in, key_in, value_in, rec_in, wq_in, wk_in, wv_in, wg_in, pk_in, pv_in, gate_in, wo_in,
    mixed_in, gated_in, keys_in, queries_in, pre_in, act_in, mis_in, thr_in, ble_in, qpre_in,
    qact_in, one_in, two_in, next_one_in, next_two_in, x_in, gain_in, tq_in, tk_in, tv_in, cq_in, ck_in, cv_in,
    gaintwo_in, branch_in, here_in, dy_in, fgate_in, fup_in, fdown_in, normed_in, rates,
    ig_out, lo_out, gg_out, gu_out, gd_out, gwo_out, gwg_out, gone_out, gtwo_out, packed_out,
    extra_out,
    gg_mid, gu_mid, gd_mid, bm_mid, gwo_mid, gwg_mid, gone_mid, gtwo_mid, packed_mid, extra_mid, bgate_mid, gmk_mid, gmv_mid, bq_mid, bk_mid, bv_mid,
    qpart_mid, kpart_mid, vpart_mid,
    brec, late, bb, gaintwo, pkacc, pvacc,
    a_first, a_passed, a_last, l_first, l_passed, l_last, m_first, m_passed, m_last,
    q_first, q_passed, q_last, k_first, k_passed, k_last, t_first, t_passed, t_last,
    mine, got, more, rest, done, send, recv, local_sems, copy_sems,
):
    places = group_places()
    me, sib, opp, diag = places
    wire, local = Wire(send, recv), Local(local_sems)
    wide = wide_places()
    half, block = STRETCH // 2, STRETCH
    tokens, width = x_in.shape
    slim = wo_in.shape[0]
    chunks = []
    for source, target in (
        (gg_mid, gg_out), (gu_mid, gu_out), (gd_mid, gd_out), (gwo_mid, gwo_out), (gwg_mid, gwg_out),
        (gone_mid, gone_out), (gtwo_mid, gtwo_out), (packed_mid, packed_out),
    ):
        chunks += [(source, i * 256, target, i * 256, 256) for i in range(source.shape[0] // 256)]
    chunks += [(extra_mid, 0, extra_out, 0, 128)]
    adds = WideSum(wire, copy_sems, wide, chunks, (mine, got, more, rest, done), RING)
    adds.ready = 0
    adds.ahead = 5
    adds.begin(adds.ahead)
    pieces = [pl.ds(c * half, half) for c in range(2)]
    blocks = [pl.ds(b * block, block) for b in range(2)]
    whole = pl.ds(0, block)
    lanes = [pl.ds(i * 256, 256) for i in range(4)]
    early, bmis = bb.at[pl.ds(0, block)], bb.at[pl.ds(block, block)]
    early_join = Gather(wire, early, whole, places)
    misses = [Gather(wire, bmis, rows, places) for rows in pieces]
    recs = [Gather(wire, brec, rows, places) for rows in pieces]
    outs = []
    for b, half_sum in enumerate((brec, late)):
        side = pl.ds(b * block, block)
        outs += [
            Scatter(
                wire, half_sum, rows, q_first.at[:, side], q_passed.at[side], q_last.at[side], places
            )
            for rows in pieces
        ]

    def feed(
        x, branch, dy, gain, gate, up, down, normed, hidden, bup, bffn, part, bm,
        first_sum,
    ):
        loads = [
            local.start(s, t)
            for s, t in (
                (x_in, x), (branch_in, branch), (gaintwo_in, gain), (fgate_in, gate), (fup_in, up),
                (dy_in, dy), (fdown_in, down),
            )
        ]
        size = 256
        count = tokens // size
        parts_of = [pl.ds(c * size, size) for c in range(count)]
        enter_all(sib, opp, wide)
        for item in loads:
            item.wait()
        sums = [Scatter(wire, part, rows, t_first, t_passed, t_last, places) for rows in parts_of]
        joins = [Gather(wire, bb, rows, places) for rows in parts_of]
        gaintwo[...] = jnp.zeros_like(gaintwo)

        def settle(c):
            rows = parts_of[c]
            back = sums[c].end().astype(bf16).astype(f32) + dy[rows, cols(me)].astype(f32)
            bm[rows, :] = back
            bb[rows, cols(me)] = back.astype(bf16)
            joins[c].start()

        for c in range(count):
            rows = parts_of[c]
            middle = x[rows, :].astype(f32) + branch[rows, :].astype(f32)
            inv = lax.rsqrt(jnp.mean(middle * middle, axis=1, keepdims=True) + epsilon)
            normed[rows, :] = (middle * inv * gain[...]).astype(bf16)
            pre = jnp.dot(normed[rows, :], gate[...], preferred_element_type=f32)
            lift = jnp.dot(normed[rows, :], up[...], preferred_element_type=f32)
            back = nt(dy[rows, :], down[...])
            sig = jax.nn.sigmoid(pre)
            act = pre * sig
            hidden[rows, :] = (act * lift).astype(bf16)
            bup[rows, :] = (back * act).astype(bf16)
            bffn[rows, :] = (back * lift * (sig * (1.0 + pre * (1.0 - sig)))).astype(bf16)

        def grads(left, right, keep, target, k):
            rows = parts_of[k]
            keep[rows, :] = tn(left[:, rows], right[...]).astype(bf16)
            return local.start(keep.at[rows], target.at[rows])

        copies = []
        for c in range(count):
            rows = parts_of[c]
            copies.append(grads(normed, bffn, first_sum, gg_mid, c))
            back = nt(bffn[rows, :], gate[...]) + nt(bup[rows, :], up[...])
            middle = x[rows, :].astype(f32) + branch[rows, :].astype(f32)
            inv = lax.rsqrt(jnp.mean(middle * middle, axis=1, keepdims=True) + epsilon)
            unit = middle * inv
            gaintwo[...] += jnp.sum(back * unit, axis=0, keepdims=True)
            back = back * gain[...]
            part[rows, :] = (
                inv * (back - unit * jnp.mean(back * unit, axis=1, keepdims=True))
            ).astype(bf16)
            sums[c].start()
            copies.pop(0).wait()
            adds.open(adds.ready + 1)
            if c >= 1:
                sums[c - 1].middle()
                adds.go(1)
            if c >= 2:
                settle(c - 2)
            if c >= 3:
                joins[c - 3].relay()
        copies = [grads(normed, bup, gate, gu_mid, 0)]
        sums[3].middle()
        settle(2)
        joins[1].relay()
        for k in range(1, 4):
            copies.append(grads(normed, bup, gate, gu_mid, k))
            if k == 2:
                settle(3)
                joins[2].relay()
        adds.go(1)
        for c, rows in enumerate(parts_of):
            (brec, late)[c // 2][pieces[c % 2], :] = jnp.dot(
                hidden[rows, :], down[...], preferred_element_type=f32
            ).astype(bf16)
            outs[c].start()
        for item in copies:
            item.wait()
        adds.open(adds.ready + 4)
        joins[3].relay()
        adds.go(2)
        copies = []
        for k in range(4):
            copies.append(grads(hidden, dy, up, gd_mid, k))
        local.start(bm, bm_mid, late=True)
        adds.go(2)
        for item in joins:
            item.end()
        for item in copies:
            item.wait()
        adds.open(adds.ready + 4)
        for item in sums + joins:
            item.drain()
        local.finish()

    def attend(
        query, key, value, rec, wk, wv, gate, wo, mixed, gated, keys, values, bias, bmix, bgate,
        pk, gwo, gmk, gmv, bq, bk, bv, kacc, vacc, bmk, bmv, part,
        normed, gwg, xl, here, out,
    ):
        loads = [
            local.start(s, t)
            for s, t in (
                (normed_in, normed), (wo_in, wo), (gate_in, gate), (mixed_in, mixed), (gated_in, gated),
                (rec_in, rec), (wk_in, wk), (wv_in, wv), (query_in, query), (key_in, key),
                (value_in, value), (pk_in, pk), (x_in.at[:, cols(me)], xl), (here_in, here),
                (pv_in, values.at[pl.ds(2 * block, NP)]),
            )
        ]
        keys[pl.ds(2 * block + NP, 128 - NP), :] = jnp.zeros((128 - NP, 256), bf16)
        values[pl.ds(2 * block + NP, 128 - NP), :] = jnp.zeros((128 - NP, 256), bf16)
        pkacc[...] = jnp.zeros_like(pkacc)
        pvacc[...] = jnp.zeros_like(pvacc)
        gmk[...] = jnp.zeros_like(gmk)
        gmv[...] = jnp.zeros_like(gmv)
        for item in outs:
            item.middle()
        for item in loads:
            item.wait()

        def through_gate(c, carried):
            rows = pl.ds(pl.multiple_of(c * half, half), half)
            back = nt(bb[rows, :], wo[...])
            sig = jax.nn.sigmoid(gate[rows, :].astype(f32))
            bmix[rows, :] = (back * sig).astype(bf16)
            bgate[rows, :] = (back * mixed[rows, :].astype(f32) * sig * (1.0 - sig)).astype(bf16)
            return carried

        lax.fori_loop(0, 4, through_gate, 0)
        local.start(bgate, bgate_mid, late=True)
        gwo[...] = tn(gated[...], bb[...]).astype(bf16)
        out_copy = local.start(gwo, gwo_mid)
        for i, side in enumerate(lanes):
            gwg[:, side] = tn(normed[:, side], bgate[...]).astype(bf16)
        gate_copy = local.start(gwg, gwg_mid)
        ones = head_ones()
        keys[pl.ds(2 * block, NP), :] = unit_rows(pk[...], ones).astype(bf16)
        sums = [Scatter(wire, part, rows, a_first, a_passed, a_last, places) for rows in pieces]
        adds.go(3)
        out_copy.wait()
        gate_copy.wait()
        adds.open(adds.ready + 2)
        for b in (1, 0):
            rows = blocks[b]
            memory = rec[rows, :]
            made = jnp.dot(memory, wk[...], preferred_element_type=f32)
            inv = lax.rsqrt(split_sums(made * made, ones) + head_floor)
            keys[pl.ds(0, block), :] = (made * inv).astype(bf16)
            values[pl.ds(0, block), :] = jnp.dot(
                memory, wv[...], preferred_element_type=f32
            ).astype(bf16)
            keys[pl.ds(block, block), :] = key[rows, :]
            values[pl.ds(block, block), :] = value[rows, :]
            bias[...] = key_bias(0, block, rates[0] - float(b * block), True)
            kacc[...] = jnp.zeros_like(kacc)
            vacc[...] = jnp.zeros_like(vacc)

            def one_head(head, total):
                asked = head_only(query[rows, :], head)
                back = head_only(bmix[rows, :], head)
                weights = jnp.exp(score_scale * nt(keys[...], asked) + bias[...])
                weights = weights * (1.0 / jnp.sum(weights, axis=0, keepdims=True))
                vacc[...] += jnp.dot(weights.astype(bf16), back, preferred_element_type=f32)
                slope = nt(values[...], back)
                slope = (
                    weights * (slope - jnp.sum(weights * slope, axis=0, keepdims=True))
                ).astype(bf16)
                kacc[...] += jnp.dot(slope, asked, preferred_element_type=f32)
                read = tn(slope, keys[...])
                lane_head = lax.broadcasted_iota(jnp.int32, read.shape, 1) // HD
                return jnp.where(lane_head == head, read, total)

            asked_back = lax.fori_loop(0, 1, one_head, jnp.zeros((block, 256), f32))
            adds.go(2)
            asked_back = lax.fori_loop(1, 2, one_head, asked_back)
            adds.go(1)
            asked_back = lax.fori_loop(2, 3, one_head, asked_back)
            adds.go(2)
            bq[rows, :] = score_scale * lax.fori_loop(3, 4, one_head, asked_back)
            adds.go(1)
            bk[rows, :] = score_scale * kacc[pl.ds(block, block), :]
            bv[rows, :] = vacc[pl.ds(block, block), :]
            pkacc[...] += score_scale * kacc[pl.ds(2 * block, NP), :]
            pvacc[...] += vacc[pl.ds(2 * block, NP), :]
            unit = jnp.dot(memory, wk[...], preferred_element_type=f32) * inv
            back = score_scale * kacc[pl.ds(0, block), :]
            bmk[...] = ((back - unit * split_sums(back * unit, ones)) * inv).astype(bf16)
            bmv[...] = vacc[pl.ds(0, block), :].astype(bf16)
            if b == 1:
                for c, item in enumerate(outs):
                    side = pl.ds(c * half, half)
                    done_rows = xl[side, :].astype(f32) + here[side, :] + item.end()
                    out[side, :] = done_rows.astype(bf16)
                    item.drain()
                local.start(out, lo_out, late=True)
            for c in range(2):
                target = part if b == 1 else late
                target[pieces[c], :] = (
                    nt(bmk[pieces[c], :], wk[...]) + nt(bmv[pieces[c], :], wv[...])
                ).astype(bf16)
                if b == 1:
                    sums[c].start()
                else:
                    brec[pieces[c], cols(me)] = sums[c].end().astype(bf16)
                    recs[c].start()
            gmk[...] += tn(memory, bmk[...])
            if b == 1:
                sums[0].middle()
            gmv[...] += tn(memory, bmv[...])
            if b == 1:
                sums[1].middle()
            adds.go(2)
        for s, t in ((gmk, gmk_mid), (gmv, gmv_mid), (bq, bq_mid), (bk, bk_mid), (bv, bv_mid)):
            local.start(s, t, late=True)
        for item in recs:
            item.relay()
        for item in sums:
            item.drain()
        adds.go(2)
        local.finish()

    def remember(
        key, query, pre, act, mis, thr, ble, qpre, qact, one, two, next_one, next_two, cone, ctwo, bble,
        bthr, bqm, mpart, bpre, klow, qlow, kout, qout, vout,
    ):
        loads = [
            local.start(s, t)
            for s, t in (
                (next_two_in, next_two), (qpre_in, qpre), (next_one_in, next_one),
                (queries_in, query), (qact_in, qact), (keys_in, key), (pre_in, pre), (act_in, act),
                (two_in, two), (mis_in, mis), (one_in, one), (thr_in, thr), (ble_in, ble),
            )
        ]
        lates = Scatter(wire, late, whole, l_first, l_passed, l_last, places)
        sums = [Scatter(wire, mpart, rows, m_first, m_passed, m_last, places) for rows in pieces]
        asks = [Scatter(wire, qlow, rows, q_first, q_passed, q_last, places) for rows in blocks]
        tells = [Scatter(wire, klow, rows, k_first, k_passed, k_last, places) for rows in pieces]
        lates.start()
        for item in loads:
            item.wait()
        for item in recs:
            item.end()
            item.drain()
        step_size, keep = rates[1], rates[2]

        def ask_back(c, source, row_start, weight_one, weight_two):
            rows = pl.ds(row_start + c * half, half)
            back = nt(source[pieces[c], :], weight_two[...])
            bqm[pieces[c], :] = (back * slope_of(qpre[rows, :].astype(f32))).astype(bf16)
            qlow[rows, :] = nt(bqm[pieces[c], :], weight_one[...]).astype(bf16)

        for c in range(2):
            ask_back(c, brec, block, next_one, next_two)
            if c == 0:
                lates.middle()
                adds.go(2)
        asks[1].start()
        early[:, cols(me)] = lates.end().astype(bf16)
        early_join.start()
        adds.go(2)

        def first_sums(c, carried):
            rows = pl.ds(pl.multiple_of(c * half, half), half)
            grad = tn(query[blocks[1], rows], bqm[...])
            cone[rows, :] = keep * grad
            next_one[rows, :] = (-step_size * grad).astype(bf16)
            grad = tn(qact[blocks[1], rows], brec[...])
            ctwo[rows, :] = keep * grad
            next_two[rows, :] = (-step_size * grad).astype(bf16)
            return carried

        for c in range(0, 4, 2):
            lax.fori_loop(c, c + 2, first_sums, 0)
            adds.go(3 if c else 2)
        for c in range(2):
            rows = pieces[c]
            back = jnp.dot(key[rows, :], next_one[...], preferred_element_type=f32)
            bble[rows, :] = back.astype(bf16)
            bthr[rows, :] = (back * slope_of(pre[rows, :].astype(f32))).astype(bf16)
            mpart[rows, :] = (
                jnp.dot(act[rows, :], next_two[...], preferred_element_type=f32)
                + jnp.dot(bthr[rows, :], two[...], preferred_element_type=f32)
            ).astype(bf16)
            sums[c].start()
            if c == 0:
                early_join.relay()
                adds.go(2)
        sums[0].middle()
        asks[1].middle()
        adds.go(3)
        sums[1].middle()
        early_join.end()
        for c in range(2):
            ask_back(c, early, 0, one, two)
            adds.go(2)
        asks[0].start()
        for c in range(2):
            rows = pieces[c]
            back = sums[c].end().astype(bf16)
            index = lax.broadcasted_iota(jnp.int32, (half, 1), 0) + c * half
            scale = jnp.where(index.astype(f32) < rates[0], 1.0 / STRETCH, 0.0)
            bmis[rows, cols(me)] = back
            misses[c].start()
            vout[rows, :] = -(back.astype(f32) * scale)
        local.start(vout, vpart_mid, late=True)

        def second_sums(c, carried):
            rows = pl.ds(pl.multiple_of(c * half, half), half)
            cone[rows, :] += tn(query[blocks[0], rows], bqm[...])
            ctwo[rows, :] += tn(bthr[:, rows], mis[...]) + tn(qact[blocks[0], rows], early[...])
            return carried

        lax.fori_loop(0, 1, second_sums, 0)
        adds.go(2)
        lax.fori_loop(1, 2, second_sums, 0)
        misses[0].relay()
        asks[0].middle()
        adds.go(3)
        lax.fori_loop(2, 3, second_sums, 0)
        misses[1].relay()
        adds.go(2)
        lax.fori_loop(3, 4, second_sums, 0)
        adds.go(2)
        for c in range(2):
            rows = pieces[c]
            misses[c].end()
            misses[c].drain()
            index = lax.broadcasted_iota(jnp.int32, (half, 1), 0) + c * half
            scale = jnp.where(index.astype(f32) < rates[0], 1.0 / STRETCH, 0.0)
            bmis[rows, :] = (bmis[rows, :].astype(f32) * scale).astype(bf16)
            values = pre[rows, :].astype(f32)
            sig = jax.nn.sigmoid(values)
            drop = 1.0 - sig
            slant = sig * drop
            curve = slant * (1.0 + values * drop) + sig * (drop - values * slant)
            back = nt(mis[rows, :], next_two[...]) + nt(bmis[rows, :], two[...])
            bpre[rows, :] = (
                back * (sig * (1.0 + values * drop))
                + bble[rows, :].astype(f32) * thr[rows, :].astype(f32) * curve
            ).astype(bf16)
            klow[rows, :] = (
                nt(ble[rows, :], next_one[...]) + nt(bpre[rows, :], one[...])
            ).astype(bf16)
            tells[c].start()
            adds.go(3 if c else 2)
        tells[0].middle()
        tells[1].middle()

        def last_sums(c, carried):
            rows = pl.ds(pl.multiple_of(c * half, half), half)
            next_one[rows, :] = (cone[rows, :] + tn(key[:, rows], bpre[...])).astype(bf16)
            next_two[rows, :] = (ctwo[rows, :] + tn(act[:, rows], bmis[...])).astype(bf16)
            return carried

        for c in range(0, 4, 2):
            lax.fori_loop(c, c + 2, last_sums, 0)
            if c == 0:
                adds.go(2)
        local.start(next_one, gone_mid, late=True)
        local.start(next_two, gtwo_mid, late=True)
        adds.go(3)
        for b in (1, 0):
            qout[blocks[b], :] = asks[b].end()
        local.start(qout, qpart_mid, late=True)
        for c in range(2):
            kout[pieces[c], :] = tells[c].end()
        local.start(kout, kpart_mid, late=True)
        for item in [lates, early_join] + sums + asks + tells:
            item.drain()
        local.finish()
        adds.open(adds.ready + 2 * width // 256)

    def finish(
        x, gain, weights, tq, tk, tv, qpre, kpre, vpre, bq, bk, bv, qpart, kpart, vpart, cot, gmk, gmv, pk,
        bm, extra, packed, normed, part, ig, conv_rows,
    ):
        loads = [
            local.start(s, t)
            for s, t in (
                (cq_in, qpre), (bq_mid, bq), (qpart_mid, qpart), (tq_in, tq), (tk_in, tk),
                (tv_in, tv), (ck_in, kpre),
                (bk_mid, bk), (kpart_mid, kpart), (cv_in, vpre), (bv_mid, bv), (vpart_mid, vpart),
                (x_in, x), (gain_in, gain), (wq_in, weights.at[:, lanes[0]]),
                (wk_in, weights.at[:, lanes[1]]), (wv_in, weights.at[:, lanes[2]]),
                (wg_in, weights.at[:, lanes[3]]), (bgate_mid, cot.at[:, lanes[3]]),
                (gmk_mid, gmk), (gmv_mid, gmv), (pk_in, pk), (bm_mid, bm),
            )
        ]
        adds.go(2)
        for item in loads:
            item.wait()
        ones = head_ones()

        def through_conv(pre, taps, at, back, normal):
            values = pre[...]
            conv = values * taps[pl.ds(0, 1), :]
            for j in range(1, KW):
                conv = conv + moved_down(values, j) * taps[pl.ds(j, 1), :]
            sig = jax.nn.sigmoid(conv)
            if normal:
                act = conv * sig
                inv = lax.rsqrt(split_sums(act * act, ones) + head_floor)
                unit = act * inv
                back = (back - unit * split_sums(back * unit, ones)) * inv
            back = back * (sig * (1.0 + conv * (1.0 - sig)))
            result = back * taps[pl.ds(0, 1), :]
            conv_rows[pl.ds(at, 1), :] = jnp.sum(back * values, axis=0, keepdims=True)
            for j in range(1, KW):
                conv_rows[pl.ds(at + j, 1), :] = jnp.sum(
                    back * moved_down(values, j), axis=0, keepdims=True
                )
                result = result + moved_up(back, j) * taps[pl.ds(j, 1), :]
            return result.astype(bf16)

        conv_rows[...] = jnp.zeros_like(conv_rows)
        cot[:, lanes[0]] = through_conv(qpre, tq, 0, bq[...] + qpart[...], True)
        adds.go(2)
        bk[whole, :] += kpart[...]
        cot[:, lanes[1]] = through_conv(kpre, tk, KW, bk[...], True)
        adds.go(2)
        bv[whole, :] += vpart[...]
        cot[:, lanes[2]] = through_conv(vpre, tv, 2 * KW, bv[...], False)
        adds.go(2)
        rows_of_x = [pl.ds(c * 256, 256) for c in range(tokens // 256)]
        sums = [Scatter(wire, part, rows, t_first, t_passed, t_last, places) for rows in rows_of_x]
        tail_rows = pl.ds(tokens, 16)
        gains = Scatter(wire, part, tail_rows, t_first, t_passed, t_last, places)
        gain_sum = jnp.zeros((1, width), f32)
        for c, rows in enumerate(rows_of_x):
            back = nt(cot[rows, :], weights[...])
            values = x[rows, :].astype(f32)
            inv = lax.rsqrt(jnp.mean(values * values, axis=1, keepdims=True) + epsilon)
            unit = values * inv
            normed[rows, :] = (unit * gain[...]).astype(bf16)
            gain_sum = gain_sum + jnp.sum(back * unit, axis=0, keepdims=True)
            back = back * gain[...]
            part[rows, :] = (
                inv * (back - unit * jnp.mean(back * unit, axis=1, keepdims=True))
            ).astype(bf16)
            sums[c].start()
            if c >= 1:
                sums[c - 1].middle()
            adds.go(2)
        row = lax.broadcasted_iota(jnp.int32, (16, width), 0)
        part[tail_rows, :] = jnp.where(
            row == 0, gain_sum, jnp.where(row == 1, gaintwo[...], 0.0)
        ).astype(bf16)
        gains.start()
        for c in range(width // 256):
            made = tn(normed[:, rows_of_x[c]], cot[:, pl.ds(0, 768)])
            packed[pl.ds(0, 256), lanes[c]] = made[:, 0:256].astype(bf16)
            packed[pl.ds(256, 256), lanes[c]] = (made[:, 256:512] + gmk[rows_of_x[c], :]).astype(bf16)
            packed[pl.ds(512, 256), lanes[c]] = (made[:, 512:768] + gmv[rows_of_x[c], :]).astype(bf16)
            if c % 2:
                adds.go(2)
        pack_copy = local.start(packed, packed_mid)
        sums[-1].middle()
        gains.middle()
        extra[...] = jnp.zeros_like(extra)
        start = pk[...].astype(f32)
        inv = lax.rsqrt(split_sums(start * start, ones) + head_floor)
        unit = start * inv
        back = pkacc[...]
        top = pl.ds(0, 16)
        extra[top, lanes[0]] = ((back - unit * split_sums(back * unit, ones)) * inv).astype(bf16)
        extra[top, lanes[1]] = pvacc[...].astype(bf16)
        extra[top, lanes[2]] = conv_rows[...].astype(bf16)
        pack_copy.wait()
        adds.open(adds.ready + 3)
        adds.go(2)
        extra[top, lanes[3]] = gains.end().astype(bf16)
        local.start(extra, extra_mid, late=True)
        for c, rows in enumerate(rows_of_x):
            ig[rows, :] = bm[rows, :] + sums[c].end()
        local.start(ig, ig_out, late=True)
        local.finish()
        adds.open(len(chunks))
        for item in sums + [gains]:
            item.drain()

    vm = lambda shape, dtype=None: pltpu.VMEM(shape, bf16 if dtype is None else dtype)
    lw = query_in.shape[1]
    tall, full, flat, weight = (tokens, lw), (tokens, width), (block, width), (width, lw)
    padded, small, square = (KEY_ROWS, lw), (block, lw), one_in.shape
    row = (1, width)
    pl.run_scoped(
        feed,
        vm(full), vm(full), vm(full), vm(row, f32), vm(square), vm(square), vm(square),
        vm(full), vm(full), vm(full), vm(full), vm(full), vm(tall, f32), vm(square),
    )
    pl.run_scoped(
        attend,
        vm(tall), vm(tall), vm(tall), vm(full), vm(weight), vm(weight), vm(tall), vm((lw, width)),
        vm(tall), vm(tall), vm(padded), vm(padded), vm((KEY_ROWS, block), f32), vm(tall),
        vm(tall), vm((NP, lw)), vm((lw, width)), vm(weight, f32), vm(weight, f32), vm(tall, f32), vm(tall, f32),
        vm(tall, f32), vm(padded, f32), vm(padded, f32), vm(small), vm(small), vm(flat), vm(full), vm((256, width)),
        vm(tall), vm(tall, f32), vm(tall),
    )
    pl.run_scoped(
        remember,
        vm(flat), vm(full), vm(flat), vm(flat), vm(flat), vm(flat), vm(flat), vm(full), vm(full),
        vm(square), vm(square), vm(square), vm(square), vm(square, f32), vm(square, f32), vm(flat),
        vm(flat), vm(flat), vm(flat), vm(flat), vm(flat), vm(full), vm(small, f32), vm(tall, f32),
        vm(small, f32),
    )
    pl.run_scoped(
        finish,
        vm(full), vm(row, f32), vm((width, width)), vm((KW, lw), f32), vm((KW, lw), f32),
        vm((KW, lw), f32), vm(tall, f32),
        vm(tall, f32), vm(tall, f32), vm(tall, f32), vm(tall, f32), vm(tall, f32), vm(tall, f32),
        vm(small, f32), vm(small, f32), vm(full), vm(weight, f32), vm(weight, f32), vm((NP, lw)),
        vm(tall, f32), vm((128, width)), vm((768, width)), vm(full),
        vm((tokens + 16, width)), vm(tall, f32), vm((16, 256), f32),
    )
    adds.go()


def run_backward_layer(*arrays):
    query, wo, one, x = arrays[0], arrays[11], arrays[23], arrays[27]
    tokens, width = x.shape
    lw = query.shape[1]
    tall, flat, weight, square = (tokens, lw), (STRETCH, width), (width, lw), (width, width)
    small, packed, extra = (STRETCH, lw), (3 * lw, width), (128, width)
    count = (5 * width + 5 * lw) // 256 + 1
    vm = lambda shape, dtype=None: pltpu.VMEM(shape, bf16 if dtype is None else dtype)
    sums = [shaped(square)] * 3 + [shaped((lw, width))] * 2 + [shaped(one.shape)] * 2
    sums += [shaped(packed), shaped(extra)]
    return call(
        backward_layer, 4,
        [shaped(tall, f32), shaped(tall)] + sums
        + [shaped(square)] * 3 + [shaped(tall, f32)] + sums[3:]
        + [shaped(tall), shaped(weight, f32), shaped(weight, f32), shaped(tall, f32),
           shaped(tall, f32), shaped(tall, f32), shaped(tall, f32), shaped(small, f32),
           shaped(small, f32)],
        (0,) * (len(arrays) - 1) + (1,),
        [vm(flat), vm(flat), vm((tokens, width)), vm((1, width), f32), vm((NP, lw), f32),
         vm((NP, lw), f32)]
        + scatter_room(STRETCH) * 3 + scatter_room(tokens) + scatter_room(STRETCH)
        + scatter_room(tokens + 16) + wide_room(RING)
        + sems(6 * count + 120)
        + [pltpu.SemaphoreType.DMA((160,)), pltpu.SemaphoreType.DMA((2 * count,))],
        65 << 30, 120 << 20,
    )(*arrays)[:11]


def widen(*refs):
    count = (len(refs) - 8) // 2
    for source, target in zip(refs[:count], refs[count + 1 : 2 * count + 1]):
        target[...] = source[...].astype(target.dtype)
    extra, small = refs[count], refs[2 * count + 1 :]
    starts = ((0, 0), (0, 256), (0, 512), (KW, 512), (2 * KW, 512), (0, 768), (1, 768))
    for target, (row, lane) in zip(small, starts):
        rows = target.shape[0]
        target[...] = extra[...].astype(f32)[row : row + rows, lane : lane + 256]


def run_widen(flat, quarter, same, extra):
    steps = 4
    ins, outs, shapes = [], [], []
    for v in flat:
        spec = pl.BlockSpec((v.shape[0] // steps, v.shape[1]), lambda i: (i, 0))
        ins.append(spec)
        outs.append(spec)
        shapes.append(shaped(v.shape, f32))
    for v, place in quarter:
        ins.append(pl.BlockSpec((256, 256), lambda i, place=place: (place, i)))
        outs.append(pl.BlockSpec((256, 256), lambda i: (i, 0)))
        shapes.append(shaped((1024, 256), f32))
    for v in same:
        spec = pl.BlockSpec((v.shape[0] // steps, v.shape[1]), lambda i: (i, 0))
        ins.append(spec)
        outs.append(spec)
        shapes.append(shaped(v.shape, v.dtype))
    ins.append(pl.BlockSpec((16, extra.shape[1]), lambda i: (0, 0)))
    for rows in (NP, NP, KW, KW, KW, 1, 1):
        outs.append(pl.BlockSpec((rows, 256), lambda i: (0, 0)))
        shapes.append(shaped((rows, 256), f32))
    return pl.pallas_call(
        widen, out_shape=shapes, grid=(steps,), in_specs=ins, out_specs=outs,
        compiler_params=pltpu.CompilerParams(vmem_limit_bytes=VMEM_LIMIT), name="widen",
    )(*flat, *(v for v, place in quarter), *same, extra)


def plain_body(
    layer_input,
    out_grad,
    lengths,
    plan,
    norm1_gain,
    w_query,
    w_key,
    w_value,
    w_gate,
    conv_query,
    conv_key,
    conv_value,
    persist_key,
    persist_value,
    mem_w1,
    mem_w2,
    w_out,
    norm2_gain,
    ffn_gate,
    ffn_up,
    ffn_down,
):
    tokens_here = layer_input.shape[0]
    local_width = w_query.shape[1]
    heads_here = local_width // HD
    blocks = tokens_here // STRETCH
    places = jnp.arange(tokens_here)
    row_mask = (places < lengths[0]).astype(f32)
    block_mask = row_mask.reshape(blocks, STRETCH)
    levels = plan[0].astype(f32)
    column_start = lax.axis_index("narrow") * local_width

    def rows_of(values, b):
        return values[b * STRETCH : (b + 1) * STRETCH]

    whole_x = gather_columns(layer_input).astype(f32)
    whole_dy = gather_columns(out_grad)
    inv_one = lax.rsqrt(jnp.mean(whole_x * whole_x, axis=1, keepdims=True) + epsilon)
    unit_one = whole_x * inv_one
    normed_one = (unit_one * norm1_gain).astype(bf16)
    key_pre = product(normed_one, w_key)
    query_pre = product(normed_one, w_query)
    value_pre = product(normed_one, w_value)
    gate_pre = product(normed_one, w_gate)
    key_conv = causal_conv(key_pre, conv_key)
    query_conv = causal_conv(query_pre, conv_query)
    value_conv = causal_conv(value_pre, conv_value)
    key_unit, key_inv = head_norm(jax.nn.silu(key_conv))
    query_unit, query_inv = head_norm(jax.nn.silu(query_conv))
    query_low = query_unit.astype(bf16)
    key_low = key_unit.astype(bf16)
    value_low = jax.nn.silu(value_conv).astype(bf16)

    weight_one, weight_two = mem_w1.astype(f32), mem_w2.astype(f32)
    moment_one = moment_two = None
    saved = []
    for b in range(blocks):
        step_size, momentum, forget = plan_rates(levels[b])
        kept = {"first": weight_one.astype(bf16), "second": weight_two.astype(bf16)}
        mask_rows = block_mask[b][:, None]
        if b < blocks - 1:
            key_rows = gather_columns(rows_of(key_low, b))
            hidden_pre = product(key_rows, kept["first"])
            hidden_act = jax.nn.silu(hidden_pre).astype(bf16)
            predicted = scatter_columns(product(hidden_act, kept["second"]))
            mismatch_here = (
                (predicted - rows_of(value_low, b).astype(f32)) * (mask_rows / STRETCH)
            ).astype(bf16)
            mismatch = gather_columns(mismatch_here)
        query_rows = gather_columns(rows_of(query_low, b))
        query_mem = product(query_rows, kept["first"])
        query_act = jax.nn.silu(query_mem).astype(bf16)
        retrieved = scatter_columns(product(query_act, kept["second"]))
        kept["recalled"] = gather_columns(retrieved.astype(bf16))
        kept.update(query_rows=query_rows, query_mem=query_mem, query_act=query_act)
        if b < blocks - 1:
            through = inner_right(mismatch, kept["second"])
            blended = (through * silu_grad(hidden_pre)).astype(bf16)
            grad_one = inner_left(key_rows, blended)
            grad_two = inner_left(hidden_act, mismatch)
            if moment_one is None:
                moment_one, moment_two = -step_size * grad_one, -step_size * grad_two
            else:
                moment_one = momentum * moment_one - step_size * grad_one
                moment_two = momentum * moment_two - step_size * grad_two
            weight_one = (1.0 - forget) * weight_one + moment_one
            weight_two = (1.0 - forget) * weight_two + moment_two
            kept.update(
                key_rows=key_rows,
                hidden_pre=hidden_pre,
                hidden_act=hidden_act,
                mismatch=mismatch,
                through=through,
                blended=blended,
            )
        saved.append(kept)

    pers_unit, pers_inv = head_norm(persist_key.astype(f32))
    pers_low = pers_unit.astype(bf16)

    def block_scores(b):
        recalled = saved[b]["recalled"]
        mem_unit, mem_inv = head_norm(product(recalled, w_key))
        mem_value = product(recalled, w_value).astype(bf16)
        all_keys = jnp.concatenate(
            [pers_low, mem_unit.astype(bf16), rows_of(key_low, b)], axis=0
        ).reshape(-1, heads_here, HD)
        all_values = jnp.concatenate(
            [persist_value, mem_value, rows_of(value_low, b)], axis=0
        ).reshape(-1, heads_here, HD)
        query_heads = rows_of(query_low, b).reshape(STRETCH, heads_here, HD)
        scores = score_scale * jnp.einsum(
            "qhd,khd->hqk", query_heads, all_keys, preferred_element_type=f32
        )
        scores = jnp.where(visible(block_mask[b])[None], scores, -1e30)
        return (mem_unit, mem_inv, all_keys, all_values, query_heads, scores)

    mixed_list = []
    for b in range(blocks):
        mem_unit, mem_inv, all_keys, all_values, query_heads, scores = block_scores(b)
        row_peak = jnp.max(scores, axis=2, keepdims=True)
        exponent = jnp.exp(scores - row_peak)
        row_total = jnp.sum(exponent, axis=2, keepdims=True)
        prob_low = (exponent / row_total).astype(bf16)
        mixed_list.append(
            jnp.einsum(
                "hqk,khd->qhd", prob_low, all_values, preferred_element_type=f32
            ).reshape(STRETCH, local_width)
        )
        saved[b].update(
            log_total=row_peak + jnp.log(row_total),
            mem_unit=mem_unit,
            mem_inv=mem_inv,
            all_keys=all_keys,
            all_values=all_values,
            query_heads=query_heads,
        )
    mixed_all = jnp.concatenate(mixed_list, axis=0)
    gate_sig = jax.nn.sigmoid(gate_pre)
    gated = (mixed_all * gate_sig).astype(bf16)
    branch_here = scatter_columns(product(gated, w_out))
    branch_full = gather_columns(branch_here.astype(bf16)).astype(f32)
    middle = whole_x + branch_full
    middle_here = layer_input.astype(f32) + branch_here
    inv_two = lax.rsqrt(jnp.mean(middle * middle, axis=1, keepdims=True) + epsilon)
    unit_two = middle * inv_two
    normed_two = (unit_two * norm2_gain).astype(bf16)
    ffn_pre = product(normed_two, ffn_gate)
    up_pre = product(normed_two, ffn_up)
    ffn_sig = jax.nn.sigmoid(ffn_pre)
    hidden_low = (ffn_pre * ffn_sig * up_pre).astype(bf16)
    back_hidden = inner_right(whole_dy, ffn_down)
    back_up_low = (back_hidden * ffn_pre * ffn_sig).astype(bf16)
    back_ffn_low = (back_hidden * up_pre * silu_grad(ffn_pre)).astype(bf16)
    back_normed_two = inner_right(back_ffn_low, ffn_gate) + inner_right(back_up_low, ffn_up)
    gain_two_part = jnp.sum(back_normed_two * unit_two, axis=0)
    middle_part = norm_back(back_normed_two, unit_two, inv_two, norm2_gain)
    back_middle_here = scatter_columns(middle_part)
    grad_ffn_down = inner_left(hidden_low, whole_dy)
    grad_ffn_gate = inner_left(normed_two, back_ffn_low)
    grad_ffn_up = inner_left(normed_two, back_up_low)
    ffn_here = scatter_columns(product(hidden_low, ffn_down))
    layer_output = (middle_here + ffn_here).astype(bf16)
    back_middle_here = back_middle_here + out_grad.astype(f32)
    back_branch = gather_columns(back_middle_here.astype(bf16))
    grad_ffn_gate, grad_ffn_up, grad_ffn_down = sum_wide(
        [grad_ffn_gate, grad_ffn_up, grad_ffn_down]
    )
    grad_w_out = inner_left(gated, back_branch)
    back_gated = inner_right(back_branch, w_out)
    back_mixed_low = (back_gated * gate_sig).astype(bf16)
    back_gate_low = (back_gated * mixed_all * gate_sig * (1.0 - gate_sig)).astype(bf16)

    back_recalled_parts = []
    mem_key_grad = mem_value_grad = 0.0
    pers_key_acc = grad_persist_value = 0.0
    back_query_att, back_key_att, back_value_att = [], [], []
    for b in range(blocks):
        kept = saved[b]
        scores = score_scale * jnp.einsum(
            "qhd,khd->hqk", kept["query_heads"], kept["all_keys"], preferred_element_type=f32
        )
        scores = jnp.where(visible(block_mask[b])[None], scores, -1e30)
        prob_rows = jnp.exp(scores - kept["log_total"])
        prob_low = prob_rows.astype(bf16)
        back_heads = rows_of(back_mixed_low, b).reshape(STRETCH, heads_here, HD)
        back_all_values = jnp.einsum(
            "hqk,qhd->khd", prob_low, back_heads, preferred_element_type=f32
        )
        back_probs = jnp.einsum(
            "qhd,khd->hqk", back_heads, kept["all_values"], preferred_element_type=f32
        )
        back_scores = (
            prob_rows * (back_probs - jnp.sum(prob_rows * back_probs, axis=2, keepdims=True))
        ).astype(bf16)
        back_query = score_scale * jnp.einsum(
            "hqk,khd->qhd", back_scores, kept["all_keys"], preferred_element_type=f32
        )
        back_all_keys = score_scale * jnp.einsum(
            "hqk,qhd->khd", back_scores, kept["query_heads"], preferred_element_type=f32
        )
        back_all_keys = back_all_keys.reshape(-1, local_width)
        back_all_values = back_all_values.reshape(-1, local_width)
        back_mem_key = head_back(
            back_all_keys[NP : NP + STRETCH], kept["mem_unit"], kept["mem_inv"]
        ).astype(bf16)
        back_mem_value = back_all_values[NP : NP + STRETCH].astype(bf16)
        back_recalled_parts.append(
            inner_right(back_mem_key, w_key) + inner_right(back_mem_value, w_value)
        )
        mem_key_grad = mem_key_grad + inner_left(kept["recalled"], back_mem_key)
        mem_value_grad = mem_value_grad + inner_left(kept["recalled"], back_mem_value)
        pers_key_acc = pers_key_acc + back_all_keys[:NP]
        grad_persist_value = grad_persist_value + back_all_values[:NP]
        back_query_att.append(back_query.reshape(STRETCH, local_width))
        back_key_att.append(back_all_keys[NP + STRETCH :])
        back_value_att.append(back_all_values[NP + STRETCH :])
    grad_persist_key = head_back(pers_key_acc, pers_unit, pers_inv)

    cot_one = cot_two = mom_one = mom_two = None
    key_total, query_total, value_total = [None] * blocks, [None] * blocks, [None] * blocks
    for b in reversed(range(blocks)):
        kept = saved[b]
        step_size, momentum, forget = plan_rates(levels[b])
        first_low, second_low = kept["first"], kept["second"]
        back_recalled = gather_columns(scatter_columns(back_recalled_parts[b]).astype(bf16))
        new_one = new_two = None
        if cot_one is None:
            key_total[b], value_total[b] = back_key_att[b], back_value_att[b]
        else:
            key_rows, hidden_pre = kept["key_rows"], kept["hidden_pre"]
            hidden_slope = silu_grad(hidden_pre)
            total_one = cot_one if mom_one is None else mom_one + cot_one
            total_two = cot_two if mom_two is None else mom_two + cot_two
            back_g1 = (-step_size * total_one).astype(bf16)
            back_g2 = (-step_size * total_two).astype(bf16)
            back_blended = product(key_rows, back_g1)
            back_through = (back_blended * hidden_slope).astype(bf16)
            mismatch_part = product(kept["hidden_act"], back_g2) + product(
                back_through, second_low
            )
            mismatch_low = scatter_columns(mismatch_part).astype(bf16)
            back_mismatch = gather_columns(mismatch_low)
            key_part = inner_right(kept["blended"], back_g1)
            back_hidden_act = inner_right(kept["mismatch"], back_g2)
            extra_pre = back_blended * kept["through"] * silu_curve(hidden_pre)
            new_one = (1.0 - forget) * cot_one
            new_two = (1.0 - forget) * cot_two + inner_left(back_through, kept["mismatch"])
        back_query_act = inner_right(back_recalled, second_low)
        back_query_pre = (back_query_act * silu_grad(kept["query_mem"])).astype(bf16)
        query_part = inner_right(back_query_pre, first_low)
        one_term = inner_left(kept["query_rows"], back_query_pre)
        two_term = inner_left(kept["query_act"], back_recalled)
        new_one = one_term if new_one is None else new_one + one_term
        new_two = two_term if new_two is None else new_two + two_term
        if cot_one is not None:
            scale_rows = (block_mask[b] / STRETCH).astype(bf16)[:, None]
            back_pred = back_mismatch * scale_rows
            value_part = -(mismatch_low.astype(f32) * scale_rows.astype(f32))
            back_hidden_act = back_hidden_act + inner_right(back_pred, second_low)
            new_two = new_two + inner_left(kept["hidden_act"], back_pred)
            back_hidden_pre = (back_hidden_act * hidden_slope + extra_pre).astype(bf16)
            key_part = key_part + inner_right(back_hidden_pre, first_low)
            new_one = new_one + inner_left(key_rows, back_hidden_pre)
            key_total[b] = back_key_att[b] + scatter_columns(key_part)
            value_total[b] = back_value_att[b] + value_part
            mom_one, mom_two = momentum * total_one, momentum * total_two
        query_total[b] = back_query_att[b] + scatter_columns(query_part)
        cot_one, cot_two = new_one, new_two
    grad_mem_w1, grad_mem_w2 = cot_one, cot_two

    back_query_total = jnp.concatenate(query_total, axis=0)
    back_key_total = jnp.concatenate(key_total, axis=0)
    back_value_total = jnp.concatenate(value_total, axis=0)
    query_conv_back = head_back(back_query_total, query_unit, query_inv) * silu_grad(query_conv)
    key_conv_back = head_back(back_key_total, key_unit, key_inv) * silu_grad(key_conv)
    value_conv_back = back_value_total * silu_grad(value_conv)
    query_pre_back, grad_conv_query = conv_back(query_conv_back, query_pre, conv_query)
    key_pre_back, grad_conv_key = conv_back(key_conv_back, key_pre, conv_key)
    value_pre_back, grad_conv_value = conv_back(value_conv_back, value_pre, conv_value)
    query_pre_low = query_pre_back.astype(bf16)
    key_pre_low = key_pre_back.astype(bf16)
    value_pre_low = value_pre_back.astype(bf16)
    back_normed_one = (
        inner_right(back_gate_low, w_gate)
        + inner_right(query_pre_low, w_query)
        + inner_right(key_pre_low, w_key)
        + inner_right(value_pre_low, w_value)
    )
    gain_one_part = jnp.sum(back_normed_one * unit_one, axis=0)
    input_part = norm_back(back_normed_one, unit_one, inv_one, norm1_gain)
    back_input_here = scatter_columns(input_part)
    grad_w_gate = inner_left(normed_one, back_gate_low)
    grad_w_query = inner_left(normed_one, query_pre_low)
    grad_w_key = inner_left(normed_one, key_pre_low) + mem_key_grad
    grad_w_value = inner_left(normed_one, value_pre_low) + mem_value_grad
    input_grad = back_middle_here + back_input_here

    gains = lax.psum(
        jnp.concatenate([gain_one_part, gain_two_part]).astype(bf16), ("narrow", "wide")
    ).astype(f32)
    full_width = whole_x.shape[1]
    grad_norm1_gain = lax.dynamic_slice_in_dim(gains, column_start, local_width, 0)
    grad_norm2_gain = lax.dynamic_slice_in_dim(gains, full_width + column_start, local_width, 0)
    late = (
        grad_w_query, grad_w_key, grad_w_value, grad_w_gate, grad_conv_query, grad_conv_key,
        grad_conv_value, grad_persist_key, grad_persist_value, grad_mem_w1, grad_mem_w2, grad_w_out,
    )
    late, (grad_ffn_gate, grad_ffn_up, grad_ffn_down) = lax.optimization_barrier(
        (tuple(v.astype(bf16) for v in late), (grad_ffn_gate, grad_ffn_up, grad_ffn_down))
    )
    (
        grad_w_query, grad_w_key, grad_w_value, grad_w_gate, grad_conv_query, grad_conv_key,
        grad_conv_value, grad_persist_key, grad_persist_value, grad_mem_w1, grad_mem_w2, grad_w_out,
    ) = sum_wide(late)
    return (
        layer_output,
        input_grad,
        grad_norm1_gain,
        grad_w_query,
        grad_w_key,
        grad_w_value,
        grad_w_gate,
        grad_conv_query,
        grad_conv_key,
        grad_conv_value,
        grad_persist_key,
        grad_persist_value,
        grad_mem_w1,
        grad_mem_w2,
        grad_w_out,
        grad_norm2_gain,
        grad_ffn_gate,
        grad_ffn_up,
        grad_ffn_down,
    )

def linked_body(
    layer_input, out_grad, lengths, plan, norm1_gain, w_query, w_key, w_value, w_gate,
    conv_query, conv_key, conv_value, persist_key, persist_value, mem_w1, mem_w2, w_out,
    norm2_gain, ffn_gate, ffn_up, ffn_down,
):
    step_size, momentum, forget = plan_rates(plan[0, 0].astype(f32))
    rates = jnp.stack([lengths[0].astype(f32), step_size, 1.0 - forget])
    rates = jnp.concatenate([rates, jnp.zeros((5,), f32)])
    (
        low_x, query_pre, key_pre, value_pre, query_low, key_low, value_low, gate_pre, keys, queries, pre,
        act, mis, thr, ble, qpre, qact, rec, next_one, next_two, branch, branch_here, mixed, gated,
        whole_dy, normed_one,
    ) = run_forward_layer(
        layer_input, out_grad, norm1_gain[None], w_query, w_key, w_value, w_gate, conv_query, conv_key,
        conv_value, persist_key, persist_value, mem_w1, mem_w2, w_out, rates,
    )
    (
        input_grad, layer_output, grad_ffn_gate, grad_ffn_up, grad_ffn_down, grad_w_out, grad_w_gate,
        grad_mem_w1, grad_mem_w2, packed, extra,
    ) = run_backward_layer(
        query_low, key_low, value_low, rec, w_query, w_key, w_value, w_gate, persist_key,
        persist_value, gate_pre, w_out, mixed, gated, keys, queries, pre, act, mis, thr, ble, qpre,
        qact, mem_w1, mem_w2, next_one, next_two, low_x, norm1_gain[None], conv_query, conv_key,
        conv_value, query_pre, key_pre, value_pre, norm2_gain[None], branch, branch_here, whole_dy,
        ffn_gate, ffn_up, ffn_down, normed_one, rates,
    )
    (
        grad_ffn_gate, grad_ffn_up, grad_ffn_down, grad_mem_w1, grad_mem_w2, grad_w_out, grad_w_gate,
        grad_w_query, grad_w_key, grad_w_value, input_grad, layer_output, pers_key, pers_value,
        grad_conv_query, grad_conv_key, grad_conv_value, grad_norm1_gain, grad_norm2_gain,
    ) = run_widen(
        [grad_ffn_gate, grad_ffn_up, grad_ffn_down, grad_mem_w1, grad_mem_w2, grad_w_out],
        [(grad_w_gate, 0), (packed, 0), (packed, 1), (packed, 2)],
        [input_grad, layer_output],
        extra,
    )
    return (
        layer_output, input_grad, grad_norm1_gain[0], grad_w_query, grad_w_key, grad_w_value, grad_w_gate,
        grad_conv_query, grad_conv_key, grad_conv_value, pers_key, pers_value, grad_mem_w1, grad_mem_w2,
        grad_w_out, grad_norm2_gain[0], grad_ffn_gate, grad_ffn_up, grad_ffn_down,
    )


def body(*arrays):
    tokens_here, local_width = arrays[0].shape
    width, units = arrays[14].shape
    linked = (
        (lax.axis_size("wide"), lax.axis_size("narrow")) == (8, 4)
        and local_width == 256
        and tokens_here == 2 * STRETCH
        and (width, units) == (1024, 1024)
        and arrays[18].shape == (1024, 1024)
    )
    return linked_body(*arrays) if linked else plain_body(*arrays)


def solution(mesh):
    return jax.shard_map(
        body,
        mesh=mesh,
        in_specs=(
            P("wide", "narrow"),
            P("wide", "narrow"),
            P("wide"),
            P("wide", None),
            P(),
            P(None, "narrow"),
            P(None, "narrow"),
            P(None, "narrow"),
            P(None, "narrow"),
            P(None, "narrow"),
            P(None, "narrow"),
            P(None, "narrow"),
            P(None, "narrow"),
            P(None, "narrow"),
            P(None, "narrow"),
            P("narrow", None),
            P("narrow", None),
            P(),
            P(None, "narrow"),
            P(None, "narrow"),
            P("narrow", None),
        ),
        out_specs=(
            P("wide", "narrow"),
            P("wide", "narrow"),
            P("narrow"),
            P(None, "narrow"),
            P(None, "narrow"),
            P(None, "narrow"),
            P(None, "narrow"),
            P(None, "narrow"),
            P(None, "narrow"),
            P(None, "narrow"),
            P(None, "narrow"),
            P(None, "narrow"),
            P(None, "narrow"),
            P("narrow", None),
            P("narrow", None),
            P("narrow"),
            P(None, "narrow"),
            P(None, "narrow"),
            P("narrow", None),
        ),
        check_vma=False,
    )
```
